32 devices in a mesh: ctx: 16 (over z, y, core), wsh: 2 (over x).
Axes of the slice: x: 2, y: 2, z: 4, core: 2. Of those that a mesh axis runs over, the one named last changes fastest.
Arguments:
- tokens: bfloat16 [2, 2, 1024, 1024], P('wsh', None, 'ctx'), may hold values from -6 to 6
- w_query: bfloat16 [1024, 1024], P('wsh'), may hold values from -0.75 to 0.75
- w_key: bfloat16 [1024, 512], P('wsh'), may hold values from -0.75 to 0.75
- w_value: bfloat16 [1024, 512], P('wsh'), may hold values from -0.375 to 0.375
- w_output: bfloat16 [1024, 1024], P('wsh'), may hold values from -1.5 to 1.5
- attn_gain: bfloat16 [1024], P('wsh'), may hold values from 0.099609375 to 1.8984375
- w_router: bfloat16 [1024, 16], P('wsh'), may hold values from -0.09375 to 0.09375
- expert_in: bfloat16 [16, 1024, 2, 512], P(None, None, None, 'wsh'), may hold values from -0.375 to 0.375
- expert_out: bfloat16 [16, 1024, 512], P(None, None, 'wsh'), may hold values from -0.5 to 0.5
- moe_gain: bfloat16 [1024], P('wsh'), may hold values from 0.099609375 to 1.8984375
- segments: int32 [2, 2048], P('wsh'), may hold values from 0 to 2, as said below
- routes: int32 [2, 2, 1024, 8], P('wsh', None, 'ctx'), may hold values from 0 to 15, all different within a row
- priority: int32 [2, 2, 1024, 8], P('wsh', None, 'ctx'), may hold values from 0 to 65535
- cotangent: bfloat16 [2, 2, 1024, 1024], P('wsh', None, 'ctx'), may hold values from -6 to 6
Outputs:
- output: bfloat16 [2, 2, 1024, 1024], P('wsh', None, 'ctx')
- grad_tokens: float32 [2, 2, 1024, 1024], P('wsh', None, 'ctx')
- grad_w_query: float32 [1024, 1024], P(('ctx', 'wsh'))
- grad_w_key: float32 [1024, 512], P(('ctx', 'wsh'))
- grad_w_value: float32 [1024, 512], P(('ctx', 'wsh'))
- grad_w_output: float32 [1024, 1024], P(('ctx', 'wsh'))
- grad_attn_gain: float32 [1024], P(('ctx', 'wsh'))
- grad_w_router: float32 [1024, 16], P(('ctx', 'wsh'))
- grad_expert_in: float32 [16, 1024, 2, 512], P(None, ('ctx', 'wsh'))
- grad_expert_out: float32 [16, 1024, 512], P(None, ('ctx', 'wsh'))
- grad_moe_gain: float32 [1024], P(('ctx', 'wsh'))
The draws below stay inside these ranges and needn't reach their ends.
Inputs may be any that keep to these rules, and one draw needn't show every extreme that they name: `segments`: each row numbers one sequence's 3 documents: ids start at 0 and rise by one at each new document; every document holds 102 to 1024 tokens, and one or more hold exactly 1024. `routes`: each token names 8 different experts.
All inputs are finite; a program needn't handle non-finite values.
Results may differ from the reference program's by a relative error of at most 0.02.
Values may be sent and summed in bfloat16 or wider, within the bound.
A program may use at most 320 MiB of HBM per device.

```python
import jax
import jax.numpy as jnp
from jax import lax

D = 1024
HEADS = 16
KV_HEADS = 8
HEAD_DIM = 64
FF = 512
TOPK = 8
EXPERTS = 16
BLK = 64
SEQS = 2
HALF = 1024
SEQLEN = 2048
CAP = 80
DOC_MAX = 1024
DOC_MIN = 102
N_CTX = 16


def length_table():
    mean_length = (DOC_MIN + DOC_MAX) // 2
    long_count = max(1, SEQLEN // (3 * DOC_MAX))
    rest_rows = SEQLEN - long_count * DOC_MAX
    short_count = (rest_rows + mean_length - 1) // mean_length
    short_lengths = [rest_rows * (member + 1) // short_count - rest_rows * member // short_count for member in range(short_count)]
    for pair_id in range(short_count // 2):
        first_len = short_lengths[2 * pair_id]
        second_len = short_lengths[2 * pair_id + 1]
        room_left = min(first_len - DOC_MIN, DOC_MAX - 1 - first_len, second_len - DOC_MIN, DOC_MAX - 1 - second_len)
        moved = (pair_id * 37 + 11) % (room_left + 1)
        short_lengths[2 * pair_id] = first_len - moved
        short_lengths[2 * pair_id + 1] = second_len + moved
    return [DOC_MAX] * long_count + short_lengths


def one_packing(key):
    table = jnp.array(length_table(), dtype=jnp.int32)
    order = jax.random.permutation(key, table.shape[0])
    doc_lengths = table[order]
    doc_starts = jnp.cumsum(doc_lengths) - doc_lengths
    start_marks = jnp.zeros((SEQLEN,), jnp.int32).at[doc_starts[1:]].set(1)
    return jnp.cumsum(start_marks).astype(jnp.int32)


def draw_segments(key, part):
    return jnp.stack([one_packing(jax.random.fold_in(key, member)) for member in range(SEQS)]).astype(jnp.int32)


def set_ends(drawn, rng, smallest, largest):
    extent = drawn.shape
    index_at = [jax.random.randint(jax.random.fold_in(rng, axis), (), 0, extent[axis]) for axis in range(len(extent))]
    drawn = drawn.at[tuple(index_at)].set(smallest)
    longest = extent.index(max(extent))
    index_at[longest] = (index_at[longest] + 1) % extent[longest]
    return drawn.at[tuple(index_at)].set(largest)


def block_levels(key, dims, pieces, least, top_value):
    level, own = 1.0, jax.random.fold_in(key, 6)
    for axis_at, blocks in pieces:
        steps = jnp.exp(jax.random.uniform(jax.random.fold_in(own, axis_at), (blocks,), jnp.float32, least / len(pieces), top_value / len(pieces)))
        level = level * jnp.repeat(steps, dims[axis_at] // blocks).reshape([-1 if axis == axis_at else 1 for axis in range(len(dims))])
    return level


def distinct(rng, rows, number_of, top, lift):
    ranking = jax.random.permutation(jax.random.fold_in(rng, 1), number_of)
    pull = ranking
    for power in range(3):
        pull = pull * pull // number_of
    pull = pull * lift // number_of
    tickets = jax.random.randint(jax.random.fold_in(rng, 2), (rows, number_of), 0, 4096) + pull
    sure = jax.random.permutation(jax.random.fold_in(rng, 3), rows)[jnp.arange(number_of) % rows]
    tickets = jnp.where(jnp.arange(rows)[:, None] == sure[None, :], 1 << 14, tickets)
    merit = tickets * number_of + jnp.arange(number_of)
    return lax.top_k(merit.astype(jnp.int32), top)[1].astype(jnp.int32)


def normal_values(key, extent, spread, limit, shards=(), held_as=jnp.bfloat16):
    values = jax.random.normal(key, extent, jnp.float32) * spread
    if len(shards) > 0:
        values = block_levels(key, extent, shards, -0.22, 0.18) * values
    return jnp.clip(values, min=-limit, max=limit).astype(held_as)


def setup_inputs(seed: int = 0) -> dict:
    keys = jax.random.split(jax.random.key(seed), 15)
    return {
        "tokens": normal_values(keys[0], (SEQS, 2, HALF, D), 1.0, 6.0, ((0, 2), (2, 16))),
        "w_query": normal_values(keys[1], (D, HEADS * HEAD_DIM), (D // 16) ** -0.5, 0.75, ((0, 2),)),
        "w_key": normal_values(keys[2], (D, KV_HEADS * HEAD_DIM), (D // 16) ** -0.5, 0.75, ((0, 2),)),
        "w_value": normal_values(keys[3], (D, KV_HEADS * HEAD_DIM), (D // 4) ** -0.5, 0.375, ((0, 2),)),
        "w_output": normal_values(keys[4], (HEADS * HEAD_DIM, D), 16 ** -0.5, 1.5, ((0, 2),)),
        "attn_gain": jnp.clip(1.0 + 0.18 * jax.random.normal(keys[5], (D,), jnp.float32), 0.099609375, 1.8984375).astype(jnp.bfloat16),
        "w_router": normal_values(keys[6], (D, EXPERTS), (4 * D) ** -0.5, 0.09375, ((0, 2),)),
        "expert_in": normal_values(keys[7], (EXPERTS, D, 2, FF), (D // 4) ** -0.5, 0.375, ((3, 2),)),
        "expert_out": normal_values(keys[8], (EXPERTS, D, FF), (FF // 4) ** -0.5, 0.5, ((2, 2),)),
        "moe_gain": jnp.clip(1.0 + 0.18 * jax.random.normal(keys[9], (D,), jnp.float32), 0.099609375, 1.8984375).astype(jnp.bfloat16),
        "segments": draw_segments(jax.random.fold_in(keys[14], 71), 0),
        "routes": distinct(keys[11], SEQS * 2 * HALF, EXPERTS, TOPK, 4096).reshape((SEQS, 2, HALF, TOPK)),
        "priority": set_ends(jax.random.randint(keys[12], (SEQS, 2, HALF, TOPK), 0, 65536), jax.random.fold_in(keys[12], 1), 0, 65535).astype(jnp.int32),
        "cotangent": normal_values(keys[13], (SEQS, 2, HALF, D), 1.0, 6.0, ((0, 2), (2, 16))),
    }


@jax.custom_vjp
def low(v):
    return lax.optimization_barrier(v.astype(jnp.bfloat16)).astype(jnp.float32)

@jax.custom_vjp
def low_back(v):
    return v

def low_keep(v):
    return (low(v), None)

def low_pass(kept, grad):
    return (grad,)

def back_keep(v):
    return (v, None)

def back_low(kept, grad):
    return (low(grad),)
low.defvjp(low_keep, low_pass)
low_back.defvjp(back_keep, back_low)
RES_MULT = 0.22
ATT_MULT = 0.015625
EPS = 1e-06
THETA = 10000.0
HIGH = lax.Precision.HIGHEST

def rms_norm(values):
    return values * lax.rsqrt(lax.optimization_barrier(jnp.mean(values * values, axis=-1, keepdims=True)) + EPS)

def rotate(values, position, sign):
    half_dim = values.shape[-1] // 2
    frequency = jnp.exp(-jnp.log(jnp.float32(THETA)) * jnp.arange(half_dim, dtype=jnp.float32) * (2.0 / values.shape[-1]))
    angles = position.astype(jnp.float32)[:, None] * frequency[None, :]
    cosine = jnp.cos(angles)[:, None, :]
    sine_part = sign * jnp.sin(angles)[:, None, :]
    lower_part = values[..., :half_dim]
    upper_part = values[..., half_dim:]
    return jnp.concatenate([lower_part * cosine - upper_part * sine_part, upper_part * cosine + lower_part * sine_part], axis=-1)

def to_sequence(array_in):
    row_width = array_in.shape[-1]
    upper_half = array_in[:, 1].reshape(SEQS, N_CTX, BLK, row_width)[:, ::-1].reshape(SEQS, HALF, row_width)
    return jnp.concatenate([array_in[:, 0], upper_half], axis=1)

def to_layout(array_in):
    row_width = array_in.shape[-1]
    upper_half = array_in[:, HALF:].reshape(SEQS, N_CTX, BLK, row_width)[:, ::-1].reshape(SEQS, HALF, row_width)
    return jnp.stack([array_in[:, :HALF], upper_half], axis=1)

def to_groups(array_in):
    trailing = array_in.shape[3:]
    shaped = array_in.reshape((SEQS, 2, N_CTX, BLK) + trailing)
    axes_order = (0, 2, 1, 3) + tuple(range(4, 4 + len(trailing)))
    return shaped.transpose(axes_order).reshape((SEQS * N_CTX, 2 * BLK) + trailing)

def from_groups(array_in):
    trailing = array_in.shape[2:]
    shaped = array_in.reshape((SEQS, N_CTX, 2, BLK) + trailing)
    axes_order = (0, 2, 1, 3) + tuple(range(4, 4 + len(trailing)))
    return shaped.transpose(axes_order).reshape((SEQS, 2, HALF) + trailing)

def attend(queries, keys_in, values_in, segment_ids):
    length = queries.shape[0]
    query_block = min(512, length)
    positions = jnp.arange(length, dtype=jnp.int32)
    group_size = HEADS // KV_HEADS
    blocked = queries.reshape(length // query_block, query_block, KV_HEADS, group_size, HEAD_DIM)

    def one_block(inputs):
        query_rows, query_pos, query_seg = inputs
        scores = low_back(jnp.einsum('qgrd,kgd->grqk', query_rows, keys_in, precision=HIGH))
        allowed = (query_seg[:, None] == segment_ids[None, :]) & (positions[None, :] <= query_pos[:, None])
        exp_values = jnp.where(allowed, jnp.exp(ATT_MULT * scores), 0.0)
        totals = lax.optimization_barrier(jnp.sum(exp_values, axis=-1))
        numerator = low_back(jnp.einsum('grqk,kgd->grqd', low(exp_values), values_in, precision=HIGH))
        return (numerator / totals[..., None]).transpose(2, 0, 1, 3)
    outputs = lax.map(jax.checkpoint(one_block), (blocked, positions.reshape(-1, query_block), segment_ids.reshape(-1, query_block)))
    return outputs.reshape(length, HEADS * HEAD_DIM)

def assign_slots(inputs):
    route_rows, prio_rows = inputs
    expert_ids = route_rows.reshape(-1)
    prio_flat = prio_rows.reshape(-1)
    order_ids = jnp.arange(expert_ids.shape[0], dtype=jnp.int32)
    same_expert = expert_ids[None, :] == expert_ids[:, None]
    earlier = (prio_flat[None, :] < prio_flat[:, None]) | (prio_flat[None, :] == prio_flat[:, None]) & (order_ids[None, :] < order_ids[:, None])
    rank_in = lax.optimization_barrier(jnp.sum((same_expert & earlier).astype(jnp.int32), axis=1))
    kept_flat = rank_in < CAP
    slot_ids = expert_ids * CAP + rank_in
    target = jnp.where(kept_flat, slot_ids, EXPERTS * CAP)
    slot_token = jnp.zeros((EXPERTS * CAP,), jnp.int32).at[target].set(order_ids // TOPK, mode='drop')
    slot_filled = jnp.zeros((EXPERTS * CAP,), jnp.int32).at[target].set(1, mode='drop')
    slot_pick = jnp.where(kept_flat, slot_ids, 0).reshape(route_rows.shape)
    return (kept_flat.reshape(route_rows.shape), slot_pick, slot_token, slot_filled)

def moe_group(inputs, inner_w, outer_w):
    hidden_in, logit_rows, route_rows, kept_mask, slot_pick, slot_token, slot_filled = inputs
    onehot = (route_rows[:, :, None] == jnp.arange(EXPERTS, dtype=jnp.int32)[None, None, :]).astype(jnp.float32)
    picked = lax.optimization_barrier(jnp.sum(onehot * logit_rows[:, None, :], axis=-1))
    gate_prob = jax.nn.softmax(picked, axis=-1)
    weight_kept = gate_prob * kept_mask.astype(jnp.float32)
    expert_rows = jnp.where(slot_filled[:, None] > 0, hidden_in[slot_token], 0.0).reshape(EXPERTS, CAP, D)
    gate_up = low_back(jnp.einsum('ecd,edhf->echf', expert_rows, inner_w, precision=HIGH))
    activation = low(jax.nn.silu(gate_up[:, :, 0]) * gate_up[:, :, 1])
    expert_rows_out = low_back(jnp.einsum('ecf,edf->ecd', activation, outer_w, precision=HIGH)).reshape(EXPERTS * CAP, D)
    return lax.optimization_barrier(jnp.sum(weight_kept[:, :, None] * expert_rows_out[slot_pick], axis=1))

def reference(tokens, w_query, w_key, w_value, w_output, attn_gain, w_router, expert_in, expert_out, moe_gain, segments, routes, priority, cotangent):
    group_routes = to_groups(routes)
    group_prio = to_groups(priority)
    kept_mask, slot_pick, slot_token, slot_filled = lax.map(assign_slots, (group_routes, group_prio))
    positions = jnp.arange(SEQLEN, dtype=jnp.int32)

    def forward(tokens_f, query_w, key_w, value_w, output_w, gain_one, router_w, inner_w, outer_w, gain_two):
        normed = low(rms_norm(tokens_f) * gain_one)
        flat_rows = normed.reshape(-1, D)
        layout_shape = (SEQS, 2, HALF, -1)
        query_lin = low_back(jnp.dot(flat_rows, query_w, precision=HIGH))
        key_lin = low_back(jnp.dot(flat_rows, key_w, precision=HIGH))
        value_lin = low(low_back(jnp.dot(flat_rows, value_w, precision=HIGH)))
        query_seq = to_sequence(query_lin.reshape(layout_shape))
        key_seq = to_sequence(key_lin.reshape(layout_shape))
        value_seq = to_sequence(value_lin.reshape(layout_shape))

        def one_sequence(inputs):
            query_rows, key_rows, value_rows, segment_ids = inputs
            rot_query = low(rotate(query_rows.reshape(SEQLEN, HEADS, HEAD_DIM), positions, 1.0))
            rot_key = low(rotate(key_rows.reshape(SEQLEN, KV_HEADS, HEAD_DIM), positions, 1.0))
            return attend(rot_query, rot_key, value_rows.reshape(SEQLEN, KV_HEADS, HEAD_DIM), segment_ids)
        attended = lax.map(one_sequence, (query_seq, key_seq, value_seq, segments))
        mixed = low(low_back(to_layout(attended))).reshape(-1, HEADS * HEAD_DIM)
        attn_out = low_back(jnp.dot(mixed, output_w, precision=HIGH))
        first_sum = tokens_f + RES_MULT * attn_out.reshape(tokens_f.shape)
        second_in = low(rms_norm(first_sum) * gain_two)
        logits = low_back(jnp.dot(second_in.reshape(-1, D), router_w, precision=HIGH)).reshape(SEQS, 2, HALF, EXPERTS)

        def one_group(inputs):
            return moe_group(inputs, inner_w, outer_w)
        expert_sum = lax.map(one_group, (to_groups(second_in), to_groups(logits), group_routes, kept_mask, slot_pick, slot_token, slot_filled))
        return first_sum + RES_MULT * from_groups(expert_sum)
    result, pullback = jax.vjp(forward, tokens.astype(jnp.float32), w_query.astype(jnp.float32), w_key.astype(jnp.float32), w_value.astype(jnp.float32), w_output.astype(jnp.float32), attn_gain.astype(jnp.float32), w_router.astype(jnp.float32), expert_in.astype(jnp.float32), expert_out.astype(jnp.float32), moe_gain.astype(jnp.float32))
    grads = pullback(cotangent.astype(jnp.float32))
    return (result.astype(jnp.bfloat16), grads[0], grads[1], grads[2], grads[3], grads[4], grads[5], grads[6], grads[7], grads[8], grads[9])
```

```python
import functools
import math

import jax
import jax.numpy as jnp
from jax import lax
from jax.experimental import pallas as pl
from jax.experimental.pallas import tpu as pltpu
from jax.sharding import PartitionSpec as P

D = 1024
HEADS = 16
KV_HEADS = 8
HEAD_DIM = 64
TOPK = 8
EXPERTS = 16
CAP = 80
PLANE = 8
INNER = 4
OWN = EXPERTS // INNER


RES_MULT = 0.22
ATT_MULT = 0.015625
EPS = 1e-06
THETA = 10000.0

MESH = pl.DeviceIdType.MESH
F32 = jnp.float32
BF16 = jnp.bfloat16
ANY = pl.BlockSpec(memory_space=pl.ANY)
VMEM = pl.BlockSpec(memory_space=pltpu.VMEM)


class Place:
    def __init__(self):
        self.c = lax.axis_index("ctx")
        self.w = lax.axis_index("wsh")
        self.core = self.c % 2
        self.y = (self.c // 2) % 2
        self.inner = self.c % INNER
        self.outer = self.c // INNER
        self.j = self.inner * 2 + self.w
        self.sib = self.c + 1 - 2 * self.core
        self.yn = self.c + 2 - 4 * self.y

    def relative(self, dy, dc, dw):
        y = self.y + dy * (1 - 2 * self.y)
        core = self.core + dc * (1 - 2 * self.core)
        w = self.w + dw * (1 - 2 * self.w)
        ctx = self.outer * INNER + y * 2 + core
        return (ctx, w), (y * 2 + core) * 2 + w


OTHERS = [(a, b, d) for a in range(2) for b in range(2) for d in range(2) if a + b + d]
XY = [(0, 0, 1), (1, 0, 0), (1, 0, 1)]


def meet(devices):
    barrier = pltpu.get_barrier_semaphore()
    for device in devices:
        pl.semaphore_signal(barrier, inc=1, device_id=device, device_id_type=MESH)
    pl.semaphore_wait(barrier, len(devices))


def remote(src, dst, send, recv, device):
    return pltpu.make_async_remote_copy(
        src_ref=src,
        dst_ref=dst,
        send_sem=send,
        recv_sem=recv,
        device_id=device,
        device_id_type=MESH,
    )


def comm_call(kernel, out_shape, in_specs, out_specs, scratch, ident, name, vmem=None):
    return pl.pallas_call(
        kernel,
        out_shape=out_shape,
        in_specs=in_specs,
        out_specs=out_specs,
        scratch_shapes=scratch,
        compiler_params=pltpu.CompilerParams(
            collective_id=ident, has_side_effects=True, vmem_limit_bytes=vmem
        ),
        name=name,
    )


DMA = pltpu.SemaphoreType.DMA


def gather_start(at, pairs, send, recv, local):
    copies = []
    for index, (src, dst) in enumerate(pairs):
        keep = pltpu.make_async_copy(src, dst.at[at.j], local.at[index])
        keep.start()
        sends = []
        for slot, bits in enumerate(XY + [(0, 1, 0)]):
            device, unused = at.relative(*bits)
            copy = remote(src, dst.at[at.j], send.at[index, slot], recv.at[index, slot], device)
            copy.start()
            sends.append(copy)
        copies.append((keep, sends))
    return copies


def gather_finish(at, pairs, copies, send, recv):
    sib, unused = at.relative(0, 1, 0)
    passed = []
    for slot, bits in enumerate(XY):
        unused, j_from = at.relative(*bits)
        for index, (src, dst) in enumerate(pairs):
            copies[index][1][slot].wait_recv()
            copy = remote(
                dst.at[j_from],
                dst.at[j_from],
                send.at[index, 4 + slot],
                recv.at[index, 4 + slot],
                sib,
            )
            copy.start()
            passed.append(copy)
    for keep, sends in copies:
        keep.wait()
        sends[3].wait_recv()
        for copy in sends:
            copy.wait_send()
    for copy in passed:
        copy.wait()


def plane_gather_kernel(count, *refs):
    ins, outs = refs[:count], refs[count : 2 * count]
    send, recv, local = refs[2 * count :]
    at = Place()
    meet([at.relative(*bits)[0] for bits in XY + [(0, 1, 0)]])
    pairs = list(zip(ins, outs))
    copies = gather_start(at, pairs, send, recv, local)
    gather_finish(at, pairs, copies, send, recv)


def plane_gather(arrays, ident, name):
    count = len(arrays)
    return comm_call(
        functools.partial(plane_gather_kernel, count),
        [jax.ShapeDtypeStruct((PLANE,) + a.shape, a.dtype) for a in arrays],
        [ANY] * count,
        [ANY] * count,
        [DMA((count, 7)), DMA((count, 7)), DMA((count,))],
        ident,
        name,
    )(*arrays)


def weights_kernel(
    wq, wk, wv, wo, small, cot, wqkv_o, wo_o, small_o, cot_o, xs, xr, fs, fr, ls, gs, gr, gl
):
    at = Place()
    meet([at.relative(*bits)[0] for bits in XY + [(0, 1, 0)]])
    partner, unused = at.relative(0, 0, 1)
    sib, unused = at.relative(0, 1, 0)
    pieces = [(wq, wqkv_o, 0), (wk, wqkv_o, 1024), (wv, wqkv_o, 1536), (wo, wo_o, 0)]
    locals_, sends, passed = [], [], []
    for index, (src, dst, col) in enumerate(pieces):
        depth, width = src.shape
        half = depth // 2
        row = at.w * depth + at.core * half
        copy = remote(
            src.at[pl.ds(at.core * half, half), :],
            dst.at[pl.ds(row, half), pl.ds(col, width)],
            xs.at[index],
            xr.at[index],
            partner,
        )
        copy.start()
        sends.append(copy)
        keep = pltpu.make_async_copy(
            src, dst.at[pl.ds(at.w * depth, depth), pl.ds(col, width)], ls.at[index]
        )
        keep.start()
        locals_.append(keep)
    last = len(pieces)
    copy = remote(small, small_o.at[at.w], xs.at[last], xr.at[last], partner)
    copy.start()
    sends.append(copy)
    keep = pltpu.make_async_copy(small, small_o.at[at.w], ls.at[last])
    keep.start()
    locals_.append(keep)
    pairs = [(cot, cot_o)]
    copies = gather_start(at, pairs, gs, gr, gl)
    for index, (src, dst, col) in enumerate(pieces):
        depth, width = src.shape
        half = depth // 2
        row = (1 - at.w) * depth + at.core * half
        sends[index].wait_recv()
        piece = dst.at[pl.ds(row, half), pl.ds(col, width)]
        copy = remote(piece, piece, fs.at[index], fr.at[index], sib)
        copy.start()
        passed.append(copy)
    sends[last].wait_recv()
    gather_finish(at, pairs, copies, gs, gr)
    for copy in sends:
        copy.wait_send()
    for copy in passed:
        copy.wait()
    for keep in locals_:
        keep.wait()


def gather_weights(wq, wk, wv, wo, small, cot):
    shape = jax.ShapeDtypeStruct
    return comm_call(
        weights_kernel,
        [
            shape((D, 2048), BF16),
            shape((D, D), BF16),
            shape((2,) + small.shape, BF16),
            shape((PLANE,) + cot.shape, BF16),
        ],
        [ANY] * 6,
        [ANY] * 4,
        [DMA((5,)), DMA((5,)), DMA((4,)), DMA((4,)), DMA((5,)), DMA((1, 7)), DMA((1, 7)), DMA((1,))],
        1,
        "gather_weights",
    )(wq, wk, wv, wo, small, cot)


def kv_gather_kernel(outers, own, full, zs, zr, ys, yr, cs, cr, local):
    at = Place()
    sib, unused = at.relative(0, 1, 0)
    side, unused = at.relative(1, 0, 0)
    other = [lax.rem(at.outer + r, outers) for r in range(outers)]
    back = [lax.rem(at.outer + outers - r, outers) for r in range(outers)]
    far = [(other[r] * INNER + at.inner, at.w) for r in range(1, outers)]
    meet([sib, side] + far)
    keep = pltpu.make_async_copy(own, full.at[:, at.c], local)
    keep.start()
    mine = full.at[:, at.c]
    waits = []
    zs_copies = []
    for r in range(1, outers):
        copy = remote(own, mine, zs.at[r], zr.at[r], far[r - 1])
        copy.start()
        zs_copies.append(copy)
        waits.append(copy)
    y_copies, c_copies = [], []
    for ref, sems, into, device in ((ys, yr, y_copies, side), (cs, cr, c_copies, sib)):
        copy = remote(own, mine, ref.at[0], sems.at[0], device)
        copy.start()
        into.append(copy)
    for r in range(1, outers):
        zs_copies[r - 1].wait_recv()
        block = full.at[:, back[r] * INNER + at.inner]
        for ref, sems, into, device in ((ys, yr, y_copies, side), (cs, cr, c_copies, sib)):
            copy = remote(block, block, ref.at[r], sems.at[r], device)
            copy.start()
            into.append(copy)
    inner_side = at.inner + 2 - 4 * at.y
    for r in range(outers):
        y_copies[r].wait_recv()
        block = full.at[:, back[r] * INNER + inner_side]
        copy = remote(block, block, cs.at[outers + r], cr.at[outers + r], sib)
        copy.start()
        c_copies.append(copy)
    for copy in zs_copies + y_copies:
        copy.wait_send()
    for copy in c_copies:
        copy.wait()
    keep.wait()


def kv_gather(own, ctx_count):
    outers = ctx_count // INNER
    return comm_call(
        functools.partial(kv_gather_kernel, outers),
        jax.ShapeDtypeStruct((2, ctx_count) + own.shape[1:], own.dtype),
        [ANY],
        ANY,
        [DMA((outers,))] * 4 + [DMA((2 * outers,))] * 2 + [DMA],
        2,
        "kv_gather",
    )(own)


def kv_reduce_kernel(outers, part, out, half_in, half_sum, y_in, y_sum, z_in, ss, sr, ys, yr, zs, zr):
    at = Place()
    sib, unused = at.relative(0, 1, 0)
    side, unused = at.relative(1, 0, 0)
    other = [lax.rem(at.outer + r, outers) for r in range(outers)]
    far = [(other[r] * INNER + at.inner, at.w) for r in range(1, outers)]
    meet([sib, side] + far)
    width = part.shape[-1] // 2
    first = []
    for k in range(2):
        cols = pl.ds(k * width, width)
        copy = remote(
            part.at[:, :, :, 1 - at.core, :, cols], half_in.at[:, :, :, :, cols], ss.at[k], sr.at[k], sib
        )
        copy.start()
        first.append(copy)
    second = []
    for k in range(2):
        cols = pl.ds(k * width, width)
        first[k].wait_recv()
        for o in range(outers):
            for y in range(2):
                for h in range(2):
                    total = part[h, o, y, at.core, :, cols].astype(F32) + half_in[
                        h, o, y, :, cols
                    ].astype(F32)
                    half_sum[y, h, o, :, cols] = total.astype(BF16)
        copy = remote(
            half_sum.at[1 - at.y, :, :, :, cols], y_in.at[:, :, :, cols], ys.at[k], yr.at[k], side
        )
        copy.start()
        second.append(copy)
    third = []
    for k in range(2):
        cols = pl.ds(k * width, width)
        second[k].wait_recv()
        for o in range(outers):
            for h in range(2):
                total = half_sum[at.y, h, o, :, cols].astype(F32) + y_in[h, o, :, cols].astype(F32)
                y_sum[o, h, :, cols] = total.astype(BF16)
        for r in range(1, outers):
            copy = remote(
                y_sum.at[other[r], :, :, cols],
                z_in.at[r, :, :, cols],
                zs.at[k, r],
                zr.at[k, r],
                far[r - 1],
            )
            copy.start()
            third.append(copy)
    for copy in third:
        copy.wait_recv()
    total = y_sum[at.outer].astype(F32)
    for r in range(1, outers):
        total = total + z_in[r].astype(F32)
    out[...] = total
    for copy in first + second + third:
        copy.wait_send()


def kv_reduce(part, ctx_count):
    outers = ctx_count // INNER
    rows, width = part.shape[-2:]
    return comm_call(
        functools.partial(kv_reduce_kernel, outers),
        jax.ShapeDtypeStruct((2, rows, width), F32),
        [VMEM],
        VMEM,
        [
            pltpu.VMEM((2, outers, 2, rows, width), BF16),
            pltpu.VMEM((2, 2, outers, rows, width), BF16),
            pltpu.VMEM((2, outers, rows, width), BF16),
            pltpu.VMEM((outers, 2, rows, width), BF16),
            pltpu.VMEM((outers, 2, rows, width), BF16),
            DMA((2,)),
            DMA((2,)),
            DMA((2,)),
            DMA((2,)),
            DMA((2, outers)),
            DMA((2, outers)),
        ],
        3,
        "kv_reduce",
        vmem=60 * 2**20,
    )(part.reshape(2, outers, 2, 2, rows, width))


def plane_reduce_kernel(count, *refs):
    parts, picks = refs[:count], refs[count]
    outs, picks_o = refs[count + 1 : 2 * count + 1], refs[2 * count + 1]
    near, summed, far, ss, sr, xs, xr, ps, pr, pl_sem = refs[2 * count + 2 :]
    at = Place()
    meet([at.relative(*bits)[0] for bits in OTHERS])
    sib, unused = at.relative(0, 1, 0)
    first = []
    for index in range(count):
        copy = remote(
            parts[index].at[:, 1 - at.core], near.at[index], ss.at[index], sr.at[index], sib
        )
        copy.start()
        first.append(copy)
    keep = pltpu.make_async_copy(picks.at[at.j], picks_o.at[at.j], pl_sem)
    keep.start()
    small = []
    for slot, bits in enumerate(OTHERS):
        device, j_to = at.relative(*bits)
        copy = remote(picks.at[j_to], picks_o.at[at.j], ps.at[slot], pr.at[slot], device)
        copy.start()
        small.append(copy)
    second = []
    for index in range(count):
        first[index].wait_recv()
        for y in range(2):
            for w in range(2):
                total = parts[index][y, at.core, w].astype(F32) + near[index, y, w].astype(F32)
                summed[index, y, w] = total.astype(BF16)
        for slot, (dy, dc, dw) in enumerate(XY):
            device, unused = at.relative(dy, dc, dw)
            y = at.y + dy * (1 - 2 * at.y)
            w = at.w + dw * (1 - 2 * at.w)
            copy = remote(
                summed.at[index, y, w], far.at[index, slot], xs.at[index, slot], xr.at[index, slot], device
            )
            copy.start()
            second.append(copy)
    for index in range(count):
        total = parts[index][at.y, at.core, at.w].astype(F32) + near[index, at.y, at.w].astype(F32)
        for slot in range(3):
            second[index * 3 + slot].wait_recv()
            total = total + far[index, slot].astype(F32)
        outs[index][...] = total
    keep.wait()
    for copy in small:
        copy.wait()
    for copy in first + second:
        copy.wait_send()


def plane_reduce(parts, picks, ident, name):
    count = len(parts)
    rows, width = parts[0].shape[-2:]
    shape = jax.ShapeDtypeStruct
    return comm_call(
        functools.partial(plane_reduce_kernel, count),
        [shape((rows, width), F32)] * count + [shape(picks.shape, picks.dtype)],
        [VMEM] * (count + 1),
        [VMEM] * (count + 1),
        [
            pltpu.VMEM((count, 2, 2, rows, width), BF16),
            pltpu.VMEM((count, 2, 2, rows, width), BF16),
            pltpu.VMEM((count, 3, rows, width), BF16),
            DMA((count,)),
            DMA((count,)),
            DMA((count, 3)),
            DMA((count, 3)),
            DMA((7,)),
            DMA((7,)),
            DMA,
        ],
        ident,
        name,
        vmem=60 * 2**20,
    )(*[p.reshape(2, 2, 2, rows, width) for p in parts], picks)


def plane_swap_kernel(src, gather_in, dst, gather_out, ss, sr, local, gs, gr, gl):
    at = Place()
    meet([at.relative(*bits)[0] for bits in OTHERS])
    keep = pltpu.make_async_copy(src.at[at.j], dst.at[at.j], local)
    keep.start()
    copies = []
    for slot, bits in enumerate(OTHERS):
        device, j_to = at.relative(*bits)
        copy = remote(src.at[j_to], dst.at[at.j], ss.at[slot], sr.at[slot], device)
        copy.start()
        copies.append(copy)
    pairs = [(gather_in, gather_out)]
    started = gather_start(at, pairs, gs, gr, gl)
    gather_finish(at, pairs, started, gs, gr)
    for copy in copies:
        copy.wait()
    keep.wait()


def plane_swap(src, gathered, ident, name):
    shape = jax.ShapeDtypeStruct
    return comm_call(
        plane_swap_kernel,
        [shape(src.shape, src.dtype), shape((PLANE,) + gathered.shape, gathered.dtype)],
        [ANY] * 2,
        [ANY] * 2,
        [DMA((7,)), DMA((7,)), DMA, DMA((1, 7)), DMA((1, 7)), DMA((1,))],
        ident,
        name,
    )(src, gathered)


def owners_kernel(devices, count, *refs):
    parts, outs = refs[:count], refs[count : 2 * count]
    send, recv, local = refs[2 * count :]
    at = Place()
    me = at.c * 2 + at.w
    rows = D // devices

    def device_of(r):
        index = lax.rem(me + r, devices)
        return index, (index // 2, lax.rem(index, 2))

    def rows_of(ref, index):
        block = pl.ds(pl.multiple_of(index * rows, rows), rows)
        return ref.at[:, block, :] if len(ref.shape) == 3 else ref.at[block, :]

    barrier = pltpu.get_barrier_semaphore()

    def greet(r, carry):
        unused, device = device_of(r)
        pl.semaphore_signal(barrier, inc=1, device_id=device, device_id_type=MESH)
        return carry

    lax.fori_loop(1, devices, greet, 0)
    pl.semaphore_wait(barrier, devices - 1)

    keeps = []
    for k in range(count):
        keep = pltpu.make_async_copy(rows_of(parts[k], me), outs[k].at[me], local.at[k])
        keep.start()
        keeps.append(keep)

    def copy_of(k, r):
        index, device = device_of(r)
        return remote(rows_of(parts[k], index), outs[k].at[me], send.at[k, r], recv.at[k, r], device)

    def start(r, carry):
        for k in range(count):
            copy_of(k, r).start()
        return carry

    lax.fori_loop(1, devices, start, 0)

    def finish(r, carry):
        for k in range(count):
            copy_of(k, r).wait()
        return carry

    lax.fori_loop(1, devices, finish, 0)
    for keep in keeps:
        keep.wait()


def owners(parts, devices, ident, name):
    count = len(parts)
    rows = D // devices
    shapes = []
    for part in parts:
        lead = part.shape[:-2]
        shapes.append(
            jax.ShapeDtypeStruct((devices,) + lead + (rows, part.shape[-1]), part.dtype)
        )
    return comm_call(
        functools.partial(owners_kernel, devices, count),
        shapes,
        [ANY] * count,
        [ANY] * count,
        [DMA((count, devices)), DMA((count, devices)), DMA((count,))],
        ident,
        name,
    )(*parts)


def rms_scale(values):
    return lax.rsqrt(jnp.mean(values * values, axis=-1, keepdims=True) + EPS)


def rotate(values, position, sign):
    half_dim = values.shape[-1] // 2
    frequency = jnp.exp(
        -jnp.log(jnp.float32(THETA))
        * jnp.arange(half_dim, dtype=jnp.float32)
        * (2.0 / values.shape[-1])
    )
    angles = position.astype(jnp.float32)[:, None] * frequency[None, :]
    cosine = jnp.cos(angles)[:, None, :]
    sine_part = sign * jnp.sin(angles)[:, None, :]
    lower_part = values[..., :half_dim]
    upper_part = values[..., half_dim:]
    return jnp.concatenate(
        [
            lower_part * cosine - upper_part * sine_part,
            upper_part * cosine + lower_part * sine_part,
        ],
        axis=-1,
    )


def seq_position(row_ids, block_rows, ctx_count, half_ids):
    return jnp.where(
        half_ids == 0,
        row_ids,
        (2 * ctx_count - 1 - row_ids // block_rows) * block_rows + row_ids % block_rows,
    )


def span_for(row_count):
    return math.gcd(row_count, 1024)


def keep_state(state):
    return state


def body(
    tokens,
    w_query,
    w_key,
    w_value,
    w_output,
    attn_gain,
    w_router,
    expert_in,
    expert_out,
    moe_gain,
    segments,
    routes,
    priority,
    cotangent,
):
    ctx_count = lax.axis_size("ctx")
    ctx_index = lax.axis_index("ctx")
    devices = ctx_count * 2
    outers = ctx_count // INNER
    owner_rows = D // devices
    block_rows = tokens.shape[2]
    half_rows = block_rows * ctx_count
    tok_count = 2 * block_rows
    plane_rows = PLANE * tok_count
    group_size = HEADS // KV_HEADS
    kv_width = KV_HEADS * HEAD_DIM
    f32 = jnp.float32
    bf16 = jnp.bfloat16
    first_expert = (ctx_index % INNER) * OWN

    small = jnp.concatenate(
        [w_router.T, attn_gain[None], moe_gain[None], jnp.zeros((14, w_router.shape[0]), bf16)]
    )
    cot_own = cotangent.reshape(tok_count, D)
    qkv_w, output_w, small_all, cot_all = gather_weights(
        w_query, w_key, w_value, w_output, small, cot_own
    )
    small_all = small_all.transpose(1, 0, 2).reshape(32, D)
    router_t = small_all[:EXPERTS]
    gain_one_f = small_all[EXPERTS].astype(f32)
    gain_two_f = small_all[EXPERTS + 1].astype(f32)

    token_rows = tokens.reshape(tok_count, D).astype(f32)
    scale_one = rms_scale(token_rows)
    normed_one = token_rows * scale_one
    hidden_one = (normed_one * gain_one_f).astype(bf16)
    qkv_lin = jnp.dot(hidden_one, qkv_w, preferred_element_type=f32)
    half_ids = jnp.arange(2, dtype=jnp.int32)[:, None]
    local_rows = ctx_index * block_rows + jnp.arange(block_rows, dtype=jnp.int32)
    query_pos = seq_position(local_rows[None, :], block_rows, ctx_count, half_ids)
    segment_ids = segments[0]
    query_seg = segment_ids[query_pos]
    flat_pos = query_pos.reshape(tok_count)
    rot_query = rotate(qkv_lin[:, :1024].reshape(tok_count, HEADS, HEAD_DIM), flat_pos, 1.0).astype(
        bf16
    )
    rot_key = rotate(
        qkv_lin[:, 1024:1536].reshape(tok_count, KV_HEADS, HEAD_DIM), flat_pos, 1.0
    ).astype(bf16)
    queries = rot_query.reshape(2, block_rows, KV_HEADS, group_size, HEAD_DIM).transpose(
        0, 2, 3, 1, 4
    )
    kv_own = jnp.concatenate(
        [rot_key.reshape(tok_count, kv_width), qkv_lin[:, 1536:].astype(bf16)], axis=1
    ).reshape(2, block_rows, 2 * kv_width)
    kv_all = kv_gather(kv_own, ctx_count).reshape(2, half_rows, 2 * kv_width)

    def score_mask(half_side, key_pos, key_seg):
        return (key_seg[None, :] == query_seg[half_side][:, None]) & (
            key_pos[None, :] <= query_pos[half_side][:, None]
        )

    def needed(half_side, key_pos):
        return jnp.min(key_pos) <= jnp.max(query_pos[half_side])

    def forward_step(state_pair, block_in):
        numerator, totals = state_pair
        key_blk, value_blk, key_pos, key_seg = block_in
        new_numer = []
        new_totals = []
        for half_side in range(2):
            allowed = score_mask(half_side, key_pos, key_seg)

            def forward_compute(state):
                part_numer, part_total = state
                scores = jnp.einsum(
                    "grqd,kgd->grqk", queries[half_side], key_blk, preferred_element_type=f32
                )
                exp_values = jnp.where(allowed[None, None], jnp.exp(ATT_MULT * scores), 0.0)
                part_total = part_total + jnp.sum(exp_values, axis=-1)
                part_numer = part_numer + jnp.einsum(
                    "grqk,kgd->grqd", exp_values.astype(bf16), value_blk, preferred_element_type=f32
                )
                return (part_numer, part_total)

            part_numer, part_total = lax.cond(
                needed(half_side, key_pos),
                forward_compute,
                keep_state,
                (numerator[half_side], totals[half_side]),
            )
            new_numer.append(part_numer)
            new_totals.append(part_total)
        return ((jnp.stack(new_numer), jnp.stack(new_totals)), None)

    start_state = (
        jnp.zeros((2, KV_HEADS, group_size, block_rows, HEAD_DIM), f32),
        jnp.zeros((2, KV_HEADS, group_size, block_rows), f32),
    )
    span_all = span_for(half_rows)
    block_total = 2 * half_rows // span_all
    all_rows = jnp.arange(half_rows, dtype=jnp.int32)
    key_pos_all = seq_position(all_rows[None, :], block_rows, ctx_count, half_ids)
    blocks_all = (
        kv_all[..., :kv_width].reshape(block_total, span_all, KV_HEADS, HEAD_DIM),
        kv_all[..., kv_width:].reshape(block_total, span_all, KV_HEADS, HEAD_DIM),
        key_pos_all.reshape(block_total, span_all),
        segment_ids[key_pos_all].reshape(block_total, span_all),
    )
    state_pair, unused = lax.scan(forward_step, start_state, blocks_all)
    numerator, totals = state_pair
    attn_raw = numerator / totals[..., None]
    mixed = attn_raw.transpose(0, 3, 1, 2, 4).reshape(tok_count, HEADS * HEAD_DIM).astype(bf16)
    attn_out = jnp.dot(mixed, output_w, preferred_element_type=f32)
    first_sum = token_rows + RES_MULT * attn_out
    scale_two = rms_scale(first_sum)
    normed_two = first_sum * scale_two
    hidden_two = (normed_two * gain_two_f).astype(bf16)
    logits = jnp.einsum("td,ed->te", hidden_two, router_t, preferred_element_type=f32)

    route_rows = routes.reshape(tok_count, TOPK)
    onehot = route_rows[:, :, None] == jnp.arange(EXPERTS, dtype=jnp.int32)[None, None, :]
    routed = jnp.any(onehot, axis=1)
    prio = jnp.sum(jnp.where(onehot, priority.reshape(tok_count, TOPK)[:, :, None], 0), axis=1)
    prio = jnp.where(routed, prio, 1 << 20)
    top = jnp.max(jnp.where(routed, logits, -jnp.inf), axis=-1, keepdims=True)
    weight = jnp.where(routed, jnp.exp(logits - top), 0.0)
    gate = weight / jnp.sum(weight, axis=-1, keepdims=True)
    order = jnp.arange(tok_count, dtype=jnp.int32)
    ahead = (prio[None, :, :] < prio[:, None, :]) | (
        (prio[None, :, :] == prio[:, None, :]) & (order[None, :, None] < order[:, None, None])
    )
    rank = jnp.sum(ahead.astype(jnp.int32), axis=1)
    kept = routed & (rank < CAP)
    kept_f = kept.astype(f32)
    gate_kept = gate * kept_f

    hidden_all, gates_all = plane_gather([hidden_two, gate_kept.T], 4, "gather_hidden")
    hidden_all = hidden_all.reshape(plane_rows, D)
    cot_rows_all = cot_all.reshape(plane_rows, D)
    own_gates = lax.dynamic_slice_in_dim(gates_all, first_expert, OWN, axis=1)
    own_gates = own_gates.transpose(1, 0, 2).reshape(OWN, plane_rows)

    inner_w = lax.dynamic_slice_in_dim(expert_in, first_expert, OWN, axis=0)
    outer_w = lax.dynamic_slice_in_dim(expert_out, first_expert, OWN, axis=0)
    hidden_units = outer_w.shape[-1]
    inner_w = inner_w.reshape(OWN, D, 2 * hidden_units)
    gate_up = jnp.einsum("td,edf->etf", hidden_all, inner_w, preferred_element_type=f32)
    gate_val = gate_up[:, :, :hidden_units]
    up_val = gate_up[:, :, hidden_units:]
    sigmoid_val = jax.nn.sigmoid(gate_val)
    silu_val = gate_val * sigmoid_val
    act = silu_val * up_val
    act_kept = (own_gates[:, :, None] * act).astype(bf16)
    moe_part = jnp.einsum("etf,edf->td", act_kept, outer_w, preferred_element_type=f32).astype(bf16)
    act_grad = RES_MULT * jnp.einsum("td,edf->etf", cot_rows_all, outer_w, preferred_element_type=f32)
    pick_part = jnp.sum(act * act_grad, axis=-1)
    act_grad = own_gates[:, :, None] * act_grad
    silu_grad = sigmoid_val * (1.0 + gate_val * (1.0 - sigmoid_val))
    gate_up_grad = jnp.concatenate(
        [act_grad * up_val * silu_grad, act_grad * silu_val], axis=-1
    ).astype(bf16)
    hidden_part = jnp.einsum("etf,edf->td", gate_up_grad, inner_w, preferred_element_type=f32).astype(
        bf16
    )
    inner_grad = jnp.einsum("td,etf->edf", hidden_all, gate_up_grad, preferred_element_type=f32).astype(
        bf16
    )
    outer_grad = (
        RES_MULT * jnp.einsum("td,etf->edf", cot_rows_all, act_kept, preferred_element_type=f32)
    ).astype(bf16)

    picks = jnp.pad(pick_part.reshape(OWN, PLANE, tok_count).transpose(1, 0, 2), ((0, 0), (0, 8 - OWN), (0, 0)))
    expert_sum, hidden_grad, picks_all = plane_reduce(
        [
            moe_part.reshape(PLANE, tok_count, D),
            hidden_part.reshape(PLANE, tok_count, D),
        ],
        picks,
        5,
        "reduce_hidden",
    )
    output = (first_sum + RES_MULT * expert_sum).astype(bf16).reshape(tokens.shape)
    gate_grad = (
        jnp.sum(picks_all[:, :OWN].reshape(INNER, 2, OWN, tok_count), axis=1)
        .reshape(EXPERTS, tok_count)
        .T
    )
    gate_grad = kept_f * gate_grad
    picked_grad = gate * (gate_grad - jnp.sum(gate * gate_grad, axis=-1, keepdims=True))
    logit_grad = picked_grad.astype(bf16)
    hidden_grad = hidden_grad + jnp.einsum(
        "te,ed->td", logit_grad, router_t, preferred_element_type=f32
    )
    router_grad = jnp.einsum("td,te->de", hidden_two, logit_grad, preferred_element_type=f32)
    gain_two_grad = jnp.sum(hidden_grad * normed_two, axis=0)
    normed_grad = hidden_grad * gain_two_f
    cot_rows = cot_own.astype(f32)
    first_grad = cot_rows + scale_two * (
        normed_grad - normed_two * jnp.mean(normed_grad * normed_two, axis=-1, keepdims=True)
    )
    attn_grad = (RES_MULT * first_grad).astype(bf16)
    mixed_grad = jnp.einsum("td,md->tm", attn_grad, output_w, preferred_element_type=f32).astype(
        bf16
    )
    mixed_grad_f = (
        mixed_grad.reshape(2, block_rows, KV_HEADS, group_size, HEAD_DIM)
        .transpose(0, 2, 3, 1, 4)
        .astype(f32)
    )
    numer_grad = (mixed_grad_f / totals[..., None]).astype(bf16)
    total_grad = -jnp.sum(mixed_grad_f * attn_raw, axis=-1) / totals

    def backward_step(grad_query, block_in):
        key_blk, value_blk, key_pos, key_seg = block_in
        span_rows = key_blk.shape[0]
        key_acc = jnp.zeros((span_rows, KV_HEADS, HEAD_DIM), f32)
        value_acc = jnp.zeros((span_rows, KV_HEADS, HEAD_DIM), f32)
        new_query = []
        for half_side in range(2):
            allowed = score_mask(half_side, key_pos, key_seg)

            def backward_compute(state):
                part_query, part_key, part_value = state
                scores = jnp.einsum(
                    "grqd,kgd->grqk", queries[half_side], key_blk, preferred_element_type=f32
                )
                exp_values = jnp.where(allowed[None, None], jnp.exp(ATT_MULT * scores), 0.0)
                weights_low = exp_values.astype(bf16)
                through = jnp.einsum(
                    "grqd,kgd->grqk", numer_grad[half_side], value_blk, preferred_element_type=f32
                )
                score_grad = (
                    ATT_MULT * exp_values * (through + total_grad[half_side][..., None])
                ).astype(bf16)
                part_query = part_query + jnp.einsum(
                    "grqk,kgd->grqd", score_grad, key_blk, preferred_element_type=f32
                )
                part_key = part_key + jnp.einsum(
                    "grqk,grqd->kgd", score_grad, queries[half_side], preferred_element_type=f32
                )
                part_value = part_value + jnp.einsum(
                    "grqk,grqd->kgd", weights_low, numer_grad[half_side], preferred_element_type=f32
                )
                return (part_query, part_key, part_value)

            part_query, key_acc, value_acc = lax.cond(
                needed(half_side, key_pos),
                backward_compute,
                keep_state,
                (grad_query[half_side], key_acc, value_acc),
            )
            new_query.append(part_query)
        joined = jnp.concatenate(
            [key_acc.reshape(span_rows, kv_width), value_acc.reshape(span_rows, kv_width)], axis=1
        )
        return (jnp.stack(new_query), joined)

    query_grad, kv_terms = lax.scan(backward_step, jnp.zeros_like(numerator), blocks_all)
    kv_terms = kv_terms.reshape(2, ctx_count, block_rows, 2 * kv_width).astype(bf16)
    kv_mine = kv_reduce(kv_terms, ctx_count)
    key_grad = (
        rotate(kv_mine[:, :, :kv_width].reshape(tok_count, KV_HEADS, HEAD_DIM), flat_pos, -1.0)
        .astype(bf16)
        .reshape(tok_count, kv_width)
    )
    value_grad = kv_mine[:, :, kv_width:].reshape(tok_count, kv_width).astype(bf16)
    query_rows_grad = query_grad.transpose(0, 3, 1, 2, 4).reshape(tok_count, HEADS, HEAD_DIM)
    query_lin_grad = (
        rotate(query_rows_grad, flat_pos, -1.0).astype(bf16).reshape(tok_count, HEADS * HEAD_DIM)
    )
    qkv_grad = jnp.concatenate([query_lin_grad, key_grad, value_grad], axis=1)
    hidden_one_grad = jnp.einsum("tm,dm->td", qkv_grad, qkv_w, preferred_element_type=f32)
    gain_one_grad = jnp.sum(hidden_one_grad * normed_one, axis=0)
    normed_one_grad = hidden_one_grad * gain_one_f
    token_grad = first_grad + scale_one * (
        normed_one_grad
        - normed_one * jnp.mean(normed_one_grad * normed_one, axis=-1, keepdims=True)
    )

    swap = jnp.concatenate(
        [
            qkv_grad.reshape(tok_count, PLANE, 2048 // PLANE),
            attn_grad.reshape(tok_count, PLANE, D // PLANE),
        ],
        axis=2,
    ).transpose(1, 0, 2)
    left_own = jnp.stack([hidden_one, mixed])
    grads_all, left_all = plane_swap(swap, left_own, 6, "swap_grads")
    left_one = left_all[:, 0].reshape(plane_rows, D)
    left_mixed = left_all[:, 1].reshape(plane_rows, D)
    grads_all = grads_all.reshape(plane_rows, 3 * D // PLANE)
    qkv_cols = 2048 // PLANE
    attn_part = jnp.concatenate(
        [
            jnp.einsum("td,tm->dm", left_one, grads_all[:, :qkv_cols], preferred_element_type=f32),
            jnp.einsum("td,tm->dm", left_mixed, grads_all[:, qkv_cols:], preferred_element_type=f32),
        ],
        axis=1,
    ).astype(bf16)
    small_part = jnp.concatenate(
        [router_grad, gain_one_grad[:, None], gain_two_grad[:, None], jnp.zeros((D, 110), f32)], axis=1
    )
    attn_in, inner_in, outer_in, small_in = owners(
        [attn_part, inner_grad, outer_grad, small_part], devices, 7, "owners"
    )
    attn_sum = jnp.sum(
        attn_in.astype(f32).reshape(outers, PLANE, owner_rows, 3 * D // PLANE), axis=0
    ).transpose(1, 0, 2)
    qkv_sum = attn_sum[:, :, :qkv_cols].reshape(owner_rows, 2048)
    output_sum = attn_sum[:, :, qkv_cols:].reshape(owner_rows, D)
    inner_sum = jnp.sum(
        inner_in.astype(f32).reshape(outers, INNER, 2, OWN, owner_rows, 2, hidden_units), axis=0
    )
    inner_sum = inner_sum.transpose(0, 2, 3, 4, 1, 5).reshape(EXPERTS, owner_rows, 2, 2 * hidden_units)
    outer_sum = jnp.sum(
        outer_in.astype(f32).reshape(outers, INNER, 2, OWN, owner_rows, hidden_units), axis=0
    )
    outer_sum = outer_sum.transpose(0, 2, 3, 1, 4).reshape(EXPERTS, owner_rows, 2 * hidden_units)
    small_sum = jnp.sum(small_in, axis=0)
    return (
        output,
        token_grad.reshape(tokens.shape),
        qkv_sum[:, :1024],
        qkv_sum[:, 1024:1536],
        qkv_sum[:, 1536:],
        output_sum,
        small_sum[:, EXPERTS],
        small_sum[:, :EXPERTS],
        inner_sum,
        outer_sum,
        small_sum[:, EXPERTS + 1],
    )


def solution(mesh):
    placed = (
        P("wsh", None, "ctx", None),
        P("wsh", None),
        P("wsh", None),
        P("wsh", None),
        P("wsh", None),
        P("wsh"),
        P("wsh", None),
        P(None, None, None, "wsh"),
        P(None, None, "wsh"),
        P("wsh"),
        P("wsh", None),
        P("wsh", None, "ctx", None),
        P("wsh", None, "ctx", None),
        P("wsh", None, "ctx", None),
    )
    return jax.shard_map(
        body,
        mesh=mesh,
        in_specs=placed,
        out_specs=(
            P("wsh", None, "ctx", None),
            P("wsh", None, "ctx", None),
            P(("ctx", "wsh"), None),
            P(("ctx", "wsh"), None),
            P(("ctx", "wsh"), None),
            P(("ctx", "wsh"), None),
            P(("ctx", "wsh")),
            P(("ctx", "wsh"), None),
            P(None, ("ctx", "wsh"), None, None),
            P(None, ("ctx", "wsh"), None),
            P(("ctx", "wsh")),
        ),
        check_vma=False,
    )
```

```python
import functools

import jax
import jax.numpy as jnp
from jax import lax
from jax.experimental import pallas as pl
from jax.experimental.pallas import tpu as pltpu
from jax.sharding import PartitionSpec as P

D = 1024
HEADS = 16
KV_HEADS = 8
HEAD_DIM = 64
TOPK = 8
EXPERTS = 16
CAP = 80
PLANE = 8
INNER = 4
OWN = EXPERTS // INNER


RES_MULT = 0.22
ATT_MULT = 0.015625
EPS = 1e-06
THETA = 10000.0

MESH = pl.DeviceIdType.MESH
F32 = jnp.float32
BF16 = jnp.bfloat16
ANY = pl.BlockSpec(memory_space=pl.ANY)
VMEM = pl.BlockSpec(memory_space=pltpu.VMEM)


class Place:
    def __init__(self):
        self.c = lax.axis_index("ctx")
        self.w = lax.axis_index("wsh")
        self.core = self.c % 2
        self.y = (self.c // 2) % 2
        self.inner = self.c % INNER
        self.outer = self.c // INNER
        self.j = self.inner * 2 + self.w
        self.sib = self.c + 1 - 2 * self.core
        self.yn = self.c + 2 - 4 * self.y

    def relative(self, dy, dc, dw):
        y = self.y + dy * (1 - 2 * self.y)
        core = self.core + dc * (1 - 2 * self.core)
        w = self.w + dw * (1 - 2 * self.w)
        ctx = self.outer * INNER + y * 2 + core
        return (ctx, w), (y * 2 + core) * 2 + w


OTHERS = [(a, b, d) for a in range(2) for b in range(2) for d in range(2) if a + b + d]
XY = [(0, 0, 1), (1, 0, 0), (1, 0, 1)]


def meet(devices):
    barrier = pltpu.get_barrier_semaphore()
    for device in devices:
        pl.semaphore_signal(barrier, inc=1, device_id=device, device_id_type=MESH)
    pl.semaphore_wait(barrier, len(devices))


def remote(src, dst, send, recv, device):
    return pltpu.make_async_remote_copy(
        src_ref=src,
        dst_ref=dst,
        send_sem=send,
        recv_sem=recv,
        device_id=device,
        device_id_type=MESH,
    )


def comm_call(kernel, out_shape, in_specs, out_specs, scratch, ident, name, vmem=None):
    return pl.pallas_call(
        kernel,
        out_shape=out_shape,
        in_specs=in_specs,
        out_specs=out_specs,
        scratch_shapes=scratch,
        compiler_params=pltpu.CompilerParams(
            collective_id=ident, has_side_effects=True, vmem_limit_bytes=vmem
        ),
        name=name,
    )


DMA = pltpu.SemaphoreType.DMA


def gather_start(at, pairs, send, recv, local):
    copies = []
    for index, (src, dst) in enumerate(pairs):
        keep = pltpu.make_async_copy(src, dst.at[at.j], local.at[index])
        keep.start()
        sends = []
        for slot, bits in enumerate(XY + [(0, 1, 0)]):
            device, unused = at.relative(*bits)
            copy = remote(src, dst.at[at.j], send.at[index, slot], recv.at[index, slot], device)
            copy.start()
            sends.append(copy)
        copies.append((keep, sends))
    return copies


def gather_finish(at, pairs, copies, send, recv):
    sib, unused = at.relative(0, 1, 0)
    passed = []
    for slot, bits in enumerate(XY):
        unused, j_from = at.relative(*bits)
        for index, (src, dst) in enumerate(pairs):
            copies[index][1][slot].wait_recv()
            copy = remote(
                dst.at[j_from],
                dst.at[j_from],
                send.at[index, 4 + slot],
                recv.at[index, 4 + slot],
                sib,
            )
            copy.start()
            passed.append(copy)
    for keep, sends in copies:
        keep.wait()
        sends[3].wait_recv()
        for copy in sends:
            copy.wait_send()
    for copy in passed:
        copy.wait()


def plane_gather_kernel(count, *refs):
    ins, outs = refs[:count], refs[count : 2 * count]
    send, recv, local = refs[2 * count :]
    at = Place()
    meet([at.relative(*bits)[0] for bits in XY + [(0, 1, 0)]])
    pairs = list(zip(ins, outs))
    copies = gather_start(at, pairs, send, recv, local)
    gather_finish(at, pairs, copies, send, recv)


def plane_gather(arrays, ident, name):
    count = len(arrays)
    return comm_call(
        functools.partial(plane_gather_kernel, count),
        [jax.ShapeDtypeStruct((PLANE,) + a.shape, a.dtype) for a in arrays],
        [ANY] * count,
        [ANY] * count,
        [DMA((count, 7)), DMA((count, 7)), DMA((count,))],
        ident,
        name,
    )(*arrays)


def weights_kernel(wq, wk, wv, small, wqkv_o, small_o, xs, xr, fs, fr):
    at = Place()
    partner, unused = at.relative(0, 0, 1)
    sib, unused = at.relative(0, 1, 0)
    meet([partner, sib])
    pieces = [(wk, 1024), (wv, 1536), (wq, 0)]
    sends, passed = [], []
    for index, (src, col) in enumerate(pieces):
        depth, width = src.shape
        half = depth // 2
        row = at.w * depth + at.core * half
        copy = remote(
            src.at[pl.ds(at.core * half, half), :],
            wqkv_o.at[pl.ds(row, half), pl.ds(col, width)],
            xs.at[index],
            xr.at[index],
            partner,
        )
        copy.start()
        sends.append(copy)
    last = len(pieces)
    copy = remote(small, small_o.at[at.w], xs.at[last], xr.at[last], partner)
    copy.start()
    sends.append(copy)
    small_o[at.w] = small[...]
    for src, col in pieces:
        depth, width = src.shape
        wqkv_o[pl.ds(at.w * depth, depth), pl.ds(col, width)] = src[...]
    for index, (src, col) in enumerate(pieces):
        depth, width = src.shape
        half = depth // 2
        row = (1 - at.w) * depth + at.core * half
        sends[index].wait_recv()
        piece = wqkv_o.at[pl.ds(row, half), pl.ds(col, width)]
        copy = remote(piece, piece, fs.at[index], fr.at[index], sib)
        copy.start()
        passed.append(copy)
    sends[last].wait_recv()
    for copy in sends:
        copy.wait_send()
    for copy in passed:
        copy.wait()


def gather_weights(wq, wk, wv, small):
    shape = jax.ShapeDtypeStruct
    return comm_call(
        weights_kernel,
        [shape((D, 2048), BF16), shape((2,) + small.shape, BF16)],
        [VMEM] * 4,
        [VMEM] * 2,
        [DMA((4,)), DMA((4,)), DMA((3,)), DMA((3,))],
        1,
        "gather_weights",
        vmem=40 * 2**20,
    )(wq, wk, wv, small)


class Blocks:
    def __init__(self, count):
        self.count = count

    def __call__(self, ref, half, ctx):
        return ref.at[ctx] if half == 0 else ref.at[2 * self.count - 1 - ctx]


def kv_gather_kernel(outers, own, full, zs, zr, ys, yr, cs, cr, local):
    at = Place()
    block_of = Blocks(outers * INNER)
    sib, unused = at.relative(0, 1, 0)
    side, unused = at.relative(1, 0, 0)
    other = [lax.rem(at.outer + r, outers) for r in range(outers)]
    back = [lax.rem(at.outer + outers - r, outers) for r in range(outers)]
    far = [(other[r] * INNER + at.inner, at.w) for r in range(1, outers)]
    meet([sib, side] + far)
    z_copies, y_copies, c_copies, keeps = {}, {}, {}, []
    for half in range(2):
        mine = block_of(full, half, at.c)
        keep = pltpu.make_async_copy(own.at[half], mine, local.at[half])
        keep.start()
        keeps.append(keep)
        for r in range(1, outers):
            copy = remote(own.at[half], mine, zs.at[half, r], zr.at[half, r], far[r - 1])
            copy.start()
            z_copies[half, r] = copy
        for send, recv, into, device in ((ys, yr, y_copies, side), (cs, cr, c_copies, sib)):
            copy = remote(own.at[half], mine, send.at[half, 0], recv.at[half, 0], device)
            copy.start()
            into[half, 0] = copy
    inner_side = at.inner + 2 - 4 * at.y
    for r in range(outers):
        for half in range(2):
            if r > 0:
                z_copies[half, r].wait_recv()
                block = block_of(full, half, back[r] * INNER + at.inner)
                for send, recv, into, device in ((ys, yr, y_copies, side), (cs, cr, c_copies, sib)):
                    copy = remote(block, block, send.at[half, r], recv.at[half, r], device)
                    copy.start()
                    into[half, r] = copy
    for r in range(outers):
        for half in range(2):
            y_copies[half, r].wait_recv()
            block = block_of(full, half, back[r] * INNER + inner_side)
            copy = remote(block, block, cs.at[half, outers + r], cr.at[half, outers + r], sib)
            copy.start()
            c_copies[half, outers + r] = copy
    for copy in list(z_copies.values()) + list(y_copies.values()):
        copy.wait_send()
    for copy in c_copies.values():
        copy.wait()
    for keep in keeps:
        keep.wait()


def kv_gather(own, ctx_count):
    outers = ctx_count // INNER
    return comm_call(
        functools.partial(kv_gather_kernel, outers),
        jax.ShapeDtypeStruct((2 * ctx_count,) + own.shape[1:], own.dtype),
        [VMEM],
        ANY,
        [DMA((2, outers))] * 4 + [DMA((2, 2 * outers))] * 2 + [DMA((2,))],
        2,
        "kv_gather",
    )(own)


def plane_reduce_kernel(count, *refs):
    parts, picks = refs[:count], refs[count]
    outs, picks_o = refs[count + 1 : 2 * count + 1], refs[2 * count + 1]
    near, summed, far, ss, sr, xs, xr, ps, pr, pl_sem = refs[2 * count + 2 :]
    at = Place()
    meet([at.relative(*bits)[0] for bits in OTHERS])
    sib, unused = at.relative(0, 1, 0)
    first = []
    for index in range(count):
        copy = remote(
            parts[index].at[:, 1 - at.core], near.at[index], ss.at[index], sr.at[index], sib
        )
        copy.start()
        first.append(copy)
    keep = pltpu.make_async_copy(picks.at[at.j], picks_o.at[at.j], pl_sem)
    keep.start()
    small = []
    for slot, bits in enumerate(OTHERS):
        device, j_to = at.relative(*bits)
        copy = remote(picks.at[j_to], picks_o.at[at.j], ps.at[slot], pr.at[slot], device)
        copy.start()
        small.append(copy)
    second = []
    for index in range(count):
        first[index].wait_recv()
        for y in range(2):
            for w in range(2):
                total = parts[index][y, at.core, w].astype(F32) + near[index, y, w].astype(F32)
                summed[index, y, w] = total.astype(BF16)
        for slot, (dy, dc, dw) in enumerate(XY):
            device, unused = at.relative(dy, dc, dw)
            y = at.y + dy * (1 - 2 * at.y)
            w = at.w + dw * (1 - 2 * at.w)
            copy = remote(
                summed.at[index, y, w], far.at[index, slot], xs.at[index, slot], xr.at[index, slot], device
            )
            copy.start()
            second.append(copy)
    for index in range(count):
        total = parts[index][at.y, at.core, at.w].astype(F32) + near[index, at.y, at.w].astype(F32)
        for slot in range(3):
            second[index * 3 + slot].wait_recv()
            total = total + far[index, slot].astype(F32)
        outs[index][...] = total
    keep.wait()
    for copy in small:
        copy.wait()
    for copy in first + second:
        copy.wait_send()


def plane_reduce(parts, picks, ident, name):
    count = len(parts)
    rows, width = parts[0].shape[-2:]
    shape = jax.ShapeDtypeStruct
    return comm_call(
        functools.partial(plane_reduce_kernel, count),
        [shape((rows, width), F32)] * count + [shape(picks.shape, picks.dtype)],
        [VMEM] * (count + 1),
        [VMEM] * (count + 1),
        [
            pltpu.VMEM((count, 2, 2, rows, width), BF16),
            pltpu.VMEM((count, 2, 2, rows, width), BF16),
            pltpu.VMEM((count, 3, rows, width), BF16),
            DMA((count,)),
            DMA((count,)),
            DMA((count, 3)),
            DMA((count, 3)),
            DMA((7,)),
            DMA((7,)),
            DMA,
        ],
        ident,
        name,
        vmem=60 * 2**20,
    )(*[p.reshape(2, 2, 2, rows, width) for p in parts], picks)


def owners_kernel(devices, count, near_count, *refs):
    total = count + near_count
    parts, nears = refs[:count], refs[count:total]
    outs, near_outs = refs[total : total + count], refs[total + count : 2 * total]
    send, recv, local, nsend, nrecv, nlocal = refs[2 * total :]
    at = Place()
    me = at.c * 2 + at.w
    rows = D // devices

    def device_of(r):
        index = lax.rem(me + r, devices)
        return index, (index // 2, lax.rem(index, 2))

    def rows_of(ref, index):
        return ref.at[pl.ds(pl.multiple_of(index * rows, rows), rows), :]

    barrier = pltpu.get_barrier_semaphore()

    def greet(r, carry):
        unused, device = device_of(r)
        pl.semaphore_signal(barrier, inc=1, device_id=device, device_id_type=MESH)
        return carry

    lax.fori_loop(1, devices, greet, 0)
    pl.semaphore_wait(barrier, devices - 1)

    def copy_of(k, r):
        index, device = device_of(r)
        return remote(rows_of(parts[k], index), outs[k].at[me], send.at[k, r], recv.at[k, r], device)

    def start(r, carry):
        for k in range(count):
            copy_of(k, r).start()
        return carry

    lax.fori_loop(1, devices, start, 0)

    near_copies = []
    for k in range(near_count):
        for slot, bits in enumerate(OTHERS):
            device, j_to = at.relative(*bits)
            copy = remote(
                nears[k].at[:, j_to], near_outs[k].at[at.j], nsend.at[k, slot], nrecv.at[k, slot], device
            )
            copy.start()
            near_copies.append(copy)
    keeps = []
    for k in range(count):
        keep = pltpu.make_async_copy(rows_of(parts[k], me), outs[k].at[me], local.at[k])
        keep.start()
        keeps.append(keep)
    for k in range(near_count):
        keep = pltpu.make_async_copy(nears[k].at[:, at.j], near_outs[k].at[at.j], nlocal.at[k])
        keep.start()
        keeps.append(keep)

    def finish(r, carry):
        for k in range(count):
            copy_of(k, r).wait()
        return carry

    lax.fori_loop(1, devices, finish, 0)
    for copy in near_copies:
        copy.wait()
    for keep in keeps:
        keep.wait()


def owners(parts, nears, devices, ident, name):
    count, near_count = len(parts), len(nears)
    rows = D // devices
    shape = jax.ShapeDtypeStruct
    shapes = [shape((devices, rows, part.shape[-1]), part.dtype) for part in parts]
    for near in nears:
        lead, members, near_rows, width = near.shape
        shapes.append(shape((members, lead, near_rows, width), near.dtype))
    return comm_call(
        functools.partial(owners_kernel, devices, count, near_count),
        shapes,
        [VMEM] * (count + near_count),
        [VMEM] * (count + near_count),
        [
            DMA((count, devices)),
            DMA((count, devices)),
            DMA((count,)),
            DMA((near_count, 7)),
            DMA((near_count, 7)),
            DMA((near_count,)),
        ],
        ident,
        name,
        vmem=60 * 2**20,
    )(*parts, *nears)


CHUNK = 256
PAIRS = KV_HEADS // 2
NEVER = -1e30


def low_lanes(shape):
    return lax.broadcasted_iota(jnp.int32, shape, 1) < HEAD_DIM


def spread(block):
    a, b = block[:, :128], block[:, 128:]
    low = low_lanes(a.shape)
    zero = jnp.zeros_like(a)
    return jnp.concatenate(
        [
            jnp.where(low, a, zero),
            jnp.where(low, pltpu.roll(a, HEAD_DIM, 1), zero),
            jnp.where(low, zero, pltpu.roll(b, HEAD_DIM, 1)),
            jnp.where(low, zero, b),
        ],
        axis=0,
    )


def unspread(four):
    rows = four.shape[0] // 4
    r0, r1, r2, r3 = (four[k * rows : (k + 1) * rows] for k in range(4))
    low = low_lanes(r0.shape)
    return jnp.concatenate(
        [
            jnp.where(low, r0, pltpu.roll(r1, HEAD_DIM, 1)),
            jnp.where(low, pltpu.roll(r2, HEAD_DIM, 1), r3),
        ],
        axis=1,
    )


def turn(values, cosine, sine):
    lane = lax.broadcasted_iota(jnp.int32, cosine.shape, 1)
    first = lane % HEAD_DIM < HEAD_DIM // 2
    blocks = []
    for start in range(0, values.shape[1], 128):
        u = values[:, start : start + 128]
        swapped = jnp.where(first, pltpu.roll(u, 96, 1), pltpu.roll(u, 32, 1))
        blocks.append(u * cosine + swapped * sine)
    return jnp.concatenate(blocks, axis=1)


def dot_nt(a, b):
    return lax.dot_general(a, b, (((1,), (1,)), ((), ())), preferred_element_type=F32)


def dot_tn(a, b):
    return lax.dot_general(a, b, (((0,), (0,)), ((), ())), preferred_element_type=F32)


def dot_nn(a, b):
    return jnp.dot(a, b, preferred_element_type=F32)


def attend_kernel(
    info,
    q_ref,
    kv_ref,
    start_ref,
    tok_ref,
    wo_ref,
    small_ref,
    route_ref,
    prio_ref,
    raw_ref,
    total_ref,
    mixed_ref,
    sum_ref,
    hid_ref,
    gate_ref,
    kept_ref,
    acc,
    acc_l,
):
    rows = q_ref.shape[0] // 2
    width = PAIRS * 128
    for half in range(2):
        base = info[4 + half]
        q_four = []
        for pair in range(PAIRS):
            block = q_ref[pl.ds(half * rows, rows), pl.ds(pair * 256, 256)].astype(F32) * ATT_MULT
            q_four.append(spread(block).astype(BF16))
        acc[...] = jnp.zeros_like(acc)
        acc_l[...] = jnp.zeros_like(acc_l)
        first = start_ref[pl.ds(half * rows, rows), :]
        place = base + lax.broadcasted_iota(jnp.int32, (rows, 1), 0)

        def step(chunk, carry):
            at_row = pl.multiple_of(chunk * CHUNK, CHUNK)
            key_pos = at_row + lax.broadcasted_iota(jnp.int32, (1, CHUNK), 1)
            bias = jnp.where((key_pos >= first) & (key_pos <= place), 0.0, NEVER)
            bias = jnp.concatenate([bias] * 4, axis=0)
            for pair in range(PAIRS):
                key = kv_ref[pl.ds(at_row, CHUNK), pl.ds(pair * 128, 128)]
                value = kv_ref[pl.ds(at_row, CHUNK), pl.ds(width + pair * 128, 128)]
                e = jnp.exp(dot_nt(q_four[pair], key) + bias)
                part = e[:, :128]
                for k in range(1, CHUNK // 128):
                    part = part + e[:, k * 128 : (k + 1) * 128]
                acc_l[pair] += part
                acc[pair] += dot_nn(e.astype(BF16), value)
            return carry

        lax.fori_loop(info[half], info[2 + half], step, 0)
        for pair in range(PAIRS):
            total = jnp.sum(acc_l[pair], axis=1, keepdims=True)
            total = jnp.broadcast_to(total, (4 * rows, 128))
            here = pl.ds(half * rows, rows), pl.ds(pair * 256, 256)
            raw_ref[here] = unspread(acc[pair] / total)
            total_ref[here] = unspread(total)
    mixed = raw_ref[...].astype(BF16)
    mixed_ref[...] = mixed
    first_sum = tok_ref[...].astype(F32) + RES_MULT * dot_nn(mixed, wo_ref[...])
    sum_ref[...] = first_sum
    scale = lax.rsqrt(jnp.mean(first_sum * first_sum, axis=1, keepdims=True) + EPS)
    gain_two = small_ref[pl.ds(EXPERTS + 1, 1), :].astype(F32)
    hidden = (first_sum * scale * gain_two).astype(BF16)
    hid_ref[...] = hidden

    logits = dot_nt(small_ref[...], hidden)[:EXPERTS]
    count = 2 * rows
    expert = lax.broadcasted_iota(jnp.int32, (EXPERTS, count), 0)
    routed = jnp.zeros((EXPERTS, count), F32)
    prio = jnp.zeros((EXPERTS, count), F32)
    for k in range(TOPK):
        same = expert == route_ref[pl.ds(k, 1), :]
        routed = jnp.where(same, 1.0, routed)
        prio = jnp.where(same, prio_ref[pl.ds(k, 1), :].astype(F32), prio)
    chosen = routed > 0.0
    order = lax.broadcasted_iota(jnp.int32, (EXPERTS, count), 1).astype(F32)
    key = jnp.where(chosen, prio * float(count) + order, 65536.0 * count)
    key_cols = jnp.concatenate([key, jnp.zeros((count - EXPERTS, count), F32)], axis=0).T
    ranks = []
    for e in range(EXPERTS):
        ahead = jnp.where(key_cols[:, e : e + 1] < key[e : e + 1, :], 1.0, 0.0)
        ranks.append(jnp.sum(ahead, axis=0, keepdims=True))
    rank = jnp.concatenate(ranks, axis=0)
    top = jnp.max(jnp.where(chosen, logits, -3e38), axis=0, keepdims=True)
    weight = jnp.where(chosen, jnp.exp(logits - top), 0.0)
    gate_ref[...] = weight / jnp.sum(weight, axis=0, keepdims=True)
    kept_ref[...] = jnp.where(chosen & (rank < CAP), 1.0, 0.0)


def local_call(kernel, out_shape, in_specs, scratch, name, cost, vmem):
    return pl.pallas_call(
        kernel,
        out_shape=out_shape,
        in_specs=in_specs,
        out_specs=[VMEM] * len(out_shape),
        scratch_shapes=scratch,
        compiler_params=pltpu.CompilerParams(vmem_limit_bytes=vmem),
        cost_estimate=pl.CostEstimate(flops=cost, bytes_accessed=16 * 2**20, transcendentals=2**21),
        name=name,
    )


SMEM = pl.BlockSpec(memory_space=pltpu.SMEM)


def attend(info, queries, kv_all, start, tokens, output_w, small, routes, priority):
    shape = jax.ShapeDtypeStruct
    count, width = queries.shape
    return local_call(
        attend_kernel,
        [
            shape((count, width), F32),
            shape((count, width), F32),
            shape((count, width), BF16),
            shape((count, D), F32),
            shape((count, D), BF16),
            shape((EXPERTS, count), F32),
            shape((EXPERTS, count), F32),
        ],
        [SMEM] + [VMEM] * 8,
        [pltpu.VMEM((PAIRS, 2 * count, 128), F32), pltpu.VMEM((PAIRS, 2 * count, 128), F32)],
        "attend",
        4 * 2**30,
        60 * 2**20,
    )(info, queries, kv_all, start, tokens, output_w, small, routes, priority)


def back_kernel(
    info,
    hg_ref,
    pick_ref,
    gate_ref,
    kept_ref,
    small_ref,
    sum_ref,
    cot_ref,
    wo_ref,
    raw_ref,
    total_ref,
    q_ref,
    kv_ref,
    start_ref,
    cos_ref,
    sin_ref,
    dy_ref,
    da_ref,
    dq_ref,
    dkv_ref,
    rows_ref,
    q_four,
    n_four,
    d_rows,
    dq_acc,
    kv_acc,
):
    count = q_ref.shape[0]
    rows = count // 2
    width = PAIRS * 128
    small = small_ref[...]
    gain_two = small[EXPERTS + 1 : EXPERTS + 2].astype(F32)
    parts = []
    for i in range(INNER):
        parts.append(pick_ref[2 * i, pl.ds(0, OWN), :] + pick_ref[2 * i + 1, pl.ds(0, OWN), :])
    gate = gate_ref[...]
    gate_grad = kept_ref[...] * jnp.concatenate(parts, axis=0)
    logit_grad = gate * (gate_grad - jnp.sum(gate * gate_grad, axis=0, keepdims=True))
    logit_grad = jnp.concatenate(
        [logit_grad, jnp.zeros((small.shape[0] - EXPERTS, count), F32)], axis=0
    ).astype(BF16)
    hidden_grad = hg_ref[...] + dot_tn(logit_grad, small)
    first_sum = sum_ref[...]
    scale = lax.rsqrt(jnp.mean(first_sum * first_sum, axis=1, keepdims=True) + EPS)
    normed = first_sum * scale
    hidden = (normed * gain_two).astype(BF16)
    router_rows = dot_nn(logit_grad, hidden)
    rows_ref[...] = router_rows
    rows_ref[pl.ds(EXPERTS + 1, 1), :] = jnp.sum(hidden_grad * normed, axis=0, keepdims=True)
    normed_grad = hidden_grad * gain_two
    first_grad = cot_ref[...].astype(F32) + scale * (
        normed_grad - normed * jnp.mean(normed_grad * normed, axis=1, keepdims=True)
    )
    dy_ref[...] = first_grad
    attn_grad = (RES_MULT * first_grad).astype(BF16)
    da_ref[...] = attn_grad
    mixed_grad = dot_nt(attn_grad, wo_ref[...]).astype(BF16).astype(F32)
    total = total_ref[...]
    numer = mixed_grad / total
    lost = mixed_grad * raw_ref[...] / total
    for half in range(2):
        here = slice(half * rows, (half + 1) * rows)
        for pair in range(PAIRS):
            cols = slice(pair * 256, (pair + 1) * 256)
            slot = half * PAIRS + pair
            q_four[slot] = spread(q_ref[here, cols].astype(F32) * ATT_MULT).astype(BF16)
            n_four[slot] = spread(numer[here, cols]).astype(BF16)
            d_rows[slot] = -jnp.sum(spread(lost[here, cols]).T, axis=0, keepdims=True)
    dq_acc[...] = jnp.zeros_like(dq_acc)

    def step(chunk, carry):
        at_row = pl.multiple_of(chunk * CHUNK, CHUNK)
        kv_acc[...] = jnp.zeros_like(kv_acc)
        key_pos = at_row + lax.broadcasted_iota(jnp.int32, (CHUNK, 1), 0)
        for half in range(2):

            @pl.when((chunk >= info[half]) & (chunk < info[2 + half]))
            def _():
                first = start_ref[pl.ds(half, 1), :]
                place = info[4 + half] + lax.broadcasted_iota(jnp.int32, (1, 4 * rows), 1) % rows
                bias = jnp.where((key_pos >= first) & (key_pos <= place), 0.0, NEVER)
                for pair in range(PAIRS):
                    slot = half * PAIRS + pair
                    key = kv_ref[pl.ds(at_row, CHUNK), pl.ds(pair * 128, 128)]
                    value = kv_ref[pl.ds(at_row, CHUNK), pl.ds(width + pair * 128, 128)]
                    e = jnp.exp(dot_nt(key, q_four[slot]) + bias)
                    through = dot_nt(value, n_four[slot])
                    dz = (e * (through + d_rows[slot])).astype(BF16)
                    kv_acc[:, pl.ds(pair * 128, 128)] += dot_nn(dz, q_four[slot])
                    kv_acc[:, pl.ds(width + pair * 128, 128)] += dot_nn(e.astype(BF16), n_four[slot])
                    dq_acc[slot] += dot_tn(dz, key)

        dkv_ref[pl.ds(at_row, CHUNK), :] = kv_acc[...].astype(BF16)
        return carry

    lax.fori_loop(0, kv_ref.shape[0] // CHUNK, step, 0)
    cosine = cos_ref[...]
    sine = -sin_ref[...]
    for half in range(2):
        here = slice(half * rows, (half + 1) * rows)
        for pair in range(PAIRS):
            block = ATT_MULT * unspread(dq_acc[half * PAIRS + pair])
            dq_ref[here, pair * 256 : (pair + 1) * 256] = turn(
                block, cosine[here], sine[here]
            ).astype(BF16)


def back(info, hidden_grad, picks, gate, kept, small, first_sum, cot, output_w, raw, total, queries, kv_all, start, cosine, sine):
    shape = jax.ShapeDtypeStruct
    count, width = queries.shape
    return local_call(
        back_kernel,
        [
            shape((count, D), F32),
            shape((count, D), BF16),
            shape((count, width), BF16),
            shape(kv_all.shape, BF16),
            shape((32, D), F32),
        ],
        [SMEM] + [VMEM] * 15,
        [
            pltpu.VMEM((2 * PAIRS, 2 * count, 128), BF16),
            pltpu.VMEM((2 * PAIRS, 2 * count, 128), BF16),
            pltpu.VMEM((2 * PAIRS, 1, 2 * count), F32),
            pltpu.VMEM((2 * PAIRS, 2 * count, 128), F32),
            pltpu.VMEM((CHUNK, 2 * PAIRS * 128), F32),
        ],
        "back",
        8 * 2**30,
        60 * 2**20,
    )(info, hidden_grad, picks, gate, kept, small, first_sum, cot, output_w, raw, total, queries, kv_all, start, cosine, sine)


def finish_kernel(
    outers,
    part,
    moe,
    sum_ref,
    dq_ref,
    da_ref,
    dy_ref,
    tok_ref,
    small_ref,
    cos_ref,
    sin_ref,
    wqkv_ref,
    left_one,
    left_mixed,
    rows_ref,
    out_ref,
    token_ref,
    attn_ref,
    small_o,
    half_in,
    y_in,
    z_in,
    m_near,
    m_x,
    m_y,
    qkv,
    swap,
    swapped,
    ss,
    sr,
    ys,
    yr,
    zs,
    zr,
    ns,
    nr,
    ws,
    wr,
):
    at = Place()
    blocks, rows, full = part.shape
    width = full // 2
    count = 2 * rows
    sib, unused = at.relative(0, 1, 0)
    side, unused = at.relative(1, 0, 0)
    across, unused = at.relative(0, 0, 1)
    other = [lax.rem(at.outer + r, outers) for r in range(outers)]
    far = [(other[r] * INNER + at.inner, at.w) for r in range(1, outers)]
    meet([at.relative(*bits)[0] for bits in OTHERS] + far)

    def own_block(half, o, y, core):
        index = (o * 2 + y) * 2 + core
        return index if half == 0 else blocks - 1 - index

    first = {}
    for k in range(2):
        cols = pl.ds(k * width, width)
        for y in range(2):
            for h in range(2):
                for o in range(outers):
                    copy = remote(
                        part.at[own_block(h, o, y, 1 - at.core), :, cols],
                        half_in.at[y, h, o, :, cols],
                        ss.at[k, y, h, o],
                        sr.at[k, y, h, o],
                        sib,
                    )
                    copy.start()
                    first[k, y, h, o] = copy
    near = remote(moe.at[:, 1 - at.core], m_near, ns.at[0], nr.at[0], sib)
    near.start()
    second = []
    for k in range(2):
        cols = pl.ds(k * width, width)
        for y in range(2):
            for h in range(2):
                for o in range(outers):
                    first[k, y, h, o].wait_recv()
                    total = part[own_block(h, o, y, at.core), :, cols].astype(F32) + half_in[
                        y, h, o, :, cols
                    ].astype(F32)
                    half_in[y, h, o, :, cols] = total.astype(BF16)
        copy = remote(
            half_in.at[1 - at.y, :, :, :, cols], y_in.at[:, :, :, cols], ys.at[k], yr.at[k], side
        )
        copy.start()
        second.append(copy)
    near.wait_recv()
    for y in range(2):
        for w in range(2):
            total = moe[y, at.core, w].astype(F32) + m_near[y, w].astype(F32)
            m_near[y, w] = total.astype(BF16)
    cross = remote(m_near.at[:, 1 - at.w], m_x, ns.at[1], nr.at[1], across)
    cross.start()
    third = []

    def z_send(k):
        cols = pl.ds(k * width, width)
        second[k].wait_recv()
        for o in range(outers):
            for h in range(2):
                total = half_in[at.y, h, o, :, cols].astype(F32) + y_in[h, o, :, cols].astype(F32)
                half_in[at.y, h, o, :, cols] = total.astype(BF16)
        for r in range(1, outers):
            copy = remote(
                half_in.at[at.y, :, other[r], :, cols],
                z_in.at[r, :, :, cols],
                zs.at[k, r],
                zr.at[k, r],
                far[r - 1],
            )
            copy.start()
            third.append(copy)

    z_send(0)
    cross.wait_recv()
    for y in range(2):
        total = m_near[y, at.w].astype(F32) + m_x[y].astype(F32)
        m_x[y] = total.astype(BF16)
    along = remote(m_x.at[1 - at.y], m_y, ns.at[2], nr.at[2], side)
    along.start()
    z_send(1)
    qkv[:, : HEADS * HEAD_DIM] = dq_ref[...]
    along.wait_recv()
    moe_sum = m_x[at.y].astype(F32) + m_y[...].astype(F32)
    out_ref[...] = (sum_ref[...] + RES_MULT * moe_sum).astype(BF16)
    tok = tok_ref[...].astype(F32)
    scale = lax.rsqrt(jnp.mean(tok * tok, axis=1, keepdims=True) + EPS)
    normed = tok * scale
    gain_one = small_ref[pl.ds(EXPERTS, 1), :].astype(F32)
    for copy in third:
        copy.wait_recv()
    cosine = cos_ref[...]
    sine = -sin_ref[...]
    base = HEADS * HEAD_DIM
    for h in range(2):
        here = slice(h * rows, (h + 1) * rows)
        total = half_in[at.y, h, at.outer].astype(F32)
        for r in range(1, outers):
            total = total + z_in[r, h].astype(F32)
        qkv[here, base : base + width] = turn(total[:, :width], cosine[here], sine[here]).astype(BF16)
        qkv[here, base + width :] = total[:, width:].astype(BF16)
    wide = full * 2 // PLANE
    for j in range(PLANE):
        swap[j, :, :wide] = qkv[:, j * wide : (j + 1) * wide]
        swap[j, :, wide:] = da_ref[:, j * (D // PLANE) : (j + 1) * (D // PLANE)]
    swaps = []
    for slot, bits in enumerate(OTHERS):
        device, j_to = at.relative(*bits)
        copy = remote(swap.at[j_to], swapped.at[at.j], ws.at[slot], wr.at[slot], device)
        copy.start()
        swaps.append(copy)
    swapped[at.j] = swap[at.j]
    hidden_grad = dot_nt(qkv[...], wqkv_ref[...])
    small = rows_ref[...]
    gain_grad = jnp.sum(hidden_grad * normed, axis=0, keepdims=True)
    line = lax.broadcasted_iota(jnp.int32, small.shape, 0)
    small = jnp.where(line == EXPERTS, gain_grad, small)
    small = jnp.concatenate([small, jnp.zeros((128 - small.shape[0], D), F32)], axis=0)
    small_o[...] = small.T.astype(BF16)
    hidden_grad = hidden_grad * gain_one
    token_ref[...] = dy_ref[...] + scale * (
        hidden_grad - normed * jnp.mean(hidden_grad * normed, axis=1, keepdims=True)
    )
    for copy in swaps:
        copy.wait_recv()
    all_rows = PLANE * count
    grads = swapped[...].reshape(all_rows, wide + D // PLANE)
    attn_ref[:, :wide] = dot_tn(left_one[...], grads[:, :wide]).astype(BF16)
    attn_ref[:, wide:] = dot_tn(left_mixed[...], grads[:, wide:]).astype(BF16)
    for copy in list(first.values()) + second + third + swaps + [near, cross, along]:
        copy.wait_send()


def finish(part, moe, arrays, ctx_count):
    outers = ctx_count // INNER
    blocks, rows, full = part.shape
    count = 2 * rows
    shape = jax.ShapeDtypeStruct
    columns = 3 * D // PLANE
    return comm_call(
        functools.partial(finish_kernel, outers),
        [
            shape((count, D), BF16),
            shape((count, D), F32),
            shape((D, columns), BF16),
            shape((D, 128), BF16),
        ],
        [VMEM] * (2 + len(arrays)),
        [VMEM] * 4,
        [
            pltpu.VMEM((2, 2, outers, rows, full), BF16),
            pltpu.VMEM((2, outers, rows, full), BF16),
            pltpu.VMEM((outers, 2, rows, full), BF16),
            pltpu.VMEM((2, 2, count, D), BF16),
            pltpu.VMEM((2, count, D), BF16),
            pltpu.VMEM((count, D), BF16),
            pltpu.VMEM((count, 2 * full), BF16),
            pltpu.VMEM((PLANE, count, columns), BF16),
            pltpu.VMEM((PLANE, count, columns), BF16),
            DMA((2, 2, 2, outers)),
            DMA((2, 2, 2, outers)),
            DMA((2,)),
            DMA((2,)),
            DMA((2, outers)),
            DMA((2, outers)),
            DMA((3,)),
            DMA((3,)),
            DMA((7,)),
            DMA((7,)),
        ],
        3,
        "finish",
        vmem=62 * 2**20,
    )(part, moe.reshape(2, 2, 2, count, D), *arrays)


def experts_kernel(
    info,
    hid_ref,
    cot_ref,
    gate_ref,
    w1_ref,
    w2_ref,
    moe_ref,
    part_ref,
    pick_ref,
    give_ref,
    keep_ref,
    hid_t,
    cot_t,
    inner,
    gate_cols,
    pick_cols,
    moe_acc,
    part_acc,
    grad,
    act_kept,
):
    e = pl.program_id(0)
    tokens = hid_ref.shape[0]
    count = tokens // PLANE
    units = w2_ref.shape[-1]
    planes, rows = give_ref.shape[1:3]
    step_rows = 2 * count
    lane = lax.broadcasted_iota(jnp.int32, (step_rows, 128), 1)

    @pl.when(e == 0)
    def _():
        hid_t[...] = hid_ref[...].T
        cot_t[...] = cot_ref[...].T
        moe_acc[...] = jnp.zeros_like(moe_acc)
        part_acc[...] = jnp.zeros_like(part_acc)
        pick_cols[...] = jnp.zeros_like(pick_cols)
        for j in range(PLANE):
            block = jnp.concatenate(
                [gate_ref[j], jnp.zeros((128 - EXPERTS, count), F32)], axis=0
            )
            gate_cols[pl.ds(j * count, count), :] = block.T

    inner[...] = w1_ref[0].reshape(D, 2 * units)

    def forward(step, carry):
        here = pl.ds(pl.multiple_of(step * step_rows, step_rows), step_rows)
        gate = jnp.sum(
            jnp.where(lane == info[0] + e, gate_cols[here, :], 0.0), axis=1, keepdims=True
        )
        both = dot_nn(hid_ref[here, :], inner[...])
        gv, uv = both[:, :units], both[:, units:]
        back_act = RES_MULT * dot_nn(cot_ref[here, :], w2_ref[0])
        sig = jax.nn.sigmoid(gv)
        silu = gv * sig
        act = silu * uv
        pick = jnp.sum(act * back_act, axis=1, keepdims=True)
        pick_cols[here, :] = jnp.where(lane == e, pick, pick_cols[here, :])
        kept = (gate * act).astype(BF16)
        act_kept[here, :] = kept
        back_act = gate * back_act
        slope = sig * (1.0 + gv * (1.0 - sig))
        low = jnp.concatenate([back_act * uv * slope, back_act * silu], axis=1).astype(BF16)
        grad[here, :] = low
        part_acc[here, :] += dot_nt(low, inner[...])
        moe_acc[here, :] += dot_nt(kept, w2_ref[0])
        return carry

    lax.fori_loop(0, tokens // step_rows, forward, 0)

    def weights(step, carry):
        for ref, side in ((give_ref, 1 - info[1]), (keep_ref, info[1])):
            here = pl.ds(pl.multiple_of((2 * step + side) * rows, rows), rows)
            ref[0, step, :, : 2 * units] = dot_nn(hid_t[here, :], grad[...]).astype(BF16)
            ref[0, step, :, 2 * units :] = (RES_MULT * dot_nn(cot_t[here, :], act_kept[...])).astype(
                BF16
            )
        return carry

    lax.fori_loop(0, planes, weights, 0)

    @pl.when(e == OWN - 1)
    def _():
        moe_ref[...] = moe_acc[...].astype(BF16)
        part_ref[...] = part_acc[...].astype(BF16)
        for j in range(PLANE):
            pick_ref[j] = pick_cols[pl.ds(j * count, count), :].T[:8]


def experts(info, hidden, cot, gates, expert_in, expert_out, outers):
    tokens = hidden.shape[0]
    count = tokens // PLANE
    units = expert_out.shape[-1]
    rows = D // outers
    shape = jax.ShapeDtypeStruct

    def whole(dims):
        return pl.BlockSpec(dims, lambda e, info: (0,) * len(dims))

    grads = shape((OWN, outers // 2, rows, 3 * units), BF16)
    grad_spec = pl.BlockSpec((1,) + grads.shape[1:], lambda e, info: (e, 0, 0, 0))
    return pl.pallas_call(
        experts_kernel,
        out_shape=[
            shape((tokens, D), BF16),
            shape((tokens, D), BF16),
            shape((PLANE, 8, count), F32),
            grads,
            grads,
        ],
        grid_spec=pltpu.PrefetchScalarGridSpec(
            num_scalar_prefetch=1,
            grid=(OWN,),
            in_specs=[
                whole((tokens, D)),
                whole((tokens, D)),
                whole(gates.shape),
                pl.BlockSpec((1, D, 2, units), lambda e, info: (info[0] + e, 0, 0, 0)),
                pl.BlockSpec((1, D, units), lambda e, info: (info[0] + e, 0, 0)),
            ],
            out_specs=[
                whole((tokens, D)),
                whole((tokens, D)),
                whole((PLANE, 8, count)),
                grad_spec,
                grad_spec,
            ],
            scratch_shapes=[
                pltpu.VMEM((D, tokens), BF16),
                pltpu.VMEM((D, tokens), BF16),
                pltpu.VMEM((D, 2 * units), BF16),
                pltpu.VMEM((tokens, 128), F32),
                pltpu.VMEM((tokens, 128), F32),
                pltpu.VMEM((tokens, D), F32),
                pltpu.VMEM((tokens, D), F32),
                pltpu.VMEM((tokens, 2 * units), BF16),
                pltpu.VMEM((tokens, units), BF16),
            ],
        ),
        compiler_params=pltpu.CompilerParams(vmem_limit_bytes=60 * 2**20),
        cost_estimate=pl.CostEstimate(
            flops=20 * 2**30, bytes_accessed=32 * 2**20, transcendentals=2**20
        ),
        name="experts",
    )(info, hidden, cot, gates, expert_in, expert_out)


def rms_scale(values):
    return lax.rsqrt(jnp.mean(values * values, axis=-1, keepdims=True) + EPS)


def rotate(values, position, sign):
    half_dim = values.shape[-1] // 2
    frequency = jnp.exp(
        -jnp.log(jnp.float32(THETA))
        * jnp.arange(half_dim, dtype=jnp.float32)
        * (2.0 / values.shape[-1])
    )
    angles = position.astype(jnp.float32)[:, None] * frequency[None, :]
    cosine = jnp.cos(angles)[:, None, :]
    sine_part = sign * jnp.sin(angles)[:, None, :]
    lower_part = values[..., :half_dim]
    upper_part = values[..., half_dim:]
    return jnp.concatenate(
        [
            lower_part * cosine - upper_part * sine_part,
            upper_part * cosine + lower_part * sine_part,
        ],
        axis=-1,
    )


def body(
    tokens,
    w_query,
    w_key,
    w_value,
    w_output,
    attn_gain,
    w_router,
    expert_in,
    expert_out,
    moe_gain,
    segments,
    routes,
    priority,
    cotangent,
):
    ctx_count = lax.axis_size("ctx")
    ctx_index = lax.axis_index("ctx")
    devices = ctx_count * 2
    outers = ctx_count // INNER
    owner_rows = D // devices
    block_rows = tokens.shape[2]
    half_rows = block_rows * ctx_count
    tok_count = 2 * block_rows
    plane_rows = PLANE * tok_count
    group_size = HEADS // KV_HEADS
    kv_width = KV_HEADS * HEAD_DIM
    f32 = jnp.float32
    bf16 = jnp.bfloat16
    first_expert = (ctx_index % INNER) * OWN

    small = jnp.concatenate(
        [w_router.T, attn_gain[None], moe_gain[None], jnp.zeros((14, w_router.shape[0]), bf16)]
    )
    cot_own = cotangent.reshape(tok_count, D)
    plane_groups = [
        [base + member for member in range(PLANE)] for base in range(0, devices, PLANE)
    ]

    def gather_plane(block):
        return lax.all_gather(
            block, ("ctx", "wsh"), axis=0, tiled=True, axis_index_groups=plane_groups
        )

    qkv_w, small_all = gather_weights(w_query, w_key, w_value, small)
    output_w = lax.all_gather(w_output, "wsh", axis=0, tiled=True)
    cot_all = gather_plane(cot_own)
    small_all = small_all.transpose(1, 0, 2).reshape(32, D)
    router_t = small_all[:EXPERTS]
    gain_one_f = small_all[EXPERTS].astype(f32)
    gain_two_f = small_all[EXPERTS + 1].astype(f32)

    token_rows = tokens.reshape(tok_count, D).astype(f32)
    scale_one = rms_scale(token_rows)
    normed_one = token_rows * scale_one
    hidden_one = (normed_one * gain_one_f).astype(bf16)
    qkv_lin = jnp.dot(hidden_one, qkv_w, preferred_element_type=f32)
    block_total = 2 * ctx_count
    block_ids = jnp.stack([ctx_index, block_total - 1 - ctx_index])
    query_pos = block_ids[:, None] * block_rows + jnp.arange(block_rows, dtype=jnp.int32)[None, :]
    flat_pos = query_pos.reshape(tok_count)
    segment_ids = segments[0]
    query_seg = jnp.stack(
        [
            lax.dynamic_slice_in_dim(segment_ids, block_ids[half] * block_rows, block_rows)
            for half in range(2)
        ]
    )
    query_start = jnp.sum(
        (segment_ids[None, None, :] < query_seg[:, :, None]).astype(jnp.int32), axis=-1
    )
    info = jnp.concatenate(
        [
            query_start[:, 0] // CHUNK,
            ((block_ids + 1) * block_rows + CHUNK - 1) // CHUNK,
            block_ids * block_rows,
            jnp.zeros((2,), jnp.int32),
        ]
    )
    start_cols = query_start.reshape(tok_count, 1)
    start_rows = jnp.tile(query_start, (1, 4))
    frequency = jnp.exp(
        -jnp.log(jnp.float32(THETA))
        * jnp.arange(HEAD_DIM // 2, dtype=jnp.float32)
        * (2.0 / HEAD_DIM)
    )
    angles = flat_pos.astype(f32)[:, None] * frequency[None, :]
    cosine, sine = jnp.cos(angles), jnp.sin(angles)
    cosine = jnp.concatenate([cosine] * 4, axis=1)
    sine = jnp.concatenate([-sine, sine] * 2, axis=1)
    rot_query = rotate(qkv_lin[:, :1024].reshape(tok_count, HEADS, HEAD_DIM), flat_pos, 1.0)
    rot_key = rotate(qkv_lin[:, 1024:1536].reshape(tok_count, KV_HEADS, HEAD_DIM), flat_pos, 1.0)
    queries = rot_query.astype(bf16).reshape(tok_count, HEADS * HEAD_DIM)
    kv_own = jnp.concatenate(
        [rot_key.astype(bf16).reshape(tok_count, kv_width), qkv_lin[:, 1536:].astype(bf16)], axis=1
    ).reshape(2, block_rows, 2 * kv_width)
    kv_all = kv_gather(kv_own, ctx_count).reshape(block_total * block_rows, 2 * kv_width)
    token_low = tokens.reshape(tok_count, D)
    attn_raw, attn_total, mixed, first_sum, hidden_two, gate, kept = attend(
        info,
        queries,
        kv_all,
        start_cols,
        token_low,
        output_w,
        small_all,
        routes.reshape(tok_count, TOPK).T,
        priority.reshape(tok_count, TOPK).T,
    )

    hidden_all, gates_all = plane_gather([hidden_two, gate * kept], 4, "gather_hidden")
    left_one = gather_plane(hidden_one)
    left_mixed = gather_plane(mixed)
    outer_index = ctx_index // INNER
    moe_part, hidden_part, picks, give, keep = experts(
        jnp.stack([first_expert, outer_index % 2]).astype(jnp.int32),
        hidden_all.reshape(plane_rows, D),
        cot_all,
        gates_all,
        expert_in,
        expert_out,
        outers,
    )

    def exchange(rows, bit):
        pairs = [(member, member ^ (bit * INNER)) for member in range(ctx_count)]
        return lax.ppermute(rows, "ctx", pairs)

    def halve(total, bit):
        side = (outer_index // bit) % 2
        split = total.reshape(total.shape[0], total.shape[1] // 2, 2, *total.shape[2:])
        return [
            lax.dynamic_index_in_dim(split, which, 2, keepdims=False) for which in (1 - side, side)
        ]

    def add(kept_rows, arrived):
        return (kept_rows.astype(f32) + arrived.astype(f32)).astype(bf16)

    portions = [slice(0, OWN // 2), slice(OWN // 2, OWN)]
    arrived = [exchange(give[portion], 1) for portion in portions]
    kept_rows = [keep[portion] for portion in portions]
    hidden_grad, picks_all = plane_reduce(
        [hidden_part.reshape(PLANE, tok_count, D)], picks, 5, "reduce_hidden"
    )
    first_grad, attn_grad, query_lin_grad, kv_terms, small_rows = back(
        info,
        hidden_grad,
        picks_all,
        gate,
        kept,
        small_all,
        first_sum,
        cot_own,
        output_w,
        attn_raw,
        attn_total,
        queries,
        kv_all,
        start_rows,
        cosine,
        sine,
    )
    bit = 2
    while bit < outers:
        if bit == 2:
            arrived[0], kv_terms = lax.optimization_barrier((arrived[0], kv_terms))
        for member in range(2):
            total = add(kept_rows[member], arrived[member])
            given, kept_rows[member] = halve(total, bit)
            if bit == 2 and member == 0:
                given, kv_terms = lax.optimization_barrier((given, kv_terms))
            arrived[member] = exchange(given, bit)
        bit *= 2
    output, token_grad, attn_part, small_part = finish(
        kv_terms.reshape(block_total, block_rows, 2 * kv_width),
        moe_part,
        [
            first_sum,
            query_lin_grad,
            attn_grad,
            first_grad,
            token_low,
            small_all,
            cosine,
            sine,
            qkv_w,
            left_one,
            left_mixed,
            small_rows,
        ],
        ctx_count,
    )
    near = jnp.concatenate(
        [add(kept_rows[member], arrived[member]) for member in range(2)], axis=0
    ).reshape(OWN, PLANE, owner_rows, -1)
    attn_in, small_in, near_in = owners([attn_part, small_part], [near], devices, 7, "owners")
    hidden_units = expert_out.shape[-1]
    qkv_cols = 2048 // PLANE
    attn_sum = jnp.sum(
        attn_in.astype(f32).reshape(outers, PLANE, owner_rows, 3 * D // PLANE), axis=0
    ).transpose(1, 0, 2)
    qkv_sum = attn_sum[:, :, :qkv_cols].reshape(owner_rows, 2048)
    output_sum = attn_sum[:, :, qkv_cols:].reshape(owner_rows, D)
    near_in = near_in.astype(f32)
    inner_sum = (
        near_in[..., : 2 * hidden_units]
        .reshape(INNER, 2, OWN, owner_rows, 2, hidden_units)
        .transpose(0, 2, 3, 4, 1, 5)
        .reshape(EXPERTS, owner_rows, 2, 2 * hidden_units)
    )
    outer_sum = (
        near_in[..., 2 * hidden_units :]
        .reshape(INNER, 2, OWN, owner_rows, hidden_units)
        .transpose(0, 2, 3, 1, 4)
        .reshape(EXPERTS, owner_rows, 2 * hidden_units)
    )
    small_sum = jnp.sum(small_in.astype(f32), axis=0)
    return (
        output.reshape(tokens.shape),
        token_grad.reshape(tokens.shape),
        qkv_sum[:, :1024],
        qkv_sum[:, 1024:1536],
        qkv_sum[:, 1536:],
        output_sum,
        small_sum[:, EXPERTS],
        small_sum[:, :EXPERTS],
        inner_sum,
        outer_sum,
        small_sum[:, EXPERTS + 1],
    )


def solution(mesh):
    placed = (
        P("wsh", None, "ctx", None),
        P("wsh", None),
        P("wsh", None),
        P("wsh", None),
        P("wsh", None),
        P("wsh"),
        P("wsh", None),
        P(None, None, None, "wsh"),
        P(None, None, "wsh"),
        P("wsh"),
        P("wsh", None),
        P("wsh", None, "ctx", None),
        P("wsh", None, "ctx", None),
        P("wsh", None, "ctx", None),
    )
    return jax.shard_map(
        body,
        mesh=mesh,
        in_specs=placed,
        out_specs=(
            P("wsh", None, "ctx", None),
            P("wsh", None, "ctx", None),
            P(("ctx", "wsh"), None),
            P(("ctx", "wsh"), None),
            P(("ctx", "wsh"), None),
            P(("ctx", "wsh"), None),
            P(("ctx", "wsh")),
            P(("ctx", "wsh"), None),
            P(None, ("ctx", "wsh"), None, None),
            P(None, ("ctx", "wsh"), None),
            P(("ctx", "wsh")),
        ),
        check_vma=False,
    )
```

```python
import functools

import jax
import jax.numpy as jnp
from jax import lax
from jax.experimental import pallas as pl
from jax.experimental.pallas import tpu as pltpu
from jax.sharding import PartitionSpec as P

D = 1024
HEADS = 16
KV_HEADS = 8
HEAD_DIM = 64
TOPK = 8
EXPERTS = 16
CAP = 80
PLANE = 8
INNER = 4
OWN = EXPERTS // INNER
FIRST = OWN // 2


RES_MULT = 0.22
ATT_MULT = 0.015625
EPS = 1e-06
THETA = 10000.0

MESH = pl.DeviceIdType.MESH
F32 = jnp.float32
BF16 = jnp.bfloat16
ANY = pl.BlockSpec(memory_space=pl.ANY)
VMEM = pl.BlockSpec(memory_space=pltpu.VMEM)


class Place:
    def __init__(self):
        self.c = lax.axis_index("ctx")
        self.w = lax.axis_index("wsh")
        self.core = self.c % 2
        self.y = (self.c // 2) % 2
        self.inner = self.c % INNER
        self.outer = self.c // INNER
        self.z = self.outer % 2
        self.q = self.z * 2 + self.core
        self.j = self.q * 2 + self.w
        self.beside = (self.c + 2 - 4 * self.y, self.w)

    def relative(self, dz, dc, dw):
        z = self.z + dz * (1 - 2 * self.z)
        core = self.core + dc * (1 - 2 * self.core)
        w = self.w + dw * (1 - 2 * self.w)
        ctx = self.c + INNER * (z - self.z) + core - self.core
        return (ctx, w), (z * 2 + core) * 2 + w


OTHERS = [(a, b, d) for a in range(2) for b in range(2) for d in range(2) if a + b + d]
XY = [(0, 0, 1), (1, 0, 0), (1, 0, 1)]


def meet(devices):
    barrier = pltpu.get_barrier_semaphore()
    for device in devices:
        pl.semaphore_signal(barrier, inc=1, device_id=device, device_id_type=MESH)
    pl.semaphore_wait(barrier, len(devices))


def remote(src, dst, send, recv, device):
    return pltpu.make_async_remote_copy(
        src_ref=src,
        dst_ref=dst,
        send_sem=send,
        recv_sem=recv,
        device_id=device,
        device_id_type=MESH,
    )


def comm_call(kernel, out_shape, in_specs, out_specs, scratch, ident, name, vmem=None, us=20):
    return pl.pallas_call(
        kernel,
        out_shape=out_shape,
        in_specs=in_specs,
        out_specs=out_specs,
        scratch_shapes=scratch,
        compiler_params=pltpu.CompilerParams(
            collective_id=ident, has_side_effects=True, vmem_limit_bytes=vmem
        ),
        cost_estimate=pl.CostEstimate(
            flops=us * 10**9, bytes_accessed=us * 3 * 2**20, transcendentals=0
        ),
        name=name,
    )


DMA = pltpu.SemaphoreType.DMA


def room(arrays, scratch=(), spare=12):
    total = 0
    for array in list(arrays) + list(scratch):
        inner = getattr(array, "inner_aval", array)
        size = jnp.dtype(inner.dtype).itemsize
        for extent in inner.shape:
            size *= extent
        total += size
    return min(total + spare * 2**20, 62 * 2**20)


class Halving:
    def __init__(self, at, outers, sums, arrived, send, recv):
        self.at, self.sums, self.arrived = at, sums, arrived
        self.send, self.recv = send, recv
        self.bits = [2**k for k in range(1, outers.bit_length() - 1)]
        self.levels = [(0, outers // 2)]
        for bit in self.bits:
            start, many = self.levels[-1]
            self.levels.append((start + many, many // 2))
        self.copies = []

    def device(self, bit):
        at = self.at
        return (at.c + INNER * bit * (1 - 2 * ((at.outer // bit) % 2)), at.w)

    def start(self, step):
        bit = self.bits[step]
        side = (self.at.outer // bit) % 2
        start, many = self.levels[step]
        for m in range(many // 2):
            copy = remote(
                self.sums.at[start + 2 * m + 1 - side],
                self.arrived.at[start + m],
                self.send.at[start + m],
                self.recv.at[start + m],
                self.device(bit),
            )
            copy.start()
            self.copies.append(copy)

    def add(self, step):
        side = (self.at.outer // self.bits[step]) % 2
        start, many = self.levels[step]
        after, half = self.levels[step + 1]
        for m in range(half):
            self.copies[len(self.copies) - half + m].wait_recv()
            total = self.sums[start + 2 * m + side].astype(F32) + self.arrived[start + m].astype(F32)
            self.sums[after + m] = total.astype(BF16)

    def finish(self):
        for step in range(len(self.bits)):
            if step > 0:
                self.start(step)
            self.add(step)
        for copy in self.copies:
            copy.wait_send()
        return self.sums[self.levels[-1][0]]


def gather_start(at, pairs, send, recv, local):
    copies = []
    for index, (src, dst) in enumerate(pairs):
        keep = pltpu.make_async_copy(src, dst.at[at.j], local.at[index])
        keep.start()
        sends = []
        for slot, bits in enumerate(XY + [(0, 1, 0)]):
            device, unused = at.relative(*bits)
            copy = remote(src, dst.at[at.j], send.at[index, slot], recv.at[index, slot], device)
            copy.start()
            sends.append(copy)
        copies.append((keep, sends))
    return copies


def gather_pass(at, pairs, copies, send, recv):
    sib, unused = at.relative(0, 1, 0)
    passed = []
    for slot, bits in enumerate(XY):
        unused, j_from = at.relative(*bits)
        for index, (src, dst) in enumerate(pairs):
            copies[index][1][slot].wait_recv()
            block = dst.at[j_from]
            copy = remote(
                block, block, send.at[index, 4 + slot], recv.at[index, 4 + slot], sib
            )
            copy.start()
            passed.append(copy)
    return passed


def gather_wait(copies, passed):
    for keep, sends in copies:
        keep.wait()
        sends[3].wait_recv()
        for copy in sends:
            copy.wait_send()
    for copy in passed:
        copy.wait()


def turn(values, cosine, sine):
    lane = lax.broadcasted_iota(jnp.int32, cosine.shape, 1)
    first = lane % HEAD_DIM < HEAD_DIM // 2
    blocks = []
    for start in range(0, values.shape[1], 128):
        u = values[:, start : start + 128]
        swapped = jnp.where(first, pltpu.roll(u, 96, 1), pltpu.roll(u, 32, 1))
        blocks.append(u * cosine + swapped * sine)
    return jnp.concatenate(blocks, axis=1)


def dot_nt(a, b):
    return lax.dot_general(a, b, (((1,), (1,)), ((), ())), preferred_element_type=F32)


def dot_tn(a, b):
    return lax.dot_general(a, b, (((0,), (0,)), ((), ())), preferred_element_type=F32)


def dot_nn(a, b):
    return jnp.dot(a, b, preferred_element_type=F32)


def owners_kernel(devices, count, near_count, *refs):
    total = count + near_count
    parts, nears = refs[:count], refs[count:total]
    outs, near_outs = refs[total : total + count], refs[total + count : 2 * total]
    send, recv, local, nsend, nrecv, nlocal = refs[2 * total :]
    at = Place()
    me = at.c * 2 + at.w
    rows = D // devices

    def device_of(r):
        index = lax.rem(me + r, devices)
        return index, (index // 2, lax.rem(index, 2))

    def rows_of(ref, index):
        return ref.at[pl.ds(pl.multiple_of(index * rows, rows), rows), :]

    barrier = pltpu.get_barrier_semaphore()

    def greet(r, carry):
        unused, device = device_of(r)
        pl.semaphore_signal(barrier, inc=1, device_id=device, device_id_type=MESH)
        return carry

    lax.fori_loop(1, devices, greet, 0)
    pl.semaphore_wait(barrier, devices - 1)

    def copy_of(k, r):
        index, device = device_of(r)
        return remote(rows_of(parts[k], index), outs[k].at[me], send.at[k, r], recv.at[k, r], device)

    def start(r, carry):
        for k in range(count):
            copy_of(k, r).start()
        return carry

    lax.fori_loop(1, devices, start, 0)

    near_copies = []
    for k in range(near_count):
        for slot, bits in enumerate(OTHERS):
            device, j_to = at.relative(*bits)
            copy = remote(
                nears[k].at[:, j_to], near_outs[k].at[at.j], nsend.at[k, slot], nrecv.at[k, slot], device
            )
            copy.start()
            near_copies.append(copy)
    keeps = []
    for k in range(count):
        keep = pltpu.make_async_copy(rows_of(parts[k], me), outs[k].at[me], local.at[k])
        keep.start()
        keeps.append(keep)
    for k in range(near_count):
        keep = pltpu.make_async_copy(nears[k].at[:, at.j], near_outs[k].at[at.j], nlocal.at[k])
        keep.start()
        keeps.append(keep)

    def finish(r, carry):
        for k in range(count):
            copy_of(k, r).wait()
        return carry

    lax.fori_loop(1, devices, finish, 0)
    for copy in near_copies:
        copy.wait()
    for keep in keeps:
        keep.wait()


def owners(parts, nears, devices, ident, name):
    count, near_count = len(parts), len(nears)
    rows = D // devices
    shape = jax.ShapeDtypeStruct
    shapes = [shape((devices, rows, part.shape[-1]), part.dtype) for part in parts]
    for near in nears:
        lead, members, near_rows, width = near.shape
        shapes.append(shape((members, lead, near_rows, width), near.dtype))
    return comm_call(
        functools.partial(owners_kernel, devices, count, near_count),
        shapes,
        [ANY] * (count + near_count),
        [VMEM] * (count + near_count),
        [
            DMA((count, devices)),
            DMA((count, devices)),
            DMA((count,)),
            DMA((near_count, 7)),
            DMA((near_count, 7)),
            DMA((near_count,)),
        ],
        ident,
        name,
        vmem=60 * 2**20,
    )(*parts, *nears)


CHUNK = 256
PAIRS = KV_HEADS // 2
NEVER = -1e30


def low_lanes(shape):
    return lax.broadcasted_iota(jnp.int32, shape, 1) < HEAD_DIM


def spread(block):
    a, b = block[:, :128], block[:, 128:]
    low = low_lanes(a.shape)
    zero = jnp.zeros_like(a)
    return jnp.concatenate(
        [
            jnp.where(low, a, zero),
            jnp.where(low, pltpu.roll(a, HEAD_DIM, 1), zero),
            jnp.where(low, zero, pltpu.roll(b, HEAD_DIM, 1)),
            jnp.where(low, zero, b),
        ],
        axis=0,
    )


def unspread(four):
    rows = four.shape[0] // 4
    r0, r1, r2, r3 = (four[k * rows : (k + 1) * rows] for k in range(4))
    low = low_lanes(r0.shape)
    return jnp.concatenate(
        [
            jnp.where(low, r0, pltpu.roll(r1, HEAD_DIM, 1)),
            jnp.where(low, pltpu.roll(r2, HEAD_DIM, 1), r3),
        ],
        axis=1,
    )


DOCS = 8


def reach(starts, place):
    first = jnp.zeros_like(place)
    for d in range(1, DOCS):
        first = jnp.where(place >= starts[d], starts[d], first)
    return first


def half_span(half, rows, keys):
    block = lax.axis_index("ctx")
    if half == 1:
        block = keys // rows - 1 - block
    base = block * rows
    return base, (base + rows + CHUNK - 1) // CHUNK


def key_block(kv, chunk, rows, col):
    many = CHUNK // rows
    picked = kv[pl.ds(chunk * many, many), :, pl.ds(col, 128)]
    return picked.reshape(CHUNK, 128)


def attend_rows(
    starts,
    q_ref,
    kv_ref,
    tok_ref,
    wo_ref,
    small_ref,
    route_ref,
    prio_ref,
    raw_ref,
    total_ref,
    mixed_ref,
    sum_ref,
    hid_ref,
    gate_ref,
    kept_ref,
    send_ref,
    acc,
    acc_l,
):
    rows = q_ref.shape[0] // 2
    width = PAIRS * 128
    keys = kv_ref.shape[0] * rows
    for half in range(2):
        base, chunks = half_span(half, rows, keys)
        q_four = []
        for pair in range(PAIRS):
            block = q_ref[pl.ds(half * rows, rows), pl.ds(pair * 256, 256)].astype(F32) * ATT_MULT
            q_four.append(spread(block).astype(BF16))
        acc[...] = jnp.zeros_like(acc)
        acc_l[...] = jnp.zeros_like(acc_l)
        place = base + lax.broadcasted_iota(jnp.int32, (rows, 1), 0)
        first = reach(starts, place)

        def step(chunk, carry):
            at_row = pl.multiple_of(chunk * CHUNK, CHUNK)
            key_pos = at_row + lax.broadcasted_iota(jnp.int32, (1, CHUNK), 1)
            bias = jnp.where((key_pos >= first) & (key_pos <= place), 0.0, NEVER)
            bias = jnp.concatenate([bias] * 4, axis=0)
            for pair in range(PAIRS):
                key = key_block(kv_ref, chunk, rows, pair * 128)
                value = key_block(kv_ref, chunk, rows, width + pair * 128)
                e = jnp.exp(dot_nt(q_four[pair], key) + bias)
                part = e[:, :128]
                for k in range(1, CHUNK // 128):
                    part = part + e[:, k * 128 : (k + 1) * 128]
                acc_l[pair] += part
                acc[pair] += dot_nn(e.astype(BF16), value)
            return carry

        lax.fori_loop(0, chunks, step, 0)
        for pair in range(PAIRS):
            total = jnp.sum(acc_l[pair], axis=1, keepdims=True)
            total = jnp.broadcast_to(total, (4 * rows, 128))
            here = pl.ds(half * rows, rows), pl.ds(pair * 256, 256)
            raw_ref[here] = unspread(acc[pair] / total)
            total_ref[here] = unspread(total)
    mixed = raw_ref[...].astype(BF16)
    mixed_ref[...] = mixed
    first_sum = tok_ref[...].astype(F32) + RES_MULT * dot_nn(mixed, wo_ref[...])
    sum_ref[...] = first_sum
    scale = lax.rsqrt(jnp.mean(first_sum * first_sum, axis=1, keepdims=True) + EPS)
    gain_two = small_ref[pl.ds(EXPERTS + 1, 1), :].astype(F32)
    hidden = (first_sum * scale * gain_two).astype(BF16)
    hid_ref[...] = hidden

    logits = dot_nt(small_ref[...], hidden)[:EXPERTS]
    count = 2 * rows
    expert = lax.broadcasted_iota(jnp.int32, (EXPERTS, count), 0)
    routed = jnp.zeros((EXPERTS, count), F32)
    prio = jnp.zeros((EXPERTS, count), F32)
    for k in range(TOPK):
        line = [
            jnp.concatenate([ref[0, pl.ds(k, 1), :], ref[1, pl.ds(k, 1), :]], axis=1)
            for ref in (route_ref, prio_ref)
        ]
        same = expert == line[0]
        routed = jnp.where(same, 1.0, routed)
        prio = jnp.where(same, line[1].astype(F32), prio)
    chosen = routed > 0.0
    order = lax.broadcasted_iota(jnp.int32, (EXPERTS, count), 1).astype(F32)
    key = jnp.where(chosen, prio * float(count) + order, 65536.0 * count)
    key_cols = jnp.concatenate([key, jnp.zeros((count - EXPERTS, count), F32)], axis=0).T
    ranks = []
    for e in range(EXPERTS):
        ahead = jnp.where(key_cols[:, e : e + 1] < key[e : e + 1, :], 1.0, 0.0)
        ranks.append(jnp.sum(ahead, axis=0, keepdims=True))
    rank = jnp.concatenate(ranks, axis=0)
    top = jnp.max(jnp.where(chosen, logits, -3e38), axis=0, keepdims=True)
    weight = jnp.where(chosen, jnp.exp(logits - top), 0.0)
    gate = weight / jnp.sum(weight, axis=0, keepdims=True)
    kept = jnp.where(chosen & (rank < CAP), 1.0, 0.0)
    gate_ref[...] = gate
    kept_ref[...] = kept
    send_ref[...] = gate * kept


SMEM = pl.BlockSpec(memory_space=pltpu.SMEM)


def finish_kernel(
    outers,
    part,
    moe,
    sum_ref,
    dq_ref,
    da_ref,
    dy_ref,
    tok_ref,
    small_ref,
    cos_ref,
    sin_ref,
    wqkv_in,
    left_in,
    rows_ref,
    z_ref,
    out_ref,
    token_ref,
    attn_ref,
    small_o,
    z_o,
    wqkv_ref,
    left_ref,
    z_sums,
    z_in_rows,
    own,
    half_in,
    y_in,
    z_in,
    m_near,
    m_x,
    m_y,
    qkv,
    swap,
    swapped,
    ss,
    sr,
    ys,
    yr,
    zs,
    zr,
    ns,
    nr,
    ws,
    wr,
    vs,
    vr,
    ls,
    os,
):
    at = Place()
    blocks, rows, full = part.shape
    loads = [
        pltpu.make_async_copy(wqkv_in, wqkv_ref, ls.at[0]),
        pltpu.make_async_copy(left_in, left_ref, ls.at[1]),
    ]
    for copy in loads:
        copy.start()
    width = full // 2
    cuts = 4
    step_width = full // cuts
    count = 2 * rows
    sib, unused = at.relative(0, 1, 0)
    side = at.beside
    along_to, unused = at.relative(1, 0, 0)
    across, unused = at.relative(0, 0, 1)
    other = [lax.rem(at.outer + r, outers) for r in range(outers)]
    far = [(other[r] * INNER + at.inner, at.w) for r in range(1, outers)]
    rest = [
        Halving(at, outers, z_sums.at[e], z_in_rows.at[e], vs.at[e], vr.at[e])
        for e in range(z_sums.shape[0])
    ]
    for e in range(len(rest)):
        z_sums[e, pl.ds(0, outers // 2)] = z_ref[:, e]
    meet([at.relative(*bits)[0] for bits in OTHERS] + far + [at.beside])
    if outers > 2:
        rest[0].start(0)

    def own_block(half, o, y, core):
        index = (o * 2 + y) * 2 + core
        return index if half == 0 else blocks - 1 - index

    own_loads = []
    for y in range(2):
        for h in range(2):
            for o in range(outers):
                copy = pltpu.make_async_copy(
                    part.at[own_block(h, o, y, at.core)], own.at[y, h, o], os.at[y, h, o]
                )
                copy.start()
                own_loads.append(copy)
    first = {}
    for k in range(cuts):
        cols = pl.ds(k * step_width, step_width)
        for y in range(2):
            for h in range(2):
                for o in range(outers):
                    copy = remote(
                        part.at[own_block(h, o, y, 1 - at.core), :, cols],
                        half_in.at[y, h, o, :, cols],
                        ss.at[k, y, h, o],
                        sr.at[k, y, h, o],
                        sib,
                    )
                    copy.start()
                    first[k, y, h, o] = copy
    near = remote(moe.at[:, 1 - at.core], m_near, ns.at[0], nr.at[0], sib)
    near.start()
    for copy in own_loads:
        copy.wait()
    second = []
    for k in range(cuts):
        cols = pl.ds(k * step_width, step_width)
        for y in range(2):
            for h in range(2):
                for o in range(outers):
                    first[k, y, h, o].wait_recv()
                    total = own[y, h, o, :, cols].astype(F32) + half_in[
                        y, h, o, :, cols
                    ].astype(F32)
                    half_in[y, h, o, :, cols] = total.astype(BF16)
        copy = remote(
            half_in.at[1 - at.y, :, :, :, cols], y_in.at[:, :, :, cols], ys.at[k], yr.at[k], side
        )
        copy.start()
        second.append(copy)
    near.wait_recv()
    for y in range(2):
        for w in range(2):
            total = moe[y, at.core, w].astype(F32) + m_near[y, w].astype(F32)
            m_near[y, w] = total.astype(BF16)
    cross = remote(m_near.at[:, 1 - at.w], m_x, ns.at[1], nr.at[1], across)
    cross.start()
    third = []

    def z_send(k):
        cols = pl.ds(k * step_width, step_width)
        second[k].wait_recv()
        for o in range(outers):
            for h in range(2):
                total = half_in[at.y, h, o, :, cols].astype(F32) + y_in[h, o, :, cols].astype(F32)
                half_in[at.y, h, o, :, cols] = total.astype(BF16)
        for r in range(1, outers):
            copy = remote(
                half_in.at[at.y, :, other[r], :, cols],
                z_in.at[r, :, :, cols],
                zs.at[k, r],
                zr.at[k, r],
                far[r - 1],
            )
            copy.start()
            third.append(copy)

    z_send(0)
    z_send(1)
    cross.wait_recv()
    for y in range(2):
        total = m_near[y, at.w].astype(F32) + m_x[y].astype(F32)
        m_x[y] = total.astype(BF16)
    along = remote(m_x.at[1 - at.z], m_y, ns.at[2], nr.at[2], along_to)
    along.start()
    for k in range(2, cuts):
        z_send(k)
    qkv[:, : HEADS * HEAD_DIM] = dq_ref[...]
    along.wait_recv()
    moe_sum = m_x[at.z].astype(F32) + m_y[...].astype(F32)
    out_ref[...] = (sum_ref[...] + RES_MULT * moe_sum).astype(BF16)
    tok = tok_ref[...].astype(F32)
    scale = lax.rsqrt(jnp.mean(tok * tok, axis=1, keepdims=True) + EPS)
    normed = tok * scale
    gain_one = small_ref[pl.ds(EXPERTS, 1), :].astype(F32)
    for copy in third:
        copy.wait_recv()
    if outers > 2:
        for halving in rest[1:]:
            halving.start(0)
    cosine = cos_ref[...]
    sine = -sin_ref[...]
    base = HEADS * HEAD_DIM
    for h in range(2):
        here = slice(h * rows, (h + 1) * rows)
        total = half_in[at.y, h, at.outer].astype(F32)
        for r in range(1, outers):
            total = total + z_in[r, h].astype(F32)
        qkv[here, base : base + width] = turn(total[:, :width], cosine[here], sine[here]).astype(BF16)
        qkv[here, base + width :] = total[:, width:].astype(BF16)
    wide = full * 2 // PLANE
    for j in range(PLANE):
        swap[j, :, :wide] = qkv[:, j * wide : (j + 1) * wide]
        swap[j, :, wide:] = da_ref[:, j * (D // PLANE) : (j + 1) * (D // PLANE)]
    swaps = []
    for slot, bits in enumerate(OTHERS):
        device, j_to = at.relative(*bits)
        copy = remote(swap.at[j_to], swapped.at[at.j], ws.at[slot], wr.at[slot], device)
        copy.start()
        swaps.append(copy)
    swapped[at.j] = swap[at.j]
    for copy in loads:
        copy.wait()
    hidden_grad = dot_nt(qkv[...], wqkv_ref[...])
    small = rows_ref[...]
    gain_grad = jnp.sum(hidden_grad * normed, axis=0, keepdims=True)
    line = lax.broadcasted_iota(jnp.int32, small.shape, 0)
    small = jnp.where(line == EXPERTS, gain_grad, small)
    small = jnp.concatenate([small, jnp.zeros((128 - small.shape[0], D), F32)], axis=0)
    small_o[...] = small.T.astype(BF16)
    hidden_grad = hidden_grad * gain_one
    token_ref[...] = dy_ref[...] + scale * (
        hidden_grad - normed * jnp.mean(hidden_grad * normed, axis=1, keepdims=True)
    )
    for copy in swaps:
        copy.wait_recv()
    all_rows = PLANE * count
    left_one = left_ref[0].reshape(all_rows, D)
    left_mixed = left_ref[1].reshape(all_rows, D)
    grads = swapped[...].reshape(all_rows, wide + D // PLANE)
    attn_ref[:, :wide] = dot_tn(left_one, grads[:, :wide]).astype(BF16)
    attn_ref[:, wide:] = dot_tn(left_mixed, grads[:, wide:]).astype(BF16)
    for e in range(len(rest)):
        z_o[e] = rest[e].finish()
    for copy in list(first.values()) + second + third + swaps + [near, cross, along]:
        copy.wait_send()


def finish(part, moe, arrays, z_half, ctx_count):
    outers = ctx_count // INNER
    blocks, rows, full = part.shape
    count = 2 * rows
    shape = jax.ShapeDtypeStruct
    columns = 3 * D // PLANE
    return comm_call(
        functools.partial(finish_kernel, outers),
        [
            shape((count, D), BF16),
            shape((count, D), F32),
            shape((D, columns), BF16),
            shape((D, 128), BF16),
            shape(z_half.shape[1:], BF16),
        ],
        [ANY] + [VMEM] * (len(arrays) - 2) + [ANY] * 2 + [VMEM] * 2,
        [VMEM] * 5,
        [
            pltpu.VMEM((D, 2 * full), BF16),
            pltpu.VMEM((2, PLANE, count, D), BF16),
            pltpu.VMEM((z_half.shape[1], outers) + z_half.shape[2:], BF16),
            pltpu.VMEM((z_half.shape[1], outers) + z_half.shape[2:], BF16),
            pltpu.VMEM((2, 2, outers, rows, full), BF16),
            pltpu.VMEM((2, 2, outers, rows, full), BF16),
            pltpu.VMEM((2, outers, rows, full), BF16),
            pltpu.VMEM((outers, 2, rows, full), BF16),
            pltpu.VMEM((2, 2, count, D), BF16),
            pltpu.VMEM((2, count, D), BF16),
            pltpu.VMEM((count, D), BF16),
            pltpu.VMEM((count, 2 * full), BF16),
            pltpu.VMEM((PLANE, count, columns), BF16),
            pltpu.VMEM((PLANE, count, columns), BF16),
            DMA((4, 2, 2, outers)),
            DMA((4, 2, 2, outers)),
            DMA((4,)),
            DMA((4,)),
            DMA((4, outers)),
            DMA((4, outers)),
            DMA((3,)),
            DMA((3,)),
            DMA((7,)),
            DMA((7,)),
            DMA((z_half.shape[1], outers)),
            DMA((z_half.shape[1], outers)),
            DMA((2,)),
            DMA((2, 2, outers)),
        ],
        3,
        "finish",
        vmem=63 * 2**20,
        us=60,
    )(part, moe.reshape(2, 2, 2, count, D), *arrays, z_half)


def gate_columns(gates, cols):
    count = gates.shape[-1]
    for j in range(PLANE):
        block = jnp.concatenate([gates[j], jnp.zeros((128 - EXPERTS, count), F32)], axis=0)
        cols[pl.ds(j * count, count), :] = block.T


def expert_step(both, back_act, gate, units):
    gv, uv = both[:, :units], both[:, units:]
    sig = jax.nn.sigmoid(gv)
    silu = gv * sig
    act = silu * uv
    pick = jnp.sum(act * back_act, axis=1, keepdims=True)
    kept = (gate * act).astype(BF16)
    back_act = gate * back_act
    slope = sig * (1.0 + gv * (1.0 - sig))
    low = jnp.concatenate([back_act * uv * slope, back_act * silu], axis=1).astype(BF16)
    return kept, pick, low


def lane_of(cols, lane):
    at = lax.broadcasted_iota(jnp.int32, cols.shape, 1)
    return jnp.sum(jnp.where(at == lane, cols, 0.0), axis=1, keepdims=True)


def opening_kernel(
    outers,
    starts,
    tok_ref,
    wq,
    wk,
    wv,
    wo,
    small,
    cot,
    cos_ref,
    sin_ref,
    route_ref,
    prio_ref,
    expert_in,
    expert_out,
    wqkv_o,
    wo_o,
    small_o,
    q_o,
    hid_o,
    kv_o,
    raw_o,
    total_o,
    mixed_o,
    sum_o,
    gate_o,
    kept_o,
    pick_o,
    z_o,
    part_o,
    kept_units_o,
    grad_o,
    left_o,
    wqkv,
    wout,
    own,
    tok_v,
    cos_v,
    sin_v,
    kv,
    cot_v,
    raw,
    out_w,
    inner_w,
    acc,
    acc_l,
    hid_two,
    gate_send,
    hid,
    gates,
    cot_t,
    backs,
    cols,
    pick_cols,
    staged,
    y_in,
    xs,
    xr,
    fs,
    fr,
    ls,
    zs,
    zr,
    ys,
    yr,
    cs,
    cr,
    hs,
    gs,
    gr,
    gl,
    es,
    ts,
    tr,
    tl,
    gd,
    us,
    ur,
    ul,
    vs,
    vr,
):
    at = Place()
    blocks, rows = kv.shape[:2]
    units = out_w.shape[-1]
    experts = at.q * OWN
    sib, unused = at.relative(0, 1, 0)
    partner, j_partner = at.relative(0, 0, 1)
    side, j_side = at.relative(1, 0, 0)
    unused, j_cross = at.relative(1, 0, 1)
    steps = sorted({1, outers - 1})
    far = [(lax.rem(at.outer + r, outers) * INNER + at.inner, at.w) for r in steps]
    expert_loads = {}

    def load_expert(e):
        copy = pltpu.make_async_copy(expert_in.at[experts + e], raw.at[e % 2], es.at[e % 2])
        copy.start()
        expert_loads[e] = copy

    def shape_expert(e):
        expert_loads[e].wait()
        inner_w[:, e * 2 * units : (e + 1) * 2 * units] = raw[e % 2].reshape(D, 2 * units)
        if e + 2 < OWN:
            load_expert(e + 2)

    out_loads = [
        pltpu.make_async_copy(expert_out.at[experts + e], out_w.at[e], es.at[2 + e])
        for e in range(OWN)
    ]
    for copy in out_loads:
        copy.start()
    load_expert(0)
    load_expert(1)
    meet([at.relative(*bits)[0] for bits in XY + [(0, 1, 0)]] + far + [at.beside])

    pieces = [(wk, wqkv, 1024), (wv, wqkv, 1536), (wq, wqkv, 0), (wo, wout, 0)]
    sends, passed, keeps = {}, {}, []

    def give(index):
        src, dst, col = pieces[index]
        depth, width = src.shape
        half = depth // 2
        copy = remote(
            src.at[pl.ds(at.core * half, half), :],
            dst.at[pl.ds(at.w * depth + at.core * half, half), pl.ds(col, width)],
            xs.at[index],
            xr.at[index],
            partner,
        )
        copy.start()
        sends[index] = copy

    def pass_on(index):
        src, dst, col = pieces[index]
        depth, width = src.shape
        half = depth // 2
        sends[index].wait_recv()
        piece = dst.at[pl.ds((1 - at.w) * depth + at.core * half, half), pl.ds(col, width)]
        copy = remote(piece, piece, fs.at[index], fr.at[index], sib)
        copy.start()
        passed[index] = copy

    wide = small.shape[1]
    mine = small_o.at[:, pl.ds(at.w * wide, wide)]
    gains = remote(small, mine, xs.at[4], xr.at[4], partner)
    gains.start()
    give(0)
    give(1)
    cot_sib = remote(cot, cot_v.at[at.j], gs.at[0], gr.at[0], sib)
    cot_sib.start()
    cot_side = remote(cot, cot_v.at[at.j], gs.at[1], gr.at[1], side)
    cot_side.start()
    cot_keep = pltpu.make_async_copy(cot, cot_v.at[at.j], gl)
    cot_keep.start()
    for index, (src, dst, col) in enumerate(pieces):
        depth, width = src.shape
        keep = pltpu.make_async_copy(
            src, dst.at[pl.ds(at.w * depth, depth), pl.ds(col, width)], ls.at[index]
        )
        keep.start()
        keeps.append(keep)
    loads = [
        pltpu.make_async_copy(src, dst, hs.at[4 + index])
        for index, (src, dst) in enumerate(
            ((tok_ref, tok_v), (cos_ref, cos_v), (sin_ref, sin_v), (small, mine))
        )
    ]
    for copy in loads:
        copy.start()
    for copy in loads:
        copy.wait()
    tok = tok_v[...].astype(F32)
    normed = tok * lax.rsqrt(jnp.mean(tok * tok, axis=1, keepdims=True) + EPS)
    gains.wait_recv()
    hidden = (normed * small_o[pl.ds(EXPERTS, 1), :].astype(F32)).astype(BF16)
    hid_o[...] = hidden
    cosine, sine = cos_v[...], sin_v[...]

    pass_on(0)
    pass_on(1)
    cot_across = remote(cot, cot_v.at[at.j], gs.at[2], gr.at[2], partner)
    cot_across.start()
    keeps[0].wait()
    keeps[1].wait()
    passed[0].wait_recv()
    key = dot_nn(hidden, wqkv[:, 1024:1536])
    key = turn(key, cosine, sine).astype(BF16)
    passed[1].wait_recv()
    value = dot_nn(hidden, wqkv[:, 1536:]).astype(BF16)
    width = key.shape[1]
    for half in range(2):
        own[half, :, :width] = key[half * rows : (half + 1) * rows]
        own[half, :, width:] = value[half * rows : (half + 1) * rows]

    def block_of(half, ctx):
        return kv.at[ctx] if half == 0 else kv.at[blocks - 1 - ctx]

    last = outers - 1
    hops = [(0, 0, 0)] + [
        (step, sign, step if sign < 0 else last + step)
        for step in range(1, outers)
        for sign in (-1, 1)
    ]

    def source(step, sign):
        return at.outer + sign * step

    def exists(step, sign):
        place = source(step, sign)
        return (place >= 0) & (place <= last)

    def block_from(half, step, sign, inner):
        place = lax.rem(source(step, sign) + outers, outers)
        return block_of(half, place * INNER + inner)

    below = (lax.rem(at.outer + last, outers) * INNER + at.inner, at.w)
    above = (lax.rem(at.outer + 1, outers) * INNER + at.inner, at.w)
    inner_side = at.inner + 2 - 4 * at.y

    def z_copy(half, slot, step, sign):
        src = own.at[half] if step == 0 else block_from(half, step, sign, at.inner)
        dst = block_from(half, step, sign, at.inner)
        slot_there = step + 1 if sign < 0 else last + step + 1
        return remote(
            src,
            dst,
            zs.at[half, slot_there],
            zr.at[half, slot_there],
            above if sign < 0 else below,
        )

    def y_copy(half, slot, step, sign):
        src = own.at[half] if step == 0 else block_from(half, step, sign, at.inner)
        dst = block_from(half, step, sign, at.inner)
        return remote(src, dst, ys.at[half, slot], yr.at[half, slot], at.beside)

    def c_copy(half, slot, step, sign, inner, base):
        src = (
            own.at[half]
            if step == 0 and base == 0
            else block_from(half, step, sign, inner)
        )
        dst = block_from(half, step, sign, inner)
        return remote(src, dst, cs.at[half, base + slot], cr.at[half, base + slot], sib)

    spots = 2 * outers - 1

    def spread_from(step, sign, slot, halves=(0, 1)):
        for half in halves:
            if step == 0:
                for way in (-1, 1):

                    @pl.when((at.outer < last) if way < 0 else (at.outer > 0))
                    def _():
                        z_copy(half, 0, 0, way).start()

            elif step < last:

                @pl.when((at.outer < last) if sign < 0 else (at.outer > 0))
                def _():
                    z_copy(half, slot, step, sign).start()

            y_copy(half, slot, step, sign).start()
            c_copy(half, slot, step, sign, at.inner, 0).start()

    spread_from(0, 0, 0)
    for half in range(2):
        keep = pltpu.make_async_copy(own.at[half], block_of(half, at.c), hs.at[half])
        keep.start()
        keeps.append(keep)

    def y_arrived(step, sign, slot):
        for half in range(2):
            y_copy(half, slot, step, sign).wait_recv()
            c_copy(half, slot, step, sign, inner_side, spots).start()

    def z_arrived(want):
        for step, sign, slot in hops[1:]:
            if step == want:

                @pl.when(exists(step, sign))
                def _():
                    for half in range(2):
                        z_copy(half, slot, step - 1, sign).wait_recv()
                        spread_from(step, sign, slot, (half,))

    def sides_arrived(want):
        for step, sign, slot in hops[1:]:
            if step == want:

                @pl.when(exists(step, sign))
                def _():
                    y_arrived(step, sign, slot)

    shape_expert(0)
    cot_across.wait_recv()
    give(2)
    cot_on = []

    def cot_pass(slot, j_from, device):
        block = cot_v.at[j_from]
        copy = remote(block, block, gs.at[slot], gr.at[slot], device)
        copy.start()
        cot_on.append(copy)

    cot_pass(3, j_partner, side)
    cot_pass(4, j_partner, sib)
    cot_side.wait_recv()
    cot_pass(5, j_side, sib)
    z_arrived(1)
    y_arrived(0, 0, 0)
    shape_expert(1)
    pass_on(2)
    give(3)
    shape_expert(2)
    if outers > 2:
        z_arrived(2)
    keeps[2].wait()
    passed[2].wait_recv()
    q_o[...] = turn(dot_nn(hidden, wqkv[:, :1024]), cosine, sine).astype(BF16)
    store = pltpu.make_async_copy(wqkv, wqkv_o, hs.at[2])
    store.start()
    shape_expert(3)
    sides_arrived(1)
    for step in range(3, outers):
        z_arrived(step)
        sides_arrived(step - 1)
    if outers > 2:
        sides_arrived(last)
    pass_on(3)
    cot_on[0].wait_recv()
    cot_pass(6, j_cross, sib)
    keeps[3].wait()
    passed[3].wait_recv()
    store_out = pltpu.make_async_copy(wout, wo_o, hs.at[3])
    store_out.start()
    def sibling_brought(step, sign, slot):
        for half in range(2):
            c_copy(half, slot, step, sign, at.inner, 0).wait_recv()
            c_copy(half, slot, step, sign, inner_side, spots).wait_recv()

    sibling_brought(0, 0, 0)
    for step, sign, slot in hops[1:]:

        @pl.when(exists(step, sign))
        def _():
            sibling_brought(step, sign, slot)

    for keep in keeps[4:]:
        keep.wait()
    store_kv = pltpu.make_async_copy(kv, kv_o, hs.at[4])
    store_kv.start()
    attend_rows(
        starts,
        q_o,
        kv,
        tok_v,
        wout,
        small_o,
        route_ref,
        prio_ref,
        raw_o,
        total_o,
        mixed_o,
        sum_o,
        hid_two,
        gate_o,
        kept_o,
        gate_send,
        acc,
        acc_l,
    )

    pairs = [(hid_two, hid), (gate_send, gates)]
    copies = gather_start(at, pairs, ts, tr, tl)
    for copy in [cot_sib] + cot_on[1:]:
        copy.wait_recv()
    cot_keep.wait()
    for copy in out_loads:
        copy.wait()
    tokens = cot_v.shape[0] * cot_v.shape[1]
    cot_rows = cot_v[...].reshape(tokens, D)
    cot_t[...] = cot_rows.T
    for e in range(OWN):
        backs[:, e * units : (e + 1) * units] = (RES_MULT * dot_nn(cot_rows, out_w[e])).astype(BF16)
    gather_wait(copies, gather_pass(at, pairs, copies, ts, tr))
    gate_columns(gates, cols)
    left_pairs = [(hid_o, left_o.at[0]), (mixed_o, left_o.at[1])]
    left_copies = gather_start(at, left_pairs, us, ur, ul)
    store_out.wait()
    passed[3].wait_send()
    hid_t = wout
    hid_t[...] = hid[...].reshape(tokens, D).T
    y_sends = [
        remote(staged.at[e, :, :, 1 - at.y], y_in.at[e], vs.at[e], vr.at[e], at.beside)
        for e in range(FIRST)
    ]
    at_lane = lax.broadcasted_iota(jnp.int32, cols.shape, 1)
    pick_cols[...] = jnp.zeros(pick_cols.shape, F32)
    store.wait()
    for index in range(3):
        passed[index].wait_send()
    low_all = wqkv

    def expert(e, carry):
        wide = pl.ds(pl.multiple_of(e * 2 * units, 2 * units), 2 * units)
        tall = pl.ds(pl.multiple_of(e * units, units), units)
        both = dot_nn(hid[...].reshape(tokens, D), inner_w[:, wide])
        kept, pick, low = expert_step(
            both, backs[:, tall].astype(F32), lane_of(cols[...], experts + e), units
        )
        backs[:, tall] = kept
        low_all[:, wide] = low
        pick_cols[...] = jnp.where(at_lane == e, pick, pick_cols[...])

        shape = staged.shape[1:5]
        staged[e, :, :, :, :, : 2 * units] = (
            dot_nn(hid_t[...], low).astype(BF16).reshape(*shape, 2 * units)
        )
        staged[e, :, :, :, :, 2 * units :] = (
            (RES_MULT * dot_nn(cot_t[...], kept)).astype(BF16).reshape(*shape, units)
        )
        for now in range(OWN):

            @pl.when(e == now)
            def _():
                if now < FIRST:
                    y_sends[now].start()
                else:
                    pltpu.make_async_copy(
                        staged.at[now], grad_o.at[now - FIRST], gd.at[now - FIRST]
                    ).start()

        return carry

    lax.fori_loop(0, OWN, expert, 0)
    left_passed = gather_pass(at, left_pairs, left_copies, us, ur)
    count = hid.shape[1]
    for j in range(PLANE):
        pick_o[j] = pick_cols[j * count : (j + 1) * count, :].T[:8]
    store_kept = pltpu.make_async_copy(backs, kept_units_o, hs.at[5])
    store_kept.start()
    for j in range(PLANE):
        here = slice(j * count, (j + 1) * count)
        hid[j] = dot_nt(low_all[here, :], inner_w[...]).astype(BF16)
    store_part = pltpu.make_async_copy(hid, part_o, hs.at[6])
    store_part.start()

    def settle(step, sign, slot):
        for half in range(2):
            if step == 0:
                for way in (-1, 1):

                    @pl.when((at.outer < last) if way < 0 else (at.outer > 0))
                    def _():
                        z_copy(half, 0, 0, way).wait_send()

            elif step < last:

                @pl.when((at.outer < last) if sign < 0 else (at.outer > 0))
                def _():
                    z_copy(half, slot, step, sign).wait_send()

            y_copy(half, slot, step, sign).wait_send()
            c_copy(half, slot, step, sign, at.inner, 0).wait_send()
            c_copy(half, slot, step, sign, inner_side, spots).wait_send()

    settle(0, 0, 0)
    for step, sign, slot in hops[1:]:

        @pl.when(exists(step, sign))
        def _():
            settle(step, sign, slot)

    for copy in sends.values():
        copy.wait_send()
    for copy in [gains, cot_sib, cot_side, cot_across] + cot_on:
        copy.wait_send()
    for e in range(FIRST):
        y_sends[e].wait()
        total = staged[e, :, :, at.y].astype(F32) + y_in[e].astype(F32)
        z_o[:, e] = total.astype(BF16)
    gather_wait(left_copies, left_passed)
    for copy in [store_kv, store_kept, store_part]:
        copy.wait()
    for e in range(FIRST, OWN):
        pltpu.make_async_copy(staged.at[e], grad_o.at[e - FIRST], gd.at[e - FIRST]).wait()


def opening(
    starts, tokens, wq, wk, wv, wo, small, cot, cosine, sine, routes, priority, expert_in, expert_out, ctx_count
):
    outers = ctx_count // INNER
    shape = jax.ShapeDtypeStruct
    count = tokens.shape[0]
    rows = count // 2
    width = wk.shape[1] + wv.shape[1]
    heads = wq.shape[1]
    wide = heads + width
    units = expert_out.shape[-1]
    many = PLANE * count
    blocks = 2 * ctx_count
    z_rows = D // (2 * outers)
    vm = pltpu.VMEM
    return comm_call(
        functools.partial(opening_kernel, outers),
        [
            shape((D, wide), BF16),
            shape((D, D), BF16),
            shape((small.shape[0], D), BF16),
            shape((count, heads), BF16),
            shape((count, D), BF16),
            shape((blocks, rows, width), BF16),
            shape((count, heads), F32),
            shape((count, heads), F32),
            shape((count, heads), BF16),
            shape((count, D), F32),
            shape((EXPERTS, count), F32),
            shape((EXPERTS, count), F32),
            shape((PLANE, 8, count), F32),
            shape((outers // 2, FIRST, 2, z_rows, 3 * units), BF16),
            shape((PLANE, count, D), BF16),
            shape((many, OWN * units), BF16),
            shape((OWN - FIRST, outers // 2, 2, 2, z_rows, 3 * units), BF16),
            shape((2, PLANE, count, D), BF16),
        ],
        [SMEM] + [ANY] * 9 + [VMEM] * 2 + [ANY] * 2,
        [ANY] * 2 + [VMEM] * 3 + [ANY] + [VMEM] * 8 + [ANY] * 4,
        [
            vm((D, wide), BF16),
            vm((D, D), BF16),
            vm((2, rows, width), BF16),
            vm((count, D), BF16),
            vm(cosine.shape, F32),
            vm(sine.shape, F32),
            vm((blocks, rows, width), BF16),
            vm((PLANE, count, D), BF16),
            vm((2, D, 2, units), BF16),
            vm((OWN, D, units), BF16),
            vm((D, OWN * 2 * units), BF16),
            vm((PAIRS, 2 * count, 128), F32),
            vm((PAIRS, 2 * count, 128), F32),
            vm((count, D), BF16),
            vm((EXPERTS, count), F32),
            vm((PLANE, count, D), BF16),
            vm((PLANE, EXPERTS, count), F32),
            vm((D, many), BF16),
            vm((many, OWN * units), BF16),
            vm((many, 128), F32),
            vm((many, 128), F32),
            vm((OWN, outers // 2, 2, 2, z_rows, 3 * units), BF16),
            vm((FIRST, outers // 2, 2, z_rows, 3 * units), BF16),
            DMA((5,)),
            DMA((5,)),
            DMA((4,)),
            DMA((4,)),
            DMA((4,)),
        ]
        + [DMA((2, 2 * outers))] * 4
        + [DMA((2, 4 * outers))] * 2
        + [DMA((8,)), DMA((7,)), DMA((7,)), DMA]
        + [DMA((2 + OWN,)), DMA((2, 7)), DMA((2, 7)), DMA((2,)), DMA((2,))]
        + [DMA((2, 7)), DMA((2, 7)), DMA((2,)), DMA((FIRST,)), DMA((FIRST,))],
        1,
        "opening",
        vmem=64 * 2**20,
        us=100,
    )(starts, tokens, wq, wk, wv, wo, small, cot, cosine, sine, routes, priority, expert_in, expert_out)


def turning_kernel(
    outers,
    starts,
    z_ref,
    grad_in,
    part_in,
    pick_send,
    kept_in,
    expert_out,
    gate_ref,
    kept_ref,
    small_ref,
    sum_ref,
    cot_ref,
    wo_in,
    raw_ref,
    total_ref,
    q_ref,
    kv_in,
    cos_ref,
    sin_ref,
    dy_ref,
    da_ref,
    dq_ref,
    rows_ref,
    moe_o,
    near_o,
    z_o,
    dkv_ref,
    part,
    kept_all,
    out_w,
    wout,
    kv,
    near,
    far_in,
    picks_all,
    q_four,
    n_four,
    d_rows,
    dq_acc,
    kv_acc,
    kv_out,
    z_sums,
    z_in,
    y_own,
    y_in,
    ls,
    ss,
    sr,
    xs,
    xr,
    ps,
    pr,
    vs,
    vr,
    us,
    ur,
    ks,
):
    at = Place()
    count = q_ref.shape[0]
    rows = count // 2
    width = PAIRS * 128
    keys = kv.shape[0] * rows
    units = out_w.shape[-1]
    experts = at.q * OWN
    loads = [
        pltpu.make_async_copy(src, dst, ls.at[index])
        for index, (src, dst) in enumerate(
            ((part_in, part), (kept_in, kept_all), (wo_in, wout), (kv_in, kv))
        )
    ]
    weights = [
        pltpu.make_async_copy(expert_out.at[experts + e], out_w.at[e], ls.at[4 + e])
        for e in range(OWN)
    ]
    for copy in loads + weights:
        copy.start()
    rest = Halving(at, outers, z_sums, z_in, vs, vr)
    z_sums[pl.ds(0, outers // 2)] = z_ref[...]
    own_rows = []
    for e in range(OWN - FIRST):
        copy = pltpu.make_async_copy(
            grad_in.at[e, :, :, at.y], y_own.at[e], ls.at[4 + OWN + e]
        )
        copy.start()
        own_rows.append(copy)
    meet(
        [at.relative(*bits)[0] for bits in OTHERS]
        + [at.beside]
        + [rest.device(bit) for bit in rest.bits]
    )
    sib, unused = at.relative(0, 1, 0)
    loads[0].wait()
    first = remote(part.at[:, 1 - at.core], near, ss, sr, sib)
    first.start()
    y_sends = []
    for e in range(OWN - FIRST):
        copy = remote(grad_in.at[e, :, :, 1 - at.y], y_in.at[e], us.at[e], ur.at[e], at.beside)
        copy.start()
        y_sends.append(copy)
    if rest.bits:
        rest.start(0)
    small_copies = []
    for slot, bits in enumerate(OTHERS):
        device, j_to = at.relative(*bits)
        copy = remote(pick_send.at[j_to], picks_all.at[at.j], ps.at[slot], pr.at[slot], device)
        copy.start()
        small_copies.append(copy)
    picks_all[at.j] = pick_send[at.j]
    first.wait_recv()
    for y in range(2):
        for w in range(2):
            total = part[y, at.core, w].astype(F32) + near[y, w].astype(F32)
            near[y, w] = total.astype(BF16)
    second = []
    for slot, (dy, dc, dw) in enumerate(XY):
        device, unused = at.relative(dy, dc, dw)
        z = at.z + dy * (1 - 2 * at.z)
        w = at.w + dw * (1 - 2 * at.w)
        copy = remote(near.at[z, w], far_in.at[slot], xs.at[slot], xr.at[slot], device)
        copy.start()
        second.append(copy)

    loads[1].wait()
    for copy in weights:
        copy.wait()

    def moe_rows(j, carry):
        here = pl.ds(pl.multiple_of(j * count, count), count)
        total = dot_nt(kept_all[here, :units], out_w[0])
        for e in range(1, OWN):
            total = total + dot_nt(kept_all[here, e * units : (e + 1) * units], out_w[e])
        moe_o[j] = total.astype(BF16)
        return carry

    lax.fori_loop(0, PLANE, moe_rows, 0)
    hidden_sum = near[at.z, at.w].astype(F32)
    for slot in range(3):
        second[slot].wait_recv()
        hidden_sum = hidden_sum + far_in[slot].astype(F32)
    for copy in [first] + second:
        copy.wait_send()
    small = small_ref[...]
    gain_two = small[EXPERTS + 1 : EXPERTS + 2].astype(F32)
    for copy in small_copies:
        copy.wait()
    parts = []
    for i in range(INNER):
        parts.append(picks_all[2 * i, pl.ds(0, OWN), :] + picks_all[2 * i + 1, pl.ds(0, OWN), :])
    gate = gate_ref[...]
    gate_grad = kept_ref[...] * jnp.concatenate(parts, axis=0)
    logit_grad = gate * (gate_grad - jnp.sum(gate * gate_grad, axis=0, keepdims=True))
    logit_grad = jnp.concatenate(
        [logit_grad, jnp.zeros((small.shape[0] - EXPERTS, count), F32)], axis=0
    ).astype(BF16)
    hidden_grad = hidden_sum + dot_tn(logit_grad, small)
    first_sum = sum_ref[...]
    scale = lax.rsqrt(jnp.mean(first_sum * first_sum, axis=1, keepdims=True) + EPS)
    normed = first_sum * scale
    hidden = (normed * gain_two).astype(BF16)
    router_rows = dot_nn(logit_grad, hidden)
    rows_ref[...] = router_rows
    rows_ref[pl.ds(EXPERTS + 1, 1), :] = jnp.sum(hidden_grad * normed, axis=0, keepdims=True)
    normed_grad = hidden_grad * gain_two
    first_grad = cot_ref[...].astype(F32) + scale * (
        normed_grad - normed * jnp.mean(normed_grad * normed, axis=1, keepdims=True)
    )
    dy_ref[...] = first_grad
    attn_grad = (RES_MULT * first_grad).astype(BF16)
    da_ref[...] = attn_grad
    loads[2].wait()
    mixed_grad = dot_nt(attn_grad, wout[...]).astype(BF16).astype(F32)
    total = total_ref[...]
    numer = mixed_grad / total
    lost = mixed_grad * raw_ref[...] / total
    for half in range(2):
        here = slice(half * rows, (half + 1) * rows)
        for pair in range(PAIRS):
            cols = slice(pair * 256, (pair + 1) * 256)
            slot = half * PAIRS + pair
            q_four[slot] = spread(q_ref[here, cols].astype(F32) * ATT_MULT).astype(BF16)
            n_four[slot] = spread(numer[here, cols]).astype(BF16)
            d_rows[slot] = -jnp.sum(spread(lost[here, cols]).T, axis=0, keepdims=True)
    dq_acc[...] = jnp.zeros_like(dq_acc)
    loads[3].wait()

    def kv_store(chunk):
        many = CHUNK // rows
        return pltpu.make_async_copy(
            kv_out.at[chunk % 2], dkv_ref.at[pl.ds(chunk * many, many)], ks.at[chunk % 2]
        )

    def step(chunk, carry):
        at_row = pl.multiple_of(chunk * CHUNK, CHUNK)
        kv_acc[...] = jnp.zeros_like(kv_acc)
        key_pos = at_row + lax.broadcasted_iota(jnp.int32, (CHUNK, 1), 0)
        for half in range(2):
            base, chunks = half_span(half, rows, keys)

            @pl.when(chunk < chunks)
            def _():
                place = base + lax.broadcasted_iota(jnp.int32, (1, 4 * rows), 1) % rows
                first = reach(starts, place)
                bias = jnp.where((key_pos >= first) & (key_pos <= place), 0.0, NEVER)
                for pair in range(PAIRS):
                    slot = half * PAIRS + pair
                    key = key_block(kv, chunk, rows, pair * 128)
                    value = key_block(kv, chunk, rows, width + pair * 128)
                    e = jnp.exp(dot_nt(key, q_four[slot]) + bias)
                    through = dot_nt(value, n_four[slot])
                    dz = (e * (through + d_rows[slot])).astype(BF16)
                    kv_acc[:, pl.ds(pair * 128, 128)] += dot_nn(dz, q_four[slot])
                    kv_acc[:, pl.ds(width + pair * 128, 128)] += dot_nn(e.astype(BF16), n_four[slot])
                    dq_acc[slot] += dot_tn(dz, key)

        many = CHUNK // rows

        @pl.when(chunk >= 2)
        def _():
            kv_store(chunk - 2).wait()

        kv_out[chunk % 2] = kv_acc[...].astype(BF16).reshape(many, rows, 2 * width)
        kv_store(chunk).start()
        return carry

    lax.fori_loop(0, keys // CHUNK, step, 0)
    cosine = cos_ref[...]
    sine = -sin_ref[...]
    for half in range(2):
        here = slice(half * rows, (half + 1) * rows)
        for pair in range(PAIRS):
            block = ATT_MULT * unspread(dq_acc[half * PAIRS + pair])
            dq_ref[here, pair * 256 : (pair + 1) * 256] = turn(
                block, cosine[here], sine[here]
            ).astype(BF16)
    for chunk in range(keys // CHUNK - 2, keys // CHUNK):
        kv_store(chunk).wait()
    near_o[...] = rest.finish()
    for copy in own_rows:
        copy.wait()
    for e in range(OWN - FIRST):
        y_sends[e].wait()
        total = y_own[e].astype(F32) + y_in[e].astype(F32)
        z_o[:, e] = total.astype(BF16)


def turning(
    outers, starts, z_first, grads, part, picks, kept_units, expert_out, gate, kept, small, first_sum, cot, output_w, raw, total, queries, kv_all, cosine, sine
):
    shape = jax.ShapeDtypeStruct
    count, width = queries.shape
    units = expert_out.shape[-1]
    vm = pltpu.VMEM
    return comm_call(
        functools.partial(turning_kernel, outers),
        [
            shape((count, D), F32),
            shape((count, D), BF16),
            shape((count, width), BF16),
            shape((32, D), F32),
            shape((PLANE, count, D), BF16),
            shape(z_first.shape[1:], BF16),
            shape((outers // 2, OWN - FIRST) + z_first.shape[2:], BF16),
            shape(kv_all.shape, BF16),
        ],
        [SMEM, VMEM, ANY, ANY, VMEM, ANY, ANY] + [VMEM] * 5 + [ANY] + [VMEM] * 3 + [ANY] + [VMEM] * 2,
        [VMEM] * 7 + [ANY],
        [
            vm((2, 2, 2, count, D), BF16),
            vm(kept_units.shape, BF16),
            vm((OWN, D, units), BF16),
            vm((D, D), BF16),
            vm(kv_all.shape, BF16),
            vm((2, 2, count, D), BF16),
            vm((3, count, D), BF16),
            vm((PLANE, 8, count), F32),
            vm((2 * PAIRS, 2 * count, 128), BF16),
            vm((2 * PAIRS, 2 * count, 128), BF16),
            vm((2 * PAIRS, 1, 2 * count), F32),
            vm((2 * PAIRS, 2 * count, 128), F32),
            vm((CHUNK, 2 * PAIRS * 128), F32),
            vm((2, CHUNK // (count // 2), count // 2, 2 * PAIRS * 128), BF16),
            vm((outers,) + z_first.shape[1:], BF16),
            vm((outers,) + z_first.shape[1:], BF16),
            vm((OWN - FIRST, outers // 2) + z_first.shape[2:], BF16),
            vm((OWN - FIRST, outers // 2) + z_first.shape[2:], BF16),
            DMA((4 + OWN + OWN - FIRST,)),
            DMA,
            DMA,
            DMA((3,)),
            DMA((3,)),
            DMA((7,)),
            DMA((7,)),
            DMA((outers,)),
            DMA((outers,)),
            DMA((OWN - FIRST,)),
            DMA((OWN - FIRST,)),
            DMA((2,)),
        ],
        5,
        "turning",
        vmem=62 * 2**20,
        us=35,
    )(
        starts,
        z_first,
        grads,
        part.reshape(2, 2, 2, count, D),
        picks,
        kept_units,
        expert_out,
        gate,
        kept,
        small,
        first_sum,
        cot,
        output_w,
        raw,
        total,
        queries,
        kv_all,
        cosine,
        sine,
    )


def assemble_kernel(
    outers, attn_in, small_in, near_one, near, wq, wk, wv, wo, small, inner, outer
):
    qkv_cols = wq.shape[1] * 2 // PLANE
    devices = outers * PLANE
    for j in range(PLANE):
        z, core, w = j // 4, (j // 2) % 2, j % 2
        total = 0.0
        for above in range(outers // 2):
            for y in range(2):
                source = (((above * 2 + z) * 2 + y) * 2 + core) * 2 + w
                total = total + attn_in[source].astype(F32)
        col = j * qkv_cols
        ref, base = (wq, 0) if col < 1024 else (wk, 1024) if col < 1536 else (wv, 1536)
        ref[:, col - base : col - base + qkv_cols] = total[:, :qkv_cols]
        wo[:, j * (D // PLANE) : (j + 1) * (D // PLANE)] = total[:, qkv_cols:]
    total = small_in[0].astype(F32)
    for i in range(1, devices):
        total = total + small_in[i].astype(F32)
    small[...] = total
    rows = wq.shape[0]
    units = outer.shape[-1] // 2
    for j in range(PLANE):
        cols = slice((j % 2) * units, (j % 2 + 1) * units)
        for k in range(OWN):
            e = (j // 2) * OWN + k
            block = (near_one[j, k] if k < FIRST else near[j, k - FIRST]).astype(F32)
            inner[e, :, :, cols] = block[:, : 2 * units].reshape(rows, 2, units)
            outer[e, :, cols] = block[:, 2 * units :]


def assemble(attn_in, small_in, near_one, near, outers):
    rows = attn_in.shape[1]
    units = near.shape[-1] // 3
    shape = jax.ShapeDtypeStruct
    outs = [
        shape((rows, 1024), F32),
        shape((rows, 512), F32),
        shape((rows, 512), F32),
        shape((rows, D), F32),
        shape((rows, 128), F32),
        shape((EXPERTS, rows, 2, 2 * units), F32),
        shape((EXPERTS, rows, 2 * units), F32),
    ]
    return pl.pallas_call(
        functools.partial(assemble_kernel, outers),
        out_shape=outs,
        in_specs=[VMEM] * 4,
        out_specs=[VMEM] * 7,
        compiler_params=pltpu.CompilerParams(
            vmem_limit_bytes=room([attn_in, small_in, near_one, near] * 2 + outs)
        ),
        name="assemble",
    )(attn_in, small_in, near_one, near)


def body(
    tokens,
    w_query,
    w_key,
    w_value,
    w_output,
    attn_gain,
    w_router,
    expert_in,
    expert_out,
    moe_gain,
    segments,
    routes,
    priority,
    cotangent,
):
    ctx_count = lax.axis_size("ctx")
    ctx_index = lax.axis_index("ctx")
    devices = ctx_count * 2
    outers = ctx_count // INNER
    owner_rows = D // devices
    block_rows = tokens.shape[2]
    half_rows = block_rows * ctx_count
    tok_count = 2 * block_rows
    f32 = jnp.float32
    bf16 = jnp.bfloat16

    small = jnp.concatenate(
        [w_router.T, attn_gain[None], moe_gain[None], jnp.zeros((14, w_router.shape[0]), bf16)]
    )
    cot_own = cotangent.reshape(tok_count, D)
    block_total = 2 * ctx_count
    block_ids = jnp.stack([ctx_index, block_total - 1 - ctx_index])
    query_pos = block_ids[:, None] * block_rows + jnp.arange(block_rows, dtype=jnp.int32)[None, :]
    flat_pos = query_pos.reshape(tok_count)
    starts = jnp.sum(
        (segments < jnp.arange(DOCS, dtype=jnp.int32)[:, None]).astype(jnp.int32), axis=1
    )
    frequency = jnp.exp(
        -jnp.log(jnp.float32(THETA))
        * jnp.arange(HEAD_DIM // 2, dtype=jnp.float32)
        * (2.0 / HEAD_DIM)
    )
    angles = flat_pos.astype(f32)[:, None] * frequency[None, :]
    cosine, sine = jnp.cos(angles), jnp.sin(angles)
    cosine = jnp.concatenate([cosine] * 4, axis=1)
    sine = jnp.concatenate([-sine, sine] * 2, axis=1)
    token_low = tokens.reshape(tok_count, D)
    (
        qkv_w,
        output_w,
        small_all,
        queries,
        hidden_one,
        kv_all,
        attn_raw,
        attn_total,
        mixed,
        first_sum,
        gate,
        kept,
        picks,
        first_half,
        part,
        kept_units,
        expert_grads,
        left,
    ) = opening(
        starts,
        token_low,
        w_query,
        w_key,
        w_value,
        w_output,
        small,
        cot_own,
        cosine,
        sine,
        routes[0].transpose(0, 2, 1),
        priority[0].transpose(0, 2, 1),
        expert_in,
        expert_out,
        ctx_count,
    )
    (
        first_grad,
        attn_grad,
        query_lin_grad,
        small_rows,
        moe_part,
        near_one,
        second_half,
        kv_terms,
    ) = turning(
        outers,
        starts,
        first_half,
        expert_grads,
        part,
        picks,
        kept_units,
        expert_out,
        gate,
        kept,
        small_all,
        first_sum,
        cot_own,
        output_w,
        attn_raw,
        attn_total,
        queries,
        kv_all,
        cosine,
        sine,
    )
    output, token_grad, attn_part, small_part, near = finish(
        kv_terms,
        moe_part,
        [
            first_sum,
            query_lin_grad,
            attn_grad,
            first_grad,
            token_low,
            small_all,
            cosine,
            sine,
            qkv_w,
            left,
            small_rows,
        ],
        second_half,
        ctx_count,
    )
    attn_in, small_in, near_one, near = owners(
        [attn_part, small_part],
        [
            rows.reshape(-1, PLANE, owner_rows, rows.shape[-1])
            for rows in (near_one, near)
        ],
        devices,
        7,
        "owners",
    )
    query_sum, key_sum, value_sum, output_sum, small_sum, inner_sum, outer_sum = assemble(
        attn_in, small_in, near_one, near, outers
    )
    return (
        output.reshape(tokens.shape),
        token_grad.reshape(tokens.shape),
        query_sum,
        key_sum,
        value_sum,
        output_sum,
        small_sum[:, EXPERTS],
        small_sum[:, :EXPERTS],
        inner_sum,
        outer_sum,
        small_sum[:, EXPERTS + 1],
    )


def solution(mesh):
    placed = (
        P("wsh", None, "ctx", None),
        P("wsh", None),
        P("wsh", None),
        P("wsh", None),
        P("wsh", None),
        P("wsh"),
        P("wsh", None),
        P(None, None, None, "wsh"),
        P(None, None, "wsh"),
        P("wsh"),
        P("wsh", None),
        P("wsh", None, "ctx", None),
        P("wsh", None, "ctx", None),
        P("wsh", None, "ctx", None),
    )
    return jax.shard_map(
        body,
        mesh=mesh,
        in_specs=placed,
        out_specs=(
            P("wsh", None, "ctx", None),
            P("wsh", None, "ctx", None),
            P(("ctx", "wsh"), None),
            P(("ctx", "wsh"), None),
            P(("ctx", "wsh"), None),
            P(("ctx", "wsh"), None),
            P(("ctx", "wsh")),
            P(("ctx", "wsh"), None),
            P(None, ("ctx", "wsh"), None, None),
            P(None, ("ctx", "wsh"), None),
            P(("ctx", "wsh")),
        ),
        check_vma=False,
    )
```

```python
import functools

import jax
import jax.numpy as jnp
from jax import lax
from jax.experimental import pallas as pl
from jax.experimental.pallas import tpu as pltpu
from jax.sharding import PartitionSpec as P

D = 1024
HEADS = 16
KV_HEADS = 8
HEAD_DIM = 64
TOPK = 8
EXPERTS = 16
CAP = 80
PLANE = 8
INNER = 4
OWN = EXPERTS // INNER
FIRST = OWN // 2


RES_MULT = 0.22
ATT_MULT = 0.015625
EPS = 1e-06
THETA = 10000.0

MESH = pl.DeviceIdType.MESH
F32 = jnp.float32
BF16 = jnp.bfloat16
ANY = pl.BlockSpec(memory_space=pl.ANY)
VMEM = pl.BlockSpec(memory_space=pltpu.VMEM)


class Place:
    def __init__(self):
        self.c = lax.axis_index("ctx")
        self.w = lax.axis_index("wsh")
        self.core = self.c % 2
        self.y = (self.c // 2) % 2
        self.inner = self.c % INNER
        self.outer = self.c // INNER
        self.z = self.outer % 2
        self.q = self.z * 2 + self.core
        self.j = self.q * 2 + self.w
        self.beside = (self.c + 2 - 4 * self.y, self.w)

    def relative(self, dz, dc, dw):
        z = self.z + dz * (1 - 2 * self.z)
        core = self.core + dc * (1 - 2 * self.core)
        w = self.w + dw * (1 - 2 * self.w)
        ctx = self.c + INNER * (z - self.z) + core - self.core
        return (ctx, w), (z * 2 + core) * 2 + w


OTHERS = [(a, b, d) for a in range(2) for b in range(2) for d in range(2) if a + b + d]
XY = [(0, 0, 1), (1, 0, 0), (1, 0, 1)]


def meet(devices):
    barrier = pltpu.get_barrier_semaphore()
    for device in devices:
        pl.semaphore_signal(barrier, inc=1, device_id=device, device_id_type=MESH)
    pl.semaphore_wait(barrier, len(devices))


def remote(src, dst, send, recv, device):
    return pltpu.make_async_remote_copy(
        src_ref=src,
        dst_ref=dst,
        send_sem=send,
        recv_sem=recv,
        device_id=device,
        device_id_type=MESH,
    )


def comm_call(kernel, out_shape, in_specs, out_specs, scratch, ident, name, vmem=None, us=20):
    return pl.pallas_call(
        kernel,
        out_shape=out_shape,
        in_specs=in_specs,
        out_specs=out_specs,
        scratch_shapes=scratch,
        compiler_params=pltpu.CompilerParams(
            collective_id=ident, has_side_effects=True, vmem_limit_bytes=vmem
        ),
        cost_estimate=pl.CostEstimate(
            flops=us * 10**9, bytes_accessed=us * 3 * 2**20, transcendentals=0
        ),
        name=name,
    )


DMA = pltpu.SemaphoreType.DMA


def room(arrays, scratch=(), spare=12):
    total = 0
    for array in list(arrays) + list(scratch):
        inner = getattr(array, "inner_aval", array)
        size = jnp.dtype(inner.dtype).itemsize
        for extent in inner.shape:
            size *= extent
        total += size
    return min(total + spare * 2**20, 62 * 2**20)


class Halving:
    def __init__(self, at, outers, sums, arrived, send, recv):
        self.at, self.sums, self.arrived = at, sums, arrived
        self.send, self.recv = send, recv
        self.bits = [2**k for k in range(1, outers.bit_length() - 1)]
        self.levels = [(0, outers // 2)]
        for bit in self.bits:
            start, many = self.levels[-1]
            self.levels.append((start + many, many // 2))
        self.copies = []

    def device(self, bit):
        at = self.at
        return (at.c + INNER * bit * (1 - 2 * ((at.outer // bit) % 2)), at.w)

    def start(self, step):
        bit = self.bits[step]
        side = (self.at.outer // bit) % 2
        start, many = self.levels[step]
        for m in range(many // 2):
            copy = remote(
                self.sums.at[start + 2 * m + 1 - side],
                self.arrived.at[start + m],
                self.send.at[start + m],
                self.recv.at[start + m],
                self.device(bit),
            )
            copy.start()
            self.copies.append(copy)

    def add(self, step):
        side = (self.at.outer // self.bits[step]) % 2
        start, many = self.levels[step]
        after, half = self.levels[step + 1]
        for m in range(half):
            self.copies[len(self.copies) - half + m].wait_recv()
            total = self.sums[start + 2 * m + side].astype(F32) + self.arrived[start + m].astype(F32)
            self.sums[after + m] = total.astype(BF16)

    def finish(self):
        for step in range(len(self.bits)):
            if step > 0:
                self.start(step)
            self.add(step)
        for copy in self.copies:
            copy.wait_send()
        return self.sums[self.levels[-1][0]]


def gather_start(at, pairs, send, recv, local):
    copies = []
    for index, (src, dst) in enumerate(pairs):
        keep = pltpu.make_async_copy(src, dst.at[at.j], local.at[index])
        keep.start()
        sends = []
        for slot, bits in enumerate(XY + [(0, 1, 0)]):
            device, unused = at.relative(*bits)
            copy = remote(src, dst.at[at.j], send.at[index, slot], recv.at[index, slot], device)
            copy.start()
            sends.append(copy)
        copies.append((keep, sends))
    return copies


def gather_pass(at, pairs, copies, send, recv):
    sib, unused = at.relative(0, 1, 0)
    passed = []
    for slot, bits in enumerate(XY):
        unused, j_from = at.relative(*bits)
        for index, (src, dst) in enumerate(pairs):
            copies[index][1][slot].wait_recv()
            block = dst.at[j_from]
            copy = remote(
                block, block, send.at[index, 4 + slot], recv.at[index, 4 + slot], sib
            )
            copy.start()
            passed.append(copy)
    return passed


def gather_wait(copies, passed):
    for keep, sends in copies:
        keep.wait()
        sends[3].wait_recv()
        for copy in sends:
            copy.wait_send()
    for copy in passed:
        copy.wait()


def turn(values, cosine, sine):
    lane = lax.broadcasted_iota(jnp.int32, cosine.shape, 1)
    first = lane % HEAD_DIM < HEAD_DIM // 2
    blocks = []
    for start in range(0, values.shape[1], 128):
        u = values[:, start : start + 128]
        swapped = jnp.where(first, pltpu.roll(u, 96, 1), pltpu.roll(u, 32, 1))
        blocks.append(u * cosine + swapped * sine)
    return jnp.concatenate(blocks, axis=1)


def dot_nt(a, b):
    return lax.dot_general(a, b, (((1,), (1,)), ((), ())), preferred_element_type=F32)


def dot_tn(a, b):
    return lax.dot_general(a, b, (((0,), (0,)), ((), ())), preferred_element_type=F32)


def dot_nn(a, b):
    return jnp.dot(a, b, preferred_element_type=F32)


def owners_kernel(devices, count, near_count, *refs):
    total = count + near_count
    parts, nears = refs[:count], refs[count:total]
    outs, near_outs = refs[total : total + count], refs[total + count : 2 * total]
    send, recv, local, nsend, nrecv, nlocal = refs[2 * total :]
    at = Place()
    me = at.c * 2 + at.w
    rows = D // devices

    def device_of(r):
        index = lax.rem(me + r, devices)
        return index, (index // 2, lax.rem(index, 2))

    def rows_of(ref, index):
        return ref.at[pl.ds(pl.multiple_of(index * rows, rows), rows), :]

    barrier = pltpu.get_barrier_semaphore()

    def greet(r, carry):
        unused, device = device_of(r)
        pl.semaphore_signal(barrier, inc=1, device_id=device, device_id_type=MESH)
        return carry

    lax.fori_loop(1, devices, greet, 0)
    pl.semaphore_wait(barrier, devices - 1)

    def copy_of(k, r):
        index, device = device_of(r)
        return remote(rows_of(parts[k], index), outs[k].at[me], send.at[k, r], recv.at[k, r], device)

    def start(r, carry):
        for k in range(count):
            copy_of(k, r).start()
        return carry

    lax.fori_loop(1, devices, start, 0)

    near_copies = []
    for k in range(near_count):
        for slot, bits in enumerate(OTHERS):
            device, j_to = at.relative(*bits)
            copy = remote(
                nears[k].at[:, j_to], near_outs[k].at[at.j], nsend.at[k, slot], nrecv.at[k, slot], device
            )
            copy.start()
            near_copies.append(copy)
    keeps = []
    for k in range(count):
        keep = pltpu.make_async_copy(rows_of(parts[k], me), outs[k].at[me], local.at[k])
        keep.start()
        keeps.append(keep)
    for k in range(near_count):
        keep = pltpu.make_async_copy(nears[k].at[:, at.j], near_outs[k].at[at.j], nlocal.at[k])
        keep.start()
        keeps.append(keep)

    def finish(r, carry):
        for k in range(count):
            copy_of(k, r).wait()
        return carry

    lax.fori_loop(1, devices, finish, 0)
    for copy in near_copies:
        copy.wait()
    for keep in keeps:
        keep.wait()


def owners(parts, nears, devices, ident, name):
    count, near_count = len(parts), len(nears)
    rows = D // devices
    shape = jax.ShapeDtypeStruct
    shapes = [shape((devices, rows, part.shape[-1]), part.dtype) for part in parts]
    for near in nears:
        lead, members, near_rows, width = near.shape
        shapes.append(shape((members, lead, near_rows, width), near.dtype))
    return comm_call(
        functools.partial(owners_kernel, devices, count, near_count),
        shapes,
        [ANY] * (count + near_count),
        [VMEM] * (count + near_count),
        [
            DMA((count, devices)),
            DMA((count, devices)),
            DMA((count,)),
            DMA((near_count, 7)),
            DMA((near_count, 7)),
            DMA((near_count,)),
        ],
        ident,
        name,
        vmem=60 * 2**20,
    )(*parts, *nears)


CHUNK = 256
PAIRS = KV_HEADS // 2
NEVER = -1e30


def low_lanes(shape):
    return lax.broadcasted_iota(jnp.int32, shape, 1) < HEAD_DIM


def spread(block):
    a, b = block[:, :128], block[:, 128:]
    low = low_lanes(a.shape)
    zero = jnp.zeros_like(a)
    return jnp.concatenate(
        [
            jnp.where(low, a, zero),
            jnp.where(low, pltpu.roll(a, HEAD_DIM, 1), zero),
            jnp.where(low, zero, pltpu.roll(b, HEAD_DIM, 1)),
            jnp.where(low, zero, b),
        ],
        axis=0,
    )


def unspread(four):
    rows = four.shape[0] // 4
    r0, r1, r2, r3 = (four[k * rows : (k + 1) * rows] for k in range(4))
    low = low_lanes(r0.shape)
    return jnp.concatenate(
        [
            jnp.where(low, r0, pltpu.roll(r1, HEAD_DIM, 1)),
            jnp.where(low, pltpu.roll(r2, HEAD_DIM, 1), r3),
        ],
        axis=1,
    )


DOCS = 8


def doc_starts(segments):
    return [
        jnp.sum(jnp.where(segments < d, 1.0, 0.0), axis=1, keepdims=True).astype(jnp.int32)
        for d in range(DOCS)
    ]


def reach(starts, place):
    first = jnp.zeros_like(place)
    for d in range(1, DOCS):
        first = jnp.where(place >= starts[d], starts[d], first)
    return first


def half_span(half, rows, keys):
    block = lax.axis_index("ctx")
    if half == 1:
        block = keys // rows - 1 - block
    base = block * rows
    return base, (base + rows + CHUNK - 1) // CHUNK


def key_block(kv, chunk, rows, col):
    many = CHUNK // rows
    picked = kv[pl.ds(chunk * many, many), :, pl.ds(col, 128)]
    return picked.reshape(CHUNK, 128)


def attend_rows(
    starts,
    q_ref,
    kv_ref,
    tok_ref,
    wo_ref,
    small_ref,
    route_ref,
    prio_ref,
    raw_ref,
    total_ref,
    mixed_ref,
    sum_ref,
    hid_ref,
    gate_ref,
    kept_ref,
    send_ref,
    acc,
    acc_l,
):
    rows = q_ref.shape[0] // 2
    width = PAIRS * 128
    keys = kv_ref.shape[0] * rows
    for half in range(2):
        base, chunks = half_span(half, rows, keys)
        q_four = []
        for pair in range(PAIRS):
            block = q_ref[pl.ds(half * rows, rows), pl.ds(pair * 256, 256)].astype(F32) * ATT_MULT
            q_four.append(spread(block).astype(BF16))
        acc[...] = jnp.zeros_like(acc)
        acc_l[...] = jnp.zeros_like(acc_l)
        place = base + lax.broadcasted_iota(jnp.int32, (rows, 1), 0)
        first = reach(starts, place)

        def step(chunk, carry):
            at_row = pl.multiple_of(chunk * CHUNK, CHUNK)
            key_pos = at_row + lax.broadcasted_iota(jnp.int32, (1, CHUNK), 1)
            bias = jnp.where((key_pos >= first) & (key_pos <= place), 0.0, NEVER)
            bias = jnp.concatenate([bias] * 4, axis=0)
            for pair in range(PAIRS):
                key = key_block(kv_ref, chunk, rows, pair * 128)
                value = key_block(kv_ref, chunk, rows, width + pair * 128)
                e = jnp.exp(dot_nt(q_four[pair], key) + bias)
                part = e[:, :128]
                for k in range(1, CHUNK // 128):
                    part = part + e[:, k * 128 : (k + 1) * 128]
                acc_l[pair] += part
                acc[pair] += dot_nn(e.astype(BF16), value)
            return carry

        lax.fori_loop(0, chunks, step, 0)
        for pair in range(PAIRS):
            total = jnp.sum(acc_l[pair], axis=1, keepdims=True)
            total = jnp.broadcast_to(total, (4 * rows, 128))
            here = pl.ds(half * rows, rows), pl.ds(pair * 256, 256)
            raw_ref[here] = unspread(acc[pair] / total)
            total_ref[here] = unspread(total)
    mixed = raw_ref[...].astype(BF16)
    mixed_ref[...] = mixed
    first_sum = tok_ref[...].astype(F32) + RES_MULT * dot_nn(mixed, wo_ref[...])
    sum_ref[...] = first_sum
    scale = lax.rsqrt(jnp.mean(first_sum * first_sum, axis=1, keepdims=True) + EPS)
    gain_two = small_ref[pl.ds(EXPERTS + 1, 1), :].astype(F32)
    hidden = (first_sum * scale * gain_two).astype(BF16)
    hid_ref[...] = hidden

    logits = dot_nt(small_ref[...], hidden)[:EXPERTS]
    count = 2 * rows
    expert = lax.broadcasted_iota(jnp.int32, (EXPERTS, count), 0)
    routed = jnp.zeros((EXPERTS, count), F32)
    prio = jnp.zeros((EXPERTS, count), F32)
    for k in range(TOPK):
        line = [
            jnp.concatenate([ref[0, pl.ds(k, 1), :], ref[1, pl.ds(k, 1), :]], axis=1)
            for ref in (route_ref, prio_ref)
        ]
        same = expert == line[0]
        routed = jnp.where(same, 1.0, routed)
        prio = jnp.where(same, line[1].astype(F32), prio)
    chosen = routed > 0.0
    order = lax.broadcasted_iota(jnp.int32, (EXPERTS, count), 1).astype(F32)
    key = jnp.where(chosen, prio * float(count) + order, 65536.0 * count)
    key_cols = jnp.concatenate([key, jnp.zeros((count - EXPERTS, count), F32)], axis=0).T
    ranks = []
    for e in range(EXPERTS):
        ahead = jnp.where(key_cols[:, e : e + 1] < key[e : e + 1, :], 1.0, 0.0)
        ranks.append(jnp.sum(ahead, axis=0, keepdims=True))
    rank = jnp.concatenate(ranks, axis=0)
    top = jnp.max(jnp.where(chosen, logits, -3e38), axis=0, keepdims=True)
    weight = jnp.where(chosen, jnp.exp(logits - top), 0.0)
    gate = weight / jnp.sum(weight, axis=0, keepdims=True)
    kept = jnp.where(chosen & (rank < CAP), 1.0, 0.0)
    gate_ref[...] = gate
    kept_ref[...] = kept
    send_ref[...] = gate * kept


SMEM = pl.BlockSpec(memory_space=pltpu.SMEM)


def finish_kernel(
    outers,
    part,
    moe,
    sum_ref,
    dq_ref,
    da_ref,
    dy_ref,
    tok_ref,
    small_ref,
    cos_ref,
    sin_ref,
    wqkv_in,
    left_in,
    rows_ref,
    z_ref,
    near_in,
    out_ref,
    token_ref,
    attn_ref,
    small_o,
    near_o,
    next_o,
    z_o,
    wqkv_ref,
    left_ref,
    z_sums,
    z_in_rows,
    own,
    half_in,
    y_in,
    z_in,
    m_own,
    m_near,
    m_x,
    m_y,
    qkv,
    swap,
    swapped,
    ss,
    sr,
    ys,
    yr,
    zs,
    zr,
    ns,
    nr,
    ws,
    wr,
    vs,
    vr,
    ls,
    os,
    ps,
    pr,
    qs,
    qr,
):
    at = Place()
    blocks, rows, full = part.shape
    loads = [
        pltpu.make_async_copy(wqkv_in, wqkv_ref, ls.at[0]),
        pltpu.make_async_copy(left_in, left_ref, ls.at[1]),
    ]
    moe_load = pltpu.make_async_copy(moe.at[:, at.core], m_own, ls.at[2])
    near_keep = pltpu.make_async_copy(near_in.at[:, at.j], near_o.at[at.j], ls.at[3])
    z_loads = [
        pltpu.make_async_copy(
            z_ref.at[:, e], z_sums.at[e, pl.ds(0, outers // 2)], ls.at[4 + e]
        )
        for e in range(z_sums.shape[0])
    ]
    for copy in z_loads + [moe_load] + loads + [near_keep]:
        copy.start()
    width = full // 2
    cuts = 4
    step_width = full // cuts
    count = 2 * rows
    sib, unused = at.relative(0, 1, 0)
    side = at.beside
    along_to, unused = at.relative(1, 0, 0)
    across, unused = at.relative(0, 0, 1)
    other = [lax.rem(at.outer + r, outers) for r in range(outers)]
    far = [(other[r] * INNER + at.inner, at.w) for r in range(1, outers)]
    rest = [
        Halving(at, outers, z_sums.at[e], z_in_rows.at[e], vs.at[e], vr.at[e])
        for e in range(z_sums.shape[0])
    ]
    meet([at.relative(*bits)[0] for bits in OTHERS] + far + [at.beside])
    for copy in z_loads:
        copy.wait()
    if outers > 2:
        rest[0].start(0)

    def own_block(half, o, y, core):
        index = (o * 2 + y) * 2 + core
        return index if half == 0 else blocks - 1 - index

    own_loads = []
    for y in range(2):
        for h in range(2):
            for o in range(outers):
                copy = pltpu.make_async_copy(
                    part.at[own_block(h, o, y, at.core)], own.at[y, h, o], os.at[y, h, o]
                )
                copy.start()
                own_loads.append(copy)
    first = {}
    for k in range(cuts):
        cols = pl.ds(k * step_width, step_width)
        for y in range(2):
            for h in range(2):
                for o in range(outers):
                    copy = remote(
                        part.at[own_block(h, o, y, 1 - at.core), :, cols],
                        half_in.at[y, h, o, :, cols],
                        ss.at[k, y, h, o],
                        sr.at[k, y, h, o],
                        sib,
                    )
                    copy.start()
                    first[k, y, h, o] = copy
    nears = []
    for slot, bits in enumerate(OTHERS):
        device, j_to = at.relative(*bits)
        copy = remote(near_in.at[:, j_to], near_o.at[at.j], ps.at[slot], pr.at[slot], device)
        copy.start()
        nears.append(copy)
    near = remote(moe.at[:, 1 - at.core], m_near, ns.at[0], nr.at[0], sib)
    near.start()
    for copy in own_loads:
        copy.wait()
    second = []
    for k in range(cuts):
        cols = pl.ds(k * step_width, step_width)
        for y in range(2):
            for h in range(2):
                for o in range(outers):
                    first[k, y, h, o].wait_recv()
                    total = own[y, h, o, :, cols].astype(F32) + half_in[
                        y, h, o, :, cols
                    ].astype(F32)
                    half_in[y, h, o, :, cols] = total.astype(BF16)
        copy = remote(
            half_in.at[1 - at.y, :, :, :, cols], y_in.at[:, :, :, cols], ys.at[k], yr.at[k], side
        )
        copy.start()
        second.append(copy)
    near.wait_recv()
    moe_load.wait()
    for y in range(2):
        for w in range(2):
            total = m_own[y, w].astype(F32) + m_near[y, w].astype(F32)
            m_near[y, w] = total.astype(BF16)
    cross = remote(m_near.at[:, 1 - at.w], m_x, ns.at[1], nr.at[1], across)
    cross.start()
    third = []

    def z_send(k):
        cols = pl.ds(k * step_width, step_width)
        second[k].wait_recv()
        for o in range(outers):
            for h in range(2):
                total = half_in[at.y, h, o, :, cols].astype(F32) + y_in[h, o, :, cols].astype(F32)
                half_in[at.y, h, o, :, cols] = total.astype(BF16)
        for r in range(1, outers):
            copy = remote(
                half_in.at[at.y, :, other[r], :, cols],
                z_in.at[r, :, :, cols],
                zs.at[k, r],
                zr.at[k, r],
                far[r - 1],
            )
            copy.start()
            third.append(copy)

    z_send(0)
    z_send(1)
    cross.wait_recv()
    for y in range(2):
        total = m_near[y, at.w].astype(F32) + m_x[y].astype(F32)
        m_x[y] = total.astype(BF16)
    along = remote(m_x.at[1 - at.z], m_y, ns.at[2], nr.at[2], along_to)
    along.start()
    for k in range(2, cuts):
        z_send(k)
    qkv[:, : HEADS * HEAD_DIM] = dq_ref[...]
    along.wait_recv()
    moe_sum = m_x[at.z].astype(F32) + m_y[...].astype(F32)
    out_ref[...] = (sum_ref[...] + RES_MULT * moe_sum).astype(BF16)
    tok = tok_ref[...].astype(F32)
    scale = lax.rsqrt(jnp.mean(tok * tok, axis=1, keepdims=True) + EPS)
    normed = tok * scale
    gain_one = small_ref[pl.ds(EXPERTS, 1), :].astype(F32)
    for copy in third:
        copy.wait_recv()
    if outers > 2:
        for halving in rest[1:]:
            halving.start(0)
    rest[0].finish()
    level = rest[0].levels[-1][0]
    owner_rows = next_o.shape[2]

    def rows_of(j):
        within = pl.multiple_of(lax.rem(j, 4) * owner_rows, owner_rows)
        return 0, level, j // 4, pl.ds(within, owner_rows)

    for slot, bits in enumerate(OTHERS):
        device, j_to = at.relative(*bits)
        copy = remote(
            z_sums.at[rows_of(j_to)], next_o.at[at.j, 0], qs.at[slot], qr.at[slot], device
        )
        copy.start()
        nears.append(copy)
    next_o[at.j, 0] = z_sums[rows_of(at.j)]
    cosine = cos_ref[...]
    sine = -sin_ref[...]
    base = HEADS * HEAD_DIM
    for h in range(2):
        here = slice(h * rows, (h + 1) * rows)
        total = half_in[at.y, h, at.outer].astype(F32)
        for r in range(1, outers):
            total = total + z_in[r, h].astype(F32)
        qkv[here, base : base + width] = turn(total[:, :width], cosine[here], sine[here]).astype(BF16)
        qkv[here, base + width :] = total[:, width:].astype(BF16)
    wide = full * 2 // PLANE
    for j in range(PLANE):
        swap[j, :, :wide] = qkv[:, j * wide : (j + 1) * wide]
        swap[j, :, wide:] = da_ref[:, j * (D // PLANE) : (j + 1) * (D // PLANE)]
    swaps = []
    for slot, bits in enumerate(OTHERS):
        device, j_to = at.relative(*bits)
        copy = remote(swap.at[j_to], swapped.at[at.j], ws.at[slot], wr.at[slot], device)
        copy.start()
        swaps.append(copy)
    swapped[at.j] = swap[at.j]
    for copy in loads:
        copy.wait()
    hidden_grad = dot_nt(qkv[...], wqkv_ref[...])
    small = rows_ref[...]
    gain_grad = jnp.sum(hidden_grad * normed, axis=0, keepdims=True)
    line = lax.broadcasted_iota(jnp.int32, small.shape, 0)
    small = jnp.where(line == EXPERTS, gain_grad, small)
    small = jnp.concatenate([small, jnp.zeros((128 - small.shape[0], D), F32)], axis=0)
    small_o[...] = small.T.astype(BF16)
    hidden_grad = hidden_grad * gain_one
    token_ref[...] = dy_ref[...] + scale * (
        hidden_grad - normed * jnp.mean(hidden_grad * normed, axis=1, keepdims=True)
    )
    for copy in swaps:
        copy.wait_recv()
    all_rows = PLANE * count
    left_one = left_ref[0].reshape(all_rows, D)
    left_mixed = left_ref[1].reshape(all_rows, D)
    grads = swapped[...].reshape(all_rows, wide + D // PLANE)
    attn_ref[:, :wide] = dot_tn(left_one, grads[:, :wide]).astype(BF16)
    attn_ref[:, wide:] = dot_tn(left_mixed, grads[:, wide:]).astype(BF16)
    for e in range(1, len(rest)):
        z_o[e - 1] = rest[e].finish()
    near_keep.wait()
    for copy in nears:
        copy.wait()
    for copy in list(first.values()) + second + third + swaps + [near, cross, along]:
        copy.wait_send()


def finish(part, moe, arrays, z_half, near, ctx_count):
    outers = ctx_count // INNER
    blocks, rows, full = part.shape
    count = 2 * rows
    shape = jax.ShapeDtypeStruct
    columns = 3 * D // PLANE
    return comm_call(
        functools.partial(finish_kernel, outers),
        [
            shape((count, D), BF16),
            shape((count, D), F32),
            shape((D, columns), BF16),
            shape((D, 128), BF16),
            shape((PLANE, near.shape[0]) + near.shape[2:], BF16),
            shape((PLANE, 1) + near.shape[2:], BF16),
            shape((z_half.shape[1] - 1,) + z_half.shape[2:], BF16),
        ],
        [ANY] * 2 + [VMEM] * (len(arrays) - 3) + [ANY] * 2 + [VMEM] + [ANY] * 2,
        [VMEM] * 7,
        [
            pltpu.VMEM((D, 2 * full), BF16),
            pltpu.VMEM((2, PLANE, count, D), BF16),
            pltpu.VMEM((z_half.shape[1], outers) + z_half.shape[2:], BF16),
            pltpu.VMEM((z_half.shape[1], outers) + z_half.shape[2:], BF16),
            pltpu.VMEM((2, 2, outers, rows, full), BF16),
            pltpu.VMEM((2, 2, outers, rows, full), BF16),
            pltpu.VMEM((2, outers, rows, full), BF16),
            pltpu.VMEM((outers, 2, rows, full), BF16),
            pltpu.VMEM((2, 2, count, D), BF16),
            pltpu.VMEM((2, 2, count, D), BF16),
            pltpu.VMEM((2, count, D), BF16),
            pltpu.VMEM((count, D), BF16),
            pltpu.VMEM((count, 2 * full), BF16),
            pltpu.VMEM((PLANE, count, columns), BF16),
            pltpu.VMEM((PLANE, count, columns), BF16),
            DMA((4, 2, 2, outers)),
            DMA((4, 2, 2, outers)),
            DMA((4,)),
            DMA((4,)),
            DMA((4, outers)),
            DMA((4, outers)),
            DMA((3,)),
            DMA((3,)),
            DMA((7,)),
            DMA((7,)),
            DMA((z_half.shape[1], outers)),
            DMA((z_half.shape[1], outers)),
            DMA((4 + z_half.shape[1],)),
            DMA((2, 2, outers)),
            DMA((7,)),
            DMA((7,)),
            DMA((7,)),
            DMA((7,)),
        ],
        3,
        "finish",
        vmem=63 * 2**20,
        us=60,
    )(part, moe.reshape(2, 2, 2, count, D), *arrays, z_half, near)


def gate_columns(gates, cols):
    count = gates.shape[-1]
    for j in range(PLANE):
        block = jnp.concatenate([gates[j], jnp.zeros((128 - EXPERTS, count), F32)], axis=0)
        cols[pl.ds(j * count, count), :] = block.T


def expert_step(both, back_act, gate, units):
    gv, uv = both[:, :units], both[:, units:]
    sig = jax.nn.sigmoid(gv)
    silu = gv * sig
    act = silu * uv
    pick = jnp.sum(act * back_act, axis=1, keepdims=True)
    kept = (gate * act).astype(BF16)
    back_act = gate * back_act
    slope = sig * (1.0 + gv * (1.0 - sig))
    low = jnp.concatenate([back_act * uv * slope, back_act * silu], axis=1).astype(BF16)
    return kept, pick, low


def lane_of(cols, lane):
    at = lax.broadcasted_iota(jnp.int32, cols.shape, 1)
    return jnp.sum(jnp.where(at == lane, cols, 0.0), axis=1, keepdims=True)


def opening_kernel(
    outers,
    seg_ref,
    tok_ref,
    wq,
    wk,
    wv,
    wo,
    small,
    cot,
    cos_ref,
    sin_ref,
    route_ref,
    prio_ref,
    expert_in,
    expert_out,
    wqkv_o,
    wo_o,
    small_o,
    q_o,
    hid_o,
    kv_o,
    raw_o,
    total_o,
    mixed_o,
    sum_o,
    gate_o,
    kept_o,
    pick_o,
    z_o,
    part_o,
    kept_units_o,
    grad_o,
    left_o,
    wqkv,
    wout,
    own,
    tok_v,
    cos_v,
    sin_v,
    kv,
    cot_v,
    raw,
    out_w,
    inner_w,
    acc,
    acc_l,
    hid_two,
    gate_send,
    hid,
    gates,
    cot_t,
    backs,
    cols,
    pick_cols,
    staged,
    y_in,
    xs,
    xr,
    fs,
    fr,
    ls,
    zs,
    zr,
    ys,
    yr,
    cs,
    cr,
    hs,
    gs,
    gr,
    gl,
    es,
    ts,
    tr,
    tl,
    gd,
    us,
    ur,
    ul,
    vs,
    vr,
):
    at = Place()
    blocks, rows = kv.shape[:2]
    units = out_w.shape[-1]
    experts = at.q * OWN
    sib, unused = at.relative(0, 1, 0)
    partner, j_partner = at.relative(0, 0, 1)
    side, j_side = at.relative(1, 0, 0)
    unused, j_cross = at.relative(1, 0, 1)
    steps = sorted({1, outers - 1})
    far = [(lax.rem(at.outer + r, outers) * INNER + at.inner, at.w) for r in steps]
    expert_loads = {}

    def load_expert(e):
        copy = pltpu.make_async_copy(expert_in.at[experts + e], raw.at[e % 2], es.at[e % 2])
        copy.start()
        expert_loads[e] = copy

    def shape_expert(e):
        expert_loads[e].wait()
        inner_w[:, e * 2 * units : (e + 1) * 2 * units] = raw[e % 2].reshape(D, 2 * units)
        if e + 2 < OWN:
            load_expert(e + 2)

    out_loads = [
        pltpu.make_async_copy(expert_out.at[experts + e], out_w.at[e], es.at[2 + e])
        for e in range(OWN)
    ]
    for copy in out_loads:
        copy.start()
    load_expert(0)
    load_expert(1)
    meet([at.relative(*bits)[0] for bits in XY + [(0, 1, 0)]] + far + [at.beside])

    pieces = [(wk, wqkv, 1024), (wv, wqkv, 1536), (wq, wqkv, 0), (wo, wout, 0)]
    sends, passed, keeps = {}, {}, []

    def give(index):
        src, dst, col = pieces[index]
        depth, width = src.shape
        half = depth // 2
        copy = remote(
            src.at[pl.ds(at.core * half, half), :],
            dst.at[pl.ds(at.w * depth + at.core * half, half), pl.ds(col, width)],
            xs.at[index],
            xr.at[index],
            partner,
        )
        copy.start()
        sends[index] = copy

    def pass_on(index):
        src, dst, col = pieces[index]
        depth, width = src.shape
        half = depth // 2
        sends[index].wait_recv()
        piece = dst.at[pl.ds((1 - at.w) * depth + at.core * half, half), pl.ds(col, width)]
        copy = remote(piece, piece, fs.at[index], fr.at[index], sib)
        copy.start()
        passed[index] = copy

    wide = small.shape[1]
    mine = small_o.at[:, pl.ds(at.w * wide, wide)]
    gains = remote(small, mine, xs.at[4], xr.at[4], partner)
    gains.start()
    give(0)
    give(1)
    cot_sib = remote(cot, cot_v.at[at.j], gs.at[0], gr.at[0], sib)
    cot_sib.start()
    cot_side = remote(cot, cot_v.at[at.j], gs.at[1], gr.at[1], side)
    cot_side.start()
    cot_keep = pltpu.make_async_copy(cot, cot_v.at[at.j], gl)
    cot_keep.start()
    for index, (src, dst, col) in enumerate(pieces):
        depth, width = src.shape
        keep = pltpu.make_async_copy(
            src, dst.at[pl.ds(at.w * depth, depth), pl.ds(col, width)], ls.at[index]
        )
        keep.start()
        keeps.append(keep)
    loads = [
        pltpu.make_async_copy(src, dst, hs.at[4 + index])
        for index, (src, dst) in enumerate(
            ((tok_ref, tok_v), (cos_ref, cos_v), (sin_ref, sin_v), (small, mine))
        )
    ]
    for copy in loads:
        copy.start()
    for copy in loads:
        copy.wait()
    tok = tok_v[...].astype(F32)
    normed = tok * lax.rsqrt(jnp.mean(tok * tok, axis=1, keepdims=True) + EPS)
    gains.wait_recv()
    hidden = (normed * small_o[pl.ds(EXPERTS, 1), :].astype(F32)).astype(BF16)
    hid_o[...] = hidden
    cosine, sine = cos_v[...], sin_v[...]

    pass_on(0)
    pass_on(1)
    cot_across = remote(cot, cot_v.at[at.j], gs.at[2], gr.at[2], partner)
    cot_across.start()
    keeps[0].wait()
    keeps[1].wait()
    passed[0].wait_recv()
    key = dot_nn(hidden, wqkv[:, 1024:1536])
    key = turn(key, cosine, sine).astype(BF16)
    passed[1].wait_recv()
    value = dot_nn(hidden, wqkv[:, 1536:]).astype(BF16)
    width = key.shape[1]
    for half in range(2):
        own[half, :, :width] = key[half * rows : (half + 1) * rows]
        own[half, :, width:] = value[half * rows : (half + 1) * rows]

    def block_of(half, ctx):
        return kv.at[ctx] if half == 0 else kv.at[blocks - 1 - ctx]

    last = outers - 1
    hops = [(0, 0, 0)] + [
        (step, sign, step if sign < 0 else last + step)
        for step in range(1, outers)
        for sign in (-1, 1)
    ]

    def source(step, sign):
        return at.outer + sign * step

    def exists(step, sign):
        place = source(step, sign)
        return (place >= 0) & (place <= last)

    def block_from(half, step, sign, inner):
        place = lax.rem(source(step, sign) + outers, outers)
        return block_of(half, place * INNER + inner)

    below = (lax.rem(at.outer + last, outers) * INNER + at.inner, at.w)
    above = (lax.rem(at.outer + 1, outers) * INNER + at.inner, at.w)
    inner_side = at.inner + 2 - 4 * at.y

    def z_copy(half, slot, step, sign):
        src = own.at[half] if step == 0 else block_from(half, step, sign, at.inner)
        dst = block_from(half, step, sign, at.inner)
        slot_there = step + 1 if sign < 0 else last + step + 1
        return remote(
            src,
            dst,
            zs.at[half, slot_there],
            zr.at[half, slot_there],
            above if sign < 0 else below,
        )

    def y_copy(half, slot, step, sign):
        src = own.at[half] if step == 0 else block_from(half, step, sign, at.inner)
        dst = block_from(half, step, sign, at.inner)
        return remote(src, dst, ys.at[half, slot], yr.at[half, slot], at.beside)

    def c_copy(half, slot, step, sign, inner, base):
        src = (
            own.at[half]
            if step == 0 and base == 0
            else block_from(half, step, sign, inner)
        )
        dst = block_from(half, step, sign, inner)
        return remote(src, dst, cs.at[half, base + slot], cr.at[half, base + slot], sib)

    spots = 2 * outers - 1

    def spread_from(step, sign, slot, halves=(0, 1)):
        for half in halves:
            if step == 0:
                for way in (-1, 1):

                    @pl.when((at.outer < last) if way < 0 else (at.outer > 0))
                    def _():
                        z_copy(half, 0, 0, way).start()

            elif step < last:

                @pl.when((at.outer < last) if sign < 0 else (at.outer > 0))
                def _():
                    z_copy(half, slot, step, sign).start()

            y_copy(half, slot, step, sign).start()
            c_copy(half, slot, step, sign, at.inner, 0).start()

    spread_from(0, 0, 0)
    for half in range(2):
        keep = pltpu.make_async_copy(own.at[half], block_of(half, at.c), hs.at[half])
        keep.start()
        keeps.append(keep)

    def y_arrived(step, sign, slot):
        for half in range(2):
            y_copy(half, slot, step, sign).wait_recv()
            c_copy(half, slot, step, sign, inner_side, spots).start()

    def z_arrived(want):
        for step, sign, slot in hops[1:]:
            if step == want:

                @pl.when(exists(step, sign))
                def _():
                    for half in range(2):
                        z_copy(half, slot, step - 1, sign).wait_recv()
                        spread_from(step, sign, slot, (half,))

    def sides_arrived(want):
        for step, sign, slot in hops[1:]:
            if step == want:

                @pl.when(exists(step, sign))
                def _():
                    y_arrived(step, sign, slot)

    shape_expert(0)
    cot_across.wait_recv()
    give(2)
    cot_on = []

    def cot_pass(slot, j_from, device):
        block = cot_v.at[j_from]
        copy = remote(block, block, gs.at[slot], gr.at[slot], device)
        copy.start()
        cot_on.append(copy)

    cot_pass(3, j_partner, side)
    cot_pass(4, j_partner, sib)
    cot_side.wait_recv()
    cot_pass(5, j_side, sib)
    z_arrived(1)
    y_arrived(0, 0, 0)
    shape_expert(1)
    pass_on(2)
    give(3)
    shape_expert(2)
    if outers > 2:
        z_arrived(2)
    keeps[2].wait()
    passed[2].wait_recv()
    q_o[...] = turn(dot_nn(hidden, wqkv[:, :1024]), cosine, sine).astype(BF16)
    store = pltpu.make_async_copy(wqkv, wqkv_o, hs.at[2])
    store.start()
    shape_expert(3)
    sides_arrived(1)
    for step in range(3, outers):
        z_arrived(step)
        sides_arrived(step - 1)
    if outers > 2:
        sides_arrived(last)
    pass_on(3)
    cot_on[0].wait_recv()
    cot_pass(6, j_cross, sib)
    keeps[3].wait()
    passed[3].wait_recv()
    store_out = pltpu.make_async_copy(wout, wo_o, hs.at[3])
    store_out.start()
    def sibling_brought(step, sign, slot):
        for half in range(2):
            c_copy(half, slot, step, sign, at.inner, 0).wait_recv()
            c_copy(half, slot, step, sign, inner_side, spots).wait_recv()

    sibling_brought(0, 0, 0)
    for step, sign, slot in hops[1:]:

        @pl.when(exists(step, sign))
        def _():
            sibling_brought(step, sign, slot)

    for keep in keeps[4:]:
        keep.wait()
    store_kv = pltpu.make_async_copy(kv, kv_o, hs.at[4])
    store_kv.start()
    attend_rows(
        doc_starts(seg_ref[...]),
        q_o,
        kv,
        tok_v,
        wout,
        small_o,
        route_ref,
        prio_ref,
        raw_o,
        total_o,
        mixed_o,
        sum_o,
        hid_two,
        gate_o,
        kept_o,
        gate_send,
        acc,
        acc_l,
    )

    pairs = [(hid_two, hid), (gate_send, gates)]
    copies = gather_start(at, pairs, ts, tr, tl)
    for copy in [cot_sib] + cot_on[1:]:
        copy.wait_recv()
    cot_keep.wait()
    for copy in out_loads:
        copy.wait()
    tokens = cot_v.shape[0] * cot_v.shape[1]
    cot_rows = cot_v[...].reshape(tokens, D)
    cot_t[...] = cot_rows.T
    for e in range(OWN):
        backs[:, e * units : (e + 1) * units] = (RES_MULT * dot_nn(cot_rows, out_w[e])).astype(BF16)
    gather_wait(copies, gather_pass(at, pairs, copies, ts, tr))
    gate_columns(gates, cols)
    left_pairs = [(hid_o, left_o.at[0]), (mixed_o, left_o.at[1])]
    left_copies = gather_start(at, left_pairs, us, ur, ul)
    store_out.wait()
    passed[3].wait_send()
    hid_t = wout
    hid_t[...] = hid[...].reshape(tokens, D).T
    y_sends = [
        remote(staged.at[e, :, :, 1 - at.y], y_in.at[e], vs.at[e], vr.at[e], at.beside)
        for e in range(FIRST)
    ]
    at_lane = lax.broadcasted_iota(jnp.int32, cols.shape, 1)
    pick_cols[...] = jnp.zeros(pick_cols.shape, F32)
    store.wait()
    for index in range(3):
        passed[index].wait_send()
    low_all = wqkv

    def expert(e, carry):
        wide = pl.ds(pl.multiple_of(e * 2 * units, 2 * units), 2 * units)
        tall = pl.ds(pl.multiple_of(e * units, units), units)
        both = dot_nn(hid[...].reshape(tokens, D), inner_w[:, wide])
        kept, pick, low = expert_step(
            both, backs[:, tall].astype(F32), lane_of(cols[...], experts + e), units
        )
        backs[:, tall] = kept
        low_all[:, wide] = low
        pick_cols[...] = jnp.where(at_lane == e, pick, pick_cols[...])

        shape = staged.shape[1:5]
        staged[e, :, :, :, :, : 2 * units] = (
            dot_nn(hid_t[...], low).astype(BF16).reshape(*shape, 2 * units)
        )
        staged[e, :, :, :, :, 2 * units :] = (
            (RES_MULT * dot_nn(cot_t[...], kept)).astype(BF16).reshape(*shape, units)
        )
        for now in range(OWN):

            @pl.when(e == now)
            def _():
                if now < FIRST:
                    y_sends[now].start()
                else:
                    pltpu.make_async_copy(
                        staged.at[now], grad_o.at[now - FIRST], gd.at[now - FIRST]
                    ).start()

        return carry

    lax.fori_loop(0, OWN, expert, 0)
    left_passed = gather_pass(at, left_pairs, left_copies, us, ur)
    count = hid.shape[1]
    for j in range(PLANE):
        pick_o[j] = pick_cols[j * count : (j + 1) * count, :].T[:8]
    store_kept = pltpu.make_async_copy(backs, kept_units_o, hs.at[5])
    store_kept.start()
    for j in range(PLANE):
        here = slice(j * count, (j + 1) * count)
        hid[j] = dot_nt(low_all[here, :], inner_w[...]).astype(BF16)
    store_part = pltpu.make_async_copy(hid, part_o, hs.at[6])
    store_part.start()

    def settle(step, sign, slot):
        for half in range(2):
            if step == 0:
                for way in (-1, 1):

                    @pl.when((at.outer < last) if way < 0 else (at.outer > 0))
                    def _():
                        z_copy(half, 0, 0, way).wait_send()

            elif step < last:

                @pl.when((at.outer < last) if sign < 0 else (at.outer > 0))
                def _():
                    z_copy(half, slot, step, sign).wait_send()

            y_copy(half, slot, step, sign).wait_send()
            c_copy(half, slot, step, sign, at.inner, 0).wait_send()
            c_copy(half, slot, step, sign, inner_side, spots).wait_send()

    settle(0, 0, 0)
    for step, sign, slot in hops[1:]:

        @pl.when(exists(step, sign))
        def _():
            settle(step, sign, slot)

    for copy in sends.values():
        copy.wait_send()
    for copy in [gains, cot_sib, cot_side, cot_across] + cot_on:
        copy.wait_send()
    for e in range(FIRST):
        y_sends[e].wait()
        total = staged[e, :, :, at.y].astype(F32) + y_in[e].astype(F32)
        z_o[:, e] = total.astype(BF16)
    gather_wait(left_copies, left_passed)
    for copy in [store_kv, store_kept, store_part]:
        copy.wait()
    for e in range(FIRST, OWN):
        pltpu.make_async_copy(staged.at[e], grad_o.at[e - FIRST], gd.at[e - FIRST]).wait()


def opening(
    starts, tokens, wq, wk, wv, wo, small, cot, cosine, sine, routes, priority, expert_in, expert_out, ctx_count
):
    outers = ctx_count // INNER
    shape = jax.ShapeDtypeStruct
    count = tokens.shape[0]
    rows = count // 2
    width = wk.shape[1] + wv.shape[1]
    heads = wq.shape[1]
    wide = heads + width
    units = expert_out.shape[-1]
    many = PLANE * count
    blocks = 2 * ctx_count
    z_rows = D // (2 * outers)
    vm = pltpu.VMEM
    return comm_call(
        functools.partial(opening_kernel, outers),
        [
            shape((D, wide), BF16),
            shape((D, D), BF16),
            shape((small.shape[0], D), BF16),
            shape((count, heads), BF16),
            shape((count, D), BF16),
            shape((blocks, rows, width), BF16),
            shape((count, heads), F32),
            shape((count, heads), F32),
            shape((count, heads), BF16),
            shape((count, D), F32),
            shape((EXPERTS, count), F32),
            shape((EXPERTS, count), F32),
            shape((PLANE, 8, count), F32),
            shape((outers // 2, FIRST, 2, z_rows, 3 * units), BF16),
            shape((PLANE, count, D), BF16),
            shape((many, OWN * units), BF16),
            shape((OWN - FIRST, outers // 2, 2, 2, z_rows, 3 * units), BF16),
            shape((2, PLANE, count, D), BF16),
        ],
        [VMEM] + [ANY] * 9 + [VMEM] * 2 + [ANY] * 2,
        [ANY] * 2 + [VMEM] * 3 + [ANY] + [VMEM] * 8 + [ANY] * 4,
        [
            vm((D, wide), BF16),
            vm((D, D), BF16),
            vm((2, rows, width), BF16),
            vm((count, D), BF16),
            vm(cosine.shape, F32),
            vm(sine.shape, F32),
            vm((blocks, rows, width), BF16),
            vm((PLANE, count, D), BF16),
            vm((2, D, 2, units), BF16),
            vm((OWN, D, units), BF16),
            vm((D, OWN * 2 * units), BF16),
            vm((PAIRS, 2 * count, 128), F32),
            vm((PAIRS, 2 * count, 128), F32),
            vm((count, D), BF16),
            vm((EXPERTS, count), F32),
            vm((PLANE, count, D), BF16),
            vm((PLANE, EXPERTS, count), F32),
            vm((D, many), BF16),
            vm((many, OWN * units), BF16),
            vm((many, 128), F32),
            vm((many, 128), F32),
            vm((OWN, outers // 2, 2, 2, z_rows, 3 * units), BF16),
            vm((FIRST, outers // 2, 2, z_rows, 3 * units), BF16),
            DMA((5,)),
            DMA((5,)),
            DMA((4,)),
            DMA((4,)),
            DMA((4,)),
        ]
        + [DMA((2, 2 * outers))] * 4
        + [DMA((2, 4 * outers))] * 2
        + [DMA((8,)), DMA((7,)), DMA((7,)), DMA]
        + [DMA((2 + OWN,)), DMA((2, 7)), DMA((2, 7)), DMA((2,)), DMA((2,))]
        + [DMA((2, 7)), DMA((2, 7)), DMA((2,)), DMA((FIRST,)), DMA((FIRST,))],
        1,
        "opening",
        vmem=64 * 2**20,
        us=100,
    )(starts, tokens, wq, wk, wv, wo, small, cot, cosine, sine, routes, priority, expert_in, expert_out)


def turning_kernel(
    outers,
    seg_ref,
    z_ref,
    grad_in,
    part_in,
    pick_send,
    kept_in,
    expert_out,
    gate_ref,
    kept_ref,
    small_ref,
    sum_in,
    cot_in,
    wo_in,
    raw_in,
    total_in,
    q_in,
    kv_in,
    cos_ref,
    sin_ref,
    dy_ref,
    da_ref,
    dq_ref,
    rows_ref,
    moe_o,
    near_o,
    z_o,
    dkv_ref,
    sum_ref,
    cot_ref,
    raw_ref,
    total_ref,
    q_ref,
    part,
    kept_all,
    out_w,
    wout,
    kv,
    near,
    far_in,
    picks_all,
    q_four,
    n_four,
    d_rows,
    dq_acc,
    kv_acc,
    kv_out,
    z_sums,
    z_in,
    y_own,
    y_in,
    ls,
    ss,
    sr,
    xs,
    xr,
    ps,
    pr,
    vs,
    vr,
    us,
    ur,
    ks,
    rs,
):
    at = Place()
    count = q_ref.shape[0]
    rows = count // 2
    width = PAIRS * 128
    keys = kv.shape[0] * rows
    units = out_w.shape[-1]
    experts = at.q * OWN
    loads = [
        pltpu.make_async_copy(src, dst, ls.at[index])
        for index, (src, dst) in enumerate(
            ((part_in, part), (kept_in, kept_all), (wo_in, wout), (kv_in, kv))
        )
    ]
    weights = [
        pltpu.make_async_copy(expert_out.at[experts + e], out_w.at[e], ls.at[4 + e])
        for e in range(OWN)
    ]
    for copy in loads + weights:
        copy.start()
    z_load = pltpu.make_async_copy(z_ref, z_sums.at[pl.ds(0, outers // 2)], rs.at[5])
    z_load.start()
    rest = Halving(at, outers, z_sums, z_in, vs, vr)
    own_rows = []
    for e in range(OWN - FIRST):
        copy = pltpu.make_async_copy(
            grad_in.at[e, :, :, at.y], y_own.at[e], ls.at[4 + OWN + e]
        )
        copy.start()
        own_rows.append(copy)
    row_loads = [
        pltpu.make_async_copy(src, dst, rs.at[index])
        for index, (src, dst) in enumerate(
            (
                (sum_in, sum_ref),
                (cot_in, cot_ref),
                (raw_in, raw_ref),
                (total_in, total_ref),
                (q_in, q_ref),
            )
        )
    ]
    for copy in row_loads:
        copy.start()
    starts = doc_starts(seg_ref[...])
    meet(
        [at.relative(*bits)[0] for bits in OTHERS]
        + [at.beside]
        + [rest.device(bit) for bit in rest.bits]
    )
    sib, unused = at.relative(0, 1, 0)
    loads[0].wait()
    first = remote(part.at[:, 1 - at.core], near, ss, sr, sib)
    first.start()
    y_sends = []
    for e in range(OWN - FIRST):
        copy = remote(grad_in.at[e, :, :, 1 - at.y], y_in.at[e], us.at[e], ur.at[e], at.beside)
        copy.start()
        y_sends.append(copy)
    z_load.wait()
    if rest.bits:
        rest.start(0)
    small_copies = []
    for slot, bits in enumerate(OTHERS):
        device, j_to = at.relative(*bits)
        copy = remote(pick_send.at[j_to], picks_all.at[at.j], ps.at[slot], pr.at[slot], device)
        copy.start()
        small_copies.append(copy)
    picks_all[at.j] = pick_send[at.j]
    first.wait_recv()
    for y in range(2):
        for w in range(2):
            total = part[y, at.core, w].astype(F32) + near[y, w].astype(F32)
            near[y, w] = total.astype(BF16)
    second = []
    for slot, (dy, dc, dw) in enumerate(XY):
        device, unused = at.relative(dy, dc, dw)
        z = at.z + dy * (1 - 2 * at.z)
        w = at.w + dw * (1 - 2 * at.w)
        copy = remote(near.at[z, w], far_in.at[slot], xs.at[slot], xr.at[slot], device)
        copy.start()
        second.append(copy)

    loads[1].wait()
    for copy in weights + row_loads:
        copy.wait()

    def moe_rows(j, carry):
        here = pl.ds(pl.multiple_of(j * count, count), count)
        total = dot_nt(kept_all[here, :units], out_w[0])
        for e in range(1, OWN):
            total = total + dot_nt(kept_all[here, e * units : (e + 1) * units], out_w[e])
        moe_o[j] = total.astype(BF16)
        return carry

    lax.fori_loop(0, PLANE, moe_rows, 0)
    hidden_sum = near[at.z, at.w].astype(F32)
    for slot in range(3):
        second[slot].wait_recv()
        hidden_sum = hidden_sum + far_in[slot].astype(F32)
    for copy in [first] + second:
        copy.wait_send()
    small = small_ref[...]
    gain_two = small[EXPERTS + 1 : EXPERTS + 2].astype(F32)
    for copy in small_copies:
        copy.wait()
    parts = []
    for i in range(INNER):
        parts.append(picks_all[2 * i, pl.ds(0, OWN), :] + picks_all[2 * i + 1, pl.ds(0, OWN), :])
    gate = gate_ref[...]
    gate_grad = kept_ref[...] * jnp.concatenate(parts, axis=0)
    logit_grad = gate * (gate_grad - jnp.sum(gate * gate_grad, axis=0, keepdims=True))
    logit_grad = jnp.concatenate(
        [logit_grad, jnp.zeros((small.shape[0] - EXPERTS, count), F32)], axis=0
    ).astype(BF16)
    hidden_grad = hidden_sum + dot_tn(logit_grad, small)
    first_sum = sum_ref[...]
    scale = lax.rsqrt(jnp.mean(first_sum * first_sum, axis=1, keepdims=True) + EPS)
    normed = first_sum * scale
    hidden = (normed * gain_two).astype(BF16)
    router_rows = dot_nn(logit_grad, hidden)
    rows_ref[...] = router_rows
    rows_ref[pl.ds(EXPERTS + 1, 1), :] = jnp.sum(hidden_grad * normed, axis=0, keepdims=True)
    normed_grad = hidden_grad * gain_two
    first_grad = cot_ref[...].astype(F32) + scale * (
        normed_grad - normed * jnp.mean(normed_grad * normed, axis=1, keepdims=True)
    )
    dy_ref[...] = first_grad
    attn_grad = (RES_MULT * first_grad).astype(BF16)
    da_ref[...] = attn_grad
    loads[2].wait()
    mixed_grad = dot_nt(attn_grad, wout[...]).astype(BF16).astype(F32)
    total = total_ref[...]
    numer = mixed_grad / total
    lost = mixed_grad * raw_ref[...] / total
    for half in range(2):
        here = slice(half * rows, (half + 1) * rows)
        for pair in range(PAIRS):
            cols = slice(pair * 256, (pair + 1) * 256)
            slot = half * PAIRS + pair
            q_four[slot] = spread(q_ref[here, cols].astype(F32) * ATT_MULT).astype(BF16)
            n_four[slot] = spread(numer[here, cols]).astype(BF16)
            d_rows[slot] = -jnp.sum(spread(lost[here, cols]).T, axis=0, keepdims=True)
    dq_acc[...] = jnp.zeros_like(dq_acc)
    loads[3].wait()

    def kv_store(chunk):
        many = CHUNK // rows
        return pltpu.make_async_copy(
            kv_out.at[chunk % 2], dkv_ref.at[pl.ds(chunk * many, many)], ks.at[chunk % 2]
        )

    def step(chunk, carry):
        at_row = pl.multiple_of(chunk * CHUNK, CHUNK)
        kv_acc[...] = jnp.zeros_like(kv_acc)
        key_pos = at_row + lax.broadcasted_iota(jnp.int32, (CHUNK, 1), 0)
        for half in range(2):
            base, chunks = half_span(half, rows, keys)

            @pl.when(chunk < chunks)
            def _():
                place = base + lax.broadcasted_iota(jnp.int32, (1, 4 * rows), 1) % rows
                first = reach(starts, place)
                bias = jnp.where((key_pos >= first) & (key_pos <= place), 0.0, NEVER)
                for pair in range(PAIRS):
                    slot = half * PAIRS + pair
                    key = key_block(kv, chunk, rows, pair * 128)
                    value = key_block(kv, chunk, rows, width + pair * 128)
                    e = jnp.exp(dot_nt(key, q_four[slot]) + bias)
                    through = dot_nt(value, n_four[slot])
                    dz = (e * (through + d_rows[slot])).astype(BF16)
                    kv_acc[:, pl.ds(pair * 128, 128)] += dot_nn(dz, q_four[slot])
                    kv_acc[:, pl.ds(width + pair * 128, 128)] += dot_nn(e.astype(BF16), n_four[slot])
                    dq_acc[slot] += dot_tn(dz, key)

        many = CHUNK // rows

        @pl.when(chunk >= 2)
        def _():
            kv_store(chunk - 2).wait()

        kv_out[chunk % 2] = kv_acc[...].astype(BF16).reshape(many, rows, 2 * width)
        kv_store(chunk).start()
        return carry

    lax.fori_loop(0, keys // CHUNK, step, 0)
    cosine = cos_ref[...]
    sine = -sin_ref[...]
    for half in range(2):
        here = slice(half * rows, (half + 1) * rows)
        for pair in range(PAIRS):
            block = ATT_MULT * unspread(dq_acc[half * PAIRS + pair])
            dq_ref[here, pair * 256 : (pair + 1) * 256] = turn(
                block, cosine[here], sine[here]
            ).astype(BF16)
    for chunk in range(keys // CHUNK - 2, keys // CHUNK):
        kv_store(chunk).wait()
    near_o[...] = rest.finish()
    for copy in own_rows:
        copy.wait()
    for e in range(OWN - FIRST):
        y_sends[e].wait()
        total = y_own[e].astype(F32) + y_in[e].astype(F32)
        z_o[:, e] = total.astype(BF16)


def turning(
    outers, segments, z_first, grads, part, picks, kept_units, expert_out, gate, kept, small, first_sum, cot, output_w, raw, total, queries, kv_all, cosine, sine
):
    shape = jax.ShapeDtypeStruct
    count, width = queries.shape
    units = expert_out.shape[-1]
    vm = pltpu.VMEM
    return comm_call(
        functools.partial(turning_kernel, outers),
        [
            shape((count, D), F32),
            shape((count, D), BF16),
            shape((count, width), BF16),
            shape((32, D), F32),
            shape((PLANE, count, D), BF16),
            shape(z_first.shape[1:], BF16),
            shape((outers // 2, OWN - FIRST) + z_first.shape[2:], BF16),
            shape(kv_all.shape, BF16),
        ],
        [VMEM] + [ANY] * 3 + [VMEM] + [ANY] * 2 + [VMEM] * 3 + [ANY] * 7 + [VMEM] * 2,
        [VMEM] * 7 + [ANY],
        [
            vm((count, D), F32),
            vm((count, D), BF16),
            vm((count, width), F32),
            vm((count, width), F32),
            vm((count, width), BF16),
            vm((2, 2, 2, count, D), BF16),
            vm(kept_units.shape, BF16),
            vm((OWN, D, units), BF16),
            vm((D, D), BF16),
            vm(kv_all.shape, BF16),
            vm((2, 2, count, D), BF16),
            vm((3, count, D), BF16),
            vm((PLANE, 8, count), F32),
            vm((2 * PAIRS, 2 * count, 128), BF16),
            vm((2 * PAIRS, 2 * count, 128), BF16),
            vm((2 * PAIRS, 1, 2 * count), F32),
            vm((2 * PAIRS, 2 * count, 128), F32),
            vm((CHUNK, 2 * PAIRS * 128), F32),
            vm((2, CHUNK // (count // 2), count // 2, 2 * PAIRS * 128), BF16),
            vm((outers,) + z_first.shape[1:], BF16),
            vm((outers,) + z_first.shape[1:], BF16),
            vm((OWN - FIRST, outers // 2) + z_first.shape[2:], BF16),
            vm((OWN - FIRST, outers // 2) + z_first.shape[2:], BF16),
            DMA((4 + OWN + OWN - FIRST,)),
            DMA,
            DMA,
            DMA((3,)),
            DMA((3,)),
            DMA((7,)),
            DMA((7,)),
            DMA((outers,)),
            DMA((outers,)),
            DMA((OWN - FIRST,)),
            DMA((OWN - FIRST,)),
            DMA((2,)),
            DMA((6,)),
        ],
        5,
        "turning",
        vmem=62 * 2**20,
        us=35,
    )(
        segments,
        z_first,
        grads,
        part.reshape(2, 2, 2, count, D),
        picks,
        kept_units,
        expert_out,
        gate,
        kept,
        small,
        first_sum,
        cot,
        output_w,
        raw,
        total,
        queries,
        kv_all,
        cosine,
        sine,
    )


def assemble_kernel(outers, counts, *refs):
    size = 2 + len(counts)
    sources, refs = refs[:size], refs[size:]
    wq, wk, wv, wo, small, inner, outer = refs[:7]
    held, sems = refs[7 : 7 + size], refs[7 + size]
    loads = [
        pltpu.make_async_copy(sources[k], held[k], sems.at[k]) for k in range(size)
    ]
    for copy in loads:
        copy.start()
    attn_in, small_in = held[:2]
    for copy in loads:
        copy.wait()
    experts = [(near, k) for near, many in zip(held[2:], counts) for k in range(many)]
    qkv_cols = wq.shape[1] * 2 // PLANE
    devices = outers * PLANE
    for j in range(PLANE):
        z, core, w = j // 4, (j // 2) % 2, j % 2
        total = 0.0
        for above in range(outers // 2):
            for y in range(2):
                source = (((above * 2 + z) * 2 + y) * 2 + core) * 2 + w
                total = total + attn_in[source].astype(F32)
        col = j * qkv_cols
        ref, base = (wq, 0) if col < 1024 else (wk, 1024) if col < 1536 else (wv, 1536)
        ref[:, col - base : col - base + qkv_cols] = total[:, :qkv_cols]
        wo[:, j * (D // PLANE) : (j + 1) * (D // PLANE)] = total[:, qkv_cols:]
    total = small_in[0].astype(F32)
    for i in range(1, devices):
        total = total + small_in[i].astype(F32)
    small[...] = total
    rows = wq.shape[0]
    units = outer.shape[-1] // 2
    for j in range(PLANE):
        cols = slice((j % 2) * units, (j % 2 + 1) * units)
        for k in range(OWN):
            e = (j // 2) * OWN + k
            near, at = experts[k]
            block = near[j, at].astype(F32)
            inner[e, :, :, cols] = block[:, : 2 * units].reshape(rows, 2, units)
            outer[e, :, cols] = block[:, 2 * units :]


def assemble(attn_in, small_in, nears, outers):
    rows = attn_in.shape[1]
    units = nears[0].shape[-1] // 3
    sources = [attn_in, small_in] + nears
    shape = jax.ShapeDtypeStruct
    outs = [
        shape((rows, 1024), F32),
        shape((rows, 512), F32),
        shape((rows, 512), F32),
        shape((rows, D), F32),
        shape((rows, 128), F32),
        shape((EXPERTS, rows, 2, 2 * units), F32),
        shape((EXPERTS, rows, 2 * units), F32),
    ]
    return pl.pallas_call(
        functools.partial(assemble_kernel, outers, [near.shape[1] for near in nears]),
        out_shape=outs,
        in_specs=[ANY] * len(sources),
        out_specs=[VMEM] * 7,
        scratch_shapes=[pltpu.VMEM(a.shape, a.dtype) for a in sources] + [DMA((len(sources),))],
        compiler_params=pltpu.CompilerParams(vmem_limit_bytes=60 * 2**20),
        name="assemble",
    )(*sources)


def body(
    tokens,
    w_query,
    w_key,
    w_value,
    w_output,
    attn_gain,
    w_router,
    expert_in,
    expert_out,
    moe_gain,
    segments,
    routes,
    priority,
    cotangent,
):
    ctx_count = lax.axis_size("ctx")
    ctx_index = lax.axis_index("ctx")
    devices = ctx_count * 2
    outers = ctx_count // INNER
    owner_rows = D // devices
    block_rows = tokens.shape[2]
    half_rows = block_rows * ctx_count
    tok_count = 2 * block_rows
    f32 = jnp.float32
    bf16 = jnp.bfloat16

    small = jnp.concatenate(
        [w_router.T, attn_gain[None], moe_gain[None], jnp.zeros((14, w_router.shape[0]), bf16)]
    )
    cot_own = cotangent.reshape(tok_count, D)
    block_total = 2 * ctx_count
    block_ids = jnp.stack([ctx_index, block_total - 1 - ctx_index])
    query_pos = block_ids[:, None] * block_rows + jnp.arange(block_rows, dtype=jnp.int32)[None, :]
    flat_pos = query_pos.reshape(tok_count)
    frequency = jnp.exp(
        -jnp.log(jnp.float32(THETA))
        * jnp.arange(HEAD_DIM // 2, dtype=jnp.float32)
        * (2.0 / HEAD_DIM)
    )
    angles = flat_pos.astype(f32)[:, None] * frequency[None, :]
    cosine, sine = jnp.cos(angles), jnp.sin(angles)
    cosine = jnp.concatenate([cosine] * 4, axis=1)
    sine = jnp.concatenate([-sine, sine] * 2, axis=1)
    token_low = tokens.reshape(tok_count, D)
    (
        qkv_w,
        output_w,
        small_all,
        queries,
        hidden_one,
        kv_all,
        attn_raw,
        attn_total,
        mixed,
        first_sum,
        gate,
        kept,
        picks,
        first_half,
        part,
        kept_units,
        expert_grads,
        left,
    ) = opening(
        segments,
        token_low,
        w_query,
        w_key,
        w_value,
        w_output,
        small,
        cot_own,
        cosine,
        sine,
        routes[0].transpose(0, 2, 1),
        priority[0].transpose(0, 2, 1),
        expert_in,
        expert_out,
        ctx_count,
    )
    (
        first_grad,
        attn_grad,
        query_lin_grad,
        small_rows,
        moe_part,
        near_one,
        second_half,
        kv_terms,
    ) = turning(
        outers,
        segments,
        first_half,
        expert_grads,
        part,
        picks,
        kept_units,
        expert_out,
        gate,
        kept,
        small_all,
        first_sum,
        cot_own,
        output_w,
        attn_raw,
        attn_total,
        queries,
        kv_all,
        cosine,
        sine,
    )
    output, token_grad, attn_part, small_part, near_first, near_next, near = finish(
        kv_terms,
        moe_part,
        [
            first_sum,
            query_lin_grad,
            attn_grad,
            first_grad,
            token_low,
            small_all,
            cosine,
            sine,
            qkv_w,
            left,
            small_rows,
        ],
        second_half,
        near_one.reshape(FIRST, PLANE, owner_rows, -1),
        ctx_count,
    )
    attn_in, small_in, near_last = owners(
        [attn_part, small_part],
        [near.reshape(-1, PLANE, owner_rows, near.shape[-1])],
        devices,
        7,
        "owners",
    )
    query_sum, key_sum, value_sum, output_sum, small_sum, inner_sum, outer_sum = assemble(
        attn_in, small_in, [near_first, near_next, near_last], outers
    )
    return (
        output.reshape(tokens.shape),
        token_grad.reshape(tokens.shape),
        query_sum,
        key_sum,
        value_sum,
        output_sum,
        small_sum[:, EXPERTS],
        small_sum[:, :EXPERTS],
        inner_sum,
        outer_sum,
        small_sum[:, EXPERTS + 1],
    )


def solution(mesh):
    placed = (
        P("wsh", None, "ctx", None),
        P("wsh", None),
        P("wsh", None),
        P("wsh", None),
        P("wsh", None),
        P("wsh"),
        P("wsh", None),
        P(None, None, None, "wsh"),
        P(None, None, "wsh"),
        P("wsh"),
        P("wsh", None),
        P("wsh", None, "ctx", None),
        P("wsh", None, "ctx", None),
        P("wsh", None, "ctx", None),
    )
    return jax.shard_map(
        body,
        mesh=mesh,
        in_specs=placed,
        out_specs=(
            P("wsh", None, "ctx", None),
            P("wsh", None, "ctx", None),
            P(("ctx", "wsh"), None),
            P(("ctx", "wsh"), None),
            P(("ctx", "wsh"), None),
            P(("ctx", "wsh"), None),
            P(("ctx", "wsh")),
            P(("ctx", "wsh"), None),
            P(None, ("ctx", "wsh"), None, None),
            P(None, ("ctx", "wsh"), None),
            P(("ctx", "wsh")),
        ),
        check_vma=False,
    )
```

```python
import functools

import jax
import jax.numpy as jnp
from jax import lax
from jax.experimental import pallas as pl
from jax.experimental.pallas import tpu as pltpu
from jax.sharding import PartitionSpec as P

D = 1024
HEADS = 16
KV_HEADS = 8
HEAD_DIM = 64
TOPK = 8
EXPERTS = 16
CAP = 80
PLANE = 8
INNER = 4
OWN = EXPERTS // INNER
PIECES = 2
FIRST = OWN // 2


RES_MULT = 0.22
ATT_MULT = 0.015625
EPS = 1e-06
THETA = 10000.0

MESH = pl.DeviceIdType.MESH
F32 = jnp.float32
BF16 = jnp.bfloat16
ANY = pl.BlockSpec(memory_space=pl.ANY)
VMEM = pl.BlockSpec(memory_space=pltpu.VMEM)


class Place:
    def __init__(self):
        self.c = lax.axis_index("ctx")
        self.w = lax.axis_index("wsh")
        self.core = self.c % 2
        self.y = (self.c // 2) % 2
        self.inner = self.c % INNER
        self.outer = self.c // INNER
        self.z = self.outer % 2
        self.q = self.z * 2 + self.core
        self.j = self.q * 2 + self.w
        self.beside = (self.c + 2 - 4 * self.y, self.w)

    def relative(self, dz, dc, dw):
        z = self.z + dz * (1 - 2 * self.z)
        core = self.core + dc * (1 - 2 * self.core)
        w = self.w + dw * (1 - 2 * self.w)
        ctx = self.c + INNER * (z - self.z) + core - self.core
        return (ctx, w), (z * 2 + core) * 2 + w


OTHERS = [(a, b, d) for a in range(2) for b in range(2) for d in range(2) if a + b + d]
XY = [(0, 0, 1), (1, 0, 0), (1, 0, 1)]


def meet(devices):
    barrier = pltpu.get_barrier_semaphore()
    for device in devices:
        pl.semaphore_signal(barrier, inc=1, device_id=device, device_id_type=MESH)
    pl.semaphore_wait(barrier, len(devices))


def remote(src, dst, send, recv, device):
    return pltpu.make_async_remote_copy(
        src_ref=src,
        dst_ref=dst,
        send_sem=send,
        recv_sem=recv,
        device_id=device,
        device_id_type=MESH,
    )


def comm_call(kernel, out_shape, in_specs, out_specs, scratch, ident, name, vmem=None, us=20):
    return pl.pallas_call(
        kernel,
        out_shape=out_shape,
        in_specs=in_specs,
        out_specs=out_specs,
        scratch_shapes=scratch,
        compiler_params=pltpu.CompilerParams(
            collective_id=ident, has_side_effects=True, vmem_limit_bytes=vmem
        ),
        cost_estimate=pl.CostEstimate(
            flops=us * 10**9, bytes_accessed=us * 3 * 2**20, transcendentals=0
        ),
        name=name,
    )


DMA = pltpu.SemaphoreType.DMA


def room(arrays, scratch=(), spare=12):
    total = 0
    for array in list(arrays) + list(scratch):
        inner = getattr(array, "inner_aval", array)
        size = jnp.dtype(inner.dtype).itemsize
        for extent in inner.shape:
            size *= extent
        total += size
    return min(total + spare * 2**20, 62 * 2**20)


def far_first(outers):
    return outers == 4


def far_partner(at):
    return (at.c + INNER * 2 * (1 - 2 * (at.outer // 2)), at.w)


class Halving:
    def __init__(self, at, outers, sums, arrived, send, recv, cols=slice(None)):
        self.cols = cols
        self.at, self.sums, self.arrived = at, sums, arrived
        self.send, self.recv = send, recv
        self.bits = [2**k for k in range(1, outers.bit_length() - 1)]
        self.levels = [(0, outers // 2)]
        for bit in self.bits:
            start, many = self.levels[-1]
            self.levels.append((start + many, many // 2))
        self.copies = []

    def pick(self, index):
        return index, slice(None), slice(None), self.cols

    def device(self, bit):
        at = self.at
        return (at.c + INNER * bit * (1 - 2 * ((at.outer // bit) % 2)), at.w)

    def start(self, step):
        bit = self.bits[step]
        side = (self.at.outer // bit) % 2
        start, many = self.levels[step]
        for m in range(many // 2):
            copy = remote(
                self.sums.at[self.pick(start + 2 * m + 1 - side)],
                self.arrived.at[self.pick(start + m)],
                self.send.at[start + m],
                self.recv.at[start + m],
                self.device(bit),
            )
            copy.start()
            self.copies.append(copy)

    def add(self, step):
        side = (self.at.outer // self.bits[step]) % 2
        start, many = self.levels[step]
        after, half = self.levels[step + 1]
        for m in range(half):
            self.copies[len(self.copies) - half + m].wait_recv()
            total = self.sums[self.pick(start + 2 * m + side)].astype(F32)
            total = total + self.arrived[self.pick(start + m)].astype(F32)
            self.sums[self.pick(after + m)] = total.astype(BF16)

    def finish(self):
        for step in range(len(self.bits)):
            if step > 0:
                self.start(step)
            self.add(step)
        for copy in self.copies:
            copy.wait_send()
        return self.sums[self.pick(self.levels[-1][0])]


def gather_start(at, pairs, send, recv, local):
    copies = []
    for index, (src, dst) in enumerate(pairs):
        keep = pltpu.make_async_copy(src, dst.at[at.j], local.at[index])
        keep.start()
        sends = []
        for slot, bits in enumerate(XY + [(0, 1, 0)]):
            device, unused = at.relative(*bits)
            copy = remote(src, dst.at[at.j], send.at[index, slot], recv.at[index, slot], device)
            copy.start()
            sends.append(copy)
        copies.append((keep, sends))
    return copies


def gather_pass(at, pairs, copies, send, recv):
    sib, unused = at.relative(0, 1, 0)
    passed = []
    for slot, bits in enumerate(XY):
        unused, j_from = at.relative(*bits)
        for index, (src, dst) in enumerate(pairs):
            copies[index][1][slot].wait_recv()
            block = dst.at[j_from]
            copy = remote(
                block, block, send.at[index, 4 + slot], recv.at[index, 4 + slot], sib
            )
            copy.start()
            passed.append(copy)
    return passed


def gather_wait(copies, passed):
    for keep, sends in copies:
        keep.wait()
        sends[3].wait_recv()
        for copy in sends:
            copy.wait_send()
    for copy in passed:
        copy.wait()


def turn(values, cosine, sine):
    lane = lax.broadcasted_iota(jnp.int32, cosine.shape, 1)
    first = lane % HEAD_DIM < HEAD_DIM // 2
    blocks = []
    for start in range(0, values.shape[1], 128):
        u = values[:, start : start + 128]
        swapped = jnp.where(first, pltpu.roll(u, 96, 1), pltpu.roll(u, 32, 1))
        blocks.append(u * cosine + swapped * sine)
    return jnp.concatenate(blocks, axis=1)


def dot_nt(a, b):
    return lax.dot_general(a, b, (((1,), (1,)), ((), ())), preferred_element_type=F32)


def dot_tn(a, b):
    return lax.dot_general(a, b, (((0,), (0,)), ((), ())), preferred_element_type=F32)


def dot_nn(a, b):
    return jnp.dot(a, b, preferred_element_type=F32)


def owners_kernel(devices, count, near_count, *refs):
    total = count + near_count
    parts, nears = refs[:count], refs[count:total]
    outs, near_outs = refs[total : total + count], refs[total + count : 2 * total]
    send, recv, local, nsend, nrecv, nlocal = refs[2 * total :]
    at = Place()
    me = at.c * 2 + at.w
    rows = D // devices

    def device_of(r):
        index = lax.rem(me + r, devices)
        return index, (index // 2, lax.rem(index, 2))

    def rows_of(ref, index):
        return ref.at[pl.ds(pl.multiple_of(index * rows, rows), rows), :]

    barrier = pltpu.get_barrier_semaphore()

    def greet(r, carry):
        unused, device = device_of(r)
        pl.semaphore_signal(barrier, inc=1, device_id=device, device_id_type=MESH)
        return carry

    lax.fori_loop(1, devices, greet, 0)
    pl.semaphore_wait(barrier, devices - 1)

    def copy_of(k, r):
        index, device = device_of(r)
        return remote(rows_of(parts[k], index), outs[k].at[me], send.at[k, r], recv.at[k, r], device)

    def start(r, carry):
        for k in range(count):
            copy_of(k, r).start()
        return carry

    lax.fori_loop(1, devices, start, 0)

    near_copies = []
    for k in range(near_count):
        for slot, bits in enumerate(OTHERS):
            device, j_to = at.relative(*bits)
            copy = remote(
                nears[k].at[:, j_to], near_outs[k].at[at.j], nsend.at[k, slot], nrecv.at[k, slot], device
            )
            copy.start()
            near_copies.append(copy)
    keeps = []
    for k in range(count):
        keep = pltpu.make_async_copy(rows_of(parts[k], me), outs[k].at[me], local.at[k])
        keep.start()
        keeps.append(keep)
    for k in range(near_count):
        keep = pltpu.make_async_copy(nears[k].at[:, at.j], near_outs[k].at[at.j], nlocal.at[k])
        keep.start()
        keeps.append(keep)

    def finish(r, carry):
        for k in range(count):
            copy_of(k, r).wait()
        return carry

    lax.fori_loop(1, devices, finish, 0)
    for copy in near_copies:
        copy.wait()
    for keep in keeps:
        keep.wait()


def owners(parts, nears, devices, ident, name):
    count, near_count = len(parts), len(nears)
    rows = D // devices
    shape = jax.ShapeDtypeStruct
    shapes = [shape((devices, rows, part.shape[-1]), part.dtype) for part in parts]
    for near in nears:
        lead, members, near_rows, width = near.shape
        shapes.append(shape((members, lead, near_rows, width), near.dtype))
    return comm_call(
        functools.partial(owners_kernel, devices, count, near_count),
        shapes,
        [ANY] * (count + near_count),
        [VMEM] * (count + near_count),
        [
            DMA((count, devices)),
            DMA((count, devices)),
            DMA((count,)),
            DMA((near_count, 7)),
            DMA((near_count, 7)),
            DMA((near_count,)),
        ],
        ident,
        name,
        vmem=60 * 2**20,
    )(*parts, *nears)


CHUNK = 256
PAIRS = KV_HEADS // 2
NEVER = -1e30


def low_lanes(shape):
    return lax.broadcasted_iota(jnp.int32, shape, 1) < HEAD_DIM


def spread(block):
    a, b = block[:, :128], block[:, 128:]
    low = low_lanes(a.shape)
    zero = jnp.zeros_like(a)
    return jnp.concatenate(
        [
            jnp.where(low, a, zero),
            jnp.where(low, pltpu.roll(a, HEAD_DIM, 1), zero),
            jnp.where(low, zero, pltpu.roll(b, HEAD_DIM, 1)),
            jnp.where(low, zero, b),
        ],
        axis=0,
    )


def unspread(four):
    rows = four.shape[0] // 4
    r0, r1, r2, r3 = (four[k * rows : (k + 1) * rows] for k in range(4))
    low = low_lanes(r0.shape)
    return jnp.concatenate(
        [
            jnp.where(low, r0, pltpu.roll(r1, HEAD_DIM, 1)),
            jnp.where(low, pltpu.roll(r2, HEAD_DIM, 1), r3),
        ],
        axis=1,
    )


DOCS = 8


def doc_starts(segments):
    return [
        jnp.sum(jnp.where(segments < d, 1.0, 0.0), axis=1, keepdims=True).astype(jnp.int32)
        for d in range(DOCS)
    ]


def reach(starts, place):
    first = jnp.zeros_like(place)
    for d in range(1, DOCS):
        first = jnp.where(place >= starts[d], starts[d], first)
    return first


def half_span(half, rows, keys):
    block = lax.axis_index("ctx")
    if half == 1:
        block = keys // rows - 1 - block
    base = block * rows
    return base, (base + rows + CHUNK - 1) // CHUNK


def key_block(kv, chunk, rows, col):
    many = CHUNK // rows
    picked = kv[pl.ds(chunk * many, many), :, pl.ds(col, 128)]
    return picked.reshape(CHUNK, 128)


def attend_rows(
    starts,
    q_ref,
    kv_ref,
    tok_ref,
    wo_ref,
    small_ref,
    route_ref,
    prio_ref,
    raw_ref,
    total_ref,
    mixed_ref,
    sum_ref,
    hid_ref,
    gate_ref,
    kept_ref,
    send_ref,
    acc,
    acc_l,
):
    rows = q_ref.shape[0] // 2
    width = PAIRS * 128
    keys = kv_ref.shape[0] * rows
    for half in range(2):
        base, chunks = half_span(half, rows, keys)
        q_four = []
        for pair in range(PAIRS):
            block = q_ref[pl.ds(half * rows, rows), pl.ds(pair * 256, 256)].astype(F32) * ATT_MULT
            q_four.append(spread(block).astype(BF16))
        acc[...] = jnp.zeros_like(acc)
        acc_l[...] = jnp.zeros_like(acc_l)
        place = base + lax.broadcasted_iota(jnp.int32, (rows, 1), 0)
        first = reach(starts, place)

        def step(chunk, carry):
            at_row = pl.multiple_of(chunk * CHUNK, CHUNK)
            key_pos = at_row + lax.broadcasted_iota(jnp.int32, (1, CHUNK), 1)
            bias = jnp.where((key_pos >= first) & (key_pos <= place), 0.0, NEVER)
            bias = jnp.concatenate([bias] * 4, axis=0)
            for pair in range(PAIRS):
                key = key_block(kv_ref, chunk, rows, pair * 128)
                value = key_block(kv_ref, chunk, rows, width + pair * 128)
                e = jnp.exp(dot_nt(q_four[pair], key) + bias)
                part = e[:, :128]
                for k in range(1, CHUNK // 128):
                    part = part + e[:, k * 128 : (k + 1) * 128]
                acc_l[pair] += part
                acc[pair] += dot_nn(e.astype(BF16), value)
            return carry

        lax.fori_loop(0, chunks, step, 0)
        for pair in range(PAIRS):
            total = jnp.sum(acc_l[pair], axis=1, keepdims=True)
            total = jnp.broadcast_to(total, (4 * rows, 128))
            here = pl.ds(half * rows, rows), pl.ds(pair * 256, 256)
            raw_ref[here] = unspread(acc[pair] / total)
            total_ref[here] = unspread(total)
    mixed = raw_ref[...].astype(BF16)
    mixed_ref[...] = mixed
    first_sum = tok_ref[...].astype(F32) + RES_MULT * dot_nn(mixed, wo_ref[...])
    sum_ref[...] = first_sum
    scale = lax.rsqrt(jnp.mean(first_sum * first_sum, axis=1, keepdims=True) + EPS)
    gain_two = small_ref[pl.ds(EXPERTS + 1, 1), :].astype(F32)
    hidden = (first_sum * scale * gain_two).astype(BF16)
    hid_ref[...] = hidden

    logits = dot_nt(small_ref[...], hidden)[:EXPERTS]
    count = 2 * rows
    expert = lax.broadcasted_iota(jnp.int32, (EXPERTS, count), 0)
    routed = jnp.zeros((EXPERTS, count), F32)
    prio = jnp.zeros((EXPERTS, count), F32)
    for k in range(TOPK):
        line = [
            jnp.concatenate([ref[0, pl.ds(k, 1), :], ref[1, pl.ds(k, 1), :]], axis=1)
            for ref in (route_ref, prio_ref)
        ]
        same = expert == line[0]
        routed = jnp.where(same, 1.0, routed)
        prio = jnp.where(same, line[1].astype(F32), prio)
    chosen = routed > 0.0
    order = lax.broadcasted_iota(jnp.int32, (EXPERTS, count), 1).astype(F32)
    key = jnp.where(chosen, prio * float(count) + order, 65536.0 * count)
    key_cols = jnp.concatenate([key, jnp.zeros((count - EXPERTS, count), F32)], axis=0).T
    ranks = []
    for e in range(EXPERTS):
        ahead = jnp.where(key_cols[:, e : e + 1] < key[e : e + 1, :], 1.0, 0.0)
        ranks.append(jnp.sum(ahead, axis=0, keepdims=True))
    rank = jnp.concatenate(ranks, axis=0)
    top = jnp.max(jnp.where(chosen, logits, -3e38), axis=0, keepdims=True)
    weight = jnp.where(chosen, jnp.exp(logits - top), 0.0)
    gate = weight / jnp.sum(weight, axis=0, keepdims=True)
    kept = jnp.where(chosen & (rank < CAP), 1.0, 0.0)
    gate_ref[...] = gate
    kept_ref[...] = kept
    send_ref[...] = gate * kept


SMEM = pl.BlockSpec(memory_space=pltpu.SMEM)


def finish_kernel(
    outers,
    part,
    moe,
    sum_ref,
    dq_ref,
    da_ref,
    dy_ref,
    tok_ref,
    small_ref,
    cos_ref,
    sin_ref,
    wqkv_in,
    left_in,
    rows_ref,
    z_ref,
    near_in,
    out_ref,
    token_ref,
    attn_ref,
    small_o,
    near_o,
    next_o,
    z_o,
    wqkv_ref,
    left_ref,
    z_sums,
    z_in_rows,
    own,
    half_in,
    y_in,
    z_in,
    m_own,
    m_near,
    m_x,
    m_y,
    qkv,
    swap,
    swapped,
    ss,
    sr,
    ys,
    yr,
    zs,
    zr,
    ns,
    nr,
    ws,
    wr,
    vs,
    vr,
    ls,
    os,
    ps,
    pr,
    qs,
    qr,
):
    at = Place()
    blocks, rows, full = part.shape
    loads = [
        pltpu.make_async_copy(wqkv_in, wqkv_ref, ls.at[0]),
        pltpu.make_async_copy(left_in, left_ref, ls.at[1]),
    ]
    moe_load = pltpu.make_async_copy(moe.at[:, at.core], m_own, ls.at[2])
    near_keep = pltpu.make_async_copy(near_in.at[:, at.j], near_o.at[at.j], ls.at[3])
    z_loads = [
        pltpu.make_async_copy(
            z_ref.at[:, e], z_sums.at[e, pl.ds(0, outers // 2)], ls.at[4 + e]
        )
        for e in range(z_sums.shape[0])
    ]
    for copy in z_loads + [moe_load] + loads + [near_keep]:
        copy.start()
    width = full // 2
    cuts = 4
    step_width = full // cuts
    count = 2 * rows
    sib, unused = at.relative(0, 1, 0)
    side = at.beside
    along_to, unused = at.relative(1, 0, 0)
    across, unused = at.relative(0, 0, 1)
    other = [lax.rem(at.outer + r, outers) for r in range(outers)]
    far = [(other[r] * INNER + at.inner, at.w) for r in range(1, outers)]
    rest = [
        Halving(at, outers, z_sums.at[e], z_in_rows.at[e], vs.at[e], vr.at[e])
        for e in range(z_sums.shape[0])
    ]
    meet([at.relative(*bits)[0] for bits in OTHERS] + far + [at.beside])
    for copy in z_loads:
        copy.wait()
    if outers > 2:
        rest[0].start(0)

    def own_block(half, o, y, core):
        index = (o * 2 + y) * 2 + core
        return index if half == 0 else blocks - 1 - index

    own_loads = []
    for y in range(2):
        for h in range(2):
            for o in range(outers):
                copy = pltpu.make_async_copy(
                    part.at[own_block(h, o, y, at.core)], own.at[y, h, o], os.at[y, h, o]
                )
                copy.start()
                own_loads.append(copy)
    first = {}
    for k in range(cuts):
        cols = pl.ds(k * step_width, step_width)
        for y in range(2):
            for h in range(2):
                for o in range(outers):
                    copy = remote(
                        part.at[own_block(h, o, y, 1 - at.core), :, cols],
                        half_in.at[y, h, o, :, cols],
                        ss.at[k, y, h, o],
                        sr.at[k, y, h, o],
                        sib,
                    )
                    copy.start()
                    first[k, y, h, o] = copy
    nears = []
    for slot, bits in enumerate(OTHERS):
        device, j_to = at.relative(*bits)
        copy = remote(near_in.at[:, j_to], near_o.at[at.j], ps.at[slot], pr.at[slot], device)
        copy.start()
        nears.append(copy)
    near = remote(moe.at[:, 1 - at.core], m_near, ns.at[0], nr.at[0], sib)
    near.start()
    for copy in own_loads:
        copy.wait()
    second = []
    for k in range(cuts):
        cols = pl.ds(k * step_width, step_width)
        for y in range(2):
            for h in range(2):
                for o in range(outers):
                    first[k, y, h, o].wait_recv()
                    total = own[y, h, o, :, cols].astype(F32) + half_in[
                        y, h, o, :, cols
                    ].astype(F32)
                    half_in[y, h, o, :, cols] = total.astype(BF16)
        copy = remote(
            half_in.at[1 - at.y, :, :, :, cols], y_in.at[:, :, :, cols], ys.at[k], yr.at[k], side
        )
        copy.start()
        second.append(copy)
    near.wait_recv()
    moe_load.wait()
    for y in range(2):
        for w in range(2):
            total = m_own[y, w].astype(F32) + m_near[y, w].astype(F32)
            m_near[y, w] = total.astype(BF16)
    cross = remote(m_near.at[:, 1 - at.w], m_x, ns.at[1], nr.at[1], across)
    cross.start()
    third = []

    def z_send(k):
        cols = pl.ds(k * step_width, step_width)
        second[k].wait_recv()
        for o in range(outers):
            for h in range(2):
                total = half_in[at.y, h, o, :, cols].astype(F32) + y_in[h, o, :, cols].astype(F32)
                half_in[at.y, h, o, :, cols] = total.astype(BF16)
        for r in range(1, outers):
            copy = remote(
                half_in.at[at.y, :, other[r], :, cols],
                z_in.at[r, :, :, cols],
                zs.at[k, r],
                zr.at[k, r],
                far[r - 1],
            )
            copy.start()
            third.append(copy)

    z_send(0)
    z_send(1)
    cross.wait_recv()
    for y in range(2):
        total = m_near[y, at.w].astype(F32) + m_x[y].astype(F32)
        m_x[y] = total.astype(BF16)
    along = remote(m_x.at[1 - at.z], m_y, ns.at[2], nr.at[2], along_to)
    along.start()
    for k in range(2, cuts):
        z_send(k)
    qkv[:, : HEADS * HEAD_DIM] = dq_ref[...]
    along.wait_recv()
    moe_sum = m_x[at.z].astype(F32) + m_y[...].astype(F32)
    out_ref[...] = (sum_ref[...] + RES_MULT * moe_sum).astype(BF16)
    tok = tok_ref[...].astype(F32)
    scale = lax.rsqrt(jnp.mean(tok * tok, axis=1, keepdims=True) + EPS)
    normed = tok * scale
    gain_one = small_ref[pl.ds(EXPERTS, 1), :].astype(F32)
    for copy in third:
        copy.wait_recv()
    if outers > 2:
        for halving in rest[1:]:
            halving.start(0)
    rest[0].finish()
    level = rest[0].levels[-1][0]
    owner_rows = next_o.shape[2]

    def rows_of(j):
        within = pl.multiple_of(lax.rem(j, 4) * owner_rows, owner_rows)
        return 0, level, j // 4, pl.ds(within, owner_rows)

    for slot, bits in enumerate(OTHERS):
        device, j_to = at.relative(*bits)
        copy = remote(
            z_sums.at[rows_of(j_to)], next_o.at[at.j, 0], qs.at[slot], qr.at[slot], device
        )
        copy.start()
        nears.append(copy)
    next_o[at.j, 0] = z_sums[rows_of(at.j)]
    cosine = cos_ref[...]
    sine = -sin_ref[...]
    base = HEADS * HEAD_DIM
    for h in range(2):
        here = slice(h * rows, (h + 1) * rows)
        total = half_in[at.y, h, at.outer].astype(F32)
        for r in range(1, outers):
            total = total + z_in[r, h].astype(F32)
        qkv[here, base : base + width] = turn(total[:, :width], cosine[here], sine[here]).astype(BF16)
        qkv[here, base + width :] = total[:, width:].astype(BF16)
    wide = full * 2 // PLANE
    for j in range(PLANE):
        swap[j, :, :wide] = qkv[:, j * wide : (j + 1) * wide]
        swap[j, :, wide:] = da_ref[:, j * (D // PLANE) : (j + 1) * (D // PLANE)]
    swaps = []
    for slot, bits in enumerate(OTHERS):
        device, j_to = at.relative(*bits)
        copy = remote(swap.at[j_to], swapped.at[at.j], ws.at[slot], wr.at[slot], device)
        copy.start()
        swaps.append(copy)
    swapped[at.j] = swap[at.j]
    for copy in loads:
        copy.wait()
    hidden_grad = dot_nt(qkv[...], wqkv_ref[...])
    small = rows_ref[...]
    gain_grad = jnp.sum(hidden_grad * normed, axis=0, keepdims=True)
    line = lax.broadcasted_iota(jnp.int32, small.shape, 0)
    small = jnp.where(line == EXPERTS, gain_grad, small)
    small = jnp.concatenate([small, jnp.zeros((128 - small.shape[0], D), F32)], axis=0)
    small_o[...] = small.T.astype(BF16)
    hidden_grad = hidden_grad * gain_one
    token_ref[...] = dy_ref[...] + scale * (
        hidden_grad - normed * jnp.mean(hidden_grad * normed, axis=1, keepdims=True)
    )
    for copy in swaps:
        copy.wait_recv()
    all_rows = PLANE * count
    left_one = left_ref[0].reshape(all_rows, D)
    left_mixed = left_ref[1].reshape(all_rows, D)
    grads = swapped[...].reshape(all_rows, wide + D // PLANE)
    attn_ref[:, :wide] = dot_tn(left_one, grads[:, :wide]).astype(BF16)
    attn_ref[:, wide:] = dot_tn(left_mixed, grads[:, wide:]).astype(BF16)
    for e in range(1, len(rest)):
        z_o[e - 1] = rest[e].finish()
    near_keep.wait()
    for copy in nears:
        copy.wait()
    for copy in list(first.values()) + second + third + swaps + [near, cross, along]:
        copy.wait_send()


def finish(part, moe, arrays, z_half, near, ctx_count):
    outers = ctx_count // INNER
    blocks, rows, full = part.shape
    count = 2 * rows
    shape = jax.ShapeDtypeStruct
    columns = 3 * D // PLANE
    return comm_call(
        functools.partial(finish_kernel, outers),
        [
            shape((count, D), BF16),
            shape((count, D), F32),
            shape((D, columns), BF16),
            shape((D, 128), BF16),
            shape((PLANE, near.shape[0]) + near.shape[2:], BF16),
            shape((PLANE, 1) + near.shape[2:], BF16),
            shape((z_half.shape[1] - 1,) + z_half.shape[2:], BF16),
        ],
        [ANY] * 2 + [VMEM] * (len(arrays) - 3) + [ANY] * 2 + [VMEM] + [ANY] * 2,
        [VMEM] * 7,
        [
            pltpu.VMEM((D, 2 * full), BF16),
            pltpu.VMEM((2, PLANE, count, D), BF16),
            pltpu.VMEM((z_half.shape[1], outers) + z_half.shape[2:], BF16),
            pltpu.VMEM((z_half.shape[1], outers) + z_half.shape[2:], BF16),
            pltpu.VMEM((2, 2, outers, rows, full), BF16),
            pltpu.VMEM((2, 2, outers, rows, full), BF16),
            pltpu.VMEM((2, outers, rows, full), BF16),
            pltpu.VMEM((outers, 2, rows, full), BF16),
            pltpu.VMEM((2, 2, count, D), BF16),
            pltpu.VMEM((2, 2, count, D), BF16),
            pltpu.VMEM((2, count, D), BF16),
            pltpu.VMEM((count, D), BF16),
            pltpu.VMEM((count, 2 * full), BF16),
            pltpu.VMEM((PLANE, count, columns), BF16),
            pltpu.VMEM((PLANE, count, columns), BF16),
            DMA((4, 2, 2, outers)),
            DMA((4, 2, 2, outers)),
            DMA((4,)),
            DMA((4,)),
            DMA((4, outers)),
            DMA((4, outers)),
            DMA((3,)),
            DMA((3,)),
            DMA((7,)),
            DMA((7,)),
            DMA((z_half.shape[1], outers)),
            DMA((z_half.shape[1], outers)),
            DMA((4 + z_half.shape[1],)),
            DMA((2, 2, outers)),
            DMA((7,)),
            DMA((7,)),
            DMA((7,)),
            DMA((7,)),
        ],
        3,
        "finish",
        vmem=63 * 2**20,
        us=60,
    )(part, moe.reshape(2, 2, 2, count, D), *arrays, z_half, near)


def gate_columns(gates, cols):
    count = gates.shape[-1]
    for j in range(PLANE):
        block = jnp.concatenate([gates[j], jnp.zeros((128 - EXPERTS, count), F32)], axis=0)
        cols[pl.ds(j * count, count), :] = block.T


def expert_step(both, back_act, gate, units):
    gv, uv = both[:, :units], both[:, units:]
    sig = jax.nn.sigmoid(gv)
    silu = gv * sig
    act = silu * uv
    pick = jnp.sum(act * back_act, axis=1, keepdims=True)
    kept = (gate * act).astype(BF16)
    back_act = gate * back_act
    slope = sig * (1.0 + gv * (1.0 - sig))
    low = jnp.concatenate([back_act * uv * slope, back_act * silu], axis=1).astype(BF16)
    return kept, pick, low


def lane_of(cols, lane):
    at = lax.broadcasted_iota(jnp.int32, cols.shape, 1)
    return jnp.sum(jnp.where(at == lane, cols, 0.0), axis=1, keepdims=True)


def opening_kernel(
    outers,
    seg_ref,
    tok_ref,
    wq,
    wk,
    wv,
    wo,
    small,
    cot,
    cos_ref,
    sin_ref,
    route_ref,
    prio_ref,
    expert_in,
    expert_out,
    wqkv_o,
    wo_o,
    small_o,
    q_o,
    hid_o,
    kv_o,
    raw_o,
    total_o,
    mixed_o,
    sum_o,
    gate_o,
    kept_o,
    pick_o,
    z_o,
    za_o,
    part_o,
    kept_units_o,
    grad_o,
    left_o,
    wqkv,
    wout,
    own,
    tok_v,
    cos_v,
    sin_v,
    kv,
    cot_v,
    raw,
    out_w,
    inner_w,
    acc,
    acc_l,
    hid_two,
    gate_send,
    hid,
    gates,
    cot_t,
    backs,
    cols,
    pick_cols,
    staged,
    y_in,
    za_in,
    xs,
    xr,
    fs,
    fr,
    ls,
    zs,
    zr,
    ys,
    yr,
    cs,
    cr,
    hs,
    gs,
    gr,
    gl,
    es,
    ts,
    tr,
    tl,
    gd,
    us,
    ur,
    ul,
    vs,
    vr,
    fas,
    far_r,
):
    at = Place()
    blocks, rows = kv.shape[:2]
    units = out_w.shape[-1]
    experts = at.q * OWN
    sib, unused = at.relative(0, 1, 0)
    partner, j_partner = at.relative(0, 0, 1)
    side, j_side = at.relative(1, 0, 0)
    unused, j_cross = at.relative(1, 0, 1)
    steps = sorted({1, outers - 1})
    far = [(lax.rem(at.outer + r, outers) * INNER + at.inner, at.w) for r in steps]
    expert_loads = {}

    def load_expert(e):
        copy = pltpu.make_async_copy(expert_in.at[experts + e], raw.at[e % 2], es.at[e % 2])
        copy.start()
        expert_loads[e] = copy

    def shape_expert(e):
        expert_loads[e].wait()
        inner_w[:, e * 2 * units : (e + 1) * 2 * units] = raw[e % 2].reshape(D, 2 * units)
        if e + 2 < OWN:
            load_expert(e + 2)

    out_loads = [
        pltpu.make_async_copy(expert_out.at[experts + e], out_w.at[e], es.at[2 + e])
        for e in range(OWN)
    ]
    for copy in out_loads:
        copy.start()
    load_expert(0)
    load_expert(1)
    meet(
        [at.relative(*bits)[0] for bits in XY + [(0, 1, 0)]] + far + [at.beside]
        + ([far_partner(at)] if far_first(outers) else [])
    )

    pieces = [(wk, wqkv, 1024), (wv, wqkv, 1536), (wq, wqkv, 0), (wo, wout, 0)]
    sends, passed, keeps = {}, {}, []

    def give(index):
        src, dst, col = pieces[index]
        depth, width = src.shape
        half = depth // 2
        copy = remote(
            src.at[pl.ds(at.core * half, half), :],
            dst.at[pl.ds(at.w * depth + at.core * half, half), pl.ds(col, width)],
            xs.at[index],
            xr.at[index],
            partner,
        )
        copy.start()
        sends[index] = copy

    def pass_on(index):
        src, dst, col = pieces[index]
        depth, width = src.shape
        half = depth // 2
        sends[index].wait_recv()
        piece = dst.at[pl.ds((1 - at.w) * depth + at.core * half, half), pl.ds(col, width)]
        copy = remote(piece, piece, fs.at[index], fr.at[index], sib)
        copy.start()
        passed[index] = copy

    wide = small.shape[1]
    mine = small_o.at[:, pl.ds(at.w * wide, wide)]
    gains = remote(small, mine, xs.at[4], xr.at[4], partner)
    gains.start()
    give(0)
    give(1)
    cot_sib = remote(cot, cot_v.at[at.j], gs.at[0], gr.at[0], sib)
    cot_sib.start()
    cot_side = remote(cot, cot_v.at[at.j], gs.at[1], gr.at[1], side)
    cot_side.start()
    cot_keep = pltpu.make_async_copy(cot, cot_v.at[at.j], gl)
    cot_keep.start()
    for index, (src, dst, col) in enumerate(pieces):
        depth, width = src.shape
        keep = pltpu.make_async_copy(
            src, dst.at[pl.ds(at.w * depth, depth), pl.ds(col, width)], ls.at[index]
        )
        keep.start()
        keeps.append(keep)
    loads = [
        pltpu.make_async_copy(src, dst, hs.at[4 + index])
        for index, (src, dst) in enumerate(
            ((tok_ref, tok_v), (cos_ref, cos_v), (sin_ref, sin_v), (small, mine))
        )
    ]
    for copy in loads:
        copy.start()
    for copy in loads:
        copy.wait()
    tok = tok_v[...].astype(F32)
    normed = tok * lax.rsqrt(jnp.mean(tok * tok, axis=1, keepdims=True) + EPS)
    gains.wait_recv()
    hidden = (normed * small_o[pl.ds(EXPERTS, 1), :].astype(F32)).astype(BF16)
    hid_o[...] = hidden
    cosine, sine = cos_v[...], sin_v[...]

    pass_on(0)
    pass_on(1)
    cot_across = remote(cot, cot_v.at[at.j], gs.at[2], gr.at[2], partner)
    cot_across.start()
    keeps[0].wait()
    keeps[1].wait()
    passed[0].wait_recv()
    key = dot_nn(hidden, wqkv[:, 1024:1536])
    key = turn(key, cosine, sine).astype(BF16)
    passed[1].wait_recv()
    value = dot_nn(hidden, wqkv[:, 1536:]).astype(BF16)
    width = key.shape[1]
    for half in range(2):
        own[half, :, :width] = key[half * rows : (half + 1) * rows]
        own[half, :, width:] = value[half * rows : (half + 1) * rows]

    def block_of(half, ctx):
        return kv.at[ctx] if half == 0 else kv.at[blocks - 1 - ctx]

    last = outers - 1
    hops = [(0, 0, 0)] + [
        (step, sign, step if sign < 0 else last + step)
        for step in range(1, outers)
        for sign in (-1, 1)
    ]

    def source(step, sign):
        return at.outer + sign * step

    def exists(step, sign):
        place = source(step, sign)
        return (place >= 0) & (place <= last)

    def block_from(half, step, sign, inner):
        place = lax.rem(source(step, sign) + outers, outers)
        return block_of(half, place * INNER + inner)

    below = (lax.rem(at.outer + last, outers) * INNER + at.inner, at.w)
    above = (lax.rem(at.outer + 1, outers) * INNER + at.inner, at.w)
    inner_side = at.inner + 2 - 4 * at.y

    def z_copy(half, slot, step, sign):
        src = own.at[half] if step == 0 else block_from(half, step, sign, at.inner)
        dst = block_from(half, step, sign, at.inner)
        slot_there = step + 1 if sign < 0 else last + step + 1
        return remote(
            src,
            dst,
            zs.at[half, slot_there],
            zr.at[half, slot_there],
            above if sign < 0 else below,
        )

    def y_copy(half, slot, step, sign):
        src = own.at[half] if step == 0 else block_from(half, step, sign, at.inner)
        dst = block_from(half, step, sign, at.inner)
        return remote(src, dst, ys.at[half, slot], yr.at[half, slot], at.beside)

    def c_copy(half, slot, step, sign, inner, base):
        src = (
            own.at[half]
            if step == 0 and base == 0
            else block_from(half, step, sign, inner)
        )
        dst = block_from(half, step, sign, inner)
        return remote(src, dst, cs.at[half, base + slot], cr.at[half, base + slot], sib)

    spots = 2 * outers - 1

    def spread_from(step, sign, slot, halves=(0, 1)):
        for half in halves:
            if step == 0:
                for way in (-1, 1):

                    @pl.when((at.outer < last) if way < 0 else (at.outer > 0))
                    def _():
                        z_copy(half, 0, 0, way).start()

            elif step < last:

                @pl.when((at.outer < last) if sign < 0 else (at.outer > 0))
                def _():
                    z_copy(half, slot, step, sign).start()

            y_copy(half, slot, step, sign).start()
            c_copy(half, slot, step, sign, at.inner, 0).start()

    spread_from(0, 0, 0)
    for half in range(2):
        keep = pltpu.make_async_copy(own.at[half], block_of(half, at.c), hs.at[half])
        keep.start()
        keeps.append(keep)

    def y_arrived(step, sign, slot):
        for half in range(2):
            y_copy(half, slot, step, sign).wait_recv()
            c_copy(half, slot, step, sign, inner_side, spots).start()

    def z_arrived(want):
        for step, sign, slot in hops[1:]:
            if step == want:

                @pl.when(exists(step, sign))
                def _():
                    for half in range(2):
                        z_copy(half, slot, step - 1, sign).wait_recv()
                        spread_from(step, sign, slot, (half,))

    def sides_arrived(want):
        for step, sign, slot in hops[1:]:
            if step == want:

                @pl.when(exists(step, sign))
                def _():
                    y_arrived(step, sign, slot)

    shape_expert(0)
    cot_across.wait_recv()
    give(2)
    cot_on = []

    def cot_pass(slot, j_from, device):
        block = cot_v.at[j_from]
        copy = remote(block, block, gs.at[slot], gr.at[slot], device)
        copy.start()
        cot_on.append(copy)

    cot_pass(3, j_partner, side)
    cot_pass(4, j_partner, sib)
    cot_side.wait_recv()
    cot_pass(5, j_side, sib)
    z_arrived(1)
    y_arrived(0, 0, 0)
    shape_expert(1)
    pass_on(2)
    give(3)
    shape_expert(2)
    if outers > 2:
        z_arrived(2)
    keeps[2].wait()
    passed[2].wait_recv()
    q_o[...] = turn(dot_nn(hidden, wqkv[:, :1024]), cosine, sine).astype(BF16)
    store = pltpu.make_async_copy(wqkv, wqkv_o, hs.at[2])
    store.start()
    shape_expert(3)
    sides_arrived(1)
    for step in range(3, outers):
        z_arrived(step)
        sides_arrived(step - 1)
    if outers > 2:
        sides_arrived(last)
    pass_on(3)
    cot_on[0].wait_recv()
    cot_pass(6, j_cross, sib)
    keeps[3].wait()
    passed[3].wait_recv()
    store_out = pltpu.make_async_copy(wout, wo_o, hs.at[3])
    store_out.start()
    def sibling_brought(step, sign, slot):
        for half in range(2):
            c_copy(half, slot, step, sign, at.inner, 0).wait_recv()
            c_copy(half, slot, step, sign, inner_side, spots).wait_recv()

    sibling_brought(0, 0, 0)
    for step, sign, slot in hops[1:]:

        @pl.when(exists(step, sign))
        def _():
            sibling_brought(step, sign, slot)

    for keep in keeps[4:]:
        keep.wait()
    store_kv = pltpu.make_async_copy(kv, kv_o, hs.at[4])
    store_kv.start()
    attend_rows(
        doc_starts(seg_ref[...]),
        q_o,
        kv,
        tok_v,
        wout,
        small_o,
        route_ref,
        prio_ref,
        raw_o,
        total_o,
        mixed_o,
        sum_o,
        hid_two,
        gate_o,
        kept_o,
        gate_send,
        acc,
        acc_l,
    )

    pairs = [(hid_two, hid), (gate_send, gates)]
    copies = gather_start(at, pairs, ts, tr, tl)
    for copy in [cot_sib] + cot_on[1:]:
        copy.wait_recv()
    cot_keep.wait()
    for copy in out_loads:
        copy.wait()
    tokens = cot_v.shape[0] * cot_v.shape[1]
    cot_rows = cot_v[...].reshape(tokens, D)
    cot_t[...] = cot_rows.T
    for e in range(OWN):
        backs[:, e * units : (e + 1) * units] = (RES_MULT * dot_nn(cot_rows, out_w[e])).astype(BF16)
    gather_wait(copies, gather_pass(at, pairs, copies, ts, tr))
    gate_columns(gates, cols)
    left_pairs = [(hid_o, left_o.at[0]), (mixed_o, left_o.at[1])]
    left_copies = gather_start(at, left_pairs, us, ur, ul)
    store_out.wait()
    passed[3].wait_send()
    hid_t = wout
    hid_t[...] = hid[...].reshape(tokens, D).T
    late = [slice(None)] * FIRST
    if far_first(outers):
        late[0] = pl.ds(units, 2 * units)
    y_sends = [
        remote(
            staged.at[e, :, :, 1 - at.y, :, late[e]],
            y_in.at[e, :, :, :, late[e]],
            vs.at[e],
            vr.at[e],
            at.beside,
        )
        for e in range(FIRST)
    ]
    upper = at.outer // 2
    if far_first(outers):
        far_send = remote(
            staged.at[0, 1 - upper, :, :, :, pl.ds(0, units)], za_in, fas, far_r, far_partner(at)
        )
    at_lane = lax.broadcasted_iota(jnp.int32, cols.shape, 1)
    pick_cols[...] = jnp.zeros(pick_cols.shape, F32)
    store.wait()
    for index in range(3):
        passed[index].wait_send()
    low_all = wqkv

    def expert(e, carry):
        wide = pl.ds(pl.multiple_of(e * 2 * units, 2 * units), 2 * units)
        tall = pl.ds(pl.multiple_of(e * units, units), units)
        many = tokens // PIECES
        groups = PLANE // PIECES
        for piece in range(PIECES):
            here = slice(piece * many, (piece + 1) * many)
            rows_in = hid[piece * groups : (piece + 1) * groups].reshape(many, D)
            both = dot_nn(rows_in, inner_w[:, wide])
            kept, pick, low = expert_step(
                both, backs[here, tall].astype(F32), lane_of(cols[here, :], experts + e), units
            )
            backs[here, tall] = kept
            low_all[here, wide] = low
            pick_cols[here, :] = jnp.where(at_lane[here] == e, pick, pick_cols[here, :])

        shape = staged.shape[1:5]
        staged[e, :, :, :, :, : 2 * units] = (
            dot_nn(hid_t[...], low_all[:, wide]).astype(BF16).reshape(*shape, 2 * units)
        )
        staged[e, :, :, :, :, 2 * units :] = (
            (RES_MULT * dot_nn(cot_t[...], backs[:, tall])).astype(BF16).reshape(*shape, units)
        )
        for now in range(OWN):

            @pl.when(e == now)
            def _():
                if now < FIRST:
                    y_sends[now].start()
                    if now == 0 and far_first(outers):
                        far_send.start()
                else:
                    pltpu.make_async_copy(
                        staged.at[now], grad_o.at[now - FIRST], gd.at[now - FIRST]
                    ).start()

        return carry

    lax.fori_loop(0, OWN, expert, 0)
    left_passed = gather_pass(at, left_pairs, left_copies, us, ur)
    count = hid.shape[1]
    for j in range(PLANE):
        pick_o[j] = pick_cols[j * count : (j + 1) * count, :].T[:8]
    store_kept = pltpu.make_async_copy(backs, kept_units_o, hs.at[5])
    store_kept.start()
    for j in range(0, PLANE, 4):
        here = slice(j * count, (j + 4) * count)
        rows_out = dot_nt(low_all[here, :], inner_w[...]).astype(BF16)
        hid[j : j + 4] = rows_out.reshape(4, count, D)
    store_part = pltpu.make_async_copy(hid, part_o, hs.at[6])
    store_part.start()

    def settle(step, sign, slot):
        for half in range(2):
            if step == 0:
                for way in (-1, 1):

                    @pl.when((at.outer < last) if way < 0 else (at.outer > 0))
                    def _():
                        z_copy(half, 0, 0, way).wait_send()

            elif step < last:

                @pl.when((at.outer < last) if sign < 0 else (at.outer > 0))
                def _():
                    z_copy(half, slot, step, sign).wait_send()

            y_copy(half, slot, step, sign).wait_send()
            c_copy(half, slot, step, sign, at.inner, 0).wait_send()
            c_copy(half, slot, step, sign, inner_side, spots).wait_send()

    settle(0, 0, 0)
    for step, sign, slot in hops[1:]:

        @pl.when(exists(step, sign))
        def _():
            settle(step, sign, slot)

    for copy in sends.values():
        copy.wait_send()
    for copy in [gains, cot_sib, cot_side, cot_across] + cot_on:
        copy.wait_send()
    for e in range(FIRST):
        y_sends[e].wait()
        total = staged[e, :, :, at.y, :, late[e]].astype(F32)
        total = total + y_in[e, :, :, :, late[e]].astype(F32)
        z_o[:, e, :, :, late[e]] = total.astype(BF16)
    if far_first(outers):
        far_send.wait()
        total = staged[0, upper, :, :, :, :units].astype(F32) + za_in[...].astype(F32)
        za_o[...] = total.astype(BF16)
    gather_wait(left_copies, left_passed)
    for copy in [store_kv, store_kept, store_part]:
        copy.wait()
    for e in range(FIRST, OWN):
        pltpu.make_async_copy(staged.at[e], grad_o.at[e - FIRST], gd.at[e - FIRST]).wait()


def opening(
    starts, tokens, wq, wk, wv, wo, small, cot, cosine, sine, routes, priority, expert_in, expert_out, ctx_count
):
    outers = ctx_count // INNER
    shape = jax.ShapeDtypeStruct
    count = tokens.shape[0]
    rows = count // 2
    width = wk.shape[1] + wv.shape[1]
    heads = wq.shape[1]
    wide = heads + width
    units = expert_out.shape[-1]
    many = PLANE * count
    blocks = 2 * ctx_count
    z_rows = D // (2 * outers)
    vm = pltpu.VMEM
    return comm_call(
        functools.partial(opening_kernel, outers),
        [
            shape((D, wide), BF16),
            shape((D, D), BF16),
            shape((small.shape[0], D), BF16),
            shape((count, heads), BF16),
            shape((count, D), BF16),
            shape((blocks, rows, width), BF16),
            shape((count, heads), F32),
            shape((count, heads), F32),
            shape((count, heads), BF16),
            shape((count, D), F32),
            shape((EXPERTS, count), F32),
            shape((EXPERTS, count), F32),
            shape((PLANE, 8, count), F32),
            shape((outers // 2, FIRST, 2, z_rows, 3 * units), BF16),
            shape((2, 2, z_rows, units), BF16),
            shape((PLANE, count, D), BF16),
            shape((many, OWN * units), BF16),
            shape((OWN - FIRST, outers // 2, 2, 2, z_rows, 3 * units), BF16),
            shape((2, PLANE, count, D), BF16),
        ],
        [VMEM] + [ANY] * 9 + [VMEM] * 2 + [ANY] * 2,
        [ANY] * 2 + [VMEM] * 3 + [ANY] + [VMEM] * 9 + [ANY] * 4,
        [
            vm((D, wide), BF16),
            vm((D, D), BF16),
            vm((2, rows, width), BF16),
            vm((count, D), BF16),
            vm(cosine.shape, F32),
            vm(sine.shape, F32),
            vm((blocks, rows, width), BF16),
            vm((PLANE, count, D), BF16),
            vm((2, D, 2, units), BF16),
            vm((OWN, D, units), BF16),
            vm((D, OWN * 2 * units), BF16),
            vm((PAIRS, 2 * count, 128), F32),
            vm((PAIRS, 2 * count, 128), F32),
            vm((count, D), BF16),
            vm((EXPERTS, count), F32),
            vm((PLANE, count, D), BF16),
            vm((PLANE, EXPERTS, count), F32),
            vm((D, many), BF16),
            vm((many, OWN * units), BF16),
            vm((many, 128), F32),
            vm((many, 128), F32),
            vm((OWN, outers // 2, 2, 2, z_rows, 3 * units), BF16),
            vm((FIRST, outers // 2, 2, z_rows, 3 * units), BF16),
            vm((2, 2, z_rows, units), BF16),
            DMA((5,)),
            DMA((5,)),
            DMA((4,)),
            DMA((4,)),
            DMA((4,)),
        ]
        + [DMA((2, 2 * outers))] * 4
        + [DMA((2, 4 * outers))] * 2
        + [DMA((8,)), DMA((7,)), DMA((7,)), DMA]
        + [DMA((2 + OWN,)), DMA((2, 7)), DMA((2, 7)), DMA((2,)), DMA((2,))]
        + [DMA((2, 7)), DMA((2, 7)), DMA((2,)), DMA((FIRST,)), DMA((FIRST,)), DMA, DMA],
        1,
        "opening",
        vmem=64 * 2**20,
        us=100,
    )(starts, tokens, wq, wk, wv, wo, small, cot, cosine, sine, routes, priority, expert_in, expert_out)


def turning_kernel(
    outers,
    seg_ref,
    z_ref,
    za_ref,
    grad_in,
    part_in,
    pick_send,
    kept_in,
    expert_out,
    gate_ref,
    kept_ref,
    small_ref,
    sum_in,
    cot_in,
    wo_in,
    raw_in,
    total_in,
    q_in,
    kv_in,
    cos_ref,
    sin_ref,
    dy_ref,
    da_ref,
    dq_ref,
    rows_ref,
    moe_o,
    near_o,
    z_o,
    dkv_ref,
    sum_ref,
    cot_ref,
    raw_ref,
    total_ref,
    q_ref,
    part,
    kept_all,
    out_w,
    wout,
    kv,
    near,
    far_in,
    picks_all,
    q_four,
    n_four,
    d_rows,
    dq_acc,
    kv_acc,
    kv_out,
    z_sums,
    z_in,
    y_own,
    y_in,
    za_own,
    za_in,
    ls,
    ss,
    sr,
    xs,
    xr,
    ps,
    pr,
    vs,
    vr,
    us,
    ur,
    ks,
    rs,
    zas,
    zar,
):
    at = Place()
    count = q_ref.shape[0]
    rows = count // 2
    width = PAIRS * 128
    keys = kv.shape[0] * rows
    units = out_w.shape[-1]
    experts = at.q * OWN
    loads = [
        pltpu.make_async_copy(src, dst, ls.at[index])
        for index, (src, dst) in enumerate(
            ((part_in, part), (kept_in, kept_all), (wo_in, wout), (kv_in, kv))
        )
    ]
    weights = [
        pltpu.make_async_copy(expert_out.at[experts + e], out_w.at[e], ls.at[4 + e])
        for e in range(OWN)
    ]
    for copy in loads + weights:
        copy.start()
    z_loads = [
        pltpu.make_async_copy(z_ref.at[:, e], z_sums.at[e, pl.ds(0, outers // 2)], rs.at[5 + e])
        for e in range(FIRST)
    ]
    za_load = pltpu.make_async_copy(za_ref.at[:, at.y], za_own, rs.at[5 + FIRST])
    for copy in z_loads + [za_load]:
        copy.start()
    late = [slice(None)] * FIRST
    if far_first(outers):
        late[0] = pl.ds(units, 2 * units)
    rest = [
        Halving(at, outers, z_sums.at[e], z_in.at[e], vs.at[e], vr.at[e], late[e])
        for e in range(FIRST)
    ]
    own_rows = []
    for e in range(OWN - FIRST):
        copy = pltpu.make_async_copy(
            grad_in.at[e, :, :, at.y], y_own.at[e], ls.at[4 + OWN + e]
        )
        copy.start()
        own_rows.append(copy)
    row_loads = [
        pltpu.make_async_copy(src, dst, rs.at[index])
        for index, (src, dst) in enumerate(
            (
                (sum_in, sum_ref),
                (cot_in, cot_ref),
                (raw_in, raw_ref),
                (total_in, total_ref),
                (q_in, q_ref),
            )
        )
    ]
    for copy in row_loads:
        copy.start()
    starts = doc_starts(seg_ref[...])
    meet(
        [at.relative(*bits)[0] for bits in OTHERS]
        + [at.beside]
        + [rest[0].device(bit) for bit in rest[0].bits]
    )
    for copy in z_loads:
        copy.wait()
    if outers > 2:
        for halving in rest:
            halving.start(0)
    if far_first(outers):
        za_send = remote(za_ref.at[:, 1 - at.y], za_in, zas, zar, at.beside)
        za_send.start()
    sib, unused = at.relative(0, 1, 0)
    loads[0].wait()
    first = remote(part.at[:, 1 - at.core], near, ss, sr, sib)
    first.start()
    y_sends = []
    for e in range(OWN - FIRST):
        copy = remote(grad_in.at[e, :, :, 1 - at.y], y_in.at[e], us.at[e], ur.at[e], at.beside)
        copy.start()
        y_sends.append(copy)
    small_copies = []
    for slot, bits in enumerate(OTHERS):
        device, j_to = at.relative(*bits)
        copy = remote(pick_send.at[j_to], picks_all.at[at.j], ps.at[slot], pr.at[slot], device)
        copy.start()
        small_copies.append(copy)
    picks_all[at.j] = pick_send[at.j]
    first.wait_recv()
    for y in range(2):
        for w in range(2):
            total = part[y, at.core, w].astype(F32) + near[y, w].astype(F32)
            near[y, w] = total.astype(BF16)
    second = []
    for slot, (dy, dc, dw) in enumerate(XY):
        device, unused = at.relative(dy, dc, dw)
        z = at.z + dy * (1 - 2 * at.z)
        w = at.w + dw * (1 - 2 * at.w)
        copy = remote(near.at[z, w], far_in.at[slot], xs.at[slot], xr.at[slot], device)
        copy.start()
        second.append(copy)

    loads[1].wait()
    for copy in weights + row_loads:
        copy.wait()

    def moe_rows(j, carry):
        here = pl.ds(pl.multiple_of(j * count, count), count)
        total = dot_nt(kept_all[here, :units], out_w[0])
        for e in range(1, OWN):
            total = total + dot_nt(kept_all[here, e * units : (e + 1) * units], out_w[e])
        moe_o[j] = total.astype(BF16)
        return carry

    lax.fori_loop(0, PLANE, moe_rows, 0)
    hidden_sum = near[at.z, at.w].astype(F32)
    for slot in range(3):
        second[slot].wait_recv()
        hidden_sum = hidden_sum + far_in[slot].astype(F32)
    for copy in [first] + second:
        copy.wait_send()
    small = small_ref[...]
    gain_two = small[EXPERTS + 1 : EXPERTS + 2].astype(F32)
    for copy in small_copies:
        copy.wait()
    parts = []
    for i in range(INNER):
        parts.append(picks_all[2 * i, pl.ds(0, OWN), :] + picks_all[2 * i + 1, pl.ds(0, OWN), :])
    gate = gate_ref[...]
    gate_grad = kept_ref[...] * jnp.concatenate(parts, axis=0)
    logit_grad = gate * (gate_grad - jnp.sum(gate * gate_grad, axis=0, keepdims=True))
    logit_grad = jnp.concatenate(
        [logit_grad, jnp.zeros((small.shape[0] - EXPERTS, count), F32)], axis=0
    ).astype(BF16)
    hidden_grad = hidden_sum + dot_tn(logit_grad, small)
    first_sum = sum_ref[...]
    scale = lax.rsqrt(jnp.mean(first_sum * first_sum, axis=1, keepdims=True) + EPS)
    normed = first_sum * scale
    hidden = (normed * gain_two).astype(BF16)
    router_rows = dot_nn(logit_grad, hidden)
    rows_ref[...] = router_rows
    rows_ref[pl.ds(EXPERTS + 1, 1), :] = jnp.sum(hidden_grad * normed, axis=0, keepdims=True)
    normed_grad = hidden_grad * gain_two
    first_grad = cot_ref[...].astype(F32) + scale * (
        normed_grad - normed * jnp.mean(normed_grad * normed, axis=1, keepdims=True)
    )
    dy_ref[...] = first_grad
    attn_grad = (RES_MULT * first_grad).astype(BF16)
    da_ref[...] = attn_grad
    loads[2].wait()
    mixed_grad = dot_nt(attn_grad, wout[...]).astype(BF16).astype(F32)
    total = total_ref[...]
    numer = mixed_grad / total
    lost = mixed_grad * raw_ref[...] / total
    for half in range(2):
        here = slice(half * rows, (half + 1) * rows)
        for pair in range(PAIRS):
            cols = slice(pair * 256, (pair + 1) * 256)
            slot = half * PAIRS + pair
            q_four[slot] = spread(q_ref[here, cols].astype(F32) * ATT_MULT).astype(BF16)
            n_four[slot] = spread(numer[here, cols]).astype(BF16)
            d_rows[slot] = -jnp.sum(spread(lost[here, cols]).T, axis=0, keepdims=True)
    dq_acc[...] = jnp.zeros_like(dq_acc)
    loads[3].wait()

    def kv_store(chunk):
        many = CHUNK // rows
        return pltpu.make_async_copy(
            kv_out.at[chunk % 2], dkv_ref.at[pl.ds(chunk * many, many)], ks.at[chunk % 2]
        )

    def step(chunk, carry):
        at_row = pl.multiple_of(chunk * CHUNK, CHUNK)
        kv_acc[...] = jnp.zeros_like(kv_acc)
        key_pos = at_row + lax.broadcasted_iota(jnp.int32, (CHUNK, 1), 0)
        for half in range(2):
            base, chunks = half_span(half, rows, keys)

            @pl.when(chunk < chunks)
            def _():
                place = base + lax.broadcasted_iota(jnp.int32, (1, 4 * rows), 1) % rows
                first = reach(starts, place)
                bias = jnp.where((key_pos >= first) & (key_pos <= place), 0.0, NEVER)
                for pair in range(PAIRS):
                    slot = half * PAIRS + pair
                    key = key_block(kv, chunk, rows, pair * 128)
                    value = key_block(kv, chunk, rows, width + pair * 128)
                    e = jnp.exp(dot_nt(key, q_four[slot]) + bias)
                    through = dot_nt(value, n_four[slot])
                    dz = (e * (through + d_rows[slot])).astype(BF16)
                    kv_acc[:, pl.ds(pair * 128, 128)] += dot_nn(dz, q_four[slot])
                    kv_acc[:, pl.ds(width + pair * 128, 128)] += dot_nn(e.astype(BF16), n_four[slot])
                    dq_acc[slot] += dot_tn(dz, key)

        many = CHUNK // rows

        @pl.when(chunk >= 2)
        def _():
            kv_store(chunk - 2).wait()

        kv_out[chunk % 2] = kv_acc[...].astype(BF16).reshape(many, rows, 2 * width)
        kv_store(chunk).start()
        return carry

    lax.fori_loop(0, keys // CHUNK, step, 0)
    cosine = cos_ref[...]
    sine = -sin_ref[...]
    for half in range(2):
        here = slice(half * rows, (half + 1) * rows)
        for pair in range(PAIRS):
            block = ATT_MULT * unspread(dq_acc[half * PAIRS + pair])
            dq_ref[here, pair * 256 : (pair + 1) * 256] = turn(
                block, cosine[here], sine[here]
            ).astype(BF16)
    for chunk in range(keys // CHUNK - 2, keys // CHUNK):
        kv_store(chunk).wait()
    for e in range(FIRST):
        near_o[e, :, :, late[e]] = rest[e].finish()
    za_load.wait()
    if far_first(outers):
        za_send.wait()
        total = za_own[...].astype(F32) + za_in[...].astype(F32)
        near_o[0, :, :, :units] = total.astype(BF16)
    for copy in own_rows:
        copy.wait()
    for e in range(OWN - FIRST):
        y_sends[e].wait()
        total = y_own[e].astype(F32) + y_in[e].astype(F32)
        z_o[:, e] = total.astype(BF16)


def turning(
    outers, segments, z_first, z_far, grads, part, picks, kept_units, expert_out, gate, kept, small, first_sum, cot, output_w, raw, total, queries, kv_all, cosine, sine
):
    shape = jax.ShapeDtypeStruct
    count, width = queries.shape
    units = expert_out.shape[-1]
    vm = pltpu.VMEM
    return comm_call(
        functools.partial(turning_kernel, outers),
        [
            shape((count, D), F32),
            shape((count, D), BF16),
            shape((count, width), BF16),
            shape((32, D), F32),
            shape((PLANE, count, D), BF16),
            shape(z_first.shape[1:], BF16),
            shape((outers // 2, OWN - FIRST) + z_first.shape[2:], BF16),
            shape(kv_all.shape, BF16),
        ],
        [VMEM] + [ANY] * 4 + [VMEM] + [ANY] * 2 + [VMEM] * 3 + [ANY] * 7 + [VMEM] * 2,
        [VMEM] * 7 + [ANY],
        [
            vm((count, D), F32),
            vm((count, D), BF16),
            vm((count, width), F32),
            vm((count, width), F32),
            vm((count, width), BF16),
            vm((2, 2, 2, count, D), BF16),
            vm(kept_units.shape, BF16),
            vm((OWN, D, units), BF16),
            vm((D, D), BF16),
            vm(kv_all.shape, BF16),
            vm((2, 2, count, D), BF16),
            vm((3, count, D), BF16),
            vm((PLANE, 8, count), F32),
            vm((2 * PAIRS, 2 * count, 128), BF16),
            vm((2 * PAIRS, 2 * count, 128), BF16),
            vm((2 * PAIRS, 1, 2 * count), F32),
            vm((2 * PAIRS, 2 * count, 128), F32),
            vm((CHUNK, 2 * PAIRS * 128), F32),
            vm((2, CHUNK // (count // 2), count // 2, 2 * PAIRS * 128), BF16),
            vm((FIRST, outers) + z_first.shape[2:], BF16),
            vm((FIRST, outers) + z_first.shape[2:], BF16),
            vm((OWN - FIRST, outers // 2) + z_first.shape[2:], BF16),
            vm((OWN - FIRST, outers // 2) + z_first.shape[2:], BF16),
            vm(z_far.shape[:1] + z_far.shape[2:], BF16),
            vm(z_far.shape[:1] + z_far.shape[2:], BF16),
            DMA((4 + OWN + OWN - FIRST,)),
            DMA,
            DMA,
            DMA((3,)),
            DMA((3,)),
            DMA((7,)),
            DMA((7,)),
            DMA((FIRST, outers)),
            DMA((FIRST, outers)),
            DMA((OWN - FIRST,)),
            DMA((OWN - FIRST,)),
            DMA((2,)),
            DMA((6 + FIRST,)),
            DMA,
            DMA,
        ],
        5,
        "turning",
        vmem=62 * 2**20,
        us=35,
    )(
        segments,
        z_first,
        z_far,
        grads,
        part.reshape(2, 2, 2, count, D),
        picks,
        kept_units,
        expert_out,
        gate,
        kept,
        small,
        first_sum,
        cot,
        output_w,
        raw,
        total,
        queries,
        kv_all,
        cosine,
        sine,
    )


def assemble_kernel(outers, counts, *refs):
    size = 2 + len(counts)
    sources, refs = refs[:size], refs[size:]
    wq, wk, wv, wo, router, gain_one, gain_two, inner, outer = refs[:9]
    held, sems = refs[9 : 9 + size], refs[9 + size]
    loads = [
        pltpu.make_async_copy(sources[k], held[k], sems.at[k]) for k in range(size)
    ]
    for copy in loads:
        copy.start()
    attn_in, small_in = held[:2]
    for copy in loads:
        copy.wait()
    experts = [(near, k) for near, many in zip(held[2:], counts) for k in range(many)]
    qkv_cols = wq.shape[1] * 2 // PLANE
    devices = outers * PLANE
    for j in range(PLANE):
        z, core, w = j // 4, (j // 2) % 2, j % 2
        total = 0.0
        for above in range(outers // 2):
            for y in range(2):
                source = (((above * 2 + z) * 2 + y) * 2 + core) * 2 + w
                total = total + attn_in[source].astype(F32)
        col = j * qkv_cols
        ref, base = (wq, 0) if col < 1024 else (wk, 1024) if col < 1536 else (wv, 1536)
        ref[:, col - base : col - base + qkv_cols] = total[:, :qkv_cols]
        wo[:, j * (D // PLANE) : (j + 1) * (D // PLANE)] = total[:, qkv_cols:]
    total = small_in[0].astype(F32)
    for i in range(1, devices):
        total = total + small_in[i].astype(F32)
    turned = total.T
    router[...] = turned[:EXPERTS]
    gain_one[...] = turned[EXPERTS : EXPERTS + 1]
    gain_two[...] = turned[EXPERTS + 1 : EXPERTS + 2]
    rows = wq.shape[0]
    units = outer.shape[-1] // 2
    for j in range(PLANE):
        cols = slice((j % 2) * units, (j % 2 + 1) * units)
        for k in range(OWN):
            e = (j // 2) * OWN + k
            near, at = experts[k]
            block = near[j, at].astype(F32)
            inner[e, :, :, cols] = block[:, : 2 * units].reshape(rows, 2, units)
            outer[e, :, cols] = block[:, 2 * units :]


def assemble(attn_in, small_in, nears, outers):
    rows = attn_in.shape[1]
    units = nears[0].shape[-1] // 3
    sources = [attn_in, small_in] + nears
    shape = jax.ShapeDtypeStruct
    outs = [
        shape((rows, 1024), F32),
        shape((rows, 512), F32),
        shape((rows, 512), F32),
        shape((rows, D), F32),
        shape((EXPERTS, rows), F32),
        shape((1, rows), F32),
        shape((1, rows), F32),
        shape((EXPERTS, rows, 2, 2 * units), F32),
        shape((EXPERTS, rows, 2 * units), F32),
    ]
    return pl.pallas_call(
        functools.partial(assemble_kernel, outers, [near.shape[1] for near in nears]),
        out_shape=outs,
        in_specs=[ANY] * len(sources),
        out_specs=[VMEM] * 9,
        scratch_shapes=[pltpu.VMEM(a.shape, a.dtype) for a in sources] + [DMA((len(sources),))],
        compiler_params=pltpu.CompilerParams(vmem_limit_bytes=60 * 2**20),
        name="assemble",
    )(*sources)


def body(
    tokens,
    w_query,
    w_key,
    w_value,
    w_output,
    attn_gain,
    w_router,
    expert_in,
    expert_out,
    moe_gain,
    segments,
    routes,
    priority,
    cotangent,
):
    ctx_count = lax.axis_size("ctx")
    ctx_index = lax.axis_index("ctx")
    devices = ctx_count * 2
    outers = ctx_count // INNER
    owner_rows = D // devices
    block_rows = tokens.shape[2]
    half_rows = block_rows * ctx_count
    tok_count = 2 * block_rows
    f32 = jnp.float32
    bf16 = jnp.bfloat16

    small = jnp.concatenate(
        [w_router.T, attn_gain[None], moe_gain[None], jnp.zeros((14, w_router.shape[0]), bf16)]
    )
    cot_own = cotangent.reshape(tok_count, D)
    block_total = 2 * ctx_count
    block_ids = jnp.stack([ctx_index, block_total - 1 - ctx_index])
    query_pos = block_ids[:, None] * block_rows + jnp.arange(block_rows, dtype=jnp.int32)[None, :]
    flat_pos = query_pos.reshape(tok_count)
    frequency = jnp.exp(
        -jnp.log(jnp.float32(THETA))
        * jnp.arange(HEAD_DIM // 2, dtype=jnp.float32)
        * (2.0 / HEAD_DIM)
    )
    angles = flat_pos.astype(f32)[:, None] * frequency[None, :]
    cosine, sine = jnp.cos(angles), jnp.sin(angles)
    cosine = jnp.concatenate([cosine] * 4, axis=1)
    sine = jnp.concatenate([-sine, sine] * 2, axis=1)
    token_low = tokens.reshape(tok_count, D)
    (
        qkv_w,
        output_w,
        small_all,
        queries,
        hidden_one,
        kv_all,
        attn_raw,
        attn_total,
        mixed,
        first_sum,
        gate,
        kept,
        picks,
        first_half,
        first_far,
        part,
        kept_units,
        expert_grads,
        left,
    ) = opening(
        segments,
        token_low,
        w_query,
        w_key,
        w_value,
        w_output,
        small,
        cot_own,
        cosine,
        sine,
        routes[0].transpose(0, 2, 1),
        priority[0].transpose(0, 2, 1),
        expert_in,
        expert_out,
        ctx_count,
    )
    (
        first_grad,
        attn_grad,
        query_lin_grad,
        small_rows,
        moe_part,
        near_one,
        second_half,
        kv_terms,
    ) = turning(
        outers,
        segments,
        first_half,
        first_far,
        expert_grads,
        part,
        picks,
        kept_units,
        expert_out,
        gate,
        kept,
        small_all,
        first_sum,
        cot_own,
        output_w,
        attn_raw,
        attn_total,
        queries,
        kv_all,
        cosine,
        sine,
    )
    output, token_grad, attn_part, small_part, near_first, near_next, near = finish(
        kv_terms,
        moe_part,
        [
            first_sum,
            query_lin_grad,
            attn_grad,
            first_grad,
            token_low,
            small_all,
            cosine,
            sine,
            qkv_w,
            left,
            small_rows,
        ],
        second_half,
        near_one.reshape(FIRST, PLANE, owner_rows, -1),
        ctx_count,
    )
    attn_in, small_in, near_last = owners(
        [attn_part, small_part],
        [near.reshape(-1, PLANE, owner_rows, near.shape[-1])],
        devices,
        7,
        "owners",
    )
    (
        query_sum,
        key_sum,
        value_sum,
        output_sum,
        router_sum,
        gain_one_sum,
        gain_two_sum,
        inner_sum,
        outer_sum,
    ) = assemble(attn_in, small_in, [near_first, near_next, near_last], outers)
    return (
        output.reshape(tokens.shape),
        token_grad.reshape(tokens.shape),
        query_sum,
        key_sum,
        value_sum,
        output_sum,
        gain_one_sum[0],
        router_sum.T,
        inner_sum,
        outer_sum,
        gain_two_sum[0],
    )


def solution(mesh):
    placed = (
        P("wsh", None, "ctx", None),
        P("wsh", None),
        P("wsh", None),
        P("wsh", None),
        P("wsh", None),
        P("wsh"),
        P("wsh", None),
        P(None, None, None, "wsh"),
        P(None, None, "wsh"),
        P("wsh"),
        P("wsh", None),
        P("wsh", None, "ctx", None),
        P("wsh", None, "ctx", None),
        P("wsh", None, "ctx", None),
    )
    return jax.shard_map(
        body,
        mesh=mesh,
        in_specs=placed,
        out_specs=(
            P("wsh", None, "ctx", None),
            P("wsh", None, "ctx", None),
            P(("ctx", "wsh"), None),
            P(("ctx", "wsh"), None),
            P(("ctx", "wsh"), None),
            P(("ctx", "wsh"), None),
            P(("ctx", "wsh")),
            P(("ctx", "wsh"), None),
            P(None, ("ctx", "wsh"), None, None),
            P(None, ("ctx", "wsh"), None),
            P(("ctx", "wsh")),
        ),
        check_vma=False,
    )
```

```python
import functools

import jax
import jax.numpy as jnp
from jax import lax
from jax.experimental import pallas as pl
from jax.experimental.pallas import tpu as pltpu
from jax.sharding import PartitionSpec as P

D = 1024
HEADS = 16
KV_HEADS = 8
HEAD_DIM = 64
TOPK = 8
EXPERTS = 16
CAP = 80
PLANE = 8
INNER = 4
OWN = EXPERTS // INNER
PIECES = 2
FIRST = OWN // 2


RES_MULT = 0.22
ATT_MULT = 0.015625
EPS = 1e-06
THETA = 10000.0

MESH = pl.DeviceIdType.MESH
F32 = jnp.float32
BF16 = jnp.bfloat16
ANY = pl.BlockSpec(memory_space=pl.ANY)
VMEM = pl.BlockSpec(memory_space=pltpu.VMEM)


class Place:
    def __init__(self):
        self.c = lax.axis_index("ctx")
        self.w = lax.axis_index("wsh")
        self.core = self.c % 2
        self.y = (self.c // 2) % 2
        self.inner = self.c % INNER
        self.outer = self.c // INNER
        self.z = self.outer % 2
        self.q = self.z * 2 + self.core
        self.j = self.q * 2 + self.w
        self.beside = (self.c + 2 - 4 * self.y, self.w)

    def relative(self, dz, dc, dw):
        z = self.z + dz * (1 - 2 * self.z)
        core = self.core + dc * (1 - 2 * self.core)
        w = self.w + dw * (1 - 2 * self.w)
        ctx = self.c + INNER * (z - self.z) + core - self.core
        return (ctx, w), (z * 2 + core) * 2 + w


OTHERS = [(a, b, d) for a in range(2) for b in range(2) for d in range(2) if a + b + d]
XY = [(0, 0, 1), (1, 0, 0), (1, 0, 1)]


def meet(devices):
    barrier = pltpu.get_barrier_semaphore()
    for device in devices:
        pl.semaphore_signal(barrier, inc=1, device_id=device, device_id_type=MESH)
    pl.semaphore_wait(barrier, len(devices))


def remote(src, dst, send, recv, device):
    return pltpu.make_async_remote_copy(
        src_ref=src,
        dst_ref=dst,
        send_sem=send,
        recv_sem=recv,
        device_id=device,
        device_id_type=MESH,
    )


def comm_call(kernel, out_shape, in_specs, out_specs, scratch, ident, name, vmem=None, us=20):
    return pl.pallas_call(
        kernel,
        out_shape=out_shape,
        in_specs=in_specs,
        out_specs=out_specs,
        scratch_shapes=scratch,
        compiler_params=pltpu.CompilerParams(
            collective_id=ident, has_side_effects=True, vmem_limit_bytes=vmem
        ),
        cost_estimate=pl.CostEstimate(
            flops=us * 10**9, bytes_accessed=us * 3 * 2**20, transcendentals=0
        ),
        name=name,
    )


DMA = pltpu.SemaphoreType.DMA


def room(arrays, scratch=(), spare=12):
    total = 0
    for array in list(arrays) + list(scratch):
        inner = getattr(array, "inner_aval", array)
        size = jnp.dtype(inner.dtype).itemsize
        for extent in inner.shape:
            size *= extent
        total += size
    return min(total + spare * 2**20, 62 * 2**20)


def far_first(outers):
    return outers == 4


def far_partner(at):
    return (at.c + INNER * 2 * (1 - 2 * (at.outer // 2)), at.w)


class Halving:
    def __init__(self, at, outers, sums, arrived, send, recv, cols=slice(None)):
        self.cols = cols
        self.at, self.sums, self.arrived = at, sums, arrived
        self.send, self.recv = send, recv
        self.bits = [2**k for k in range(1, outers.bit_length() - 1)]
        self.levels = [(0, outers // 2)]
        for bit in self.bits:
            start, many = self.levels[-1]
            self.levels.append((start + many, many // 2))
        self.copies = []

    def pick(self, index):
        return index, slice(None), slice(None), self.cols

    def device(self, bit):
        at = self.at
        return (at.c + INNER * bit * (1 - 2 * ((at.outer // bit) % 2)), at.w)

    def start(self, step):
        bit = self.bits[step]
        side = (self.at.outer // bit) % 2
        start, many = self.levels[step]
        for m in range(many // 2):
            copy = remote(
                self.sums.at[self.pick(start + 2 * m + 1 - side)],
                self.arrived.at[self.pick(start + m)],
                self.send.at[start + m],
                self.recv.at[start + m],
                self.device(bit),
            )
            copy.start()
            self.copies.append(copy)

    def add(self, step):
        side = (self.at.outer // self.bits[step]) % 2
        start, many = self.levels[step]
        after, half = self.levels[step + 1]
        for m in range(half):
            self.copies[len(self.copies) - half + m].wait_recv()
            total = self.sums[self.pick(start + 2 * m + side)].astype(F32)
            total = total + self.arrived[self.pick(start + m)].astype(F32)
            self.sums[self.pick(after + m)] = total.astype(BF16)

    def finish(self):
        for step in range(len(self.bits)):
            if step > 0:
                self.start(step)
            self.add(step)
        for copy in self.copies:
            copy.wait_send()
        return self.sums[self.pick(self.levels[-1][0])]


def gather_start(at, pairs, send, recv, local):
    copies = []
    for index, (src, dst) in enumerate(pairs):
        keep = pltpu.make_async_copy(src, dst.at[at.j], local.at[index])
        keep.start()
        sends = []
        for slot, bits in enumerate(XY + [(0, 1, 0)]):
            device, unused = at.relative(*bits)
            copy = remote(src, dst.at[at.j], send.at[index, slot], recv.at[index, slot], device)
            copy.start()
            sends.append(copy)
        copies.append((keep, sends))
    return copies


def gather_pass(at, pairs, copies, send, recv):
    sib, unused = at.relative(0, 1, 0)
    passed = []
    for slot, bits in enumerate(XY):
        unused, j_from = at.relative(*bits)
        for index, (src, dst) in enumerate(pairs):
            copies[index][1][slot].wait_recv()
            block = dst.at[j_from]
            copy = remote(
                block, block, send.at[index, 4 + slot], recv.at[index, 4 + slot], sib
            )
            copy.start()
            passed.append(copy)
    return passed


def gather_wait(copies, passed):
    for keep, sends in copies:
        keep.wait()
        sends[3].wait_recv()
        for copy in sends:
            copy.wait_send()
    for copy in passed:
        copy.wait()


def turn(values, cosine, sine):
    lane = lax.broadcasted_iota(jnp.int32, cosine.shape, 1)
    first = lane % HEAD_DIM < HEAD_DIM // 2
    blocks = []
    for start in range(0, values.shape[1], 128):
        u = values[:, start : start + 128]
        swapped = jnp.where(first, pltpu.roll(u, 96, 1), pltpu.roll(u, 32, 1))
        blocks.append(u * cosine + swapped * sine)
    return jnp.concatenate(blocks, axis=1)


def dot_nt(a, b):
    return lax.dot_general(a, b, (((1,), (1,)), ((), ())), preferred_element_type=F32)


def dot_tn(a, b):
    return lax.dot_general(a, b, (((0,), (0,)), ((), ())), preferred_element_type=F32)


def dot_nn(a, b):
    return jnp.dot(a, b, preferred_element_type=F32)


def owners_kernel(devices, count, near_count, *refs):
    total = count + near_count
    parts, nears = refs[:count], refs[count:total]
    outs, near_outs = refs[total : total + count], refs[total + count : 2 * total]
    send, recv, local, nsend, nrecv, nlocal = refs[2 * total :]
    at = Place()
    me = at.c * 2 + at.w
    rows = D // devices

    def device_of(r):
        index = lax.rem(me + r, devices)
        return index, (index // 2, lax.rem(index, 2))

    def rows_of(ref, index):
        return ref.at[pl.ds(pl.multiple_of(index * rows, rows), rows), :]

    barrier = pltpu.get_barrier_semaphore()

    def greet(r, carry):
        unused, device = device_of(r)
        pl.semaphore_signal(barrier, inc=1, device_id=device, device_id_type=MESH)
        return carry

    lax.fori_loop(1, devices, greet, 0)
    pl.semaphore_wait(barrier, devices - 1)

    def copy_of(k, r):
        index, device = device_of(r)
        return remote(rows_of(parts[k], index), outs[k].at[me], send.at[k, r], recv.at[k, r], device)

    def start(r, carry):
        for k in range(count):
            copy_of(k, r).start()
        return carry

    lax.fori_loop(1, devices, start, 0)

    near_copies = []
    for k in range(near_count):
        for slot, bits in enumerate(OTHERS):
            device, j_to = at.relative(*bits)
            copy = remote(
                nears[k].at[:, j_to], near_outs[k].at[at.j], nsend.at[k, slot], nrecv.at[k, slot], device
            )
            copy.start()
            near_copies.append(copy)
    keeps = []
    for k in range(count):
        keep = pltpu.make_async_copy(rows_of(parts[k], me), outs[k].at[me], local.at[k])
        keep.start()
        keeps.append(keep)
    for k in range(near_count):
        keep = pltpu.make_async_copy(nears[k].at[:, at.j], near_outs[k].at[at.j], nlocal.at[k])
        keep.start()
        keeps.append(keep)

    def finish(r, carry):
        for k in range(count):
            copy_of(k, r).wait()
        return carry

    lax.fori_loop(1, devices, finish, 0)
    for copy in near_copies:
        copy.wait()
    for keep in keeps:
        keep.wait()


def owners(parts, nears, devices, ident, name):
    count, near_count = len(parts), len(nears)
    rows = D // devices
    shape = jax.ShapeDtypeStruct
    shapes = [shape((devices, rows, part.shape[-1]), part.dtype) for part in parts]
    for near in nears:
        lead, members, near_rows, width = near.shape
        shapes.append(shape((members, lead, near_rows, width), near.dtype))
    return comm_call(
        functools.partial(owners_kernel, devices, count, near_count),
        shapes,
        [ANY] * (count + near_count),
        [VMEM] * (count + near_count),
        [
            DMA((count, devices)),
            DMA((count, devices)),
            DMA((count,)),
            DMA((near_count, 7)),
            DMA((near_count, 7)),
            DMA((near_count,)),
        ],
        ident,
        name,
        vmem=60 * 2**20,
    )(*parts, *nears)


CHUNK = 256
PAIRS = KV_HEADS // 2
NEVER = -1e30


def low_lanes(shape):
    return lax.broadcasted_iota(jnp.int32, shape, 1) < HEAD_DIM


def spread(block):
    a, b = block[:, :128], block[:, 128:]
    low = low_lanes(a.shape)
    zero = jnp.zeros_like(a)
    return jnp.concatenate(
        [
            jnp.where(low, a, zero),
            jnp.where(low, pltpu.roll(a, HEAD_DIM, 1), zero),
            jnp.where(low, zero, pltpu.roll(b, HEAD_DIM, 1)),
            jnp.where(low, zero, b),
        ],
        axis=0,
    )


def unspread(four):
    rows = four.shape[0] // 4
    r0, r1, r2, r3 = (four[k * rows : (k + 1) * rows] for k in range(4))
    low = low_lanes(r0.shape)
    return jnp.concatenate(
        [
            jnp.where(low, r0, pltpu.roll(r1, HEAD_DIM, 1)),
            jnp.where(low, pltpu.roll(r2, HEAD_DIM, 1), r3),
        ],
        axis=1,
    )


DOCS = 8


def doc_starts(segments):
    return [
        jnp.sum(jnp.where(segments < d, 1.0, 0.0), axis=1, keepdims=True).astype(jnp.int32)
        for d in range(DOCS)
    ]


def reach(starts, place):
    first = jnp.zeros_like(place)
    for d in range(1, DOCS):
        first = jnp.where(place >= starts[d], starts[d], first)
    return first


def half_span(half, rows, keys):
    block = lax.axis_index("ctx")
    if half == 1:
        block = keys // rows - 1 - block
    base = block * rows
    return base, (base + rows + CHUNK - 1) // CHUNK


def key_block(kv, chunk, rows, col):
    many = CHUNK // rows
    picked = kv[pl.ds(chunk * many, many), :, pl.ds(col, 128)]
    return picked.reshape(CHUNK, 128)


def attend_rows(
    starts,
    q_ref,
    kv_ref,
    tok_ref,
    wo_ref,
    small_ref,
    route_ref,
    prio_ref,
    raw_ref,
    total_ref,
    mixed_ref,
    sum_ref,
    hid_ref,
    gate_ref,
    kept_ref,
    send_ref,
    acc,
    acc_l,
):
    rows = q_ref.shape[0] // 2
    width = PAIRS * 128
    keys = kv_ref.shape[0] * rows
    for half in range(2):
        base, chunks = half_span(half, rows, keys)
        q_four = []
        for pair in range(PAIRS):
            block = q_ref[pl.ds(half * rows, rows), pl.ds(pair * 256, 256)].astype(F32) * ATT_MULT
            q_four.append(spread(block).astype(BF16))
        acc[...] = jnp.zeros_like(acc)
        acc_l[...] = jnp.zeros_like(acc_l)
        place = base + lax.broadcasted_iota(jnp.int32, (rows, 1), 0)
        first = reach(starts, place)

        def step(chunk, carry):
            at_row = pl.multiple_of(chunk * CHUNK, CHUNK)
            key_pos = at_row + lax.broadcasted_iota(jnp.int32, (1, CHUNK), 1)
            bias = jnp.where((key_pos >= first) & (key_pos <= place), 0.0, NEVER)
            bias = jnp.concatenate([bias] * 4, axis=0)
            for pair in range(PAIRS):
                key = key_block(kv_ref, chunk, rows, pair * 128)
                value = key_block(kv_ref, chunk, rows, width + pair * 128)
                e = jnp.exp(dot_nt(q_four[pair], key) + bias)
                part = e[:, :128]
                for k in range(1, CHUNK // 128):
                    part = part + e[:, k * 128 : (k + 1) * 128]
                acc_l[pair] += part
                acc[pair] += dot_nn(e.astype(BF16), value)
            return carry

        lax.fori_loop(0, chunks, step, 0)
        for pair in range(PAIRS):
            total = jnp.sum(acc_l[pair], axis=1, keepdims=True)
            total = jnp.broadcast_to(total, (4 * rows, 128))
            here = pl.ds(half * rows, rows), pl.ds(pair * 256, 256)
            raw_ref[here] = unspread(acc[pair] / total)
            total_ref[here] = unspread(total)
    mixed = raw_ref[...].astype(BF16)
    mixed_ref[...] = mixed
    first_sum = tok_ref[...].astype(F32) + RES_MULT * dot_nn(mixed, wo_ref[...])
    sum_ref[...] = first_sum
    scale = lax.rsqrt(jnp.mean(first_sum * first_sum, axis=1, keepdims=True) + EPS)
    gain_two = small_ref[pl.ds(EXPERTS + 1, 1), :].astype(F32)
    hidden = (first_sum * scale * gain_two).astype(BF16)
    hid_ref[...] = hidden

    logits = dot_nt(small_ref[...], hidden)[:EXPERTS]
    count = 2 * rows
    expert = lax.broadcasted_iota(jnp.int32, (EXPERTS, count), 0)
    routed = jnp.zeros((EXPERTS, count), F32)
    prio = jnp.zeros((EXPERTS, count), F32)
    for k in range(TOPK):
        line = [
            jnp.concatenate([ref[0, pl.ds(k, 1), :], ref[1, pl.ds(k, 1), :]], axis=1)
            for ref in (route_ref, prio_ref)
        ]
        same = expert == line[0]
        routed = jnp.where(same, 1.0, routed)
        prio = jnp.where(same, line[1].astype(F32), prio)
    chosen = routed > 0.0
    order = lax.broadcasted_iota(jnp.int32, (EXPERTS, count), 1).astype(F32)
    key = jnp.where(chosen, prio * float(count) + order, 65536.0 * count)
    key_cols = jnp.concatenate([key, jnp.zeros((count - EXPERTS, count), F32)], axis=0).T
    ranks = []
    for e in range(EXPERTS):
        ahead = jnp.where(key_cols[:, e : e + 1] < key[e : e + 1, :], 1.0, 0.0)
        ranks.append(jnp.sum(ahead, axis=0, keepdims=True))
    rank = jnp.concatenate(ranks, axis=0)
    top = jnp.max(jnp.where(chosen, logits, -3e38), axis=0, keepdims=True)
    weight = jnp.where(chosen, jnp.exp(logits - top), 0.0)
    gate = weight / jnp.sum(weight, axis=0, keepdims=True)
    kept = jnp.where(chosen & (rank < CAP), 1.0, 0.0)
    gate_ref[...] = gate
    kept_ref[...] = kept
    send_ref[...] = gate * kept


SMEM = pl.BlockSpec(memory_space=pltpu.SMEM)


def finish_kernel(
    outers,
    part,
    moe,
    sum_ref,
    dq_ref,
    da_ref,
    dy_ref,
    tok_ref,
    small_ref,
    cos_ref,
    sin_ref,
    wqkv_in,
    left_in,
    rows_ref,
    z_ref,
    near_in,
    out_ref,
    token_ref,
    attn_ref,
    small_o,
    near_o,
    next_o,
    z_o,
    wqkv_ref,
    left_ref,
    z_sums,
    z_in_rows,
    own,
    half_in,
    y_in,
    z_in,
    m_own,
    m_near,
    m_x,
    m_y,
    qkv,
    swap,
    swapped,
    ss,
    sr,
    ys,
    yr,
    zs,
    zr,
    ns,
    nr,
    ws,
    wr,
    vs,
    vr,
    ls,
    os,
    ps,
    pr,
    qs,
    qr,
):
    at = Place()
    blocks, rows, full = part.shape
    loads = [
        pltpu.make_async_copy(wqkv_in, wqkv_ref, ls.at[0]),
        pltpu.make_async_copy(left_in, left_ref, ls.at[1]),
    ]
    moe_load = pltpu.make_async_copy(moe.at[:, at.core], m_own, ls.at[2])
    near_keep = pltpu.make_async_copy(near_in.at[:, at.j], near_o.at[at.j], ls.at[3])
    z_loads = [
        pltpu.make_async_copy(
            z_ref.at[:, e], z_sums.at[e, pl.ds(0, outers // 2)], ls.at[4 + e]
        )
        for e in range(z_sums.shape[0])
    ]
    for copy in z_loads + [moe_load] + loads + [near_keep]:
        copy.start()
    width = full // 2
    cuts = 4
    step_width = full // cuts
    count = 2 * rows
    sib, unused = at.relative(0, 1, 0)
    side = at.beside
    along_to, unused = at.relative(1, 0, 0)
    across, unused = at.relative(0, 0, 1)
    other = [lax.rem(at.outer + r, outers) for r in range(outers)]
    far = [(other[r] * INNER + at.inner, at.w) for r in range(1, outers)]
    rest = [
        Halving(at, outers, z_sums.at[e], z_in_rows.at[e], vs.at[e], vr.at[e])
        for e in range(z_sums.shape[0])
    ]
    meet([at.relative(*bits)[0] for bits in OTHERS] + far + [at.beside])
    for copy in z_loads:
        copy.wait()
    if outers > 2:
        rest[0].start(0)

    def own_block(half, o, y, core):
        index = (o * 2 + y) * 2 + core
        return index if half == 0 else blocks - 1 - index

    own_loads = []
    for y in range(2):
        for h in range(2):
            for o in range(outers):
                copy = pltpu.make_async_copy(
                    part.at[own_block(h, o, y, at.core)], own.at[y, h, o], os.at[y, h, o]
                )
                copy.start()
                own_loads.append(copy)
    first = {}
    for k in range(cuts):
        cols = pl.ds(k * step_width, step_width)
        for y in range(2):
            for h in range(2):
                for o in range(outers):
                    copy = remote(
                        part.at[own_block(h, o, y, 1 - at.core), :, cols],
                        half_in.at[y, h, o, :, cols],
                        ss.at[k, y, h, o],
                        sr.at[k, y, h, o],
                        sib,
                    )
                    copy.start()
                    first[k, y, h, o] = copy
    nears = []
    for slot, bits in enumerate(OTHERS):
        device, j_to = at.relative(*bits)
        copy = remote(near_in.at[:, j_to], near_o.at[at.j], ps.at[slot], pr.at[slot], device)
        copy.start()
        nears.append(copy)
    near = remote(moe.at[:, 1 - at.core], m_near, ns.at[0], nr.at[0], sib)
    near.start()
    for copy in own_loads:
        copy.wait()
    second = []
    for k in range(cuts):
        cols = pl.ds(k * step_width, step_width)
        for y in range(2):
            for h in range(2):
                for o in range(outers):
                    first[k, y, h, o].wait_recv()
                    total = own[y, h, o, :, cols].astype(F32) + half_in[
                        y, h, o, :, cols
                    ].astype(F32)
                    half_in[y, h, o, :, cols] = total.astype(BF16)
        copy = remote(
            half_in.at[1 - at.y, :, :, :, cols], y_in.at[:, :, :, cols], ys.at[k], yr.at[k], side
        )
        copy.start()
        second.append(copy)
    near.wait_recv()
    moe_load.wait()
    for y in range(2):
        for w in range(2):
            total = m_own[y, w].astype(F32) + m_near[y, w].astype(F32)
            m_near[y, w] = total.astype(BF16)
    cross = remote(m_near.at[:, 1 - at.w], m_x, ns.at[1], nr.at[1], across)
    cross.start()
    third = []

    def z_send(k):
        cols = pl.ds(k * step_width, step_width)
        second[k].wait_recv()
        for o in range(outers):
            for h in range(2):
                total = half_in[at.y, h, o, :, cols].astype(F32) + y_in[h, o, :, cols].astype(F32)
                half_in[at.y, h, o, :, cols] = total.astype(BF16)
        for r in range(1, outers):
            copy = remote(
                half_in.at[at.y, :, other[r], :, cols],
                z_in.at[r, :, :, cols],
                zs.at[k, r],
                zr.at[k, r],
                far[r - 1],
            )
            copy.start()
            third.append(copy)

    z_send(0)
    z_send(1)
    cross.wait_recv()
    for y in range(2):
        total = m_near[y, at.w].astype(F32) + m_x[y].astype(F32)
        m_x[y] = total.astype(BF16)
    along = remote(m_x.at[1 - at.z], m_y, ns.at[2], nr.at[2], along_to)
    along.start()
    for k in range(2, cuts):
        z_send(k)
    qkv[:, : HEADS * HEAD_DIM] = dq_ref[...]
    along.wait_recv()
    moe_sum = m_x[at.z].astype(F32) + m_y[...].astype(F32)
    out_ref[...] = (sum_ref[...] + RES_MULT * moe_sum).astype(BF16)
    tok = tok_ref[...].astype(F32)
    scale = lax.rsqrt(jnp.mean(tok * tok, axis=1, keepdims=True) + EPS)
    normed = tok * scale
    gain_one = small_ref[pl.ds(EXPERTS, 1), :].astype(F32)
    for copy in third:
        copy.wait_recv()
    if outers > 2:
        for halving in rest[1:]:
            halving.start(0)
    rest[0].finish()
    level = rest[0].levels[-1][0]
    owner_rows = next_o.shape[2]

    def rows_of(j):
        within = pl.multiple_of(lax.rem(j, 4) * owner_rows, owner_rows)
        return 0, level, j // 4, pl.ds(within, owner_rows)

    for slot, bits in enumerate(OTHERS):
        device, j_to = at.relative(*bits)
        copy = remote(
            z_sums.at[rows_of(j_to)], next_o.at[at.j, 0], qs.at[slot], qr.at[slot], device
        )
        copy.start()
        nears.append(copy)
    next_o[at.j, 0] = z_sums[rows_of(at.j)]
    cosine = cos_ref[...]
    sine = -sin_ref[...]
    base = HEADS * HEAD_DIM
    for h in range(2):
        here = slice(h * rows, (h + 1) * rows)
        total = half_in[at.y, h, at.outer].astype(F32)
        for r in range(1, outers):
            total = total + z_in[r, h].astype(F32)
        qkv[here, base : base + width] = turn(total[:, :width], cosine[here], sine[here]).astype(BF16)
        qkv[here, base + width :] = total[:, width:].astype(BF16)
    wide = full * 2 // PLANE
    for j in range(PLANE):
        swap[j, :, :wide] = qkv[:, j * wide : (j + 1) * wide]
        swap[j, :, wide:] = da_ref[:, j * (D // PLANE) : (j + 1) * (D // PLANE)]
    swaps = []
    for slot, bits in enumerate(OTHERS):
        device, j_to = at.relative(*bits)
        copy = remote(swap.at[j_to], swapped.at[at.j], ws.at[slot], wr.at[slot], device)
        copy.start()
        swaps.append(copy)
    swapped[at.j] = swap[at.j]
    for copy in loads:
        copy.wait()
    hidden_grad = dot_nt(qkv[...], wqkv_ref[...])
    small = rows_ref[...]
    gain_grad = jnp.sum(hidden_grad * normed, axis=0, keepdims=True)
    line = lax.broadcasted_iota(jnp.int32, small.shape, 0)
    small = jnp.where(line == EXPERTS, gain_grad, small)
    small = jnp.concatenate([small, jnp.zeros((128 - small.shape[0], D), F32)], axis=0)
    small_o[...] = small.T.astype(BF16)
    hidden_grad = hidden_grad * gain_one
    token_ref[...] = dy_ref[...] + scale * (
        hidden_grad - normed * jnp.mean(hidden_grad * normed, axis=1, keepdims=True)
    )
    for copy in swaps:
        copy.wait_recv()
    all_rows = PLANE * count
    left_one = left_ref[0].reshape(all_rows, D)
    left_mixed = left_ref[1].reshape(all_rows, D)
    grads = swapped[...].reshape(all_rows, wide + D // PLANE)
    attn_ref[:, :wide] = dot_tn(left_one, grads[:, :wide]).astype(BF16)
    attn_ref[:, wide:] = dot_tn(left_mixed, grads[:, wide:]).astype(BF16)
    for e in range(1, len(rest)):
        z_o[e - 1] = rest[e].finish()
    near_keep.wait()
    for copy in nears:
        copy.wait()
    for copy in list(first.values()) + second + third + swaps + [near, cross, along]:
        copy.wait_send()


def finish(part, moe, arrays, z_half, near, ctx_count):
    outers = ctx_count // INNER
    blocks, rows, full = part.shape
    count = 2 * rows
    shape = jax.ShapeDtypeStruct
    columns = 3 * D // PLANE
    return comm_call(
        functools.partial(finish_kernel, outers),
        [
            shape((count, D), BF16),
            shape((count, D), F32),
            shape((D, columns), BF16),
            shape((D, 128), BF16),
            shape((PLANE, near.shape[0]) + near.shape[2:], BF16),
            shape((PLANE, 1) + near.shape[2:], BF16),
            shape((z_half.shape[1] - 1,) + z_half.shape[2:], BF16),
        ],
        [ANY] * 2 + [VMEM] * (len(arrays) - 3) + [ANY] * 2 + [VMEM] + [ANY] * 2,
        [VMEM] * 7,
        [
            pltpu.VMEM((D, 2 * full), BF16),
            pltpu.VMEM((2, PLANE, count, D), BF16),
            pltpu.VMEM((z_half.shape[1], outers) + z_half.shape[2:], BF16),
            pltpu.VMEM((z_half.shape[1], outers) + z_half.shape[2:], BF16),
            pltpu.VMEM((2, 2, outers, rows, full), BF16),
            pltpu.VMEM((2, 2, outers, rows, full), BF16),
            pltpu.VMEM((2, outers, rows, full), BF16),
            pltpu.VMEM((outers, 2, rows, full), BF16),
            pltpu.VMEM((2, 2, count, D), BF16),
            pltpu.VMEM((2, 2, count, D), BF16),
            pltpu.VMEM((2, count, D), BF16),
            pltpu.VMEM((count, D), BF16),
            pltpu.VMEM((count, 2 * full), BF16),
            pltpu.VMEM((PLANE, count, columns), BF16),
            pltpu.VMEM((PLANE, count, columns), BF16),
            DMA((4, 2, 2, outers)),
            DMA((4, 2, 2, outers)),
            DMA((4,)),
            DMA((4,)),
            DMA((4, outers)),
            DMA((4, outers)),
            DMA((3,)),
            DMA((3,)),
            DMA((7,)),
            DMA((7,)),
            DMA((z_half.shape[1], outers)),
            DMA((z_half.shape[1], outers)),
            DMA((4 + z_half.shape[1],)),
            DMA((2, 2, outers)),
            DMA((7,)),
            DMA((7,)),
            DMA((7,)),
            DMA((7,)),
        ],
        3,
        "finish",
        vmem=63 * 2**20,
        us=60,
    )(part, moe.reshape(2, 2, 2, count, D), *arrays, z_half, near)


def gate_columns(gates, cols):
    count = gates.shape[-1]
    for j in range(PLANE):
        block = jnp.concatenate([gates[j], jnp.zeros((128 - EXPERTS, count), F32)], axis=0)
        cols[pl.ds(j * count, count), :] = block.T


def expert_step(both, back_act, gate, units):
    gv, uv = both[:, :units], both[:, units:]
    sig = jax.nn.sigmoid(gv)
    silu = gv * sig
    act = silu * uv
    pick = jnp.sum(act * back_act, axis=1, keepdims=True)
    kept = (gate * act).astype(BF16)
    back_act = gate * back_act
    slope = sig * (1.0 + gv * (1.0 - sig))
    low = jnp.concatenate([back_act * uv * slope, back_act * silu], axis=1).astype(BF16)
    return kept, pick, low


def lane_of(cols, lane):
    at = lax.broadcasted_iota(jnp.int32, cols.shape, 1)
    return jnp.sum(jnp.where(at == lane, cols, 0.0), axis=1, keepdims=True)


def opening_kernel(
    outers,
    seg_ref,
    tok_ref,
    wq,
    wk,
    wv,
    wo,
    small,
    cot,
    cos_ref,
    sin_ref,
    route_ref,
    prio_ref,
    expert_in,
    expert_out,
    wqkv_o,
    wo_o,
    small_o,
    q_o,
    hid_o,
    kv_o,
    raw_o,
    total_o,
    mixed_o,
    sum_o,
    gate_o,
    kept_o,
    pick_o,
    z_o,
    za_o,
    part_o,
    kept_units_o,
    grad_o,
    left_o,
    wqkv,
    wout,
    own,
    tok_v,
    cos_v,
    sin_v,
    kv,
    cot_v,
    raw,
    out_w,
    inner_w,
    acc,
    acc_l,
    hid_two,
    gate_send,
    hid,
    gates,
    cot_t,
    backs,
    cols,
    pick_cols,
    staged,
    y_in,
    za_in,
    xs,
    xr,
    fs,
    fr,
    ls,
    zs,
    zr,
    ys,
    yr,
    cs,
    cr,
    hs,
    gs,
    gr,
    gl,
    es,
    ts,
    tr,
    tl,
    gd,
    us,
    ur,
    ul,
    vs,
    vr,
    fas,
    far_r,
):
    at = Place()
    blocks, rows = kv.shape[:2]
    units = out_w.shape[-1]
    experts = at.q * OWN
    sib, unused = at.relative(0, 1, 0)
    partner, j_partner = at.relative(0, 0, 1)
    side, j_side = at.relative(1, 0, 0)
    unused, j_cross = at.relative(1, 0, 1)
    steps = sorted({1, outers - 1})
    far = [(lax.rem(at.outer + r, outers) * INNER + at.inner, at.w) for r in steps]
    expert_loads = {}

    def load_expert(e):
        copy = pltpu.make_async_copy(expert_in.at[experts + e], raw.at[e % 2], es.at[e % 2])
        copy.start()
        expert_loads[e] = copy

    def shape_expert(e):
        expert_loads[e].wait()
        inner_w[:, e * 2 * units : (e + 1) * 2 * units] = raw[e % 2].reshape(D, 2 * units)
        if e + 2 < OWN:
            load_expert(e + 2)

    out_loads = [
        pltpu.make_async_copy(expert_out.at[experts + e], out_w.at[e], es.at[2 + e])
        for e in range(OWN)
    ]
    for copy in out_loads:
        copy.start()
    load_expert(0)
    load_expert(1)
    meet(
        [at.relative(*bits)[0] for bits in XY + [(0, 1, 0)]] + far + [at.beside]
        + ([far_partner(at)] if far_first(outers) else [])
    )

    pieces = [(wk, wqkv, 1024), (wv, wqkv, 1536), (wq, wqkv, 0), (wo, wout, 0)]
    sends, passed, keeps = {}, {}, []

    def give(index):
        src, dst, col = pieces[index]
        depth, width = src.shape
        half = depth // 2
        copy = remote(
            src.at[pl.ds(at.core * half, half), :],
            dst.at[pl.ds(at.w * depth + at.core * half, half), pl.ds(col, width)],
            xs.at[index],
            xr.at[index],
            partner,
        )
        copy.start()
        sends[index] = copy

    def pass_on(index):
        src, dst, col = pieces[index]
        depth, width = src.shape
        half = depth // 2
        sends[index].wait_recv()
        piece = dst.at[pl.ds((1 - at.w) * depth + at.core * half, half), pl.ds(col, width)]
        copy = remote(piece, piece, fs.at[index], fr.at[index], sib)
        copy.start()
        passed[index] = copy

    wide = small.shape[1]
    mine = small_o.at[:, pl.ds(at.w * wide, wide)]
    gains = remote(small, mine, xs.at[4], xr.at[4], partner)
    gains.start()
    give(0)
    give(1)
    cot_sib = remote(cot, cot_v.at[at.j], gs.at[0], gr.at[0], sib)
    cot_sib.start()
    cot_side = remote(cot, cot_v.at[at.j], gs.at[1], gr.at[1], side)
    cot_side.start()
    cot_keep = pltpu.make_async_copy(cot, cot_v.at[at.j], gl)
    cot_keep.start()
    for index, (src, dst, col) in enumerate(pieces):
        depth, width = src.shape
        keep = pltpu.make_async_copy(
            src, dst.at[pl.ds(at.w * depth, depth), pl.ds(col, width)], ls.at[index]
        )
        keep.start()
        keeps.append(keep)
    loads = [
        pltpu.make_async_copy(src, dst, hs.at[4 + index])
        for index, (src, dst) in enumerate(
            ((tok_ref, tok_v), (cos_ref, cos_v), (sin_ref, sin_v), (small, mine))
        )
    ]
    for copy in loads:
        copy.start()
    for copy in loads:
        copy.wait()
    tok = tok_v[...].astype(F32)
    normed = tok * lax.rsqrt(jnp.mean(tok * tok, axis=1, keepdims=True) + EPS)
    gains.wait_recv()
    hidden = (normed * small_o[pl.ds(EXPERTS, 1), :].astype(F32)).astype(BF16)
    hid_o[...] = hidden
    cosine, sine = cos_v[...], sin_v[...]

    pass_on(0)
    pass_on(1)
    cot_across = remote(cot, cot_v.at[at.j], gs.at[2], gr.at[2], partner)
    cot_across.start()
    keeps[0].wait()
    keeps[1].wait()
    passed[0].wait_recv()
    key = dot_nn(hidden, wqkv[:, 1024:1536])
    key = turn(key, cosine, sine).astype(BF16)
    passed[1].wait_recv()
    value = dot_nn(hidden, wqkv[:, 1536:]).astype(BF16)
    width = key.shape[1]
    for half in range(2):
        own[half, :, :width] = key[half * rows : (half + 1) * rows]
        own[half, :, width:] = value[half * rows : (half + 1) * rows]

    def block_of(half, ctx):
        return kv.at[ctx] if half == 0 else kv.at[blocks - 1 - ctx]

    last = outers - 1
    hops = [(0, 0, 0)] + [
        (step, sign, step if sign < 0 else last + step)
        for step in range(1, outers)
        for sign in (-1, 1)
    ]

    def source(step, sign):
        return at.outer + sign * step

    def exists(step, sign):
        place = source(step, sign)
        return (place >= 0) & (place <= last)

    def block_from(half, step, sign, inner):
        place = lax.rem(source(step, sign) + outers, outers)
        return block_of(half, place * INNER + inner)

    below = (lax.rem(at.outer + last, outers) * INNER + at.inner, at.w)
    above = (lax.rem(at.outer + 1, outers) * INNER + at.inner, at.w)
    inner_side = at.inner + 2 - 4 * at.y

    def z_copy(half, slot, step, sign):
        src = own.at[half] if step == 0 else block_from(half, step, sign, at.inner)
        dst = block_from(half, step, sign, at.inner)
        slot_there = step + 1 if sign < 0 else last + step + 1
        return remote(
            src,
            dst,
            zs.at[half, slot_there],
            zr.at[half, slot_there],
            above if sign < 0 else below,
        )

    def y_copy(half, slot, step, sign):
        src = own.at[half] if step == 0 else block_from(half, step, sign, at.inner)
        dst = block_from(half, step, sign, at.inner)
        return remote(src, dst, ys.at[half, slot], yr.at[half, slot], at.beside)

    def c_copy(half, slot, step, sign, inner, base):
        src = (
            own.at[half]
            if step == 0 and base == 0
            else block_from(half, step, sign, inner)
        )
        dst = block_from(half, step, sign, inner)
        return remote(src, dst, cs.at[half, base + slot], cr.at[half, base + slot], sib)

    spots = 2 * outers - 1

    def spread_from(step, sign, slot, halves=(0, 1)):
        for half in halves:
            if step == 0:
                for way in (-1, 1):

                    @pl.when((at.outer < last) if way < 0 else (at.outer > 0))
                    def _():
                        z_copy(half, 0, 0, way).start()

            elif step < last:

                @pl.when((at.outer < last) if sign < 0 else (at.outer > 0))
                def _():
                    z_copy(half, slot, step, sign).start()

            y_copy(half, slot, step, sign).start()
            c_copy(half, slot, step, sign, at.inner, 0).start()

    spread_from(0, 0, 0)
    for half in range(2):
        keep = pltpu.make_async_copy(own.at[half], block_of(half, at.c), hs.at[half])
        keep.start()
        keeps.append(keep)

    def y_arrived(step, sign, slot):
        for half in range(2):
            y_copy(half, slot, step, sign).wait_recv()
            c_copy(half, slot, step, sign, inner_side, spots).start()

    def z_arrived(want):
        for step, sign, slot in hops[1:]:
            if step == want:

                @pl.when(exists(step, sign))
                def _():
                    for half in range(2):
                        z_copy(half, slot, step - 1, sign).wait_recv()
                        spread_from(step, sign, slot, (half,))

    def sides_arrived(want):
        for step, sign, slot in hops[1:]:
            if step == want:

                @pl.when(exists(step, sign))
                def _():
                    y_arrived(step, sign, slot)

    shape_expert(0)
    cot_across.wait_recv()
    give(2)
    cot_on = []

    def cot_pass(slot, j_from, device):
        block = cot_v.at[j_from]
        copy = remote(block, block, gs.at[slot], gr.at[slot], device)
        copy.start()
        cot_on.append(copy)

    cot_pass(3, j_partner, side)
    cot_pass(4, j_partner, sib)
    cot_side.wait_recv()
    cot_pass(5, j_side, sib)
    z_arrived(1)
    y_arrived(0, 0, 0)
    shape_expert(1)
    pass_on(2)
    give(3)
    shape_expert(2)
    if outers > 2:
        z_arrived(2)
    keeps[2].wait()
    passed[2].wait_recv()
    q_o[...] = turn(dot_nn(hidden, wqkv[:, :1024]), cosine, sine).astype(BF16)
    store = pltpu.make_async_copy(wqkv, wqkv_o, hs.at[2])
    store.start()
    shape_expert(3)
    sides_arrived(1)
    for step in range(3, outers):
        z_arrived(step)
        sides_arrived(step - 1)
    if outers > 2:
        sides_arrived(last)
    pass_on(3)
    cot_on[0].wait_recv()
    cot_pass(6, j_cross, sib)
    keeps[3].wait()
    passed[3].wait_recv()
    store_out = pltpu.make_async_copy(wout, wo_o, hs.at[3])
    store_out.start()
    def sibling_brought(step, sign, slot):
        for half in range(2):
            c_copy(half, slot, step, sign, at.inner, 0).wait_recv()
            c_copy(half, slot, step, sign, inner_side, spots).wait_recv()

    sibling_brought(0, 0, 0)
    for step, sign, slot in hops[1:]:

        @pl.when(exists(step, sign))
        def _():
            sibling_brought(step, sign, slot)

    for keep in keeps[4:]:
        keep.wait()
    store_kv = pltpu.make_async_copy(kv, kv_o, hs.at[4])
    store_kv.start()
    attend_rows(
        doc_starts(seg_ref[...]),
        q_o,
        kv,
        tok_v,
        wout,
        small_o,
        route_ref,
        prio_ref,
        raw_o,
        total_o,
        mixed_o,
        sum_o,
        hid_two,
        gate_o,
        kept_o,
        gate_send,
        acc,
        acc_l,
    )

    pairs = [(hid_two, hid), (gate_send, gates)]
    copies = gather_start(at, pairs, ts, tr, tl)
    for copy in [cot_sib] + cot_on[1:]:
        copy.wait_recv()
    cot_keep.wait()
    for copy in out_loads:
        copy.wait()
    tokens = cot_v.shape[0] * cot_v.shape[1]
    cot_rows = cot_v[...].reshape(tokens, D)
    cot_t[...] = cot_rows.T
    for e in range(OWN):
        backs[:, e * units : (e + 1) * units] = (RES_MULT * dot_nn(cot_rows, out_w[e])).astype(BF16)
    gather_wait(copies, gather_pass(at, pairs, copies, ts, tr))
    gate_columns(gates, cols)
    left_pairs = [(hid_o, left_o.at[0]), (mixed_o, left_o.at[1])]
    left_copies = gather_start(at, left_pairs, us, ur, ul)
    store_out.wait()
    passed[3].wait_send()
    hid_t = wout
    hid_t[...] = hid[...].reshape(tokens, D).T
    late = [slice(None)] * FIRST
    if far_first(outers):
        late[0] = pl.ds(units, 2 * units)
    y_sends = [
        remote(
            staged.at[e, :, :, 1 - at.y, :, late[e]],
            y_in.at[e, :, :, :, late[e]],
            vs.at[e],
            vr.at[e],
            at.beside,
        )
        for e in range(FIRST)
    ]
    upper = at.outer // 2
    if far_first(outers):
        far_send = remote(
            staged.at[0, 1 - upper, :, :, :, pl.ds(0, units)], za_in, fas, far_r, far_partner(at)
        )
    at_lane = lax.broadcasted_iota(jnp.int32, cols.shape, 1)
    pick_cols[...] = jnp.zeros(pick_cols.shape, F32)
    store.wait()
    for index in range(3):
        passed[index].wait_send()
    low_all = wqkv

    def expert(e, carry):
        wide = pl.ds(pl.multiple_of(e * 2 * units, 2 * units), 2 * units)
        tall = pl.ds(pl.multiple_of(e * units, units), units)
        many = tokens // PIECES
        groups = PLANE // PIECES
        for piece in range(PIECES):
            here = slice(piece * many, (piece + 1) * many)
            rows_in = hid[piece * groups : (piece + 1) * groups].reshape(many, D)
            both = dot_nn(rows_in, inner_w[:, wide])
            kept, pick, low = expert_step(
                both, backs[here, tall].astype(F32), lane_of(cols[here, :], experts + e), units
            )
            backs[here, tall] = kept
            low_all[here, wide] = low
            pick_cols[here, :] = jnp.where(at_lane[here] == e, pick, pick_cols[here, :])

        shape = staged.shape[1:5]
        staged[e, :, :, :, :, : 2 * units] = (
            dot_nn(hid_t[...], low_all[:, wide]).astype(BF16).reshape(*shape, 2 * units)
        )
        staged[e, :, :, :, :, 2 * units :] = (
            (RES_MULT * dot_nn(cot_t[...], backs[:, tall])).astype(BF16).reshape(*shape, units)
        )
        for now in range(OWN):

            @pl.when(e == now)
            def _():
                if now < FIRST:
                    y_sends[now].start()
                    if now == 0 and far_first(outers):
                        far_send.start()
                else:
                    pltpu.make_async_copy(
                        staged.at[now], grad_o.at[now - FIRST], gd.at[now - FIRST]
                    ).start()

        return carry

    lax.fori_loop(0, OWN, expert, 0)
    left_passed = gather_pass(at, left_pairs, left_copies, us, ur)
    count = hid.shape[1]
    for j in range(PLANE):
        pick_o[j] = pick_cols[j * count : (j + 1) * count, :].T[:8]
    store_kept = pltpu.make_async_copy(backs, kept_units_o, hs.at[5])
    store_kept.start()
    for j in range(0, PLANE, 4):
        here = slice(j * count, (j + 4) * count)
        rows_out = dot_nt(low_all[here, :], inner_w[...]).astype(BF16)
        hid[j : j + 4] = rows_out.reshape(4, count, D)
    store_part = pltpu.make_async_copy(hid, part_o, hs.at[6])
    store_part.start()

    def settle(step, sign, slot):
        for half in range(2):
            if step == 0:
                for way in (-1, 1):

                    @pl.when((at.outer < last) if way < 0 else (at.outer > 0))
                    def _():
                        z_copy(half, 0, 0, way).wait_send()

            elif step < last:

                @pl.when((at.outer < last) if sign < 0 else (at.outer > 0))
                def _():
                    z_copy(half, slot, step, sign).wait_send()

            y_copy(half, slot, step, sign).wait_send()
            c_copy(half, slot, step, sign, at.inner, 0).wait_send()
            c_copy(half, slot, step, sign, inner_side, spots).wait_send()

    settle(0, 0, 0)
    for step, sign, slot in hops[1:]:

        @pl.when(exists(step, sign))
        def _():
            settle(step, sign, slot)

    for copy in sends.values():
        copy.wait_send()
    for copy in [gains, cot_sib, cot_side, cot_across] + cot_on:
        copy.wait_send()
    for e in range(FIRST):
        y_sends[e].wait()
        total = staged[e, :, :, at.y, :, late[e]].astype(F32)
        total = total + y_in[e, :, :, :, late[e]].astype(F32)
        z_o[:, e, :, :, late[e]] = total.astype(BF16)
    if far_first(outers):
        far_send.wait()
        total = staged[0, upper, :, :, :, :units].astype(F32) + za_in[...].astype(F32)
        za_o[...] = total.astype(BF16)
    gather_wait(left_copies, left_passed)
    for copy in [store_kv, store_kept, store_part]:
        copy.wait()
    for e in range(FIRST, OWN):
        pltpu.make_async_copy(staged.at[e], grad_o.at[e - FIRST], gd.at[e - FIRST]).wait()


def opening(
    starts, tokens, wq, wk, wv, wo, small, cot, cosine, sine, routes, priority, expert_in, expert_out, ctx_count
):
    outers = ctx_count // INNER
    shape = jax.ShapeDtypeStruct
    count = tokens.shape[0]
    rows = count // 2
    width = wk.shape[1] + wv.shape[1]
    heads = wq.shape[1]
    wide = heads + width
    units = expert_out.shape[-1]
    many = PLANE * count
    blocks = 2 * ctx_count
    z_rows = D // (2 * outers)
    vm = pltpu.VMEM
    return comm_call(
        functools.partial(opening_kernel, outers),
        [
            shape((D, wide), BF16),
            shape((D, D), BF16),
            shape((small.shape[0], D), BF16),
            shape((count, heads), BF16),
            shape((count, D), BF16),
            shape((blocks, rows, width), BF16),
            shape((count, heads), F32),
            shape((count, heads), F32),
            shape((count, heads), BF16),
            shape((count, D), F32),
            shape((EXPERTS, count), F32),
            shape((EXPERTS, count), F32),
            shape((PLANE, 8, count), F32),
            shape((outers // 2, FIRST, 2, z_rows, 3 * units), BF16),
            shape((2, 2, z_rows, units), BF16),
            shape((PLANE, count, D), BF16),
            shape((many, OWN * units), BF16),
            shape((OWN - FIRST, outers // 2, 2, 2, z_rows, 3 * units), BF16),
            shape((2, PLANE, count, D), BF16),
        ],
        [VMEM] + [ANY] * 9 + [VMEM] * 2 + [ANY] * 2,
        [ANY] * 2 + [VMEM] * 3 + [ANY] + [VMEM] * 9 + [ANY] * 4,
        [
            vm((D, wide), BF16),
            vm((D, D), BF16),
            vm((2, rows, width), BF16),
            vm((count, D), BF16),
            vm(cosine.shape, F32),
            vm(sine.shape, F32),
            vm((blocks, rows, width), BF16),
            vm((PLANE, count, D), BF16),
            vm((2, D, 2, units), BF16),
            vm((OWN, D, units), BF16),
            vm((D, OWN * 2 * units), BF16),
            vm((PAIRS, 2 * count, 128), F32),
            vm((PAIRS, 2 * count, 128), F32),
            vm((count, D), BF16),
            vm((EXPERTS, count), F32),
            vm((PLANE, count, D), BF16),
            vm((PLANE, EXPERTS, count), F32),
            vm((D, many), BF16),
            vm((many, OWN * units), BF16),
            vm((many, 128), F32),
            vm((many, 128), F32),
            vm((OWN, outers // 2, 2, 2, z_rows, 3 * units), BF16),
            vm((FIRST, outers // 2, 2, z_rows, 3 * units), BF16),
            vm((2, 2, z_rows, units), BF16),
            DMA((5,)),
            DMA((5,)),
            DMA((4,)),
            DMA((4,)),
            DMA((4,)),
        ]
        + [DMA((2, 2 * outers))] * 4
        + [DMA((2, 4 * outers))] * 2
        + [DMA((8,)), DMA((7,)), DMA((7,)), DMA]
        + [DMA((2 + OWN,)), DMA((2, 7)), DMA((2, 7)), DMA((2,)), DMA((2,))]
        + [DMA((2, 7)), DMA((2, 7)), DMA((2,)), DMA((FIRST,)), DMA((FIRST,)), DMA, DMA],
        1,
        "opening",
        vmem=64 * 2**20,
        us=100,
    )(starts, tokens, wq, wk, wv, wo, small, cot, cosine, sine, routes, priority, expert_in, expert_out)


def turning_kernel(
    outers,
    seg_ref,
    z_ref,
    za_ref,
    grad_in,
    part_in,
    pick_send,
    kept_in,
    expert_out,
    gate_ref,
    kept_ref,
    small_ref,
    sum_in,
    cot_in,
    wo_in,
    raw_in,
    total_in,
    q_in,
    kv_in,
    cos_ref,
    sin_ref,
    dy_ref,
    da_ref,
    dq_ref,
    rows_ref,
    moe_o,
    near_o,
    z_o,
    dkv_ref,
    sum_ref,
    cot_ref,
    raw_ref,
    total_ref,
    q_ref,
    part,
    kept_all,
    out_w,
    wout,
    kv,
    near,
    far_in,
    picks_all,
    q_four,
    n_four,
    d_rows,
    dq_acc,
    kv_acc,
    kv_out,
    z_sums,
    z_in,
    y_own,
    y_in,
    za_own,
    za_in,
    ls,
    ss,
    sr,
    xs,
    xr,
    ps,
    pr,
    vs,
    vr,
    us,
    ur,
    ks,
    rs,
    zas,
    zar,
):
    at = Place()
    count = q_ref.shape[0]
    rows = count // 2
    width = PAIRS * 128
    keys = kv.shape[0] * rows
    units = out_w.shape[-1]
    experts = at.q * OWN
    loads = [
        pltpu.make_async_copy(src, dst, ls.at[index])
        for index, (src, dst) in enumerate(
            ((part_in, part), (kept_in, kept_all), (wo_in, wout), (kv_in, kv))
        )
    ]
    weights = [
        pltpu.make_async_copy(expert_out.at[experts + e], out_w.at[e], ls.at[4 + e])
        for e in range(OWN)
    ]
    for copy in loads + weights:
        copy.start()
    z_loads = [
        pltpu.make_async_copy(z_ref.at[:, e], z_sums.at[e, pl.ds(0, outers // 2)], rs.at[5 + e])
        for e in range(FIRST)
    ]
    za_load = pltpu.make_async_copy(za_ref.at[:, at.y], za_own, rs.at[5 + FIRST])
    for copy in z_loads + [za_load]:
        copy.start()
    late = [slice(None)] * FIRST
    if far_first(outers):
        late[0] = pl.ds(units, 2 * units)
    rest = [
        Halving(at, outers, z_sums.at[e], z_in.at[e], vs.at[e], vr.at[e], late[e])
        for e in range(FIRST)
    ]
    own_rows = []
    for e in range(OWN - FIRST):
        copy = pltpu.make_async_copy(
            grad_in.at[e, :, :, at.y], y_own.at[e], ls.at[4 + OWN + e]
        )
        copy.start()
        own_rows.append(copy)
    row_loads = [
        pltpu.make_async_copy(src, dst, rs.at[index])
        for index, (src, dst) in enumerate(
            (
                (sum_in, sum_ref),
                (cot_in, cot_ref),
                (raw_in, raw_ref),
                (total_in, total_ref),
                (q_in, q_ref),
            )
        )
    ]
    for copy in row_loads:
        copy.start()
    starts = doc_starts(seg_ref[...])
    meet(
        [at.relative(*bits)[0] for bits in OTHERS]
        + [at.beside]
        + [rest[0].device(bit) for bit in rest[0].bits]
    )
    for copy in z_loads:
        copy.wait()
    if outers > 2:
        rest[0].start(0)
    if far_first(outers):
        za_send = remote(za_ref.at[:, 1 - at.y], za_in, zas, zar, at.beside)
        za_send.start()
    sib, unused = at.relative(0, 1, 0)
    loads[0].wait()
    first = remote(part.at[:, 1 - at.core], near, ss, sr, sib)
    first.start()
    y_sends = []
    for e in range(OWN - FIRST):
        copy = remote(grad_in.at[e, :, :, 1 - at.y], y_in.at[e], us.at[e], ur.at[e], at.beside)
        copy.start()
        y_sends.append(copy)
    small_copies = []
    for slot, bits in enumerate(OTHERS):
        device, j_to = at.relative(*bits)
        copy = remote(pick_send.at[j_to], picks_all.at[at.j], ps.at[slot], pr.at[slot], device)
        copy.start()
        small_copies.append(copy)
    picks_all[at.j] = pick_send[at.j]
    first.wait_recv()
    for y in range(2):
        for w in range(2):
            total = part[y, at.core, w].astype(F32) + near[y, w].astype(F32)
            near[y, w] = total.astype(BF16)
    second = []
    for slot, (dy, dc, dw) in enumerate(XY):
        device, unused = at.relative(dy, dc, dw)
        z = at.z + dy * (1 - 2 * at.z)
        w = at.w + dw * (1 - 2 * at.w)
        copy = remote(near.at[z, w], far_in.at[slot], xs.at[slot], xr.at[slot], device)
        copy.start()
        second.append(copy)

    loads[1].wait()
    for copy in weights + row_loads:
        copy.wait()

    def moe_rows(j, carry):
        here = pl.ds(pl.multiple_of(j * count, count), count)
        total = dot_nt(kept_all[here, :units], out_w[0])
        for e in range(1, OWN):
            total = total + dot_nt(kept_all[here, e * units : (e + 1) * units], out_w[e])
        moe_o[j] = total.astype(BF16)
        return carry

    lax.fori_loop(0, PLANE, moe_rows, 0)
    hidden_sum = near[at.z, at.w].astype(F32)
    for slot in range(3):
        second[slot].wait_recv()
        hidden_sum = hidden_sum + far_in[slot].astype(F32)
    if outers > 2:
        for halving in rest[1:]:
            halving.start(0)
    for copy in [first] + second:
        copy.wait_send()
    small = small_ref[...]
    gain_two = small[EXPERTS + 1 : EXPERTS + 2].astype(F32)
    for copy in small_copies:
        copy.wait()
    parts = []
    for i in range(INNER):
        parts.append(picks_all[2 * i, pl.ds(0, OWN), :] + picks_all[2 * i + 1, pl.ds(0, OWN), :])
    gate = gate_ref[...]
    gate_grad = kept_ref[...] * jnp.concatenate(parts, axis=0)
    logit_grad = gate * (gate_grad - jnp.sum(gate * gate_grad, axis=0, keepdims=True))
    logit_grad = jnp.concatenate(
        [logit_grad, jnp.zeros((small.shape[0] - EXPERTS, count), F32)], axis=0
    ).astype(BF16)
    hidden_grad = hidden_sum + dot_tn(logit_grad, small)
    first_sum = sum_ref[...]
    scale = lax.rsqrt(jnp.mean(first_sum * first_sum, axis=1, keepdims=True) + EPS)
    normed = first_sum * scale
    hidden = (normed * gain_two).astype(BF16)
    router_rows = dot_nn(logit_grad, hidden)
    rows_ref[...] = router_rows
    rows_ref[pl.ds(EXPERTS + 1, 1), :] = jnp.sum(hidden_grad * normed, axis=0, keepdims=True)
    normed_grad = hidden_grad * gain_two
    first_grad = cot_ref[...].astype(F32) + scale * (
        normed_grad - normed * jnp.mean(normed_grad * normed, axis=1, keepdims=True)
    )
    dy_ref[...] = first_grad
    attn_grad = (RES_MULT * first_grad).astype(BF16)
    da_ref[...] = attn_grad
    loads[2].wait()
    mixed_grad = dot_nt(attn_grad, wout[...]).astype(BF16).astype(F32)
    total = total_ref[...]
    numer = mixed_grad / total
    lost = mixed_grad * raw_ref[...] / total
    for half in range(2):
        here = slice(half * rows, (half + 1) * rows)
        for pair in range(PAIRS):
            cols = slice(pair * 256, (pair + 1) * 256)
            slot = half * PAIRS + pair
            q_four[slot] = spread(q_ref[here, cols].astype(F32) * ATT_MULT).astype(BF16)
            n_four[slot] = spread(numer[here, cols]).astype(BF16)
            d_rows[slot] = -jnp.sum(spread(lost[here, cols]).T, axis=0, keepdims=True)
    dq_acc[...] = jnp.zeros_like(dq_acc)
    loads[3].wait()

    def kv_store(chunk):
        many = CHUNK // rows
        return pltpu.make_async_copy(
            kv_out.at[chunk % 2], dkv_ref.at[pl.ds(chunk * many, many)], ks.at[chunk % 2]
        )

    def step(chunk, carry):
        at_row = pl.multiple_of(chunk * CHUNK, CHUNK)
        kv_acc[...] = jnp.zeros_like(kv_acc)
        key_pos = at_row + lax.broadcasted_iota(jnp.int32, (CHUNK, 1), 0)
        for half in range(2):
            base, chunks = half_span(half, rows, keys)

            @pl.when(chunk < chunks)
            def _():
                place = base + lax.broadcasted_iota(jnp.int32, (1, 4 * rows), 1) % rows
                first = reach(starts, place)
                bias = jnp.where((key_pos >= first) & (key_pos <= place), 0.0, NEVER)
                for pair in range(PAIRS):
                    slot = half * PAIRS + pair
                    key = key_block(kv, chunk, rows, pair * 128)
                    value = key_block(kv, chunk, rows, width + pair * 128)
                    e = jnp.exp(dot_nt(key, q_four[slot]) + bias)
                    through = dot_nt(value, n_four[slot])
                    dz = (e * (through + d_rows[slot])).astype(BF16)
                    kv_acc[:, pl.ds(pair * 128, 128)] += dot_nn(dz, q_four[slot])
                    kv_acc[:, pl.ds(width + pair * 128, 128)] += dot_nn(e.astype(BF16), n_four[slot])
                    dq_acc[slot] += dot_tn(dz, key)

        many = CHUNK // rows

        @pl.when(chunk >= 2)
        def _():
            kv_store(chunk - 2).wait()

        kv_out[chunk % 2] = kv_acc[...].astype(BF16).reshape(many, rows, 2 * width)
        kv_store(chunk).start()
        return carry

    lax.fori_loop(0, keys // CHUNK, step, 0)
    cosine = cos_ref[...]
    sine = -sin_ref[...]
    for half in range(2):
        here = slice(half * rows, (half + 1) * rows)
        for pair in range(PAIRS):
            block = ATT_MULT * unspread(dq_acc[half * PAIRS + pair])
            dq_ref[here, pair * 256 : (pair + 1) * 256] = turn(
                block, cosine[here], sine[here]
            ).astype(BF16)
    for chunk in range(keys // CHUNK - 2, keys // CHUNK):
        kv_store(chunk).wait()
    for e in range(FIRST):
        near_o[e, :, :, late[e]] = rest[e].finish()
    za_load.wait()
    if far_first(outers):
        za_send.wait()
        total = za_own[...].astype(F32) + za_in[...].astype(F32)
        near_o[0, :, :, :units] = total.astype(BF16)
    for copy in own_rows:
        copy.wait()
    for e in range(OWN - FIRST):
        y_sends[e].wait()
        total = y_own[e].astype(F32) + y_in[e].astype(F32)
        z_o[:, e] = total.astype(BF16)


def turning(
    outers, segments, z_first, z_far, grads, part, picks, kept_units, expert_out, gate, kept, small, first_sum, cot, output_w, raw, total, queries, kv_all, cosine, sine
):
    shape = jax.ShapeDtypeStruct
    count, width = queries.shape
    units = expert_out.shape[-1]
    vm = pltpu.VMEM
    return comm_call(
        functools.partial(turning_kernel, outers),
        [
            shape((count, D), F32),
            shape((count, D), BF16),
            shape((count, width), BF16),
            shape((32, D), F32),
            shape((PLANE, count, D), BF16),
            shape(z_first.shape[1:], BF16),
            shape((outers // 2, OWN - FIRST) + z_first.shape[2:], BF16),
            shape(kv_all.shape, BF16),
        ],
        [VMEM] + [ANY] * 4 + [VMEM] + [ANY] * 2 + [VMEM] * 3 + [ANY] * 7 + [VMEM] * 2,
        [VMEM] * 7 + [ANY],
        [
            vm((count, D), F32),
            vm((count, D), BF16),
            vm((count, width), F32),
            vm((count, width), F32),
            vm((count, width), BF16),
            vm((2, 2, 2, count, D), BF16),
            vm(kept_units.shape, BF16),
            vm((OWN, D, units), BF16),
            vm((D, D), BF16),
            vm(kv_all.shape, BF16),
            vm((2, 2, count, D), BF16),
            vm((3, count, D), BF16),
            vm((PLANE, 8, count), F32),
            vm((2 * PAIRS, 2 * count, 128), BF16),
            vm((2 * PAIRS, 2 * count, 128), BF16),
            vm((2 * PAIRS, 1, 2 * count), F32),
            vm((2 * PAIRS, 2 * count, 128), F32),
            vm((CHUNK, 2 * PAIRS * 128), F32),
            vm((2, CHUNK // (count // 2), count // 2, 2 * PAIRS * 128), BF16),
            vm((FIRST, outers) + z_first.shape[2:], BF16),
            vm((FIRST, outers) + z_first.shape[2:], BF16),
            vm((OWN - FIRST, outers // 2) + z_first.shape[2:], BF16),
            vm((OWN - FIRST, outers // 2) + z_first.shape[2:], BF16),
            vm(z_far.shape[:1] + z_far.shape[2:], BF16),
            vm(z_far.shape[:1] + z_far.shape[2:], BF16),
            DMA((4 + OWN + OWN - FIRST,)),
            DMA,
            DMA,
            DMA((3,)),
            DMA((3,)),
            DMA((7,)),
            DMA((7,)),
            DMA((FIRST, outers)),
            DMA((FIRST, outers)),
            DMA((OWN - FIRST,)),
            DMA((OWN - FIRST,)),
            DMA((2,)),
            DMA((6 + FIRST,)),
            DMA,
            DMA,
        ],
        5,
        "turning",
        vmem=62 * 2**20,
        us=35,
    )(
        segments,
        z_first,
        z_far,
        grads,
        part.reshape(2, 2, 2, count, D),
        picks,
        kept_units,
        expert_out,
        gate,
        kept,
        small,
        first_sum,
        cot,
        output_w,
        raw,
        total,
        queries,
        kv_all,
        cosine,
        sine,
    )


def assemble_kernel(outers, counts, *refs):
    size = 2 + len(counts)
    sources, refs = refs[:size], refs[size:]
    wq, wk, wv, wo, router, gain_one, gain_two, inner, outer = refs[:9]
    held, sems = refs[9 : 9 + size], refs[9 + size]
    loads = [
        pltpu.make_async_copy(sources[k], held[k], sems.at[k]) for k in range(size)
    ]
    for copy in loads:
        copy.start()
    attn_in, small_in = held[:2]
    for copy in loads:
        copy.wait()
    experts = [(near, k) for near, many in zip(held[2:], counts) for k in range(many)]
    qkv_cols = wq.shape[1] * 2 // PLANE
    devices = outers * PLANE
    for j in range(PLANE):
        z, core, w = j // 4, (j // 2) % 2, j % 2
        total = 0.0
        for above in range(outers // 2):
            for y in range(2):
                source = (((above * 2 + z) * 2 + y) * 2 + core) * 2 + w
                total = total + attn_in[source].astype(F32)
        col = j * qkv_cols
        ref, base = (wq, 0) if col < 1024 else (wk, 1024) if col < 1536 else (wv, 1536)
        ref[:, col - base : col - base + qkv_cols] = total[:, :qkv_cols]
        wo[:, j * (D // PLANE) : (j + 1) * (D // PLANE)] = total[:, qkv_cols:]
    total = small_in[0].astype(F32)
    for i in range(1, devices):
        total = total + small_in[i].astype(F32)
    turned = total.T
    router[...] = turned[:EXPERTS]
    gain_one[...] = turned[EXPERTS : EXPERTS + 1]
    gain_two[...] = turned[EXPERTS + 1 : EXPERTS + 2]
    rows = wq.shape[0]
    units = outer.shape[-1] // 2
    for j in range(PLANE):
        cols = slice((j % 2) * units, (j % 2 + 1) * units)
        for k in range(OWN):
            e = (j // 2) * OWN + k
            near, at = experts[k]
            block = near[j, at].astype(F32)
            inner[e, :, :, cols] = block[:, : 2 * units].reshape(rows, 2, units)
            outer[e, :, cols] = block[:, 2 * units :]


def assemble(attn_in, small_in, nears, outers):
    rows = attn_in.shape[1]
    units = nears[0].shape[-1] // 3
    sources = [attn_in, small_in] + nears
    shape = jax.ShapeDtypeStruct
    outs = [
        shape((rows, 1024), F32),
        shape((rows, 512), F32),
        shape((rows, 512), F32),
        shape((rows, D), F32),
        shape((EXPERTS, rows), F32),
        shape((1, rows), F32),
        shape((1, rows), F32),
        shape((EXPERTS, rows, 2, 2 * units), F32),
        shape((EXPERTS, rows, 2 * units), F32),
    ]
    return pl.pallas_call(
        functools.partial(assemble_kernel, outers, [near.shape[1] for near in nears]),
        out_shape=outs,
        in_specs=[ANY] * len(sources),
        out_specs=[VMEM] * 9,
        scratch_shapes=[pltpu.VMEM(a.shape, a.dtype) for a in sources] + [DMA((len(sources),))],
        compiler_params=pltpu.CompilerParams(vmem_limit_bytes=60 * 2**20),
        name="assemble",
    )(*sources)


def body(
    tokens,
    w_query,
    w_key,
    w_value,
    w_output,
    attn_gain,
    w_router,
    expert_in,
    expert_out,
    moe_gain,
    segments,
    routes,
    priority,
    cotangent,
):
    ctx_count = lax.axis_size("ctx")
    ctx_index = lax.axis_index("ctx")
    devices = ctx_count * 2
    outers = ctx_count // INNER
    owner_rows = D // devices
    block_rows = tokens.shape[2]
    half_rows = block_rows * ctx_count
    tok_count = 2 * block_rows
    f32 = jnp.float32
    bf16 = jnp.bfloat16

    small = jnp.concatenate(
        [w_router.T, attn_gain[None], moe_gain[None], jnp.zeros((14, w_router.shape[0]), bf16)]
    )
    cot_own = cotangent.reshape(tok_count, D)
    block_total = 2 * ctx_count
    block_ids = jnp.stack([ctx_index, block_total - 1 - ctx_index])
    query_pos = block_ids[:, None] * block_rows + jnp.arange(block_rows, dtype=jnp.int32)[None, :]
    flat_pos = query_pos.reshape(tok_count)
    frequency = jnp.exp(
        -jnp.log(jnp.float32(THETA))
        * jnp.arange(HEAD_DIM // 2, dtype=jnp.float32)
        * (2.0 / HEAD_DIM)
    )
    angles = flat_pos.astype(f32)[:, None] * frequency[None, :]
    cosine, sine = jnp.cos(angles), jnp.sin(angles)
    cosine = jnp.concatenate([cosine] * 4, axis=1)
    sine = jnp.concatenate([-sine, sine] * 2, axis=1)
    token_low = tokens.reshape(tok_count, D)
    (
        qkv_w,
        output_w,
        small_all,
        queries,
        hidden_one,
        kv_all,
        attn_raw,
        attn_total,
        mixed,
        first_sum,
        gate,
        kept,
        picks,
        first_half,
        first_far,
        part,
        kept_units,
        expert_grads,
        left,
    ) = opening(
        segments,
        token_low,
        w_query,
        w_key,
        w_value,
        w_output,
        small,
        cot_own,
        cosine,
        sine,
        routes[0].transpose(0, 2, 1),
        priority[0].transpose(0, 2, 1),
        expert_in,
        expert_out,
        ctx_count,
    )
    (
        first_grad,
        attn_grad,
        query_lin_grad,
        small_rows,
        moe_part,
        near_one,
        second_half,
        kv_terms,
    ) = turning(
        outers,
        segments,
        first_half,
        first_far,
        expert_grads,
        part,
        picks,
        kept_units,
        expert_out,
        gate,
        kept,
        small_all,
        first_sum,
        cot_own,
        output_w,
        attn_raw,
        attn_total,
        queries,
        kv_all,
        cosine,
        sine,
    )
    output, token_grad, attn_part, small_part, near_first, near_next, near = finish(
        kv_terms,
        moe_part,
        [
            first_sum,
            query_lin_grad,
            attn_grad,
            first_grad,
            token_low,
            small_all,
            cosine,
            sine,
            qkv_w,
            left,
            small_rows,
        ],
        second_half,
        near_one.reshape(FIRST, PLANE, owner_rows, -1),
        ctx_count,
    )
    attn_in, small_in, near_last = owners(
        [attn_part, small_part],
        [near.reshape(-1, PLANE, owner_rows, near.shape[-1])],
        devices,
        7,
        "owners",
    )
    (
        query_sum,
        key_sum,
        value_sum,
        output_sum,
        router_sum,
        gain_one_sum,
        gain_two_sum,
        inner_sum,
        outer_sum,
    ) = assemble(attn_in, small_in, [near_first, near_next, near_last], outers)
    return (
        output.reshape(tokens.shape),
        token_grad.reshape(tokens.shape),
        query_sum,
        key_sum,
        value_sum,
        output_sum,
        gain_one_sum[0],
        router_sum.T,
        inner_sum,
        outer_sum,
        gain_two_sum[0],
    )


def solution(mesh):
    placed = (
        P("wsh", None, "ctx", None),
        P("wsh", None),
        P("wsh", None),
        P("wsh", None),
        P("wsh", None),
        P("wsh"),
        P("wsh", None),
        P(None, None, None, "wsh"),
        P(None, None, "wsh"),
        P("wsh"),
        P("wsh", None),
        P("wsh", None, "ctx", None),
        P("wsh", None, "ctx", None),
        P("wsh", None, "ctx", None),
    )
    return jax.shard_map(
        body,
        mesh=mesh,
        in_specs=placed,
        out_specs=(
            P("wsh", None, "ctx", None),
            P("wsh", None, "ctx", None),
            P(("ctx", "wsh"), None),
            P(("ctx", "wsh"), None),
            P(("ctx", "wsh"), None),
            P(("ctx", "wsh"), None),
            P(("ctx", "wsh")),
            P(("ctx", "wsh"), None),
            P(None, ("ctx", "wsh"), None, None),
            P(None, ("ctx", "wsh"), None),
            P(("ctx", "wsh")),
        ),
        check_vma=False,
    )
```

```python
import functools

import jax
import jax.numpy as jnp
from jax import lax
from jax.experimental import pallas as pl
from jax.experimental.pallas import tpu as pltpu
from jax.sharding import PartitionSpec as P

D = 1024
HEADS = 16
KV_HEADS = 8
HEAD_DIM = 64
TOPK = 8
EXPERTS = 16
CAP = 80
PLANE = 8
INNER = 4
OWN = EXPERTS // INNER
PIECES = 2
FIRST = OWN // 2


RES_MULT = 0.22
ATT_MULT = 0.015625
EPS = 1e-06
THETA = 10000.0

MESH = pl.DeviceIdType.MESH
F32 = jnp.float32
BF16 = jnp.bfloat16
ANY = pl.BlockSpec(memory_space=pl.ANY)
VMEM = pl.BlockSpec(memory_space=pltpu.VMEM)


class Place:
    def __init__(self):
        self.c = lax.axis_index("ctx")
        self.w = lax.axis_index("wsh")
        self.core = self.c % 2
        self.y = (self.c // 2) % 2
        self.inner = self.c % INNER
        self.outer = self.c // INNER
        self.z = self.outer % 2
        self.q = self.z * 2 + self.core
        self.j = self.q * 2 + self.w
        self.beside = (self.c + 2 - 4 * self.y, self.w)

    def relative(self, dz, dc, dw):
        z = self.z + dz * (1 - 2 * self.z)
        core = self.core + dc * (1 - 2 * self.core)
        w = self.w + dw * (1 - 2 * self.w)
        ctx = self.c + INNER * (z - self.z) + core - self.core
        return (ctx, w), (z * 2 + core) * 2 + w


OTHERS = [(a, b, d) for a in range(2) for b in range(2) for d in range(2) if a + b + d]
XY = [(0, 0, 1), (1, 0, 0), (1, 0, 1)]


def meet(devices):
    barrier = pltpu.get_barrier_semaphore()
    for device in devices:
        pl.semaphore_signal(barrier, inc=1, device_id=device, device_id_type=MESH)
    pl.semaphore_wait(barrier, len(devices))


def remote(src, dst, send, recv, device):
    return pltpu.make_async_remote_copy(
        src_ref=src,
        dst_ref=dst,
        send_sem=send,
        recv_sem=recv,
        device_id=device,
        device_id_type=MESH,
    )


def comm_call(kernel, out_shape, in_specs, out_specs, scratch, ident, name, vmem=None, us=20):
    return pl.pallas_call(
        kernel,
        out_shape=out_shape,
        in_specs=in_specs,
        out_specs=out_specs,
        scratch_shapes=scratch,
        compiler_params=pltpu.CompilerParams(
            collective_id=ident, has_side_effects=True, vmem_limit_bytes=vmem
        ),
        cost_estimate=pl.CostEstimate(
            flops=us * 10**9, bytes_accessed=us * 3 * 2**20, transcendentals=0
        ),
        name=name,
    )


DMA = pltpu.SemaphoreType.DMA


def room(arrays, scratch=(), spare=12):
    total = 0
    for array in list(arrays) + list(scratch):
        inner = getattr(array, "inner_aval", array)
        size = jnp.dtype(inner.dtype).itemsize
        for extent in inner.shape:
            size *= extent
        total += size
    return min(total + spare * 2**20, 62 * 2**20)


def far_first(outers):
    return outers == 4


def far_partner(at):
    return (at.c + INNER * 2 * (1 - 2 * (at.outer // 2)), at.w)


class Halving:
    def __init__(self, at, outers, sums, arrived, send, recv, cols=slice(None)):
        self.cols = cols
        self.at, self.sums, self.arrived = at, sums, arrived
        self.send, self.recv = send, recv
        self.bits = [2**k for k in range(1, outers.bit_length() - 1)]
        self.levels = [(0, outers // 2)]
        for bit in self.bits:
            start, many = self.levels[-1]
            self.levels.append((start + many, many // 2))
        self.copies = []

    def pick(self, index):
        return index, slice(None), slice(None), self.cols

    def device(self, bit):
        at = self.at
        return (at.c + INNER * bit * (1 - 2 * ((at.outer // bit) % 2)), at.w)

    def start(self, step):
        bit = self.bits[step]
        side = (self.at.outer // bit) % 2
        start, many = self.levels[step]
        for m in range(many // 2):
            copy = remote(
                self.sums.at[self.pick(start + 2 * m + 1 - side)],
                self.arrived.at[self.pick(start + m)],
                self.send.at[start + m],
                self.recv.at[start + m],
                self.device(bit),
            )
            copy.start()
            self.copies.append(copy)

    def add(self, step):
        side = (self.at.outer // self.bits[step]) % 2
        start, many = self.levels[step]
        after, half = self.levels[step + 1]
        for m in range(half):
            self.copies[len(self.copies) - half + m].wait_recv()
            total = self.sums[self.pick(start + 2 * m + side)].astype(F32)
            total = total + self.arrived[self.pick(start + m)].astype(F32)
            self.sums[self.pick(after + m)] = total.astype(BF16)

    def finish(self):
        for step in range(len(self.bits)):
            if step > 0:
                self.start(step)
            self.add(step)
        for copy in self.copies:
            copy.wait_send()
        return self.sums[self.pick(self.levels[-1][0])]


def gather_start(at, pairs, send, recv, local):
    copies = []
    for index, (src, dst) in enumerate(pairs):
        keep = pltpu.make_async_copy(src, dst.at[at.j], local.at[index])
        keep.start()
        sends = []
        for slot, bits in enumerate(XY + [(0, 1, 0)]):
            device, unused = at.relative(*bits)
            copy = remote(src, dst.at[at.j], send.at[index, slot], recv.at[index, slot], device)
            copy.start()
            sends.append(copy)
        copies.append((keep, sends))
    return copies


def gather_pass(at, pairs, copies, send, recv):
    sib, unused = at.relative(0, 1, 0)
    passed = []
    for slot, bits in enumerate(XY):
        unused, j_from = at.relative(*bits)
        for index, (src, dst) in enumerate(pairs):
            copies[index][1][slot].wait_recv()
            block = dst.at[j_from]
            copy = remote(
                block, block, send.at[index, 4 + slot], recv.at[index, 4 + slot], sib
            )
            copy.start()
            passed.append(copy)
    return passed


def gather_wait(copies, passed):
    for keep, sends in copies:
        keep.wait()
        sends[3].wait_recv()
        for copy in sends:
            copy.wait_send()
    for copy in passed:
        copy.wait()


def turn(values, cosine, sine):
    lane = lax.broadcasted_iota(jnp.int32, cosine.shape, 1)
    first = lane % HEAD_DIM < HEAD_DIM // 2
    blocks = []
    for start in range(0, values.shape[1], 128):
        u = values[:, start : start + 128]
        swapped = jnp.where(first, pltpu.roll(u, 96, 1), pltpu.roll(u, 32, 1))
        blocks.append(u * cosine + swapped * sine)
    return jnp.concatenate(blocks, axis=1)


def dot_nt(a, b):
    return lax.dot_general(a, b, (((1,), (1,)), ((), ())), preferred_element_type=F32)


def dot_tn(a, b):
    return lax.dot_general(a, b, (((0,), (0,)), ((), ())), preferred_element_type=F32)


def dot_nn(a, b):
    return jnp.dot(a, b, preferred_element_type=F32)


def owners_kernel(devices, count, near_count, *refs):
    total = count + near_count
    parts, nears = refs[:count], refs[count:total]
    outs, near_outs = refs[total : total + count], refs[total + count : 2 * total]
    send, recv, local, nsend, nrecv, nlocal = refs[2 * total :]
    at = Place()
    me = at.c * 2 + at.w
    rows = D // devices

    def device_of(r):
        index = lax.rem(me + r, devices)
        return index, (index // 2, lax.rem(index, 2))

    def rows_of(ref, index):
        return ref.at[pl.ds(pl.multiple_of(index * rows, rows), rows), :]

    barrier = pltpu.get_barrier_semaphore()

    def greet(r, carry):
        unused, device = device_of(r)
        pl.semaphore_signal(barrier, inc=1, device_id=device, device_id_type=MESH)
        return carry

    lax.fori_loop(1, devices, greet, 0)
    pl.semaphore_wait(barrier, devices - 1)

    def copy_of(k, r):
        index, device = device_of(r)
        return remote(rows_of(parts[k], index), outs[k].at[me], send.at[k, r], recv.at[k, r], device)

    def start(r, carry):
        for k in range(count):
            copy_of(k, r).start()
        return carry

    near_copies = []
    for k in range(near_count):
        for slot, bits in enumerate(OTHERS):
            device, j_to = at.relative(*bits)
            copy = remote(
                nears[k].at[:, j_to], near_outs[k].at[at.j], nsend.at[k, slot], nrecv.at[k, slot], device
            )
            copy.start()
            near_copies.append(copy)
    lax.fori_loop(1, devices, start, 0)

    keeps = []
    for k in range(count):
        keep = pltpu.make_async_copy(rows_of(parts[k], me), outs[k].at[me], local.at[k])
        keep.start()
        keeps.append(keep)
    for k in range(near_count):
        keep = pltpu.make_async_copy(nears[k].at[:, at.j], near_outs[k].at[at.j], nlocal.at[k])
        keep.start()
        keeps.append(keep)

    def finish(r, carry):
        for k in range(count):
            copy_of(k, r).wait()
        return carry

    lax.fori_loop(1, devices, finish, 0)
    for copy in near_copies:
        copy.wait()
    for keep in keeps:
        keep.wait()


def owners(parts, nears, devices, ident, name):
    count, near_count = len(parts), len(nears)
    rows = D // devices
    shape = jax.ShapeDtypeStruct
    shapes = [shape((devices, rows, part.shape[-1]), part.dtype) for part in parts]
    for near in nears:
        lead, members, near_rows, width = near.shape
        shapes.append(shape((members, lead, near_rows, width), near.dtype))
    return comm_call(
        functools.partial(owners_kernel, devices, count, near_count),
        shapes,
        [ANY] * (count + near_count),
        [VMEM] * (count + near_count),
        [
            DMA((count, devices)),
            DMA((count, devices)),
            DMA((count,)),
            DMA((near_count, 7)),
            DMA((near_count, 7)),
            DMA((near_count,)),
        ],
        ident,
        name,
        vmem=60 * 2**20,
    )(*parts, *nears)


CHUNK = 256
PAIRS = KV_HEADS // 2
NEVER = -1e30


def low_lanes(shape):
    return lax.broadcasted_iota(jnp.int32, shape, 1) < HEAD_DIM


def spread(block):
    a, b = block[:, :128], block[:, 128:]
    low = low_lanes(a.shape)
    zero = jnp.zeros_like(a)
    return jnp.concatenate(
        [
            jnp.where(low, a, zero),
            jnp.where(low, pltpu.roll(a, HEAD_DIM, 1), zero),
            jnp.where(low, zero, pltpu.roll(b, HEAD_DIM, 1)),
            jnp.where(low, zero, b),
        ],
        axis=0,
    )


def unspread(four):
    rows = four.shape[0] // 4
    r0, r1, r2, r3 = (four[k * rows : (k + 1) * rows] for k in range(4))
    low = low_lanes(r0.shape)
    return jnp.concatenate(
        [
            jnp.where(low, r0, pltpu.roll(r1, HEAD_DIM, 1)),
            jnp.where(low, pltpu.roll(r2, HEAD_DIM, 1), r3),
        ],
        axis=1,
    )


DOCS = 8


def doc_starts(segments):
    return [
        jnp.sum(jnp.where(segments < d, 1.0, 0.0), axis=1, keepdims=True).astype(jnp.int32)
        for d in range(DOCS)
    ]


def reach(starts, place):
    first = jnp.zeros_like(place)
    for d in range(1, DOCS):
        first = jnp.where(place >= starts[d], starts[d], first)
    return first


def half_span(half, rows, keys):
    block = lax.axis_index("ctx")
    if half == 1:
        block = keys // rows - 1 - block
    base = block * rows
    return base, (base + rows + CHUNK - 1) // CHUNK


def key_block(kv, chunk, rows, col):
    many = CHUNK // rows
    picked = kv[pl.ds(chunk * many, many), :, pl.ds(col, 128)]
    return picked.reshape(CHUNK, 128)


def attend_rows(
    starts,
    q_ref,
    kv_ref,
    tok_ref,
    wo_ref,
    small_ref,
    route_ref,
    prio_ref,
    raw_ref,
    total_ref,
    mixed_ref,
    sum_ref,
    hid_ref,
    gate_ref,
    kept_ref,
    send_ref,
    acc,
    acc_l,
):
    rows = q_ref.shape[0] // 2
    width = PAIRS * 128
    keys = kv_ref.shape[0] * rows
    for half in range(2):
        base, chunks = half_span(half, rows, keys)
        q_four = []
        for pair in range(PAIRS):
            block = q_ref[pl.ds(half * rows, rows), pl.ds(pair * 256, 256)].astype(F32) * ATT_MULT
            q_four.append(spread(block).astype(BF16))
        acc[...] = jnp.zeros_like(acc)
        acc_l[...] = jnp.zeros_like(acc_l)
        place = base + lax.broadcasted_iota(jnp.int32, (rows, 1), 0)
        first = reach(starts, place)

        def step(chunk, carry):
            at_row = pl.multiple_of(chunk * CHUNK, CHUNK)
            key_pos = at_row + lax.broadcasted_iota(jnp.int32, (1, CHUNK), 1)
            bias = jnp.where((key_pos >= first) & (key_pos <= place), 0.0, NEVER)
            bias = jnp.concatenate([bias] * 4, axis=0)
            for pair in range(PAIRS):
                key = key_block(kv_ref, chunk, rows, pair * 128)
                value = key_block(kv_ref, chunk, rows, width + pair * 128)
                e = jnp.exp(dot_nt(q_four[pair], key) + bias)
                part = e[:, :128]
                for k in range(1, CHUNK // 128):
                    part = part + e[:, k * 128 : (k + 1) * 128]
                acc_l[pair] += part
                acc[pair] += dot_nn(e.astype(BF16), value)
            return carry

        lax.fori_loop(0, chunks, step, 0)
        for pair in range(PAIRS):
            total = jnp.sum(acc_l[pair], axis=1, keepdims=True)
            total = jnp.broadcast_to(total, (4 * rows, 128))
            here = pl.ds(half * rows, rows), pl.ds(pair * 256, 256)
            raw_ref[here] = unspread(acc[pair] / total)
            total_ref[here] = unspread(total)
    mixed = raw_ref[...].astype(BF16)
    mixed_ref[...] = mixed
    first_sum = tok_ref[...].astype(F32) + RES_MULT * dot_nn(mixed, wo_ref[...])
    sum_ref[...] = first_sum
    scale = lax.rsqrt(jnp.mean(first_sum * first_sum, axis=1, keepdims=True) + EPS)
    gain_two = small_ref[pl.ds(EXPERTS + 1, 1), :].astype(F32)
    hidden = (first_sum * scale * gain_two).astype(BF16)
    hid_ref[...] = hidden

    logits = dot_nt(small_ref[...], hidden)[:EXPERTS]
    count = 2 * rows
    expert = lax.broadcasted_iota(jnp.int32, (EXPERTS, count), 0)
    routed = jnp.zeros((EXPERTS, count), F32)
    prio = jnp.zeros((EXPERTS, count), F32)
    for k in range(TOPK):
        line = [
            jnp.concatenate([ref[0, pl.ds(k, 1), :], ref[1, pl.ds(k, 1), :]], axis=1)
            for ref in (route_ref, prio_ref)
        ]
        same = expert == line[0]
        routed = jnp.where(same, 1.0, routed)
        prio = jnp.where(same, line[1].astype(F32), prio)
    chosen = routed > 0.0
    order = lax.broadcasted_iota(jnp.int32, (EXPERTS, count), 1).astype(F32)
    key = jnp.where(chosen, prio * float(count) + order, 65536.0 * count)
    key_cols = jnp.concatenate([key, jnp.zeros((count - EXPERTS, count), F32)], axis=0).T
    ranks = []
    for e in range(EXPERTS):
        ahead = jnp.where(key_cols[:, e : e + 1] < key[e : e + 1, :], 1.0, 0.0)
        ranks.append(jnp.sum(ahead, axis=0, keepdims=True))
    rank = jnp.concatenate(ranks, axis=0)
    top = jnp.max(jnp.where(chosen, logits, -3e38), axis=0, keepdims=True)
    weight = jnp.where(chosen, jnp.exp(logits - top), 0.0)
    gate = weight / jnp.sum(weight, axis=0, keepdims=True)
    kept = jnp.where(chosen & (rank < CAP), 1.0, 0.0)
    gate_ref[...] = gate
    kept_ref[...] = kept
    send_ref[...] = gate * kept


SMEM = pl.BlockSpec(memory_space=pltpu.SMEM)


def finish_kernel(
    outers,
    part,
    moe,
    sum_ref,
    dq_ref,
    da_ref,
    dy_ref,
    tok_ref,
    small_ref,
    cos_ref,
    sin_ref,
    wqkv_in,
    left_in,
    rows_ref,
    z_ref,
    near_in,
    out_ref,
    token_ref,
    attn_ref,
    small_o,
    near_o,
    next_o,
    z_o,
    wqkv_ref,
    left_ref,
    z_sums,
    z_in_rows,
    own,
    half_in,
    y_in,
    z_in,
    m_own,
    m_near,
    m_x,
    m_y,
    qkv,
    swap,
    swapped,
    ss,
    sr,
    ys,
    yr,
    zs,
    zr,
    ns,
    nr,
    ws,
    wr,
    vs,
    vr,
    ls,
    os,
    ps,
    pr,
    qs,
    qr,
):
    at = Place()
    blocks, rows, full = part.shape
    loads = [
        pltpu.make_async_copy(wqkv_in, wqkv_ref, ls.at[0]),
        pltpu.make_async_copy(left_in, left_ref, ls.at[1]),
    ]
    moe_load = pltpu.make_async_copy(moe.at[:, at.core], m_own, ls.at[2])
    near_keep = pltpu.make_async_copy(near_in.at[:, at.j], near_o.at[at.j], ls.at[3])
    z_loads = [
        pltpu.make_async_copy(
            z_ref.at[:, e], z_sums.at[e, pl.ds(0, outers // 2)], ls.at[4 + e]
        )
        for e in range(z_sums.shape[0])
    ]
    for copy in z_loads + [moe_load] + loads + [near_keep]:
        copy.start()
    width = full // 2
    cuts = 4
    step_width = full // cuts
    count = 2 * rows
    sib, unused = at.relative(0, 1, 0)
    side = at.beside
    along_to, unused = at.relative(1, 0, 0)
    across, unused = at.relative(0, 0, 1)
    other = [lax.rem(at.outer + r, outers) for r in range(outers)]
    far = [(other[r] * INNER + at.inner, at.w) for r in range(1, outers)]
    rest = [
        Halving(at, outers, z_sums.at[e], z_in_rows.at[e], vs.at[e], vr.at[e])
        for e in range(z_sums.shape[0])
    ]
    meet([at.relative(*bits)[0] for bits in OTHERS] + far + [at.beside])
    for copy in z_loads:
        copy.wait()
    if outers > 2:
        rest[0].start(0)

    def own_block(half, o, y, core):
        index = (o * 2 + y) * 2 + core
        return index if half == 0 else blocks - 1 - index

    own_loads = []
    for y in range(2):
        for h in range(2):
            for o in range(outers):
                copy = pltpu.make_async_copy(
                    part.at[own_block(h, o, y, at.core)], own.at[y, h, o], os.at[y, h, o]
                )
                copy.start()
                own_loads.append(copy)
    first = {}
    for k in range(cuts):
        cols = pl.ds(k * step_width, step_width)
        for y in range(2):
            for h in range(2):
                for o in range(outers):
                    copy = remote(
                        part.at[own_block(h, o, y, 1 - at.core), :, cols],
                        half_in.at[y, h, o, :, cols],
                        ss.at[k, y, h, o],
                        sr.at[k, y, h, o],
                        sib,
                    )
                    copy.start()
                    first[k, y, h, o] = copy
    nears = []
    for slot, bits in enumerate(OTHERS):
        device, j_to = at.relative(*bits)
        copy = remote(near_in.at[:, j_to], near_o.at[at.j], ps.at[slot], pr.at[slot], device)
        copy.start()
        nears.append(copy)
    near = remote(moe.at[:, 1 - at.core], m_near, ns.at[0], nr.at[0], sib)
    near.start()
    for copy in own_loads:
        copy.wait()
    second = []
    for k in range(cuts):
        cols = pl.ds(k * step_width, step_width)
        for y in range(2):
            for h in range(2):
                for o in range(outers):
                    first[k, y, h, o].wait_recv()
                    total = own[y, h, o, :, cols].astype(F32) + half_in[
                        y, h, o, :, cols
                    ].astype(F32)
                    half_in[y, h, o, :, cols] = total.astype(BF16)
        copy = remote(
            half_in.at[1 - at.y, :, :, :, cols], y_in.at[:, :, :, cols], ys.at[k], yr.at[k], side
        )
        copy.start()
        second.append(copy)
    near.wait_recv()
    moe_load.wait()
    for y in range(2):
        for w in range(2):
            total = m_own[y, w].astype(F32) + m_near[y, w].astype(F32)
            m_near[y, w] = total.astype(BF16)
    cross = remote(m_near.at[:, 1 - at.w], m_x, ns.at[1], nr.at[1], across)
    cross.start()
    third = []

    def z_send(k):
        cols = pl.ds(k * step_width, step_width)
        second[k].wait_recv()
        for o in range(outers):
            for h in range(2):
                total = half_in[at.y, h, o, :, cols].astype(F32) + y_in[h, o, :, cols].astype(F32)
                half_in[at.y, h, o, :, cols] = total.astype(BF16)
        for r in range(1, outers):
            copy = remote(
                half_in.at[at.y, :, other[r], :, cols],
                z_in.at[r, :, :, cols],
                zs.at[k, r],
                zr.at[k, r],
                far[r - 1],
            )
            copy.start()
            third.append(copy)

    z_send(0)
    z_send(1)
    cross.wait_recv()
    for y in range(2):
        total = m_near[y, at.w].astype(F32) + m_x[y].astype(F32)
        m_x[y] = total.astype(BF16)
    along = remote(m_x.at[1 - at.z], m_y, ns.at[2], nr.at[2], along_to)
    along.start()
    for k in range(2, cuts):
        z_send(k)
    qkv[:, : HEADS * HEAD_DIM] = dq_ref[...]
    along.wait_recv()
    moe_sum = m_x[at.z].astype(F32) + m_y[...].astype(F32)
    out_ref[...] = (sum_ref[...] + RES_MULT * moe_sum).astype(BF16)
    tok = tok_ref[...].astype(F32)
    scale = lax.rsqrt(jnp.mean(tok * tok, axis=1, keepdims=True) + EPS)
    normed = tok * scale
    gain_one = small_ref[pl.ds(EXPERTS, 1), :].astype(F32)
    for copy in third:
        copy.wait_recv()
    if outers > 2:
        for halving in rest[1:]:
            halving.start(0)
    rest[0].finish()
    level = rest[0].levels[-1][0]
    owner_rows = next_o.shape[2]

    def rows_of(j):
        within = pl.multiple_of(lax.rem(j, 4) * owner_rows, owner_rows)
        return 0, level, j // 4, pl.ds(within, owner_rows)

    for slot, bits in enumerate(OTHERS):
        device, j_to = at.relative(*bits)
        copy = remote(
            z_sums.at[rows_of(j_to)], next_o.at[at.j, 0], qs.at[slot], qr.at[slot], device
        )
        copy.start()
        nears.append(copy)
    next_o[at.j, 0] = z_sums[rows_of(at.j)]
    cosine = cos_ref[...]
    sine = -sin_ref[...]
    base = HEADS * HEAD_DIM
    for h in range(2):
        here = slice(h * rows, (h + 1) * rows)
        total = half_in[at.y, h, at.outer].astype(F32)
        for r in range(1, outers):
            total = total + z_in[r, h].astype(F32)
        qkv[here, base : base + width] = turn(total[:, :width], cosine[here], sine[here]).astype(BF16)
        qkv[here, base + width :] = total[:, width:].astype(BF16)
    wide = full * 2 // PLANE
    for j in range(PLANE):
        swap[j, :, :wide] = qkv[:, j * wide : (j + 1) * wide]
        swap[j, :, wide:] = da_ref[:, j * (D // PLANE) : (j + 1) * (D // PLANE)]
    swaps = []
    for slot, bits in enumerate(OTHERS):
        device, j_to = at.relative(*bits)
        copy = remote(swap.at[j_to], swapped.at[at.j], ws.at[slot], wr.at[slot], device)
        copy.start()
        swaps.append(copy)
    swapped[at.j] = swap[at.j]
    for copy in loads:
        copy.wait()
    hidden_grad = dot_nt(qkv[...], wqkv_ref[...])
    small = rows_ref[...]
    gain_grad = jnp.sum(hidden_grad * normed, axis=0, keepdims=True)
    line = lax.broadcasted_iota(jnp.int32, small.shape, 0)
    small = jnp.where(line == EXPERTS, gain_grad, small)
    small = jnp.concatenate([small, jnp.zeros((128 - small.shape[0], D), F32)], axis=0)
    small_o[...] = small.T.astype(BF16)
    hidden_grad = hidden_grad * gain_one
    token_ref[...] = dy_ref[...] + scale * (
        hidden_grad - normed * jnp.mean(hidden_grad * normed, axis=1, keepdims=True)
    )
    for copy in swaps:
        copy.wait_recv()
    all_rows = PLANE * count
    left_one = left_ref[0].reshape(all_rows, D)
    left_mixed = left_ref[1].reshape(all_rows, D)
    grads = swapped[...].reshape(all_rows, wide + D // PLANE)
    attn_ref[:, :wide] = dot_tn(left_one, grads[:, :wide]).astype(BF16)
    attn_ref[:, wide:] = dot_tn(left_mixed, grads[:, wide:]).astype(BF16)
    for e in range(1, len(rest)):
        z_o[e - 1] = rest[e].finish()
    near_keep.wait()
    for copy in nears:
        copy.wait()
    for copy in list(first.values()) + second + third + swaps + [near, cross, along]:
        copy.wait_send()


def finish(part, moe, arrays, z_half, near, ctx_count):
    outers = ctx_count // INNER
    blocks, rows, full = part.shape
    count = 2 * rows
    shape = jax.ShapeDtypeStruct
    columns = 3 * D // PLANE
    return comm_call(
        functools.partial(finish_kernel, outers),
        [
            shape((count, D), BF16),
            shape((count, D), F32),
            shape((D, columns), BF16),
            shape((D, 128), BF16),
            shape((PLANE, near.shape[0]) + near.shape[2:], BF16),
            shape((PLANE, 1) + near.shape[2:], BF16),
            shape((z_half.shape[1] - 1,) + z_half.shape[2:], BF16),
        ],
        [ANY] * 2 + [VMEM] * (len(arrays) - 3) + [ANY] * 2 + [VMEM] + [ANY] * 2,
        [VMEM] * 7,
        [
            pltpu.VMEM((D, 2 * full), BF16),
            pltpu.VMEM((2, PLANE, count, D), BF16),
            pltpu.VMEM((z_half.shape[1], outers) + z_half.shape[2:], BF16),
            pltpu.VMEM((z_half.shape[1], outers) + z_half.shape[2:], BF16),
            pltpu.VMEM((2, 2, outers, rows, full), BF16),
            pltpu.VMEM((2, 2, outers, rows, full), BF16),
            pltpu.VMEM((2, outers, rows, full), BF16),
            pltpu.VMEM((outers, 2, rows, full), BF16),
            pltpu.VMEM((2, 2, count, D), BF16),
            pltpu.VMEM((2, 2, count, D), BF16),
            pltpu.VMEM((2, count, D), BF16),
            pltpu.VMEM((count, D), BF16),
            pltpu.VMEM((count, 2 * full), BF16),
            pltpu.VMEM((PLANE, count, columns), BF16),
            pltpu.VMEM((PLANE, count, columns), BF16),
            DMA((4, 2, 2, outers)),
            DMA((4, 2, 2, outers)),
            DMA((4,)),
            DMA((4,)),
            DMA((4, outers)),
            DMA((4, outers)),
            DMA((3,)),
            DMA((3,)),
            DMA((7,)),
            DMA((7,)),
            DMA((z_half.shape[1], outers)),
            DMA((z_half.shape[1], outers)),
            DMA((4 + z_half.shape[1],)),
            DMA((2, 2, outers)),
            DMA((7,)),
            DMA((7,)),
            DMA((7,)),
            DMA((7,)),
        ],
        3,
        "finish",
        vmem=63 * 2**20,
        us=60,
    )(part, moe.reshape(2, 2, 2, count, D), *arrays, z_half, near)


def gate_columns(gates, cols):
    count = gates.shape[-1]
    for j in range(PLANE):
        block = jnp.concatenate([gates[j], jnp.zeros((128 - EXPERTS, count), F32)], axis=0)
        cols[pl.ds(j * count, count), :] = block.T


def expert_step(both, back_act, gate, units):
    gv, uv = both[:, :units], both[:, units:]
    sig = jax.nn.sigmoid(gv)
    silu = gv * sig
    act = silu * uv
    pick = jnp.sum(act * back_act, axis=1, keepdims=True)
    kept = (gate * act).astype(BF16)
    back_act = gate * back_act
    slope = sig * (1.0 + gv * (1.0 - sig))
    low = jnp.concatenate([back_act * uv * slope, back_act * silu], axis=1).astype(BF16)
    return kept, pick, low


def lane_of(cols, lane):
    at = lax.broadcasted_iota(jnp.int32, cols.shape, 1)
    return jnp.sum(jnp.where(at == lane, cols, 0.0), axis=1, keepdims=True)


def opening_kernel(
    outers,
    seg_ref,
    tok_ref,
    wq,
    wk,
    wv,
    wo,
    small,
    cot,
    cos_ref,
    sin_ref,
    route_ref,
    prio_ref,
    expert_in,
    expert_out,
    wqkv_o,
    wo_o,
    small_o,
    q_o,
    hid_o,
    kv_o,
    raw_o,
    total_o,
    mixed_o,
    sum_o,
    gate_o,
    kept_o,
    pick_o,
    z_o,
    za_o,
    part_o,
    kept_units_o,
    grad_o,
    left_o,
    wqkv,
    wout,
    own,
    tok_v,
    cos_v,
    sin_v,
    kv,
    cot_v,
    raw,
    out_w,
    inner_w,
    acc,
    acc_l,
    hid_two,
    gate_send,
    hid,
    gates,
    cot_t,
    backs,
    cols,
    pick_cols,
    staged,
    y_in,
    za_in,
    xs,
    xr,
    fs,
    fr,
    ls,
    zs,
    zr,
    ys,
    yr,
    cs,
    cr,
    hs,
    gs,
    gr,
    gl,
    es,
    ts,
    tr,
    tl,
    gd,
    us,
    ur,
    ul,
    vs,
    vr,
    fas,
    far_r,
):
    at = Place()
    blocks, rows = kv.shape[:2]
    units = out_w.shape[-1]
    experts = at.q * OWN
    sib, unused = at.relative(0, 1, 0)
    partner, j_partner = at.relative(0, 0, 1)
    side, j_side = at.relative(1, 0, 0)
    unused, j_cross = at.relative(1, 0, 1)
    steps = sorted({1, outers - 1})
    far = [(lax.rem(at.outer + r, outers) * INNER + at.inner, at.w) for r in steps]
    expert_loads = {}

    def load_expert(e):
        copy = pltpu.make_async_copy(expert_in.at[experts + e], raw.at[e % 2], es.at[e % 2])
        copy.start()
        expert_loads[e] = copy

    def shape_expert(e):
        expert_loads[e].wait()
        inner_w[:, e * 2 * units : (e + 1) * 2 * units] = raw[e % 2].reshape(D, 2 * units)
        if e + 2 < OWN:
            load_expert(e + 2)

    out_loads = [
        pltpu.make_async_copy(expert_out.at[experts + e], out_w.at[e], es.at[2 + e])
        for e in range(OWN)
    ]
    for copy in out_loads:
        copy.start()
    load_expert(0)
    load_expert(1)
    meet(
        [at.relative(*bits)[0] for bits in XY + [(0, 1, 0)]] + far + [at.beside]
        + ([far_partner(at)] if far_first(outers) else [])
    )

    pieces = [(wk, wqkv, 1024), (wv, wqkv, 1536), (wq, wqkv, 0), (wo, wout, 0)]
    sends, passed, keeps = {}, {}, []

    def give(index):
        src, dst, col = pieces[index]
        depth, width = src.shape
        half = depth // 2
        copy = remote(
            src.at[pl.ds(at.core * half, half), :],
            dst.at[pl.ds(at.w * depth + at.core * half, half), pl.ds(col, width)],
            xs.at[index],
            xr.at[index],
            partner,
        )
        copy.start()
        sends[index] = copy

    def pass_on(index):
        src, dst, col = pieces[index]
        depth, width = src.shape
        half = depth // 2
        sends[index].wait_recv()
        piece = dst.at[pl.ds((1 - at.w) * depth + at.core * half, half), pl.ds(col, width)]
        copy = remote(piece, piece, fs.at[index], fr.at[index], sib)
        copy.start()
        passed[index] = copy

    wide = small.shape[1]
    mine = small_o.at[:, pl.ds(at.w * wide, wide)]
    gains = remote(small, mine, xs.at[4], xr.at[4], partner)
    gains.start()
    give(0)
    give(1)
    cot_sib = remote(cot, cot_v.at[at.j], gs.at[0], gr.at[0], sib)
    cot_sib.start()
    cot_side = remote(cot, cot_v.at[at.j], gs.at[1], gr.at[1], side)
    cot_side.start()
    cot_keep = pltpu.make_async_copy(cot, cot_v.at[at.j], gl)
    cot_keep.start()
    for index, (src, dst, col) in enumerate(pieces):
        depth, width = src.shape
        keep = pltpu.make_async_copy(
            src, dst.at[pl.ds(at.w * depth, depth), pl.ds(col, width)], ls.at[index]
        )
        keep.start()
        keeps.append(keep)
    loads = [
        pltpu.make_async_copy(src, dst, hs.at[4 + index])
        for index, (src, dst) in enumerate(
            ((tok_ref, tok_v), (cos_ref, cos_v), (sin_ref, sin_v), (small, mine))
        )
    ]
    for copy in loads:
        copy.start()
    for copy in loads:
        copy.wait()
    tok = tok_v[...].astype(F32)
    normed = tok * lax.rsqrt(jnp.mean(tok * tok, axis=1, keepdims=True) + EPS)
    gains.wait_recv()
    hidden = (normed * small_o[pl.ds(EXPERTS, 1), :].astype(F32)).astype(BF16)
    hid_o[...] = hidden
    cosine, sine = cos_v[...], sin_v[...]

    pass_on(0)
    pass_on(1)
    cot_across = remote(cot, cot_v.at[at.j], gs.at[2], gr.at[2], partner)
    cot_across.start()
    keeps[0].wait()
    keeps[1].wait()
    passed[0].wait_recv()
    key = dot_nn(hidden, wqkv[:, 1024:1536])
    key = turn(key, cosine, sine).astype(BF16)
    passed[1].wait_recv()
    value = dot_nn(hidden, wqkv[:, 1536:]).astype(BF16)
    width = key.shape[1]
    for half in range(2):
        own[half, :, :width] = key[half * rows : (half + 1) * rows]
        own[half, :, width:] = value[half * rows : (half + 1) * rows]

    def block_of(half, ctx):
        return kv.at[ctx] if half == 0 else kv.at[blocks - 1 - ctx]

    last = outers - 1
    hops = [(0, 0, 0)] + [
        (step, sign, step if sign < 0 else last + step)
        for step in range(1, outers)
        for sign in (-1, 1)
    ]

    def source(step, sign):
        return at.outer + sign * step

    def exists(step, sign):
        place = source(step, sign)
        return (place >= 0) & (place <= last)

    def block_from(half, step, sign, inner):
        place = lax.rem(source(step, sign) + outers, outers)
        return block_of(half, place * INNER + inner)

    below = (lax.rem(at.outer + last, outers) * INNER + at.inner, at.w)
    above = (lax.rem(at.outer + 1, outers) * INNER + at.inner, at.w)
    inner_side = at.inner + 2 - 4 * at.y

    def z_copy(half, slot, step, sign):
        src = own.at[half] if step == 0 else block_from(half, step, sign, at.inner)
        dst = block_from(half, step, sign, at.inner)
        slot_there = step + 1 if sign < 0 else last + step + 1
        return remote(
            src,
            dst,
            zs.at[half, slot_there],
            zr.at[half, slot_there],
            above if sign < 0 else below,
        )

    def y_copy(half, slot, step, sign):
        src = own.at[half] if step == 0 else block_from(half, step, sign, at.inner)
        dst = block_from(half, step, sign, at.inner)
        return remote(src, dst, ys.at[half, slot], yr.at[half, slot], at.beside)

    def c_copy(half, slot, step, sign, inner, base):
        src = (
            own.at[half]
            if step == 0 and base == 0
            else block_from(half, step, sign, inner)
        )
        dst = block_from(half, step, sign, inner)
        return remote(src, dst, cs.at[half, base + slot], cr.at[half, base + slot], sib)

    spots = 2 * outers - 1

    def spread_from(step, sign, slot, halves=(0, 1)):
        for half in halves:
            if step == 0:
                for way in (-1, 1):

                    @pl.when((at.outer < last) if way < 0 else (at.outer > 0))
                    def _():
                        z_copy(half, 0, 0, way).start()

            elif step < last:

                @pl.when((at.outer < last) if sign < 0 else (at.outer > 0))
                def _():
                    z_copy(half, slot, step, sign).start()

            y_copy(half, slot, step, sign).start()
            c_copy(half, slot, step, sign, at.inner, 0).start()

    spread_from(0, 0, 0)
    for half in range(2):
        keep = pltpu.make_async_copy(own.at[half], block_of(half, at.c), hs.at[half])
        keep.start()
        keeps.append(keep)

    def y_arrived(step, sign, slot):
        for half in range(2):
            y_copy(half, slot, step, sign).wait_recv()
            c_copy(half, slot, step, sign, inner_side, spots).start()

    def z_arrived(want):
        for step, sign, slot in hops[1:]:
            if step == want:

                @pl.when(exists(step, sign))
                def _():
                    for half in range(2):
                        z_copy(half, slot, step - 1, sign).wait_recv()
                        spread_from(step, sign, slot, (half,))

    def sides_arrived(want):
        for step, sign, slot in hops[1:]:
            if step == want:

                @pl.when(exists(step, sign))
                def _():
                    y_arrived(step, sign, slot)

    shape_expert(0)
    cot_across.wait_recv()
    give(2)
    cot_on = []

    def cot_pass(slot, j_from, device):
        block = cot_v.at[j_from]
        copy = remote(block, block, gs.at[slot], gr.at[slot], device)
        copy.start()
        cot_on.append(copy)

    cot_pass(3, j_partner, side)
    cot_pass(4, j_partner, sib)
    cot_side.wait_recv()
    cot_pass(5, j_side, sib)
    z_arrived(1)
    y_arrived(0, 0, 0)
    shape_expert(1)
    pass_on(2)
    give(3)
    shape_expert(2)
    if outers > 2:
        z_arrived(2)
    keeps[2].wait()
    passed[2].wait_recv()
    q_o[...] = turn(dot_nn(hidden, wqkv[:, :1024]), cosine, sine).astype(BF16)
    store = pltpu.make_async_copy(wqkv, wqkv_o, hs.at[2])
    store.start()
    shape_expert(3)
    sides_arrived(1)
    for step in range(3, outers):
        z_arrived(step)
        sides_arrived(step - 1)
    if outers > 2:
        sides_arrived(last)
    pass_on(3)
    cot_on[0].wait_recv()
    cot_pass(6, j_cross, sib)
    keeps[3].wait()
    passed[3].wait_recv()
    store_out = pltpu.make_async_copy(wout, wo_o, hs.at[3])
    store_out.start()
    def sibling_brought(step, sign, slot):
        for half in range(2):
            c_copy(half, slot, step, sign, at.inner, 0).wait_recv()
            c_copy(half, slot, step, sign, inner_side, spots).wait_recv()

    sibling_brought(0, 0, 0)
    for step, sign, slot in hops[1:]:

        @pl.when(exists(step, sign))
        def _():
            sibling_brought(step, sign, slot)

    for keep in keeps[4:]:
        keep.wait()
    store_kv = pltpu.make_async_copy(kv, kv_o, hs.at[4])
    store_kv.start()
    attend_rows(
        doc_starts(seg_ref[...]),
        q_o,
        kv,
        tok_v,
        wout,
        small_o,
        route_ref,
        prio_ref,
        raw_o,
        total_o,
        mixed_o,
        sum_o,
        hid_two,
        gate_o,
        kept_o,
        gate_send,
        acc,
        acc_l,
    )

    pairs = [(hid_two, hid), (gate_send, gates)]
    copies = gather_start(at, pairs, ts, tr, tl)
    for copy in [cot_sib] + cot_on[1:]:
        copy.wait_recv()
    cot_keep.wait()
    for copy in out_loads:
        copy.wait()
    tokens = cot_v.shape[0] * cot_v.shape[1]
    cot_rows = cot_v[...].reshape(tokens, D)
    cot_t[...] = cot_rows.T
    for e in range(OWN):
        backs[:, e * units : (e + 1) * units] = (RES_MULT * dot_nn(cot_rows, out_w[e])).astype(BF16)
    gather_wait(copies, gather_pass(at, pairs, copies, ts, tr))
    gate_columns(gates, cols)
    left_pairs = [(hid_o, left_o.at[0]), (mixed_o, left_o.at[1])]
    left_copies = gather_start(at, left_pairs, us, ur, ul)
    store_out.wait()
    passed[3].wait_send()
    hid_t = wout
    hid_t[...] = hid[...].reshape(tokens, D).T
    late = [slice(None)] * FIRST
    if far_first(outers):
        late[0] = pl.ds(units, 2 * units)
    y_sends = [
        remote(
            staged.at[e, :, :, 1 - at.y, :, late[e]],
            y_in.at[e, :, :, :, late[e]],
            vs.at[e],
            vr.at[e],
            at.beside,
        )
        for e in range(FIRST)
    ]
    upper = at.outer // 2
    if far_first(outers):
        far_send = remote(
            staged.at[0, 1 - upper, :, :, :, pl.ds(0, units)], za_in, fas, far_r, far_partner(at)
        )
    at_lane = lax.broadcasted_iota(jnp.int32, cols.shape, 1)
    pick_cols[...] = jnp.zeros(pick_cols.shape, F32)
    store.wait()
    for index in range(3):
        passed[index].wait_send()
    low_all = wqkv

    def expert(e, carry):
        wide = pl.ds(pl.multiple_of(e * 2 * units, 2 * units), 2 * units)
        tall = pl.ds(pl.multiple_of(e * units, units), units)
        many = tokens // PIECES
        groups = PLANE // PIECES
        for piece in range(PIECES):
            here = slice(piece * many, (piece + 1) * many)
            rows_in = hid[piece * groups : (piece + 1) * groups].reshape(many, D)
            both = dot_nn(rows_in, inner_w[:, wide])
            kept, pick, low = expert_step(
                both, backs[here, tall].astype(F32), lane_of(cols[here, :], experts + e), units
            )
            backs[here, tall] = kept
            low_all[here, wide] = low
            pick_cols[here, :] = jnp.where(at_lane[here] == e, pick, pick_cols[here, :])

        shape = staged.shape[1:5]
        staged[e, :, :, :, :, : 2 * units] = (
            dot_nn(hid_t[...], low_all[:, wide]).astype(BF16).reshape(*shape, 2 * units)
        )
        staged[e, :, :, :, :, 2 * units :] = (
            (RES_MULT * dot_nn(cot_t[...], backs[:, tall])).astype(BF16).reshape(*shape, units)
        )
        for now in range(OWN):

            @pl.when(e == now)
            def _():
                if now < FIRST:
                    y_sends[now].start()
                    if now == 0 and far_first(outers):
                        far_send.start()
                else:
                    pltpu.make_async_copy(
                        staged.at[now], grad_o.at[now - FIRST], gd.at[now - FIRST]
                    ).start()

        return carry

    lax.fori_loop(0, OWN, expert, 0)
    left_passed = gather_pass(at, left_pairs, left_copies, us, ur)
    count = hid.shape[1]
    for j in range(PLANE):
        pick_o[j] = pick_cols[j * count : (j + 1) * count, :].T[:8]
    store_kept = pltpu.make_async_copy(backs, kept_units_o, hs.at[5])
    store_kept.start()
    for j in range(0, PLANE, 4):
        here = slice(j * count, (j + 4) * count)
        rows_out = dot_nt(low_all[here, :], inner_w[...]).astype(BF16)
        hid[j : j + 4] = rows_out.reshape(4, count, D)
    store_part = pltpu.make_async_copy(hid, part_o, hs.at[6])
    store_part.start()

    def settle(step, sign, slot):
        for half in range(2):
            if step == 0:
                for way in (-1, 1):

                    @pl.when((at.outer < last) if way < 0 else (at.outer > 0))
                    def _():
                        z_copy(half, 0, 0, way).wait_send()

            elif step < last:

                @pl.when((at.outer < last) if sign < 0 else (at.outer > 0))
                def _():
                    z_copy(half, slot, step, sign).wait_send()

            y_copy(half, slot, step, sign).wait_send()
            c_copy(half, slot, step, sign, at.inner, 0).wait_send()
            c_copy(half, slot, step, sign, inner_side, spots).wait_send()

    settle(0, 0, 0)
    for step, sign, slot in hops[1:]:

        @pl.when(exists(step, sign))
        def _():
            settle(step, sign, slot)

    for copy in sends.values():
        copy.wait_send()
    for copy in [gains, cot_sib, cot_side, cot_across] + cot_on:
        copy.wait_send()
    for e in range(FIRST):
        y_sends[e].wait()
        total = staged[e, :, :, at.y, :, late[e]].astype(F32)
        total = total + y_in[e, :, :, :, late[e]].astype(F32)
        z_o[:, e, :, :, late[e]] = total.astype(BF16)
    if far_first(outers):
        far_send.wait()
        total = staged[0, upper, :, :, :, :units].astype(F32) + za_in[...].astype(F32)
        za_o[...] = total.astype(BF16)
    gather_wait(left_copies, left_passed)
    for copy in [store_kv, store_kept, store_part]:
        copy.wait()
    for e in range(FIRST, OWN):
        pltpu.make_async_copy(staged.at[e], grad_o.at[e - FIRST], gd.at[e - FIRST]).wait()


def opening(
    starts, tokens, wq, wk, wv, wo, small, cot, cosine, sine, routes, priority, expert_in, expert_out, ctx_count
):
    outers = ctx_count // INNER
    shape = jax.ShapeDtypeStruct
    count = tokens.shape[0]
    rows = count // 2
    width = wk.shape[1] + wv.shape[1]
    heads = wq.shape[1]
    wide = heads + width
    units = expert_out.shape[-1]
    many = PLANE * count
    blocks = 2 * ctx_count
    z_rows = D // (2 * outers)
    vm = pltpu.VMEM
    return comm_call(
        functools.partial(opening_kernel, outers),
        [
            shape((D, wide), BF16),
            shape((D, D), BF16),
            shape((small.shape[0], D), BF16),
            shape((count, heads), BF16),
            shape((count, D), BF16),
            shape((blocks, rows, width), BF16),
            shape((count, heads), F32),
            shape((count, heads), F32),
            shape((count, heads), BF16),
            shape((count, D), F32),
            shape((EXPERTS, count), F32),
            shape((EXPERTS, count), F32),
            shape((PLANE, 8, count), F32),
            shape((outers // 2, FIRST, 2, z_rows, 3 * units), BF16),
            shape((2, 2, z_rows, units), BF16),
            shape((PLANE, count, D), BF16),
            shape((many, OWN * units), BF16),
            shape((OWN - FIRST, outers // 2, 2, 2, z_rows, 3 * units), BF16),
            shape((2, PLANE, count, D), BF16),
        ],
        [VMEM] + [ANY] * 9 + [VMEM] * 2 + [ANY] * 2,
        [ANY] * 2 + [VMEM] * 3 + [ANY] + [VMEM] * 9 + [ANY] * 4,
        [
            vm((D, wide), BF16),
            vm((D, D), BF16),
            vm((2, rows, width), BF16),
            vm((count, D), BF16),
            vm(cosine.shape, F32),
            vm(sine.shape, F32),
            vm((blocks, rows, width), BF16),
            vm((PLANE, count, D), BF16),
            vm((2, D, 2, units), BF16),
            vm((OWN, D, units), BF16),
            vm((D, OWN * 2 * units), BF16),
            vm((PAIRS, 2 * count, 128), F32),
            vm((PAIRS, 2 * count, 128), F32),
            vm((count, D), BF16),
            vm((EXPERTS, count), F32),
            vm((PLANE, count, D), BF16),
            vm((PLANE, EXPERTS, count), F32),
            vm((D, many), BF16),
            vm((many, OWN * units), BF16),
            vm((many, 128), F32),
            vm((many, 128), F32),
            vm((OWN, outers // 2, 2, 2, z_rows, 3 * units), BF16),
            vm((FIRST, outers // 2, 2, z_rows, 3 * units), BF16),
            vm((2, 2, z_rows, units), BF16),
            DMA((5,)),
            DMA((5,)),
            DMA((4,)),
            DMA((4,)),
            DMA((4,)),
        ]
        + [DMA((2, 2 * outers))] * 4
        + [DMA((2, 4 * outers))] * 2
        + [DMA((8,)), DMA((7,)), DMA((7,)), DMA]
        + [DMA((2 + OWN,)), DMA((2, 7)), DMA((2, 7)), DMA((2,)), DMA((2,))]
        + [DMA((2, 7)), DMA((2, 7)), DMA((2,)), DMA((FIRST,)), DMA((FIRST,)), DMA, DMA],
        1,
        "opening",
        vmem=64 * 2**20,
        us=100,
    )(starts, tokens, wq, wk, wv, wo, small, cot, cosine, sine, routes, priority, expert_in, expert_out)


def turning_kernel(
    outers,
    seg_ref,
    z_ref,
    za_ref,
    grad_in,
    part_in,
    pick_send,
    kept_in,
    expert_out,
    gate_ref,
    kept_ref,
    small_ref,
    sum_in,
    cot_in,
    wo_in,
    raw_in,
    total_in,
    q_in,
    kv_in,
    cos_ref,
    sin_ref,
    dy_ref,
    da_ref,
    dq_ref,
    rows_ref,
    moe_o,
    near_o,
    z_o,
    dkv_ref,
    sum_ref,
    cot_ref,
    raw_ref,
    total_ref,
    q_ref,
    part,
    kept_all,
    out_w,
    wout,
    kv,
    near,
    far_in,
    picks_all,
    q_four,
    n_four,
    d_rows,
    dq_acc,
    kv_acc,
    kv_out,
    z_sums,
    z_in,
    y_own,
    y_in,
    za_own,
    za_in,
    ls,
    ss,
    sr,
    xs,
    xr,
    ps,
    pr,
    vs,
    vr,
    us,
    ur,
    ks,
    rs,
    zas,
    zar,
):
    at = Place()
    count = q_ref.shape[0]
    rows = count // 2
    width = PAIRS * 128
    keys = kv.shape[0] * rows
    units = out_w.shape[-1]
    experts = at.q * OWN
    loads = [
        pltpu.make_async_copy(src, dst, ls.at[index])
        for index, (src, dst) in enumerate(
            ((part_in, part), (kept_in, kept_all), (wo_in, wout), (kv_in, kv))
        )
    ]
    weights = [
        pltpu.make_async_copy(expert_out.at[experts + e], out_w.at[e], ls.at[4 + e])
        for e in range(OWN)
    ]
    for copy in loads + weights:
        copy.start()
    z_loads = [
        pltpu.make_async_copy(z_ref.at[:, e], z_sums.at[e, pl.ds(0, outers // 2)], rs.at[5 + e])
        for e in range(FIRST)
    ]
    za_load = pltpu.make_async_copy(za_ref.at[:, at.y], za_own, rs.at[5 + FIRST])
    for copy in z_loads + [za_load]:
        copy.start()
    late = [slice(None)] * FIRST
    if far_first(outers):
        late[0] = pl.ds(units, 2 * units)
    rest = [
        Halving(at, outers, z_sums.at[e], z_in.at[e], vs.at[e], vr.at[e], late[e])
        for e in range(FIRST)
    ]
    own_rows = []
    for e in range(OWN - FIRST):
        copy = pltpu.make_async_copy(
            grad_in.at[e, :, :, at.y], y_own.at[e], ls.at[4 + OWN + e]
        )
        copy.start()
        own_rows.append(copy)
    row_loads = [
        pltpu.make_async_copy(src, dst, rs.at[index])
        for index, (src, dst) in enumerate(
            (
                (sum_in, sum_ref),
                (cot_in, cot_ref),
                (raw_in, raw_ref),
                (total_in, total_ref),
                (q_in, q_ref),
            )
        )
    ]
    for copy in row_loads:
        copy.start()
    starts = doc_starts(seg_ref[...])
    meet(
        [at.relative(*bits)[0] for bits in OTHERS]
        + [at.beside]
        + [rest[0].device(bit) for bit in rest[0].bits]
    )
    for copy in z_loads:
        copy.wait()
    if outers > 2:
        rest[0].start(0)
    if far_first(outers):
        za_send = remote(za_ref.at[:, 1 - at.y], za_in, zas, zar, at.beside)
        za_send.start()
    sib, unused = at.relative(0, 1, 0)
    loads[0].wait()
    first = remote(part.at[:, 1 - at.core], near, ss, sr, sib)
    first.start()
    y_sends = []
    for e in range(OWN - FIRST):
        copy = remote(grad_in.at[e, :, :, 1 - at.y], y_in.at[e], us.at[e], ur.at[e], at.beside)
        copy.start()
        y_sends.append(copy)
    small_copies = []
    for slot, bits in enumerate(OTHERS):
        device, j_to = at.relative(*bits)
        copy = remote(pick_send.at[j_to], picks_all.at[at.j], ps.at[slot], pr.at[slot], device)
        copy.start()
        small_copies.append(copy)
    picks_all[at.j] = pick_send[at.j]
    first.wait_recv()
    for y in range(2):
        for w in range(2):
            total = part[y, at.core, w].astype(F32) + near[y, w].astype(F32)
            near[y, w] = total.astype(BF16)
    second = []
    for slot, (dy, dc, dw) in enumerate(XY):
        device, unused = at.relative(dy, dc, dw)
        z = at.z + dy * (1 - 2 * at.z)
        w = at.w + dw * (1 - 2 * at.w)
        copy = remote(near.at[z, w], far_in.at[slot], xs.at[slot], xr.at[slot], device)
        copy.start()
        second.append(copy)

    loads[1].wait()
    for copy in weights + row_loads:
        copy.wait()

    def moe_rows(j, carry):
        here = pl.ds(pl.multiple_of(j * count, count), count)
        total = dot_nt(kept_all[here, :units], out_w[0])
        for e in range(1, OWN):
            total = total + dot_nt(kept_all[here, e * units : (e + 1) * units], out_w[e])
        moe_o[j] = total.astype(BF16)
        return carry

    lax.fori_loop(0, PLANE, moe_rows, 0)
    hidden_sum = near[at.z, at.w].astype(F32)
    for slot in range(3):
        second[slot].wait_recv()
        hidden_sum = hidden_sum + far_in[slot].astype(F32)
    if outers > 2:
        for halving in rest[1:]:
            halving.start(0)
    for copy in [first] + second:
        copy.wait_send()
    small = small_ref[...]
    gain_two = small[EXPERTS + 1 : EXPERTS + 2].astype(F32)
    for copy in small_copies:
        copy.wait()
    parts = []
    for i in range(INNER):
        parts.append(picks_all[2 * i, pl.ds(0, OWN), :] + picks_all[2 * i + 1, pl.ds(0, OWN), :])
    gate = gate_ref[...]
    gate_grad = kept_ref[...] * jnp.concatenate(parts, axis=0)
    logit_grad = gate * (gate_grad - jnp.sum(gate * gate_grad, axis=0, keepdims=True))
    logit_grad = jnp.concatenate(
        [logit_grad, jnp.zeros((small.shape[0] - EXPERTS, count), F32)], axis=0
    ).astype(BF16)
    hidden_grad = hidden_sum + dot_tn(logit_grad, small)
    first_sum = sum_ref[...]
    scale = lax.rsqrt(jnp.mean(first_sum * first_sum, axis=1, keepdims=True) + EPS)
    normed = first_sum * scale
    hidden = (normed * gain_two).astype(BF16)
    router_rows = dot_nn(logit_grad, hidden)
    rows_ref[...] = router_rows
    rows_ref[pl.ds(EXPERTS + 1, 1), :] = jnp.sum(hidden_grad * normed, axis=0, keepdims=True)
    normed_grad = hidden_grad * gain_two
    first_grad = cot_ref[...].astype(F32) + scale * (
        normed_grad - normed * jnp.mean(normed_grad * normed, axis=1, keepdims=True)
    )
    dy_ref[...] = first_grad
    attn_grad = (RES_MULT * first_grad).astype(BF16)
    da_ref[...] = attn_grad
    loads[2].wait()
    mixed_grad = dot_nt(attn_grad, wout[...]).astype(BF16).astype(F32)
    total = total_ref[...]
    numer = mixed_grad / total
    lost = mixed_grad * raw_ref[...] / total
    for half in range(2):
        here = slice(half * rows, (half + 1) * rows)
        for pair in range(PAIRS):
            cols = slice(pair * 256, (pair + 1) * 256)
            slot = half * PAIRS + pair
            q_four[slot] = spread(q_ref[here, cols].astype(F32) * ATT_MULT).astype(BF16)
            n_four[slot] = spread(numer[here, cols]).astype(BF16)
            d_rows[slot] = -jnp.sum(spread(lost[here, cols]).T, axis=0, keepdims=True)
    dq_acc[...] = jnp.zeros_like(dq_acc)
    loads[3].wait()

    def kv_store(chunk):
        many = CHUNK // rows
        return pltpu.make_async_copy(
            kv_out.at[chunk % 2], dkv_ref.at[pl.ds(chunk * many, many)], ks.at[chunk % 2]
        )

    def step(chunk, carry):
        at_row = pl.multiple_of(chunk * CHUNK, CHUNK)
        kv_acc[...] = jnp.zeros_like(kv_acc)
        key_pos = at_row + lax.broadcasted_iota(jnp.int32, (CHUNK, 1), 0)
        for half in range(2):
            base, chunks = half_span(half, rows, keys)

            @pl.when(chunk < chunks)
            def _():
                place = base + lax.broadcasted_iota(jnp.int32, (1, 4 * rows), 1) % rows
                first = reach(starts, place)
                bias = jnp.where((key_pos >= first) & (key_pos <= place), 0.0, NEVER)
                for pair in range(PAIRS):
                    slot = half * PAIRS + pair
                    key = key_block(kv, chunk, rows, pair * 128)
                    value = key_block(kv, chunk, rows, width + pair * 128)
                    e = jnp.exp(dot_nt(key, q_four[slot]) + bias)
                    through = dot_nt(value, n_four[slot])
                    dz = (e * (through + d_rows[slot])).astype(BF16)
                    kv_acc[:, pl.ds(pair * 128, 128)] += dot_nn(dz, q_four[slot])
                    kv_acc[:, pl.ds(width + pair * 128, 128)] += dot_nn(e.astype(BF16), n_four[slot])
                    dq_acc[slot] += dot_tn(dz, key)

        many = CHUNK // rows

        @pl.when(chunk >= 2)
        def _():
            kv_store(chunk - 2).wait()

        kv_out[chunk % 2] = kv_acc[...].astype(BF16).reshape(many, rows, 2 * width)
        kv_store(chunk).start()
        return carry

    lax.fori_loop(0, keys // CHUNK, step, 0)
    cosine = cos_ref[...]
    sine = -sin_ref[...]
    for half in range(2):
        here = slice(half * rows, (half + 1) * rows)
        for pair in range(PAIRS):
            block = ATT_MULT * unspread(dq_acc[half * PAIRS + pair])
            dq_ref[here, pair * 256 : (pair + 1) * 256] = turn(
                block, cosine[here], sine[here]
            ).astype(BF16)
    for chunk in range(keys // CHUNK - 2, keys // CHUNK):
        kv_store(chunk).wait()
    for e in range(FIRST):
        near_o[e, :, :, late[e]] = rest[e].finish()
    za_load.wait()
    if far_first(outers):
        za_send.wait()
        total = za_own[...].astype(F32) + za_in[...].astype(F32)
        near_o[0, :, :, :units] = total.astype(BF16)
    for copy in own_rows:
        copy.wait()
    for e in range(OWN - FIRST):
        y_sends[e].wait()
        total = y_own[e].astype(F32) + y_in[e].astype(F32)
        z_o[:, e] = total.astype(BF16)


def turning(
    outers, segments, z_first, z_far, grads, part, picks, kept_units, expert_out, gate, kept, small, first_sum, cot, output_w, raw, total, queries, kv_all, cosine, sine
):
    shape = jax.ShapeDtypeStruct
    count, width = queries.shape
    units = expert_out.shape[-1]
    vm = pltpu.VMEM
    return comm_call(
        functools.partial(turning_kernel, outers),
        [
            shape((count, D), F32),
            shape((count, D), BF16),
            shape((count, width), BF16),
            shape((32, D), F32),
            shape((PLANE, count, D), BF16),
            shape(z_first.shape[1:], BF16),
            shape((outers // 2, OWN - FIRST) + z_first.shape[2:], BF16),
            shape(kv_all.shape, BF16),
        ],
        [VMEM] + [ANY] * 4 + [VMEM] + [ANY] * 2 + [VMEM] * 3 + [ANY] * 7 + [VMEM] * 2,
        [VMEM] * 7 + [ANY],
        [
            vm((count, D), F32),
            vm((count, D), BF16),
            vm((count, width), F32),
            vm((count, width), F32),
            vm((count, width), BF16),
            vm((2, 2, 2, count, D), BF16),
            vm(kept_units.shape, BF16),
            vm((OWN, D, units), BF16),
            vm((D, D), BF16),
            vm(kv_all.shape, BF16),
            vm((2, 2, count, D), BF16),
            vm((3, count, D), BF16),
            vm((PLANE, 8, count), F32),
            vm((2 * PAIRS, 2 * count, 128), BF16),
            vm((2 * PAIRS, 2 * count, 128), BF16),
            vm((2 * PAIRS, 1, 2 * count), F32),
            vm((2 * PAIRS, 2 * count, 128), F32),
            vm((CHUNK, 2 * PAIRS * 128), F32),
            vm((2, CHUNK // (count // 2), count // 2, 2 * PAIRS * 128), BF16),
            vm((FIRST, outers) + z_first.shape[2:], BF16),
            vm((FIRST, outers) + z_first.shape[2:], BF16),
            vm((OWN - FIRST, outers // 2) + z_first.shape[2:], BF16),
            vm((OWN - FIRST, outers // 2) + z_first.shape[2:], BF16),
            vm(z_far.shape[:1] + z_far.shape[2:], BF16),
            vm(z_far.shape[:1] + z_far.shape[2:], BF16),
            DMA((4 + OWN + OWN - FIRST,)),
            DMA,
            DMA,
            DMA((3,)),
            DMA((3,)),
            DMA((7,)),
            DMA((7,)),
            DMA((FIRST, outers)),
            DMA((FIRST, outers)),
            DMA((OWN - FIRST,)),
            DMA((OWN - FIRST,)),
            DMA((2,)),
            DMA((6 + FIRST,)),
            DMA,
            DMA,
        ],
        5,
        "turning",
        vmem=62 * 2**20,
        us=35,
    )(
        segments,
        z_first,
        z_far,
        grads,
        part.reshape(2, 2, 2, count, D),
        picks,
        kept_units,
        expert_out,
        gate,
        kept,
        small,
        first_sum,
        cot,
        output_w,
        raw,
        total,
        queries,
        kv_all,
        cosine,
        sine,
    )


def assemble_kernel(outers, counts, *refs):
    size = 2 + len(counts)
    sources, refs = refs[:size], refs[size:]
    wq, wk, wv, wo, router, gain_one, gain_two, inner, outer = refs[:9]
    held, sems = refs[9 : 9 + size], refs[9 + size]
    loads = [
        pltpu.make_async_copy(sources[k], held[k], sems.at[k]) for k in range(size)
    ]
    for copy in loads:
        copy.start()
    attn_in, small_in = held[:2]
    for copy in loads:
        copy.wait()
    experts = [(near, k) for near, many in zip(held[2:], counts) for k in range(many)]
    qkv_cols = wq.shape[1] * 2 // PLANE
    devices = outers * PLANE
    for j in range(PLANE):
        z, core, w = j // 4, (j // 2) % 2, j % 2
        total = 0.0
        for above in range(outers // 2):
            for y in range(2):
                source = (((above * 2 + z) * 2 + y) * 2 + core) * 2 + w
                total = total + attn_in[source].astype(F32)
        col = j * qkv_cols
        ref, base = (wq, 0) if col < 1024 else (wk, 1024) if col < 1536 else (wv, 1536)
        ref[:, col - base : col - base + qkv_cols] = total[:, :qkv_cols]
        wo[:, j * (D // PLANE) : (j + 1) * (D // PLANE)] = total[:, qkv_cols:]
    total = small_in[0].astype(F32)
    for i in range(1, devices):
        total = total + small_in[i].astype(F32)
    turned = total.T
    router[...] = turned[:EXPERTS]
    gain_one[...] = turned[EXPERTS : EXPERTS + 1]
    gain_two[...] = turned[EXPERTS + 1 : EXPERTS + 2]
    rows = wq.shape[0]
    units = outer.shape[-1] // 2
    for j in range(PLANE):
        cols = slice((j % 2) * units, (j % 2 + 1) * units)
        for k in range(OWN):
            e = (j // 2) * OWN + k
            near, at = experts[k]
            block = near[j, at].astype(F32)
            inner[e, :, :, cols] = block[:, : 2 * units].reshape(rows, 2, units)
            outer[e, :, cols] = block[:, 2 * units :]


def assemble(attn_in, small_in, nears, outers):
    rows = attn_in.shape[1]
    units = nears[0].shape[-1] // 3
    sources = [attn_in, small_in] + nears
    shape = jax.ShapeDtypeStruct
    outs = [
        shape((rows, 1024), F32),
        shape((rows, 512), F32),
        shape((rows, 512), F32),
        shape((rows, D), F32),
        shape((EXPERTS, rows), F32),
        shape((1, rows), F32),
        shape((1, rows), F32),
        shape((EXPERTS, rows, 2, 2 * units), F32),
        shape((EXPERTS, rows, 2 * units), F32),
    ]
    return pl.pallas_call(
        functools.partial(assemble_kernel, outers, [near.shape[1] for near in nears]),
        out_shape=outs,
        in_specs=[ANY] * len(sources),
        out_specs=[VMEM] * 9,
        scratch_shapes=[pltpu.VMEM(a.shape, a.dtype) for a in sources] + [DMA((len(sources),))],
        compiler_params=pltpu.CompilerParams(vmem_limit_bytes=60 * 2**20),
        name="assemble",
    )(*sources)


def body(
    tokens,
    w_query,
    w_key,
    w_value,
    w_output,
    attn_gain,
    w_router,
    expert_in,
    expert_out,
    moe_gain,
    segments,
    routes,
    priority,
    cotangent,
):
    ctx_count = lax.axis_size("ctx")
    ctx_index = lax.axis_index("ctx")
    devices = ctx_count * 2
    outers = ctx_count // INNER
    owner_rows = D // devices
    block_rows = tokens.shape[2]
    half_rows = block_rows * ctx_count
    tok_count = 2 * block_rows
    f32 = jnp.float32
    bf16 = jnp.bfloat16

    small = jnp.concatenate(
        [w_router.T, attn_gain[None], moe_gain[None], jnp.zeros((14, w_router.shape[0]), bf16)]
    )
    cot_own = cotangent.reshape(tok_count, D)
    block_total = 2 * ctx_count
    block_ids = jnp.stack([ctx_index, block_total - 1 - ctx_index])
    query_pos = block_ids[:, None] * block_rows + jnp.arange(block_rows, dtype=jnp.int32)[None, :]
    flat_pos = query_pos.reshape(tok_count)
    frequency = jnp.exp(
        -jnp.log(jnp.float32(THETA))
        * jnp.arange(HEAD_DIM // 2, dtype=jnp.float32)
        * (2.0 / HEAD_DIM)
    )
    angles = flat_pos.astype(f32)[:, None] * frequency[None, :]
    cosine, sine = jnp.cos(angles), jnp.sin(angles)
    cosine = jnp.concatenate([cosine] * 4, axis=1)
    sine = jnp.concatenate([-sine, sine] * 2, axis=1)
    token_low = tokens.reshape(tok_count, D)
    (
        qkv_w,
        output_w,
        small_all,
        queries,
        hidden_one,
        kv_all,
        attn_raw,
        attn_total,
        mixed,
        first_sum,
        gate,
        kept,
        picks,
        first_half,
        first_far,
        part,
        kept_units,
        expert_grads,
        left,
    ) = opening(
        segments,
        token_low,
        w_query,
        w_key,
        w_value,
        w_output,
        small,
        cot_own,
        cosine,
        sine,
        routes[0].transpose(0, 2, 1),
        priority[0].transpose(0, 2, 1),
        expert_in,
        expert_out,
        ctx_count,
    )
    (
        first_grad,
        attn_grad,
        query_lin_grad,
        small_rows,
        moe_part,
        near_one,
        second_half,
        kv_terms,
    ) = turning(
        outers,
        segments,
        first_half,
        first_far,
        expert_grads,
        part,
        picks,
        kept_units,
        expert_out,
        gate,
        kept,
        small_all,
        first_sum,
        cot_own,
        output_w,
        attn_raw,
        attn_total,
        queries,
        kv_all,
        cosine,
        sine,
    )
    output, token_grad, attn_part, small_part, near_first, near_next, near = finish(
        kv_terms,
        moe_part,
        [
            first_sum,
            query_lin_grad,
            attn_grad,
            first_grad,
            token_low,
            small_all,
            cosine,
            sine,
            qkv_w,
            left,
            small_rows,
        ],
        second_half,
        near_one.reshape(FIRST, PLANE, owner_rows, -1),
        ctx_count,
    )
    attn_in, small_in, near_last = owners(
        [attn_part, small_part],
        [near.reshape(-1, PLANE, owner_rows, near.shape[-1])],
        devices,
        7,
        "owners",
    )
    (
        query_sum,
        key_sum,
        value_sum,
        output_sum,
        router_sum,
        gain_one_sum,
        gain_two_sum,
        inner_sum,
        outer_sum,
    ) = assemble(attn_in, small_in, [near_first, near_next, near_last], outers)
    return (
        output.reshape(tokens.shape),
        token_grad.reshape(tokens.shape),
        query_sum,
        key_sum,
        value_sum,
        output_sum,
        gain_one_sum[0],
        router_sum.T,
        inner_sum,
        outer_sum,
        gain_two_sum[0],
    )


def solution(mesh):
    placed = (
        P("wsh", None, "ctx", None),
        P("wsh", None),
        P("wsh", None),
        P("wsh", None),
        P("wsh", None),
        P("wsh"),
        P("wsh", None),
        P(None, None, None, "wsh"),
        P(None, None, "wsh"),
        P("wsh"),
        P("wsh", None),
        P("wsh", None, "ctx", None),
        P("wsh", None, "ctx", None),
        P("wsh", None, "ctx", None),
    )
    return jax.shard_map(
        body,
        mesh=mesh,
        in_specs=placed,
        out_specs=(
            P("wsh", None, "ctx", None),
            P("wsh", None, "ctx", None),
            P(("ctx", "wsh"), None),
            P(("ctx", "wsh"), None),
            P(("ctx", "wsh"), None),
            P(("ctx", "wsh"), None),
            P(("ctx", "wsh")),
            P(("ctx", "wsh"), None),
            P(None, ("ctx", "wsh"), None, None),
            P(None, ("ctx", "wsh"), None),
            P(("ctx", "wsh")),
        ),
        check_vma=False,
    )
```
